32 devices in a mesh: dp: 4 (over x, core), ctx: 2 (over y), tensor: 4 (over z).
Axes of the slice: x: 2, y: 2, z: 4, core: 2. Of those that a mesh axis runs over, the one named last changes fastest.
Arguments:
- block_input: bfloat16 [8, 1024, 2048], P('dp', 'ctx'), may hold values from -6 to 6
- out_grad: bfloat16 [8, 1024, 2048], P('dp', 'ctx'), may hold values from -6 to 6
- lengths: int32 [8], P('dp'), may hold values from 256 to 1024, as said below
- attn_gain: float32 [2048], replicated, may hold values from 0.5 to 1.5
- attn_shift: float32 [2048], replicated, may hold values from -2 to 2
- ffn_gain: float32 [2048], replicated, may hold values from 0.5 to 1.5
- ffn_shift: float32 [2048], replicated, may hold values from -2 to 2
- w_qkv: float32 [2048, 6144], P(('dp', 'ctx'), 'tensor'), may hold values from -0.125 to 0.125
- b_qkv: float32 [6144], P('tensor'), may hold values from -2 to 2
- w_proj: float32 [2048, 2048], P('tensor', ('dp', 'ctx')), may hold values from -0.5 to 0.5
- b_proj: float32 [2048], replicated, may hold values from -2 to 2
- w_in: float32 [2048, 8192], P(('dp', 'ctx'), 'tensor'), may hold values from -0.125 to 0.125
- b_in: float32 [8192], P('tensor'), may hold values from -2 to 2
- w_out: float32 [8192, 2048], P('tensor', ('dp', 'ctx')), may hold values from -0.0625 to 0.0625
- b_out: float32 [2048], replicated, may hold values from -2 to 2
Outputs:
- block_output: bfloat16 [8, 1024, 2048], P('dp', 'ctx')
- input_grad: bfloat16 [8, 1024, 2048], P('dp', 'ctx')
- grad_attn_gain: float32 [2048], replicated
- grad_attn_shift: float32 [2048], replicated
- grad_ffn_gain: float32 [2048], replicated
- grad_ffn_shift: float32 [2048], replicated
- grad_w_qkv: float32 [2048, 6144], P(('dp', 'ctx'), 'tensor')
- grad_b_qkv: float32 [6144], P('tensor')
- grad_w_proj: float32 [2048, 2048], P('tensor', ('dp', 'ctx'))
- grad_b_proj: float32 [2048], replicated
- grad_w_in: float32 [2048, 8192], P(('dp', 'ctx'), 'tensor')
- grad_b_in: float32 [8192], P('tensor')
- grad_w_out: float32 [8192, 2048], P('tensor', ('dp', 'ctx'))
- grad_b_out: float32 [2048], replicated
The draws below stay inside these ranges and needn't reach their ends.
Inputs may be any that keep to these rules, and one draw needn't show every extreme that they name: `lengths`: one slot has exactly 1024 valid positions and one exactly a quarter of 1024.
All inputs are finite; a program needn't handle non-finite values.
Results may differ from the reference program's by a relative error of at most 0.014.
Values may be sent and summed in bfloat16 or wider, within the bound.
No kernel may reach another device: no remote copies, remote signals or barrier semaphores. Data moves between devices by JAX's collectives and lax.ppermute only.
A program may use at most 256 MiB of HBM per device.

```python
import math
import jax
import jax.numpy as jnp
from jax import lax

D = 2048
HEADS = 8
HD = 256
ROT = 64
FF = 8192
SEQ = 1024
SLOTS = 8


def draw_lengths(key, part):
    base = jax.random.randint(key, (SLOTS,), SEQ // 4, SEQ + 1, dtype=jnp.int32)
    order = jax.random.permutation(jax.random.fold_in(key, 1), SLOTS)
    base = base.at[order[0]].set(SEQ)
    base = base.at[order[1]].set(SEQ // 4)
    return base.astype(jnp.int32)


def block_levels(rng, extent, cuts, low, top_value):
    gain = 1.0
    for dim, shards_of in cuts:
        draws = jax.random.uniform(jax.random.fold_in(jax.random.fold_in(rng, 6), dim), (shards_of,), jnp.float32, low / len(cuts), top_value / len(cuts))
        gain = gain * jnp.repeat(jnp.exp(draws), extent[dim] // shards_of).reshape((-1,) + (1,) * (len(extent) - 1 - dim))
    return gain


def gaussian(key, extent, scale, limit, pieces=(), kind=jnp.bfloat16):
    factor_of = block_levels(key, extent, pieces, -0.22, 0.18) if pieces else 1.0
    drawn = jax.random.normal(key, extent, jnp.float32) * scale * factor_of
    return jnp.minimum(jnp.maximum(drawn, -limit), limit).astype(kind)


def setup_inputs(seed: int = 0) -> dict:
    key_of = jax.random.split(jax.random.key(seed), 16)
    block_input = gaussian(key_of[0], (SLOTS, SEQ, D), 1.0, 6.0, ((0, 4), (1, 2)))
    out_grad = gaussian(key_of[1], (SLOTS, SEQ, D), 1.0, 6.0, ((0, 4), (1, 2)))
    lengths = draw_lengths(jax.random.fold_in(key_of[15], 71), 0)
    attn_gain = jnp.clip(1.0 + 0.1 * jax.random.normal(key_of[3], (D,), jnp.float32), 0.5, 1.5)
    attn_shift = gaussian(key_of[4], (D,), 0.3, 2.0, (), jnp.float32)
    ffn_gain = jnp.clip(1.0 + 0.1 * jax.random.normal(key_of[5], (D,), jnp.float32), 0.5, 1.5)
    ffn_shift = gaussian(key_of[6], (D,), 0.3, 2.0, (), jnp.float32)
    w_qkv = gaussian(key_of[7], (D, 3 * D), D ** -0.5, 0.125, ((0, 8), (1, 4)), jnp.float32)
    b_qkv = gaussian(key_of[8], (3 * D,), 0.3, 2.0, ((0, 4),), jnp.float32)
    w_proj = gaussian(key_of[9], (D, D), (D // 16) ** -0.5, 0.5, ((0, 4), (1, 8)), jnp.float32)
    b_proj = gaussian(key_of[10], (D,), 0.3, 2.0, (), jnp.float32)
    w_in = gaussian(key_of[11], (D, FF), D ** -0.5, 0.125, ((0, 8), (1, 4)), jnp.float32)
    b_in = gaussian(key_of[12], (FF,), 0.3, 2.0, ((0, 4),), jnp.float32)
    w_out = gaussian(key_of[13], (FF, D), FF ** -0.5, 0.0625, ((0, 4), (1, 8)), jnp.float32)
    b_out = gaussian(key_of[14], (D,), 0.3, 2.0, (), jnp.float32)
    return {"block_input": block_input, "out_grad": out_grad, "lengths": lengths, "attn_gain": attn_gain, "attn_shift": attn_shift, "ffn_gain": ffn_gain, "ffn_shift": ffn_shift, "w_qkv": w_qkv, "b_qkv": b_qkv, "w_proj": w_proj, "b_proj": b_proj, "w_in": w_in, "b_in": b_in, "w_out": w_out, "b_out": b_out}


@jax.custom_vjp
def low(v):
    return lax.optimization_barrier(v.astype(jnp.bfloat16)).astype(jnp.float32)

@jax.custom_vjp
def low_back(v):
    return v

def low_keep(v):
    return (low(v), None)

def low_pass(kept, grad):
    return (grad,)

def back_keep(v):
    return (v, None)

def back_low(kept, grad):
    return (low(grad),)
low.defvjp(low_keep, low_pass)
low_back.defvjp(back_keep, back_low)
exact_prec = lax.Precision.HIGHEST
neg_big = -1e+30

def matmul(left_side, right_side):
    return jnp.dot(left_side, right_side, precision=exact_prec, preferred_element_type=jnp.float32)

def rotary_tables(positions):
    half_rot = ROT // 2
    exponent = jnp.arange(half_rot, dtype=jnp.float32) * (2.0 / ROT)
    inv_freq = jnp.exp(-math.log(10000.0) * exponent)
    angles = positions[:, None] * inv_freq[None, :]
    return (jnp.cos(angles), jnp.sin(angles))

def rotate(values, cos_tab, sine_tab):
    half_rot = ROT // 2
    first_half = values[..., :half_rot]
    second = values[..., half_rot:ROT]
    cos_b = cos_tab[:, None, :]
    sin_b = sine_tab[:, None, :]
    return jnp.concatenate([first_half * cos_b - second * sin_b, second * cos_b + first_half * sin_b, values[..., ROT:]], axis=-1)

def attend_block(block_index, queries, keys_in, values_in, length):
    q_block = math.gcd(SEQ, 512)
    key_pos = jnp.arange(SEQ, dtype=jnp.int32)
    row_block = lax.dynamic_slice_in_dim(queries, block_index * q_block, q_block, 0)
    scores = jnp.einsum('qhd,khd->hqk', row_block, keys_in, precision=exact_prec) * (1.0 / math.sqrt(HD))
    scores = low_back(scores)
    query_pos = block_index * q_block + jnp.arange(q_block, dtype=jnp.int32)
    allowed = (key_pos[None, :] <= query_pos[:, None]) & (key_pos[None, :] < length)
    masked = jnp.where(allowed[None], scores, neg_big)
    row_top = lax.optimization_barrier(jnp.max(masked, axis=-1, keepdims=True))
    expo_vals = jnp.where(allowed[None], jnp.exp(masked - row_top), 0.0)
    probs_f = expo_vals / lax.optimization_barrier(jnp.sum(expo_vals, axis=-1, keepdims=True))
    return jnp.einsum('hqk,khd->qhd', low(probs_f), values_in, precision=exact_prec)

def attend_slot(packed):
    queries, keys_in, values_in, length = packed
    q_block = math.gcd(SEQ, 512)
    checked = jax.checkpoint(attend_block)

    def one_block(block_index):
        return checked(block_index, queries, keys_in, values_in, length)
    blocks_out = lax.map(one_block, jnp.arange(SEQ // q_block, dtype=jnp.int32))
    return blocks_out.reshape(SEQ, HEADS, HD)

def forward(inputs, attn_gain, attn_shift, ffn_gain, ffn_shift, w_qkv, b_qkv, w_proj, b_proj, w_in, b_in, w_out, b_out, lengths):
    positions = jnp.arange(SEQ, dtype=jnp.int32)
    valid_mask = (positions[None, :] < lengths[:, None]).astype(jnp.float32)[..., None]
    row_mean = lax.optimization_barrier(jnp.mean(inputs, axis=-1, keepdims=True))
    centered = inputs - row_mean
    inv_std = lax.rsqrt(lax.optimization_barrier(jnp.mean(centered * centered, axis=-1, keepdims=True)) + 1e-05)
    normed = centered * inv_std
    attn_in = low(normed * attn_gain + attn_shift).reshape(-1, D)
    ffn_in = low(normed * ffn_gain + ffn_shift).reshape(-1, D)
    qkv = low_back(matmul(attn_in, low(w_qkv)) + b_qkv).reshape(SLOTS, SEQ, HEADS, 3, HD)
    cos_tab, sine_tab = rotary_tables(positions.astype(jnp.float32))
    queries = low(rotate(qkv[:, :, :, 0], cos_tab, sine_tab))
    keys_in = low(rotate(qkv[:, :, :, 1], cos_tab, sine_tab))
    values_in = low(qkv[:, :, :, 2])
    attended = lax.map(attend_slot, (queries, keys_in, values_in, lengths))
    attended = low(low_back(attended)).reshape(-1, D)
    hidden = low_back(matmul(ffn_in, low(w_in)) + b_in)
    activated = low(jax.nn.gelu(hidden, approximate=False))
    summed = matmul(attended, low(w_proj)) + matmul(activated, low(w_out))
    return valid_mask * (inputs + (summed + b_proj + b_out).reshape(SLOTS, SEQ, D))

def reference(block_input, out_grad, lengths, attn_gain, attn_shift, ffn_gain, ffn_shift, w_qkv, b_qkv, w_proj, b_proj, w_in, b_in, w_out, b_out):
    inputs = block_input.astype(jnp.float32)
    cotangent = out_grad.astype(jnp.float32)

    def closed(inputs_f, gain_a, shift_a, gain_f, shift_f, wq_f, bq_f, wp_f, bp_f, wi_f, bi_f, wo_f, bo_f):
        return forward(inputs_f, gain_a, shift_a, gain_f, shift_f, wq_f, bq_f, wp_f, bp_f, wi_f, bi_f, wo_f, bo_f, lengths)
    result, pullback = jax.vjp(closed, inputs, attn_gain, attn_shift, ffn_gain, ffn_shift, w_qkv, b_qkv, w_proj, b_proj, w_in, b_in, w_out, b_out)
    grads = pullback(cotangent)
    return (result.astype(jnp.bfloat16), grads[0].astype(jnp.bfloat16), grads[1], grads[2], grads[3], grads[4], grads[5], grads[6], grads[7], grads[8], grads[9], grads[10], grads[11], grads[12])
```

```python
import functools
import math

import jax
import jax.numpy as jnp
from jax import lax
from jax.experimental import pallas as pl
from jax.experimental.pallas import tpu as pltpu
from jax.sharding import PartitionSpec as P

HD = 256
ROT = 64
NBLK = 8
BF = jnp.bfloat16
F32 = jnp.float32

neg_big = -1e30
inv_sqrt_two = 0.7071067811865476
inv_sqrt_tau = 0.3989422804014327


def cost(flops, nbytes, trans=0):
    return pl.CostEstimate(flops=int(flops), bytes_accessed=int(nbytes), transcendentals=int(trans))


def params(n, mb=60):
    return pltpu.CompilerParams(
        dimension_semantics=("arbitrary",) * n, vmem_limit_bytes=int(mb * 1024 * 1024)
    )


def nn(a, b):
    return lax.dot_general(a, b, (((1,), (0,)), ((), ())), preferred_element_type=F32)


def nt(a, b):
    return lax.dot_general(a, b, (((1,), (1,)), ((), ())), preferred_element_type=F32)


def tn(a, b):
    return lax.dot_general(a, b, (((0,), (0,)), ((), ())), preferred_element_type=F32)


def block_cols(r):
    return pl.ds(pl.multiple_of(r, 128), 256)


def row_valid(meta, row0, rows, local_len):
    slot = row0 // local_len
    pos = meta[0] * local_len + row0 % local_len + lax.broadcasted_iota(jnp.int32, (rows, 1), 0)
    return (pos < meta[2 + NBLK + slot]).astype(F32)


def norm_kernel(local_len, meta, x_ref, g_ref, ga, sa, gf, sf, h1_ref, h2_ref, g_out, st_ref, gs_ref):
    rows = x_ref.shape[0]
    i = pl.program_id(0)
    x = x_ref[...].astype(F32)
    mean = jnp.mean(x, axis=-1, keepdims=True)
    cen = x - mean
    inv = lax.rsqrt(jnp.mean(cen * cen, axis=-1, keepdims=True) + 1e-05)
    mask = row_valid(meta, i * rows, rows, local_len)
    lane = lax.broadcasted_iota(jnp.int32, (rows, 128), 1)
    st_ref[...] = jnp.where(lane == 0, mean, inv)
    for r in range(NBLK):
        src = block_cols(meta[1 + r] * 256)
        dst = slice(r * 256, (r + 1) * 256)
        xh = (x_ref[:, src].astype(F32) - mean) * inv
        h1_ref[:, dst] = (xh * ga[:, src] + sa[:, src]).astype(BF)
        h2_ref[:, dst] = (xh * gf[:, src] + sf[:, src]).astype(BF)
        gm = g_ref[:, src].astype(F32) * mask
        g_out[:, dst] = gm.astype(BF)
        part = jnp.sum(gm, axis=0, keepdims=True)

        @pl.when(i == 0)
        def _():
            gs_ref[:, src] = part

        @pl.when(i > 0)
        def _():
            gs_ref[:, src] = gs_ref[:, src] + part


def norm_call(meta, x2, g2, ga, sa, gf, sf, local_len):
    m, d = x2.shape
    rows = 256
    row_spec = pl.BlockSpec((rows, d), lambda i, mt: (i, 0))
    vec = pl.BlockSpec((1, d), lambda i, mt: (0, 0))
    return pl.pallas_call(
        functools.partial(norm_kernel, local_len),
        name="norm",
        grid_spec=pltpu.PrefetchScalarGridSpec(
            num_scalar_prefetch=1,
            grid=(m // rows,),
            in_specs=[row_spec, row_spec, vec, vec, vec, vec],
            out_specs=[row_spec, row_spec, row_spec, pl.BlockSpec((rows, 128), lambda i, mt: (i, 0)), vec],
        ),
        out_shape=[jax.ShapeDtypeStruct((m, d), BF)] * 3
        + [jax.ShapeDtypeStruct((m, 128), F32), jax.ShapeDtypeStruct((1, d), F32)],
        compiler_params=params(1),
        cost_estimate=cost(20 * m * d, 10 * m * d),
    )(meta, x2, g2, ga, sa, gf, sf)


def rotate_tile(y, cosf, s1, s2, sign):
    head = y[:, :128]
    rot = (
        head * cosf
        + pltpu.roll(head, 96, 1) * (s1 * sign)
        + pltpu.roll(head, 32, 1) * (s2 * sign)
    )
    return rot, y[:, 128:]


def rotated(out, y, cosf, s1, s2):
    local_len = cosf.shape[0]
    for s in range(y.shape[0] // local_len):
        rows = slice(s * local_len, (s + 1) * local_len)
        rot, rest = rotate_tile(y[rows], cosf[...], s1[...], s2[...], 1.0)
        out[rows, :128] = rot.astype(BF)
        out[rows, 128:] = rest.astype(BF)


def kv_kernel(h1, wa, wb, b_ref, cosf, s1, s2, kv_ref):
    half = wa.shape[0]
    part = lax.rem(pl.program_id(0), 2)
    y = nn(h1[:, :half], wa[...]) + nn(h1[:, half:], wb[...]) + b_ref[...]

    @pl.when(part == 0)
    def _():
        rotated(kv_ref, y, cosf, s1, s2)

    @pl.when(part == 1)
    def _():
        kv_ref[...] = y.astype(BF)


def kv_call(h1, wa, wb, b_qkv, tabs, nheads):
    m, d = h1.shape
    local_len = tabs[0].shape[0]

    def src(j):
        return (0, (j // 2) * 3 + 1 + j % 2)

    tab = pl.BlockSpec((local_len, 128), lambda j: (0, 0))
    return pl.pallas_call(
        kv_kernel,
        name="kv",
        grid=(2 * nheads,),
        in_specs=[
            pl.BlockSpec((m, d), lambda j: (0, 0)),
            pl.BlockSpec((d // 2, HD), src),
            pl.BlockSpec((d // 2, HD), src),
            pl.BlockSpec((1, HD), src),
            tab,
            tab,
            tab,
        ],
        out_specs=pl.BlockSpec((m, HD), lambda j: (0, j)),
        out_shape=jax.ShapeDtypeStruct((m, 2 * nheads * HD), BF),
        compiler_params=params(1),
        cost_estimate=cost(4 * m * d * nheads * HD, 2 * (m * d + 2 * d * nheads * HD + 2 * m * nheads * HD)),
    )(h1, wa, wb, b_qkv, *tabs)


def qd_kernel(nheads, h1, g, wa, wb, b_ref, cosf, s1, s2, q_ref, dob_ref):
    j = pl.program_id(0)
    half = wa.shape[0]

    @pl.when(j < nheads)
    def _():
        rotated(q_ref, nn(h1[:, :half], wa[...]) + nn(h1[:, half:], wb[...]) + b_ref[...], cosf, s1, s2)

    @pl.when(j >= nheads)
    def _():
        dob_ref[...] = (nn(g[:, :half], wa[...]) + nn(g[:, half:], wb[...])).astype(BF)


def qd_call(h1, g, wa, wb, b_qkv, tabs, nheads):
    m, d = h1.shape
    local_len = tabs[0].shape[0]
    full = pl.BlockSpec((m, d), lambda j: (0, 0))
    w_spec = pl.BlockSpec((d // 2, HD), lambda j: (0, jnp.where(j < nheads, 3 * j, 2 * nheads + j)))
    tab = pl.BlockSpec((local_len, 128), lambda j: (0, 0))
    return pl.pallas_call(
        functools.partial(qd_kernel, nheads),
        name="qd",
        grid=(2 * nheads,),
        in_specs=[
            full,
            full,
            w_spec,
            w_spec,
            pl.BlockSpec((1, HD), lambda j: (0, 3 * jnp.minimum(j, nheads - 1))),
            tab,
            tab,
            tab,
        ],
        out_specs=[
            pl.BlockSpec((m, HD), lambda j: (0, jnp.minimum(j, nheads - 1))),
            pl.BlockSpec((m, HD), lambda j: (0, jnp.maximum(j - nheads, 0))),
        ],
        out_shape=[jax.ShapeDtypeStruct((m, nheads * HD), BF)] * 2,
        compiler_params=params(1),
        cost_estimate=cost(4 * m * d * nheads * HD, 2 * (2 * m * d + 2 * d * nheads * HD + 2 * m * nheads * HD)),
    )(h1, g, wa, wb, b_qkv, *tabs)


def attn_kernel(nprev, local_len, meta, q_ref, kv_ref, pv_ref, dob_ref, cosf, s1, s2, ob_ref, dq_ref, dkv_ref, dpv_ref, sc_ref, dq_acc):
    slot = pl.program_id(0)
    ctx = meta[0]
    length = meta[2 + NBLK + slot]
    scale = 1.0 / math.sqrt(HD)
    n_vis = jnp.minimum(ctx, (length + local_len - 1) // local_len)
    q = q_ref[...]
    dob = dob_ref[...]
    own_k = kv_ref[:, :HD]
    own_v = kv_ref[:, HD:]

    ri = lax.broadcasted_iota(jnp.int32, (local_len, local_len), 0)
    ci = lax.broadcasted_iota(jnp.int32, (local_len, local_len), 1)
    s_own = nt(q, own_k) * scale
    s_own = jnp.where((ci <= ri) & (ci < length - ctx * local_len), s_own, neg_big)
    sc_ref[nprev] = s_own

    def prev_rows(jb):
        return pl.ds(pl.multiple_of(jb * local_len, local_len), local_len)

    def score(jb, top):
        s = nt(q, pv_ref[prev_rows(jb), :HD]) * scale
        s = jnp.where(ci[:1] < length - jb * local_len, s, neg_big)
        sc_ref[jb] = s
        return jnp.maximum(top, jnp.max(s, axis=1, keepdims=True))

    top = lax.fori_loop(0, n_vis, score, jnp.max(s_own, axis=1, keepdims=True))

    e_own = jnp.exp(sc_ref[nprev] - top)
    sc_ref[nprev] = e_own

    def expo(jb, tot):
        e = jnp.exp(sc_ref[jb] - top)
        sc_ref[jb] = e
        return tot + jnp.sum(e, axis=1, keepdims=True)

    tot = lax.fori_loop(0, n_vis, expo, jnp.sum(e_own, axis=1, keepdims=True))
    inv = 1.0 / tot
    att = nn((sc_ref[nprev] * inv).astype(BF), own_v)

    def out_step(jb, acc):
        return acc + nn((sc_ref[jb] * inv).astype(BF), pv_ref[prev_rows(jb), HD:])

    att = lax.fori_loop(0, n_vis, out_step, att)
    ob_ref[...] = att.astype(BF)
    delta = jnp.sum(dob.astype(F32) * att, axis=1, keepdims=True)

    def back(p, k, v):
        pb = p.astype(BF)
        ds = (p * (nt(dob, v) - delta)).astype(BF)
        return nn(ds, k) * scale, tn(ds, q) * scale, tn(pb, dob)

    dq, dk, dv = back(sc_ref[nprev] * inv, own_k, own_v)
    dq_acc[...] = dq
    dkv_ref[:, :HD] = dk
    dkv_ref[:, HD:] = dv

    def back_step(jb, carry):
        rows = prev_rows(jb)
        dqp, dkp, dvp = back(sc_ref[jb] * inv, pv_ref[rows, :HD], pv_ref[rows, HD:])
        dq_acc[...] += dqp
        dpv_ref[rows, :HD] = dkp.astype(BF)
        dpv_ref[rows, HD:] = dvp.astype(BF)
        return carry

    lax.fori_loop(0, n_vis, back_step, 0)

    def clear(jb, carry):
        dpv_ref[prev_rows(jb), :] = jnp.zeros((local_len, 2 * HD), BF)
        return carry

    lax.fori_loop(n_vis, nprev, clear, 0)
    rot, rest = rotate_tile(dq_acc[...], cosf[...], s1[...], s2[...], -1.0)
    dq_ref[:, :128] = rot.astype(BF)
    dq_ref[:, 128:] = rest.astype(BF)


def attn_call(meta, q, kv, pv, dob, tabs, nheads):
    local_len = tabs[0].shape[0]
    slots = q.shape[0] // local_len
    nprev = pv.shape[0] // q.shape[0]
    one = pl.BlockSpec((local_len, HD), lambda s, h, mt: (s, h))
    two = pl.BlockSpec((local_len, 2 * HD), lambda s, h, mt: (s, h))
    prev = pl.BlockSpec((nprev * local_len, 2 * HD), lambda s, h, mt: (s, h))
    tab = pl.BlockSpec((local_len, 128), lambda s, h, mt: (0, 0))
    m = q.shape[0]
    return pl.pallas_call(
        functools.partial(attn_kernel, nprev, local_len),
        name="attn",
        grid_spec=pltpu.PrefetchScalarGridSpec(
            num_scalar_prefetch=1,
            grid=(slots, nheads),
            in_specs=[one, two, prev, one, tab, tab, tab],
            out_specs=[one, one, two, prev],
            scratch_shapes=[
                pltpu.VMEM((nprev + 1, local_len, local_len), F32),
                pltpu.VMEM((local_len, HD), F32),
            ],
        ),
        out_shape=[
            jax.ShapeDtypeStruct((m, nheads * HD), BF),
            jax.ShapeDtypeStruct((m, nheads * HD), BF),
            jax.ShapeDtypeStruct((m, 2 * nheads * HD), F32),
            jax.ShapeDtypeStruct((nprev * m, 2 * nheads * HD), BF),
        ],
        compiler_params=params(2),
        cost_estimate=cost(12 * m * nheads * HD * (nprev + 1) * local_len, 20 * m * nheads * HD, m * nheads * (nprev + 1) * local_len),
    )(meta, q, kv, pv, dob, *tabs)


def join_kernel(nheads, dq_ref, dkv_ref, rv_ref, cosf, s1, s2, out_ref, sum_ref):
    i = pl.program_id(0)

    @pl.when(i == 0)
    def _():
        sum_ref[...] = jnp.zeros_like(sum_ref)

    for h in range(nheads):
        base = h * 3 * HD
        out_ref[:, base : base + HD] = dq_ref[:, h * HD : (h + 1) * HD]
        kc = slice(h * 2 * HD, h * 2 * HD + HD)
        vc = slice(h * 2 * HD + HD, (h + 1) * 2 * HD)
        dk = dkv_ref[:, kc] + rv_ref[:, kc].astype(F32)
        rot, rest = rotate_tile(dk, cosf[...], s1[...], s2[...], -1.0)
        out_ref[:, base + HD : base + HD + 128] = rot.astype(BF)
        out_ref[:, base + HD + 128 : base + 2 * HD] = rest.astype(BF)
        out_ref[:, base + 2 * HD : base + 3 * HD] = (dkv_ref[:, vc] + rv_ref[:, vc].astype(F32)).astype(BF)
    sum_ref[...] += jnp.sum(out_ref[...].astype(F32), axis=0, keepdims=True)


def join_call(dq, dkv, rv, tabs, nheads):
    m = dq.shape[0]
    local_len = tabs[0].shape[0]
    rows = 256
    per = local_len // rows

    def spec(c):
        return pl.BlockSpec((rows, c), lambda i: (i, 0))

    tab = pl.BlockSpec((rows, 128), lambda i: (i % per, 0))
    n = 3 * nheads * HD
    return pl.pallas_call(
        functools.partial(join_kernel, nheads),
        name="join",
        grid=(m // rows,),
        in_specs=[spec(nheads * HD), spec(2 * nheads * HD), spec(2 * nheads * HD), tab, tab, tab],
        out_specs=[spec(n), pl.BlockSpec((1, n), lambda i: (0, 0))],
        out_shape=[jax.ShapeDtypeStruct((m, n), BF), jax.ShapeDtypeStruct((1, n), F32)],
        compiler_params=params(1),
        cost_estimate=cost(10 * m * n, 8 * m * n),
    )(dq, dkv, rv, *tabs)


def hidden_kernel(h2, wa, wb, b_ref, gb_ref, dg_ref):
    half = wa.shape[0]
    u = nn(h2[:, :half], wa[...]) + nn(h2[:, half:], wb[...]) + b_ref[...]
    cdf = 0.5 * (1.0 + lax.erf(u * inv_sqrt_two))
    gb_ref[...] = (u * cdf).astype(BF)
    dg_ref[...] = (cdf + u * (jnp.exp(-0.5 * u * u) * inv_sqrt_tau)).astype(BF)


def hidden_call(h2, wa, wb, b_in):
    m, d = h2.shape
    f = wa.shape[1]
    t = 256
    col = pl.BlockSpec((m, t), lambda j: (0, j))
    w_spec = pl.BlockSpec((d // 2, t), lambda j: (0, j))
    return pl.pallas_call(
        hidden_kernel,
        name="hidden",
        grid=(f // t,),
        in_specs=[pl.BlockSpec((m, d), lambda j: (0, 0)), w_spec, w_spec, pl.BlockSpec((1, t), lambda j: (0, j))],
        out_specs=[col, col],
        out_shape=[jax.ShapeDtypeStruct((m, f), BF)] * 2,
        compiler_params=params(1),
        cost_estimate=cost(2 * m * d * f, 2 * (m * d + d * f + 2 * m * f), 2 * m * f),
    )(h2, wa, wb, b_in)


def dhid_kernel(g, w0, w1, w2, w3, dg_ref, du_ref, sum_ref):
    n = w0.shape[0]
    a = nn(g[:, :n], w0[...]) + nn(g[:, n : 2 * n], w1[...])
    a += nn(g[:, 2 * n : 3 * n], w2[...]) + nn(g[:, 3 * n :], w3[...])
    du = (a * dg_ref[...].astype(F32)).astype(BF)
    du_ref[...] = du
    sum_ref[...] = jnp.sum(du.astype(F32), axis=0, keepdims=True)


def dhid_call(g, quarters, dg):
    m, d = g.shape
    f = dg.shape[1]
    t = 256
    col = pl.BlockSpec((m, t), lambda j: (0, j))
    w_spec = pl.BlockSpec((d // 4, t), lambda j: (0, j))
    return pl.pallas_call(
        dhid_kernel,
        name="dhid",
        grid=(f // t,),
        in_specs=[pl.BlockSpec((m, d), lambda j: (0, 0))] + [w_spec] * 4 + [col],
        out_specs=[col, pl.BlockSpec((1, t), lambda j: (0, j))],
        out_shape=[jax.ShapeDtypeStruct((m, f), BF), jax.ShapeDtypeStruct((1, f), F32)],
        compiler_params=params(1),
        cost_estimate=cost(2 * m * d * f, 2 * (m * d + d * f + 2 * m * f)),
    )(g, *quarters, dg)


def out_kernel(ob, gb, wp, wo, y_ref):
    y_ref[...] = (nt(ob[...], wp[...]) + nt(gb[...], wo[...])).astype(BF)


def out_call(ob, gb, g1, quarter, c):
    m, f = gb.shape
    nf = ob.shape[1]
    n = quarter.shape[0]
    rows = 512
    last = g1.shape[1] // nf - 1
    return pl.pallas_call(
        out_kernel,
        name="outp",
        grid=(m // rows,),
        in_specs=[
            pl.BlockSpec((rows, nf), lambda i: (i, 0)),
            pl.BlockSpec((rows, f), lambda i: (i, 0)),
            pl.BlockSpec((n, nf), lambda i: (c % 2, last)),
            pl.BlockSpec((n, f), lambda i: (0, 0)),
        ],
        out_specs=pl.BlockSpec((rows, n), lambda i: (i, 0)),
        out_shape=jax.ShapeDtypeStruct((m, n), BF),
        compiler_params=params(1),
        cost_estimate=cost(2 * m * n * (f + nf), 2 * (m * f + m * nf + n * (f + nf) + m * n)),
    )(ob, gb, g1, quarter)


def back_kernel(c, meta, dqkv, du, w1, w2, x_ref, st_ref, ga, gf, prev, dn_ref, sums_ref):
    i = pl.program_id(0)
    dh1 = nt(dqkv[...], w1[...])
    dh2 = nt(du[...], w2[...])
    for k in range(2):
        src = block_cols(lax.rem(meta[1 + 2 * c + k], 2) * 256)
        dst = slice(k * 256, (k + 1) * 256)
        a, b = dh1[:, dst], dh2[:, dst]
        xh = (x_ref[:, src].astype(F32) - st_ref[:, 0:1]) * st_ref[:, 1:2]
        dn_ref[:, dst] = (a * ga[:, src] + b * gf[:, src]).astype(BF)
        for j, v in enumerate((a * xh, a, b * xh, b)):
            part = jnp.sum(v, axis=0, keepdims=True)

            @pl.when(i == 0)
            def _():
                sums_ref[j : j + 1, src] = part

            @pl.when(i > 0)
            def _():
                sums_ref[j : j + 1, src] = sums_ref[j : j + 1, src] + part


def back_call(meta, dqkv, du, g1, g2, x2, st, ga, gf, sums, c):
    m, d = x2.shape
    nq = dqkv.shape[1]
    f = du.shape[1]
    n = d // 4
    rows = 512

    def absolute(r, at):
        return pl.BlockSpec((r, n), lambda i, mt: (i if at else 0, mt[1 + 2 * c] // 2))

    return pl.pallas_call(
        functools.partial(back_kernel, c),
        name="backn",
        grid_spec=pltpu.PrefetchScalarGridSpec(
            num_scalar_prefetch=1,
            grid=(m // rows,),
            in_specs=[
                pl.BlockSpec((rows, nq), lambda i, mt: (i, 0)),
                pl.BlockSpec((rows, f), lambda i, mt: (i, 0)),
                pl.BlockSpec((n, nq), lambda i, mt: (c % 2, 0)),
                pl.BlockSpec((n, f), lambda i, mt: (c % 2, 0)),
                absolute(rows, True),
                pl.BlockSpec((rows, 128), lambda i, mt: (i, 0)),
                absolute(1, False),
                absolute(1, False),
                pl.BlockSpec(memory_space=pl.ANY),
            ],
            out_specs=[pl.BlockSpec((rows, n), lambda i, mt: (i, 0)), absolute(4, False)],
        ),
        out_shape=[jax.ShapeDtypeStruct((m, n), BF), jax.ShapeDtypeStruct((4, d), F32)],
        input_output_aliases={9: 1},
        compiler_params=params(1),
        cost_estimate=cost(2 * m * n * (f + nq), 2 * (m * f + m * nq + n * (f + nq) + 2 * m * n)),
    )(meta, dqkv, du, g1, g2, x2, st, ga, gf, sums)


def wgrad_kernel(pairs, adds, split, *refs):
    j = pl.program_id(0)
    half_way = sum(pairs) // 2
    start = 0
    for p, count in enumerate(pairs):
        a, b = refs[2 * p], refs[2 * p + 1]

        @pl.when((j >= start) & (j < start + count))
        def _():
            y = tn(a[...], b[...])
            if adds:
                y = y + refs[2 * len(pairs)][...].astype(F32)
            y = y.astype(BF)
            if not split:
                refs[-1][...] = y
                return
            keep_x, send_x, keep_y, send_y = refs[-4:]
            n = y.shape[0] // 4

            @pl.when(j < half_way)
            def _():
                keep_x[...] = y[: 2 * n]
                send_x[...] = y[2 * n :]

            @pl.when(j >= half_way)
            def _():
                keep_y[:n] = y[:n]
                send_y[:n] = y[n : 2 * n]
                keep_y[n:] = y[2 * n : 3 * n]
                send_y[n:] = y[3 * n :]

        start += count


def wgrad_call(*flat, half, add=None, split=False):
    pairs = list(zip(flat[::2], flat[1::2]))
    m, d = pairs[0][0].shape
    t = 512
    counts = tuple(b.shape[1] // t for _, b in pairs)
    total = sum(counts)
    in_specs, ops, start = [], [], 0
    for (a, b), c in zip(pairs, counts):
        in_specs.append(pl.BlockSpec((m, d // 2), lambda j: (0, half)))
        in_specs.append(
            pl.BlockSpec((m, t), lambda j, s=start, c=c: (0, jnp.clip(j - s, 0, c - 1)))
        )
        ops += [a, b]
        start += c
    col = pl.BlockSpec((d // 2, t), lambda j: (0, j))
    if add is not None:
        in_specs.append(col)
        ops.append(add)
    if split:
        h = total // 2
        left = pl.BlockSpec((d // 4, t), lambda j: (0, jnp.minimum(j, h - 1)))
        right = pl.BlockSpec((d // 4, t), lambda j: (0, jnp.maximum(j - h, 0)))
        out_specs = [left, left, right, right]
        out_shape = [jax.ShapeDtypeStruct((d // 4, h * t), BF)] * 4
    else:
        out_specs = col
        out_shape = jax.ShapeDtypeStruct((d // 2, total * t), BF)
    return pl.pallas_call(
        functools.partial(wgrad_kernel, counts, add is not None, split),
        name="wgrad",
        grid=(total,),
        in_specs=in_specs,
        out_specs=out_specs,
        out_shape=out_shape,
        compiler_params=params(1),
        cost_estimate=cost(m * d * total * t, 2 * (m * d // 2 * len(pairs) + m * total * t + d * total * t)),
    )(*ops)


def pack_kernel(*refs):
    out, at = refs[-1], 0
    for ref in refs[:-1]:
        n = ref.shape[0]
        out[at : at + n] = ref[...]
        at += n


def pack_call(*pieces):
    rows = sum(p.shape[0] for p in pieces)
    cols = pieces[0].shape[1]
    t = 512
    return pl.pallas_call(
        pack_kernel,
        name="pack",
        grid=(cols // t,),
        in_specs=[pl.BlockSpec((p.shape[0], t), lambda j: (0, j)) for p in pieces],
        out_specs=pl.BlockSpec((rows, t), lambda j: (0, j)),
        out_shape=jax.ShapeDtypeStruct((rows, cols), BF),
        compiler_params=params(1),
        cost_estimate=cost(0, 4 * rows * cols),
    )(*pieces)


def half_sum_kernel(keep_x, got_x, keep_y, got_y, mid_x, send_y, mid_y, send_x):
    n = mid_x.shape[0]
    for keep, got, mid, send in ((keep_x, got_x, mid_x, send_y), (keep_y, got_y, mid_y, send_x)):
        mid[...] = keep[:n].astype(F32) + got[:n].astype(F32)
        send[...] = (keep[n:].astype(F32) + got[n:].astype(F32)).astype(BF)


def half_sum_call(*ops):
    rows, cols = ops[0].shape
    t = 512
    n = rows // 2
    small = pl.BlockSpec((n, t), lambda j: (0, j))
    return pl.pallas_call(
        half_sum_kernel,
        name="hsum",
        grid=(cols // t,),
        in_specs=[pl.BlockSpec((rows, t), lambda j: (0, j))] * 4,
        out_specs=[small] * 4,
        out_shape=[jax.ShapeDtypeStruct((n, cols), F32), jax.ShapeDtypeStruct((n, cols), BF)] * 2,
        compiler_params=params(1),
        cost_estimate=cost(8 * n * cols, 28 * n * cols),
    )(*ops)


def last_sum_kernel(plan, mid_x, got_y, mid_y, got_x, *outs):
    j = pl.program_id(0)
    half = sum(c for c, _ in plan) // 2
    at = 0
    for (count, turned), out in zip(plan, outs):
        for k in range(at, at + count):
            mid, got = (mid_x, got_y) if k < half else (mid_y, got_x)

            @pl.when(j == k)
            def _():
                v = mid[...] + got[...].astype(F32)
                out[...] = v.T if turned else v

        at += count


def last_sum_call(*ops, plan):
    n, cols = ops[0].shape
    t = 512
    h = cols // t
    left = pl.BlockSpec((n, t), lambda j: (0, jnp.minimum(j, h - 1)))
    right = pl.BlockSpec((n, t), lambda j: (0, jnp.maximum(j - h, 0)))
    out_specs, out_shape, at = [], [], 0
    for count, turned in plan:
        def place(j, at=at, count=count):
            return jnp.clip(j - at, 0, count - 1)

        if turned:
            out_specs.append(pl.BlockSpec((t, n), lambda j, f=place: (f(j), 0)))
            out_shape.append(jax.ShapeDtypeStruct((count * t, n), F32))
        else:
            out_specs.append(pl.BlockSpec((n, t), lambda j, f=place: (0, f(j))))
            out_shape.append(jax.ShapeDtypeStruct((n, count * t), F32))
        at += count
    return pl.pallas_call(
        functools.partial(last_sum_kernel, plan),
        name="lsum",
        grid=(2 * h,),
        in_specs=[left, left, right, right],
        out_specs=out_specs,
        out_shape=out_shape,
        compiler_params=params(1),
        cost_estimate=cost(4 * n * cols, 20 * n * cols),
    )(*ops)


def total_of(meta, refs, c, cols):
    here, sent = refs[2 * c], refs[2 * c + 1]
    return jnp.where(meta[1 + NBLK] > 0, here[:, cols].astype(F32), sent[:, cols].astype(F32))


def block_out_kernel(local_len, meta, x_ref, b_ref, *refs):
    y_ref = refs[-1]
    rows = x_ref.shape[0]
    mask = row_valid(meta, pl.program_id(0) * rows, rows, local_len)
    for r in range(NBLK):
        col = block_cols(meta[1 + r] * 256)
        k = r % 2 * 256
        s = total_of(meta, refs, r // 2, slice(k, k + 256))
        y_ref[:, col] = (mask * (x_ref[:, col].astype(F32) + s + b_ref[:, col])).astype(BF)


def input_grad_kernel(local_len, meta, x_ref, g_ref, st_ref, *refs):
    y_ref = refs[-1]
    rows = x_ref.shape[0]
    mask = row_valid(meta, pl.program_id(0) * rows, rows, local_len)
    mean = st_ref[:, 0:1]
    inv = st_ref[:, 1:2]
    one = jnp.zeros((rows, 1), F32)
    two = jnp.zeros((rows, 1), F32)
    for r in range(NBLK):
        col = block_cols(meta[1 + r] * 256)
        k = r % 2 * 256
        dn = total_of(meta, refs, r // 2, slice(k, k + 256))
        one += jnp.sum(dn, axis=1, keepdims=True)
        two += jnp.sum(dn * ((x_ref[:, col].astype(F32) - mean) * inv), axis=1, keepdims=True)
    d = x_ref.shape[1]
    one = one / d
    two = two / d
    for r in range(NBLK):
        col = block_cols(meta[1 + r] * 256)
        k = r % 2 * 256
        dn = total_of(meta, refs, r // 2, slice(k, k + 256))
        xh = (x_ref[:, col].astype(F32) - mean) * inv
        y_ref[:, col] = (g_ref[:, col].astype(F32) * mask + inv * (dn - one - xh * two)).astype(BF)


def rows_call(meta, *ops, body, name, specs):
    rows = 256
    m, d = ops[0].shape
    made = {
        "row": pl.BlockSpec((rows, d), lambda i, mt: (i, 0)),
        "part": pl.BlockSpec((rows, d // 4), lambda i, mt: (i, 0)),
        "stat": pl.BlockSpec((rows, 128), lambda i, mt: (i, 0)),
        "vec": pl.BlockSpec((1, d), lambda i, mt: (0, 0)),
    }
    return pl.pallas_call(
        body,
        name=name,
        grid_spec=pltpu.PrefetchScalarGridSpec(
            num_scalar_prefetch=1,
            grid=(m // rows,),
            in_specs=[made[s] for s in specs],
            out_specs=made["row"],
        ),
        out_shape=jax.ShapeDtypeStruct((m, d), BF),
        compiler_params=params(1),
        cost_estimate=cost(10 * m * d, 8 * m * d),
    )(meta, *ops)


def after(v, *others):
    return lax.optimization_barrier((v,) + others)[0]


class Order:
    def __init__(self):
        self.last = ()

    def __call__(self, f, first, *rest, **named):
        out = f(after(first, *self.last), *rest, **named)
        self.last = (jax.tree.leaves(out)[0],)
        return out


def add_bf(a, b):
    return lax.optimization_barrier((a.astype(F32) + b.astype(F32)).astype(BF))


def pick_bf(a, b, middle, other):
    total = (a.astype(F32) + b.astype(F32)).astype(BF)
    return lax.optimization_barrier(jnp.where(middle > 0, total, other))


class Pipe:
    LAG = 3

    def __init__(self, run, middle, count):
        self.run, self.middle, self.count = run, middle, count
        self.parts, self.got, self.sums, self.crossed = [], [], [], []
        self.here, self.sent = [], []

    def send(self, part=None):
        step = len(self.got)
        back = step - self.LAG
        pairs = []
        v = part
        if part is not None:
            self.parts.append(part)
            pairs += [(0, 1), (3, 2)]
        if back >= 0:
            pairs += [(1, 0), (2, 3)]
            a, b = self.sums[back], self.crossed[back]
            if part is None:
                v = self.run(add_bf, a, b)
            else:
                v = self.run(pick_bf, a, b, self.middle, part)
        got = lax.ppermute(v, "tensor", pairs)
        self.got.append(got)
        if back >= 0:
            self.here.append(v)
            self.sent.append(got)

    def cross(self):
        k = len(self.sums)
        v = self.run(add_bf, self.parts[k], self.got[k])
        self.sums.append(v)
        self.crossed.append(lax.ppermute(v, "tensor", [(1, 2), (2, 1)]))


class PlainPipe:
    def __init__(self, run, middle, count):
        self.here, self.sent = [], []

    def send(self, part=None):
        if part is not None:
            total = lax.psum(part, "tensor")
            self.here.append(total)
            self.sent.append(total)

    def cross(self):
        pass


class SmallMesh:
    def x(self, v):
        return lax.ppermute(v, "dp", [(0, 2), (2, 0), (1, 3), (3, 1)])

    def core(self, v):
        return lax.ppermute(v, "dp", [(0, 1), (1, 0), (2, 3), (3, 2)])

    def y(self, v):
        return lax.ppermute(v, "ctx", [(0, 1), (1, 0)])

    def perm(self):
        r = jnp.arange(NBLK, dtype=jnp.int32)
        dp = lax.axis_index("dp") ^ (((r >> 1) & 1) * 2 + (r >> 2))
        return dp * 2 + (lax.axis_index("ctx") ^ (r & 1))

    def middle(self):
        z = lax.axis_index("tensor")
        return ((z == 1) | (z == 2)).astype(jnp.int32)

    pipe = Pipe

    def first_hop(self, own):
        return self.x(own), self.y(own)

    def diagonal(self, own, hop):
        n = own.shape[0] // 2
        return [self.x(hop[1][:n]), self.y(hop[0][n:])]

    def diagonal_x(self, own, hop):
        return [self.x(hop[1])]

    def pack(self, run, own, hop, diag):
        return run(pack_call, own, hop[1], hop[0], *diag)

    def both(self, near):
        return near, self.core(near)

    def quarters_near(self, run, own, hop):
        return self.both(run(pack_call, own, hop[1]))

    def quarters_far(self, run, hop, diag):
        return self.both(run(pack_call, hop[0], *diag))

    def scatter_cross(self, theirs):
        return self.core(theirs)

    def scatter_own(self, run, pairs, got):
        keep_x, send_x, keep_y, send_y = run(wgrad_call, *pairs, half=0, add=got, split=True)
        return keep_x, self.x(send_x), keep_y, self.y(send_y)

    def scatter_half(self, run, parts):
        mid_x, to_y, mid_y, to_x = run(half_sum_call, *parts)
        return mid_x, self.y(to_y), mid_y, self.x(to_x)

    def scatter_last(self, run, plan, parts):
        return run(last_sum_call, *parts, plan=plan)

    def previous(self, kv, slots):
        return lax.ppermute(kv, "ctx", [(0, 1)])

    def give_back(self, dpv, dkv, slots):
        return dkv, lax.ppermute(dpv, "ctx", [(1, 0)])

    def small_sum(self, group, everywhere):
        n = group.shape[0]
        v = jnp.concatenate([group, everywhere])
        v = v + self.core(v)
        v = v + self.x(v)
        v = v + self.y(v)
        w = v[n:]
        w = w + lax.ppermute(w, "tensor", [(0, 1), (1, 0), (2, 3), (3, 2)])
        w = w + lax.ppermute(w, "tensor", [(0, 2), (2, 0), (1, 3), (3, 1)])
        return v[:n], w


class AnyMesh:
    def perm(self):
        return jnp.arange(NBLK, dtype=jnp.int32)

    def middle(self):
        return jnp.ones((), jnp.int32)

    pipe = PlainPipe

    def first_hop(self, own):
        return lax.all_gather(own, ("dp", "ctx"), axis=0, tiled=True)

    def diagonal(self, own, hop):
        return ()

    diagonal_x = diagonal

    def both(self, full):
        n = full.shape[0] // 2
        return full[:n], full[n:]

    def pack(self, run, own, hop, diag):
        return hop

    def quarters_near(self, run, own, hop):
        n = hop.shape[0] // 4
        return hop[:n], hop[2 * n : 3 * n]

    def quarters_far(self, run, hop, diag):
        n = hop.shape[0] // 4
        return hop[n : 2 * n], hop[3 * n :]

    def scatter_cross(self, theirs):
        return theirs

    def scatter_own(self, run, pairs, got):
        full = jnp.concatenate([run(wgrad_call, *pairs, half=0), got], axis=0)
        return lax.psum_scatter(full, ("dp", "ctx"), scatter_dimension=0, tiled=True).astype(F32)

    def scatter_half(self, run, parts):
        return parts

    def scatter_last(self, run, plan, parts):
        outs, at = [], 0
        for count, turned in plan:
            v = parts[:, at * 512 : (at + count) * 512]
            outs.append(v.T if turned else v)
            at += count
        return outs

    def previous(self, kv, slots):
        own = kv.reshape(slots, -1, kv.shape[1])
        full = lax.all_gather(own, "ctx", axis=1, tiled=True)
        return full.reshape(-1, kv.shape[1])

    def give_back(self, dpv, dkv, slots):
        cols = dkv.shape[1]
        full = dpv.reshape(slots, -1, cols)
        got = lax.psum_scatter(full, "ctx", scatter_dimension=1, tiled=True)
        return dkv, got.reshape(-1, cols)

    def small_sum(self, group, everywhere):
        return lax.psum(group, ("dp", "ctx")), lax.psum(everywhere, ("dp", "ctx", "tensor"))


def rotary_tables(positions):
    half_rot = ROT // 2
    lane = jnp.arange(128, dtype=jnp.int32)
    exponent = (lane % half_rot).astype(F32) * (2.0 / ROT)
    angles = positions[:, None] * jnp.exp(-math.log(10000.0) * exponent)[None, :]
    cos_all, sin_all = jnp.cos(angles), jnp.sin(angles)
    cosf = jnp.where(lane < ROT, cos_all, 1.0)
    s1 = jnp.where(lane < half_rot, -sin_all, 0.0)
    s2 = jnp.where((lane >= half_rot) & (lane < ROT), sin_all, 0.0)
    return cosf, s1, s2


def local(small, block_input, out_grad, lengths, attn_gain, attn_shift, ffn_gain, ffn_shift, w_qkv, b_qkv, w_proj, b_proj, w_in, b_in, w_out, b_out):
    comm = SmallMesh() if small else AnyMesh()
    slots, local_len, d = block_input.shape
    m = slots * local_len
    nheads = b_qkv.shape[0] // (3 * HD)
    nq = 3 * nheads * HD
    ctx = lax.axis_index("ctx")
    meta = jnp.concatenate([ctx[None].astype(jnp.int32), comm.perm(), comm.middle()[None], lengths])

    run = Order()
    x2 = block_input.reshape(m, d)
    og2 = out_grad.reshape(m, d)
    ga, sa, gf, sf = (v.reshape(1, d) for v in (attn_gain, attn_shift, ffn_gain, ffn_shift))
    bq = b_qkv.reshape(1, nq)
    positions = ctx * local_len + jnp.arange(local_len, dtype=jnp.int32)
    tabs = rotary_tables(positions.astype(F32))

    own1 = jnp.concatenate([w_qkv, w_proj.T], axis=1).astype(BF)
    hop1 = comm.first_hop(own1)
    run.last = (own1,)
    h1, h2, g, stats, g_sum = run(norm_call, meta, x2, og2, ga, sa, gf, sf, local_len)
    own2 = w_in.astype(BF)
    own3 = w_out.T.astype(BF)
    diag1 = comm.diagonal(own1, hop1)
    hop2 = comm.first_hop(own2)
    near1 = comm.pack(run, own1, hop1, diag1)
    g1 = comm.both(near1)
    kv = run(kv_call, h1, *g1, bq, tabs, nheads)
    pv = comm.previous(kv, slots)
    diag2 = comm.diagonal_x(own2, hop2)
    hop3 = comm.first_hop(own3)
    q, dob = run(qd_call, h1, g, *g1, bq, tabs, nheads)
    near2 = comm.pack(run, own2, hop2, diag2)
    g2 = comm.both(near2)
    diag3 = comm.diagonal_x(own3, hop3)
    gb, dg = run(hidden_call, h2, *g2, b_in.reshape(1, -1))
    cross3 = comm.scatter_cross(run(wgrad_call, g, gb, half=1))
    one, three = comm.quarters_near(run, own3, hop3)
    ob, dq, dkv, dpv = run(attn_call, meta, q, kv, pv, dob, tabs, nheads)
    dkv, rv = comm.give_back(dpv, dkv, slots)

    pipe = comm.pipe(run, meta[1 + NBLK], 8)

    def out_part(c, quarter):
        return run(out_call, ob, gb, g1[c // 2], quarter, c)

    pipe.send(out_part(0, one))
    two, four = comm.quarters_far(run, hop3, diag3)
    pipe.send(out_part(2, three))
    pipe.send(out_part(1, two))
    last_out = out_part(3, four)
    pipe.cross()
    du, bin_sum = run(dhid_call, g, (one, two, three, four), dg)
    dqkv, bqkv_sum = run(join_call, dq, dkv, rv, tabs, nheads)
    pipe.cross()
    gain_sums = jnp.zeros((4, d), F32)
    dn_parts = []

    def back_part(c):
        nonlocal gain_sums
        part, gain_sums = run(back_call, meta, dqkv, du, g1[c // 2], g2[c // 2], x2, stats, ga, gf, gain_sums, c)
        dn_parts.append(part)

    ff = du.shape[1] // 512
    back_part(0)
    pipe.send(last_out)
    back_part(1)
    state3 = comm.scatter_own(run, (g, gb), cross3)
    pipe.cross()
    pipe.send(dn_parts[0])
    back_part(2)
    cross2 = comm.scatter_cross(run(wgrad_call, h2, du, half=1))
    pipe.cross()
    pipe.send(dn_parts[1])
    back_part(3)
    state3 = comm.scatter_half(run, state3)
    state2 = comm.scatter_own(run, (h2, du), cross2)
    pipe.cross()
    pipe.send(dn_parts[2])
    group, gains = comm.small_sum(
        jnp.concatenate([g_sum.reshape(-1), bqkv_sum.reshape(-1), bin_sum.reshape(-1)]),
        gain_sums.reshape(-1),
    )
    gains = gains.reshape(4, d)
    bias_grad = group[:d]
    (grad_out,) = comm.scatter_last(run, ((ff, True),), state3)
    cross1 = comm.scatter_cross(run(wgrad_call, h1, dqkv, g, ob, half=1))
    state2 = comm.scatter_half(run, state2)
    pipe.cross()
    pipe.send(dn_parts[3])
    state1 = comm.scatter_own(run, (h1, dqkv, g, ob), cross1)
    (grad_in,) = comm.scatter_last(run, ((ff, False),), state2)
    pipe.cross()
    pipe.send()
    state1 = comm.scatter_half(run, state1)
    order = (0, 2, 1, 3)

    def sums_of(first, order):
        return [v for c in order for v in (pipe.here[first + c], pipe.sent[first + c])]

    block_output = run(
        rows_call, meta, x2, (b_proj + b_out).reshape(1, d), *sums_of(0, order),
        body=functools.partial(block_out_kernel, local_len), name="bout", specs=("row", "vec") + ("part",) * 8,
    ).reshape(slots, local_len, d)
    pipe.cross()
    pipe.send()
    grad_qkv, grad_proj = comm.scatter_last(
        run, ((nq // 512, False), (nheads * HD // 512, True)), state1
    )
    pipe.send()
    input_grad = run(
        rows_call, meta, x2, og2, stats, *sums_of(4, range(4)),
        body=functools.partial(input_grad_kernel, local_len), name="igrad", specs=("row", "row", "stat") + ("part",) * 8,
    ).reshape(slots, local_len, d)
    return (
        block_output,
        input_grad,
        gains[0],
        gains[1],
        gains[2],
        gains[3],
        grad_qkv,
        group[d : d + nq],
        grad_proj,
        bias_grad,
        grad_in,
        group[d + nq :],
        grad_out,
        bias_grad,
    )


def solution(mesh):
    small = mesh.shape["dp"] == 4 and mesh.shape["ctx"] == 2 and mesh.shape["tensor"] == 4
    placed = (
        P("dp", "ctx", None),
        P("dp", "ctx", None),
        P("dp"),
        P(),
        P(),
        P(),
        P(),
        P(("dp", "ctx"), "tensor"),
        P("tensor"),
        P("tensor", ("dp", "ctx")),
        P(),
        P(("dp", "ctx"), "tensor"),
        P("tensor"),
        P("tensor", ("dp", "ctx")),
        P(),
    )
    return jax.shard_map(
        functools.partial(local, small),
        mesh=mesh,
        in_specs=placed,
        out_specs=(
            P("dp", "ctx", None),
            P("dp", "ctx", None),
            P(),
            P(),
            P(),
            P(),
            P(("dp", "ctx"), "tensor"),
            P("tensor"),
            P("tensor", ("dp", "ctx")),
            P(),
            P(("dp", "ctx"), "tensor"),
            P("tensor"),
            P("tensor", ("dp", "ctx")),
            P(),
        ),
        check_vma=False,
    )
```

```python
import functools
import math

import jax
import jax.numpy as jnp
from jax import lax
from jax.experimental import pallas as pl
from jax.experimental.pallas import tpu as pltpu
from jax.sharding import PartitionSpec as P

HD = 256
ROT = 64
NBLK = 8
BF = jnp.bfloat16
F32 = jnp.float32

neg_big = -1e30
inv_sqrt_two = 0.7071067811865476
inv_sqrt_tau = 0.3989422804014327


COST_SCALE = 20


def cost(flops, nbytes, trans=0):
    k = COST_SCALE
    return pl.CostEstimate(flops=int(k * flops), bytes_accessed=int(k * nbytes), transcendentals=int(k * trans))


def params(n, mb=60):
    return pltpu.CompilerParams(
        dimension_semantics=("arbitrary",) * n, vmem_limit_bytes=int(mb * 1024 * 1024)
    )


def nn(a, b):
    return lax.dot_general(a, b, (((1,), (0,)), ((), ())), preferred_element_type=F32)


def nn_rows(a, pieces):
    total, at = None, 0
    for w in pieces:
        y = nn(a[:, at : at + w.shape[0]], w[...])
        total = y if total is None else total + y
        at += w.shape[0]
    return total


def nt(a, b):
    return lax.dot_general(a, b, (((1,), (1,)), ((), ())), preferred_element_type=F32)


def tn(a, b):
    return lax.dot_general(a, b, (((0,), (0,)), ((), ())), preferred_element_type=F32)


def block_cols(r):
    return pl.ds(pl.multiple_of(r, 128), 256)


def row_valid(meta, row0, rows, local_len):
    slot = row0 // local_len
    pos = meta[0] * local_len + row0 % local_len + lax.broadcasted_iota(jnp.int32, (rows, 1), 0)
    return (pos < meta[3 + NBLK + slot]).astype(F32)


def norm_kernel(local_len, meta, x_ref, g_ref, ga, sa, gf, sf, h1_ref, h2_ref, g_out, st_ref, gs_ref):
    rows = x_ref.shape[0]
    i = pl.program_id(0)
    x = x_ref[...].astype(F32)
    mean = jnp.mean(x, axis=-1, keepdims=True)
    cen = x - mean
    inv = lax.rsqrt(jnp.mean(cen * cen, axis=-1, keepdims=True) + 1e-05)
    mask = row_valid(meta, i * rows, rows, local_len)
    lane = lax.broadcasted_iota(jnp.int32, (rows, 128), 1)
    st_ref[...] = jnp.where(lane == 0, mean, inv)
    for r in range(NBLK):
        src = block_cols(meta[1 + r] * 256)
        dst = slice(r * 256, (r + 1) * 256)
        xh = (x_ref[:, src].astype(F32) - mean) * inv
        h1_ref[:, dst] = (xh * ga[:, src] + sa[:, src]).astype(BF)
        h2_ref[:, dst] = (xh * gf[:, src] + sf[:, src]).astype(BF)
        gm = g_ref[:, src].astype(F32) * mask
        g_out[:, dst] = gm.astype(BF)
        part = jnp.sum(gm, axis=0, keepdims=True)

        @pl.when(i == 0)
        def _():
            gs_ref[:, src] = part

        @pl.when(i > 0)
        def _():
            gs_ref[:, src] = gs_ref[:, src] + part


def norm_call(meta, x2, g2, ga, sa, gf, sf, local_len):
    m, d = x2.shape
    rows = 256
    row_spec = pl.BlockSpec((rows, d), lambda i, mt: (i, 0))
    vec = pl.BlockSpec((1, d), lambda i, mt: (0, 0))
    return pl.pallas_call(
        functools.partial(norm_kernel, local_len),
        name="norm",
        grid_spec=pltpu.PrefetchScalarGridSpec(
            num_scalar_prefetch=1,
            grid=(m // rows,),
            in_specs=[row_spec, row_spec, vec, vec, vec, vec],
            out_specs=[row_spec, row_spec, row_spec, pl.BlockSpec((rows, 128), lambda i, mt: (i, 0)), vec],
        ),
        out_shape=[jax.ShapeDtypeStruct((m, d), BF)] * 3
        + [jax.ShapeDtypeStruct((m, 128), F32), jax.ShapeDtypeStruct((1, d), F32)],
        compiler_params=params(1),
        cost_estimate=cost(20 * m * d, 10 * m * d),
    )(meta, x2, g2, ga, sa, gf, sf)


def rotate_tile(y, cosf, s1, s2, sign):
    head = y[:, :128]
    rot = (
        head * cosf
        + pltpu.roll(head, 96, 1) * (s1 * sign)
        + pltpu.roll(head, 32, 1) * (s2 * sign)
    )
    return rot, y[:, 128:]


def rotated(out, y, cosf, s1, s2):
    local_len = cosf.shape[0]
    for s in range(y.shape[0] // local_len):
        rows = slice(s * local_len, (s + 1) * local_len)
        rot, rest = rotate_tile(y[rows], cosf[...], s1[...], s2[...], 1.0)
        out[rows, :128] = rot.astype(BF)
        out[rows, 128:] = rest.astype(BF)


def kv_kernel(h1, w0, w1, w2, w3, w4, w5, b_ref, cosf, s1, s2, kv_ref):
    part = lax.rem(pl.program_id(0), 2)
    y = nn_rows(h1, (w0, w1, w2, w3, w4, w5)) + b_ref[...]

    @pl.when(part == 0)
    def _():
        rotated(kv_ref, y, cosf, s1, s2)

    @pl.when(part == 1)
    def _():
        kv_ref[...] = y.astype(BF)


def kv_call(h1, pieces, b_qkv, tabs, nheads):
    m, d = h1.shape
    local_len = tabs[0].shape[0]

    def src(j):
        return (0, (j // 2) * 3 + 1 + j % 2)

    tab = pl.BlockSpec((local_len, 128), lambda j: (0, 0))
    return pl.pallas_call(
        kv_kernel,
        name="kv",
        grid=(2 * nheads,),
        in_specs=[
            pl.BlockSpec((m, d), lambda j: (0, 0)),
            *[pl.BlockSpec((p.shape[0], HD), src) for p in pieces],
            pl.BlockSpec((1, HD), src),
            tab,
            tab,
            tab,
        ],
        out_specs=pl.BlockSpec((m, HD), lambda j: (0, j)),
        out_shape=jax.ShapeDtypeStruct((m, 2 * nheads * HD), BF),
        compiler_params=params(1),
        cost_estimate=cost(4 * m * d * nheads * HD, 2 * (m * d + 2 * d * nheads * HD + 2 * m * nheads * HD)),
    )(h1, *pieces, b_qkv, *tabs)


def qd_kernel(nheads, h1, g, w0, w1, w2, w3, w4, w5, b_ref, cosf, s1, s2, q_ref, dob_ref):
    j = pl.program_id(0)
    pieces = (w0, w1, w2, w3, w4, w5)

    @pl.when(j < nheads)
    def _():
        rotated(q_ref, nn_rows(h1, pieces) + b_ref[...], cosf, s1, s2)

    @pl.when(j >= nheads)
    def _():
        dob_ref[...] = nn_rows(g, pieces).astype(BF)


def qd_call(h1, g, pieces, b_qkv, tabs, nheads):
    m, d = h1.shape
    local_len = tabs[0].shape[0]
    full = pl.BlockSpec((m, d), lambda j: (0, 0))

    def src(j):
        return (0, jnp.where(j < nheads, 3 * j, 2 * nheads + j))

    tab = pl.BlockSpec((local_len, 128), lambda j: (0, 0))
    return pl.pallas_call(
        functools.partial(qd_kernel, nheads),
        name="qd",
        grid=(2 * nheads,),
        in_specs=[
            full,
            full,
            *[pl.BlockSpec((p.shape[0], HD), src) for p in pieces],
            pl.BlockSpec((1, HD), lambda j: (0, 3 * jnp.minimum(j, nheads - 1))),
            tab,
            tab,
            tab,
        ],
        out_specs=[
            pl.BlockSpec((m, HD), lambda j: (0, jnp.minimum(j, nheads - 1))),
            pl.BlockSpec((m, HD), lambda j: (0, jnp.maximum(j - nheads, 0))),
        ],
        out_shape=[jax.ShapeDtypeStruct((m, nheads * HD), BF)] * 2,
        compiler_params=params(1),
        cost_estimate=cost(4 * m * d * nheads * HD, 2 * (2 * m * d + 2 * d * nheads * HD + 2 * m * nheads * HD)),
    )(h1, g, *pieces, b_qkv, *tabs)


def attn_kernel(nprev, local_len, meta, q_ref, kv_ref, pv_ref, dob_ref, cosf, s1, s2, ob_ref, dq_ref, dkv_ref, dpv_ref, sc_ref, dq_acc):
    slot = pl.program_id(0)
    ctx = meta[0]
    length = meta[3 + NBLK + slot]
    scale = 1.0 / math.sqrt(HD)
    n_vis = jnp.minimum(ctx, (length + local_len - 1) // local_len)
    q = q_ref[...]
    dob = dob_ref[...]
    own_k = kv_ref[:, :HD]
    own_v = kv_ref[:, HD:]

    ri = lax.broadcasted_iota(jnp.int32, (local_len, local_len), 0)
    ci = lax.broadcasted_iota(jnp.int32, (local_len, local_len), 1)
    s_own = nt(q, own_k) * scale
    s_own = jnp.where((ci <= ri) & (ci < length - ctx * local_len), s_own, neg_big)
    sc_ref[nprev] = s_own

    def prev_rows(jb):
        return pl.ds(pl.multiple_of(jb * local_len, local_len), local_len)

    def score(jb, top):
        s = nt(q, pv_ref[prev_rows(jb), :HD]) * scale
        s = jnp.where(ci[:1] < length - jb * local_len, s, neg_big)
        sc_ref[jb] = s
        return jnp.maximum(top, jnp.max(s, axis=1, keepdims=True))

    top = lax.fori_loop(0, n_vis, score, jnp.max(s_own, axis=1, keepdims=True))

    e_own = jnp.exp(sc_ref[nprev] - top)
    sc_ref[nprev] = e_own

    def expo(jb, tot):
        e = jnp.exp(sc_ref[jb] - top)
        sc_ref[jb] = e
        return tot + jnp.sum(e, axis=1, keepdims=True)

    tot = lax.fori_loop(0, n_vis, expo, jnp.sum(e_own, axis=1, keepdims=True))
    inv = 1.0 / tot
    att = nn((sc_ref[nprev] * inv).astype(BF), own_v)

    def out_step(jb, acc):
        return acc + nn((sc_ref[jb] * inv).astype(BF), pv_ref[prev_rows(jb), HD:])

    att = lax.fori_loop(0, n_vis, out_step, att)
    ob_ref[...] = att.astype(BF)
    delta = jnp.sum(dob.astype(F32) * att, axis=1, keepdims=True)

    def back(p, k, v):
        pb = p.astype(BF)
        ds = (p * (nt(dob, v) - delta)).astype(BF)
        return nn(ds, k) * scale, tn(ds, q) * scale, tn(pb, dob)

    dq, dk, dv = back(sc_ref[nprev] * inv, own_k, own_v)
    dq_acc[...] = dq
    dkv_ref[:, :HD] = dk
    dkv_ref[:, HD:] = dv

    def back_step(jb, carry):
        rows = prev_rows(jb)
        dqp, dkp, dvp = back(sc_ref[jb] * inv, pv_ref[rows, :HD], pv_ref[rows, HD:])
        dq_acc[...] += dqp
        dpv_ref[rows, :HD] = dkp.astype(BF)
        dpv_ref[rows, HD:] = dvp.astype(BF)
        return carry

    lax.fori_loop(0, n_vis, back_step, 0)

    def clear(jb, carry):
        dpv_ref[prev_rows(jb), :] = jnp.zeros((local_len, 2 * HD), BF)
        return carry

    lax.fori_loop(n_vis, nprev, clear, 0)
    rot, rest = rotate_tile(dq_acc[...], cosf[...], s1[...], s2[...], -1.0)
    dq_ref[:, :128] = rot.astype(BF)
    dq_ref[:, 128:] = rest.astype(BF)


def attn_call(meta, q, kv, pv, dob, tabs, nheads):
    local_len = tabs[0].shape[0]
    slots = q.shape[0] // local_len
    nprev = pv.shape[0] // q.shape[0]
    one = pl.BlockSpec((local_len, HD), lambda s, h, mt: (s, h))
    two = pl.BlockSpec((local_len, 2 * HD), lambda s, h, mt: (s, h))
    prev = pl.BlockSpec((nprev * local_len, 2 * HD), lambda s, h, mt: (s, h))
    tab = pl.BlockSpec((local_len, 128), lambda s, h, mt: (0, 0))
    m = q.shape[0]
    return pl.pallas_call(
        functools.partial(attn_kernel, nprev, local_len),
        name="attn",
        grid_spec=pltpu.PrefetchScalarGridSpec(
            num_scalar_prefetch=1,
            grid=(slots, nheads),
            in_specs=[one, two, prev, one, tab, tab, tab],
            out_specs=[one, one, two, prev],
            scratch_shapes=[
                pltpu.VMEM((nprev + 1, local_len, local_len), F32),
                pltpu.VMEM((local_len, HD), F32),
            ],
        ),
        out_shape=[
            jax.ShapeDtypeStruct((m, nheads * HD), BF),
            jax.ShapeDtypeStruct((m, nheads * HD), BF),
            jax.ShapeDtypeStruct((m, 2 * nheads * HD), F32),
            jax.ShapeDtypeStruct((nprev * m, 2 * nheads * HD), BF),
        ],
        compiler_params=params(2),
        cost_estimate=cost(12 * m * nheads * HD * (nprev + 1) * local_len, 20 * m * nheads * HD, m * nheads * (nprev + 1) * local_len),
    )(meta, q, kv, pv, dob, *tabs)


def join_kernel(nheads, dq_ref, dkv_ref, rv_ref, cosf, s1, s2, out_ref, sum_ref):
    i = pl.program_id(0)

    @pl.when(i == 0)
    def _():
        sum_ref[...] = jnp.zeros_like(sum_ref)

    for h in range(nheads):
        base = h * 3 * HD
        out_ref[:, base : base + HD] = dq_ref[:, h * HD : (h + 1) * HD]
        kc = slice(h * 2 * HD, h * 2 * HD + HD)
        vc = slice(h * 2 * HD + HD, (h + 1) * 2 * HD)
        dk = dkv_ref[:, kc] + rv_ref[:, kc].astype(F32)
        rot, rest = rotate_tile(dk, cosf[...], s1[...], s2[...], -1.0)
        out_ref[:, base + HD : base + HD + 128] = rot.astype(BF)
        out_ref[:, base + HD + 128 : base + 2 * HD] = rest.astype(BF)
        out_ref[:, base + 2 * HD : base + 3 * HD] = (dkv_ref[:, vc] + rv_ref[:, vc].astype(F32)).astype(BF)
    sum_ref[...] += jnp.sum(out_ref[...].astype(F32), axis=0, keepdims=True)


def join_call(dq, dkv, rv, tabs, nheads):
    m = dq.shape[0]
    local_len = tabs[0].shape[0]
    rows = 256
    per = local_len // rows

    def spec(c):
        return pl.BlockSpec((rows, c), lambda i: (i, 0))

    tab = pl.BlockSpec((rows, 128), lambda i: (i % per, 0))
    n = 3 * nheads * HD
    return pl.pallas_call(
        functools.partial(join_kernel, nheads),
        name="join",
        grid=(m // rows,),
        in_specs=[spec(nheads * HD), spec(2 * nheads * HD), spec(2 * nheads * HD), tab, tab, tab],
        out_specs=[spec(n), pl.BlockSpec((1, n), lambda i: (0, 0))],
        out_shape=[jax.ShapeDtypeStruct((m, n), BF), jax.ShapeDtypeStruct((1, n), F32)],
        compiler_params=params(1),
        cost_estimate=cost(10 * m * n, 8 * m * n),
    )(dq, dkv, rv, *tabs)


def hidden_kernel(h2, w0, w1, w2, w3, w4, w5, b_ref, gb_ref, dg_ref):
    u = nn_rows(h2, (w0, w1, w2, w3, w4, w5)) + b_ref[...]
    cdf = 0.5 * (1.0 + lax.erf(u * inv_sqrt_two))
    gb_ref[...] = (u * cdf).astype(BF)
    dg_ref[...] = (cdf + u * (jnp.exp(-0.5 * u * u) * inv_sqrt_tau)).astype(BF)


def hidden_call(h2, pieces, b_in):
    m, d = h2.shape
    f = pieces[0].shape[1]
    t = 256
    col = pl.BlockSpec((m, t), lambda j: (0, j))
    w_specs = [pl.BlockSpec((p.shape[0], t), lambda j: (0, j)) for p in pieces]
    return pl.pallas_call(
        hidden_kernel,
        name="hidden",
        grid=(f // t,),
        in_specs=[pl.BlockSpec((m, d), lambda j: (0, 0)), *w_specs, pl.BlockSpec((1, t), lambda j: (0, j))],
        out_specs=[col, col],
        out_shape=[jax.ShapeDtypeStruct((m, f), BF)] * 2,
        compiler_params=params(1),
        cost_estimate=cost(2 * m * d * f, 2 * (m * d + d * f + 2 * m * f), 2 * m * f),
    )(h2, *pieces, b_in)


def dhid_kernel(g, w0, w1, w2, w3, w4, w5, dg_ref, du_ref, sum_ref):
    a = nn_rows(g, (w0, w1, w2, w3, w4, w5))
    du = (a * dg_ref[...].astype(F32)).astype(BF)
    du_ref[...] = du
    sum_ref[...] = jnp.sum(du.astype(F32), axis=0, keepdims=True)


def dhid_call(g, pieces, dg):
    m, d = g.shape
    f = dg.shape[1]
    t = 256
    col = pl.BlockSpec((m, t), lambda j: (0, j))
    w_specs = [pl.BlockSpec((p.shape[0], t), lambda j: (0, j)) for p in pieces]
    return pl.pallas_call(
        dhid_kernel,
        name="dhid",
        grid=(f // t,),
        in_specs=[pl.BlockSpec((m, d), lambda j: (0, 0))] + w_specs + [col],
        out_specs=[col, pl.BlockSpec((1, t), lambda j: (0, j))],
        out_shape=[jax.ShapeDtypeStruct((m, f), BF), jax.ShapeDtypeStruct((1, f), F32)],
        compiler_params=params(1),
        cost_estimate=cost(2 * m * d * f, 2 * (m * d + d * f + 2 * m * f)),
    )(g, *pieces, dg)


def out_kernel(count, ob, gb, *refs):
    j = pl.program_id(0)
    ps, os, ya, yb = refs[:count], refs[count : 2 * count], refs[-2], refs[-1]
    each = 4 // count
    for k in range(4):

        @pl.when(j == k)
        def _():
            y = ya if k < 2 else yb
            y[...] = (nt(ob[...], ps[k // each][...]) + nt(gb[...], os[k // each][...])).astype(BF)


def piece_spec(count, i, cols, at=0, prefetch=False):
    each = 4 // count

    def place(j, *_):
        return (jnp.clip(j - i * each, 0, each - 1), at)

    if prefetch:
        return pl.BlockSpec((256, cols), lambda j, mt: place(j))
    return pl.BlockSpec((256, cols), lambda j: place(j))


def out_call(ob, gb, proj, out):
    m, f = gb.shape
    nf = ob.shape[1]
    count = len(out)
    last = proj[0].shape[1] // nf - 1
    part = jax.ShapeDtypeStruct((m, 512), BF)
    return pl.pallas_call(
        functools.partial(out_kernel, count),
        name="outp",
        grid=(4,),
        in_specs=[pl.BlockSpec((m, nf), lambda j: (0, 0)), pl.BlockSpec((m, f), lambda j: (0, 0))]
        + [piece_spec(count, i, nf, last) for i in range(count)]
        + [piece_spec(count, i, f) for i in range(count)],
        out_specs=[
            pl.BlockSpec((m, 256), lambda j: (0, jnp.minimum(j, 1))),
            pl.BlockSpec((m, 256), lambda j: (0, jnp.maximum(j - 2, 0))),
        ],
        out_shape=[part, part],
        compiler_params=params(1),
        cost_estimate=cost(2048 * m * (f + nf), 2 * (m * f + m * nf + 1024 * (f + nf) + 1024 * m)),
    )(ob, gb, *proj, *out)


def back_kernel(meta, dqkv, du, w10, w11, w12, w20, w21, w22, x_ref, st_ref, ga, gf, prev, da_ref, db_ref, sums_ref):
    j = pl.program_id(0)
    for w1, w2, dn_ref, mine in ((w10, w20, da_ref, j < 2), (w11, w21, db_ref, j == 2), (w12, w22, db_ref, j == 3)):

        @pl.when(mine)
        def _():
            dh1 = nt(dqkv[...], w1[...])
            dh2 = nt(du[...], w2[...])
            xh = (x_ref[...].astype(F32) - st_ref[:, 0:1]) * st_ref[:, 1:2]
            dn_ref[...] = (dh1 * ga[...] + dh2 * gf[...]).astype(BF)
            sums_ref[0:1, :] = jnp.sum(dh1 * xh, axis=0, keepdims=True)
            sums_ref[1:2, :] = jnp.sum(dh1, axis=0, keepdims=True)
            sums_ref[2:3, :] = jnp.sum(dh2 * xh, axis=0, keepdims=True)
            sums_ref[3:4, :] = jnp.sum(dh2, axis=0, keepdims=True)


def back_call(meta, dqkv, du, g1, g2, x2, st, ga, gf, sums, half):
    m, d = x2.shape
    nq = dqkv.shape[1]
    f = du.shape[1]
    n = d // 4

    def absolute(rows):
        return pl.BlockSpec((rows, 256), lambda j, mt: (0, mt[1 + 4 * half + j]))

    part = jax.ShapeDtypeStruct((m, n), BF)
    at = slice(3 * half, 3 * half + 3)
    return pl.pallas_call(
        back_kernel,
        name="backn",
        grid_spec=pltpu.PrefetchScalarGridSpec(
            num_scalar_prefetch=1,
            grid=(4,),
            in_specs=[
                pl.BlockSpec((m, nq), lambda j, mt: (0, 0)),
                pl.BlockSpec((m, f), lambda j, mt: (0, 0)),
                pl.BlockSpec((256, nq), lambda j, mt: (jnp.minimum(j, 1), 0)),
                pl.BlockSpec((256, nq), lambda j, mt: (0, 0)),
                pl.BlockSpec((256, nq), lambda j, mt: (0, 0)),
                pl.BlockSpec((256, f), lambda j, mt: (jnp.minimum(j, 1), 0)),
                pl.BlockSpec((256, f), lambda j, mt: (0, 0)),
                pl.BlockSpec((256, f), lambda j, mt: (0, 0)),
                absolute(m),
                pl.BlockSpec((m, 128), lambda j, mt: (0, 0)),
                absolute(1),
                absolute(1),
                pl.BlockSpec(memory_space=pl.ANY),
            ],
            out_specs=[
                pl.BlockSpec((m, n // 2), lambda j, mt: (0, jnp.minimum(j, 1))),
                pl.BlockSpec((m, n // 2), lambda j, mt: (0, jnp.maximum(j - 2, 0))),
                absolute(4),
            ],
        ),
        out_shape=[part, part, jax.ShapeDtypeStruct((4, d), F32)],
        input_output_aliases={13: 2},
        compiler_params=params(1),
        cost_estimate=cost(4 * m * n * (f + nq), 2 * (m * f + m * nq + 2 * n * (f + nq) + 4 * m * n)),
    )(meta, dqkv, du, *g1[at], *g2[at], x2, st, ga, gf, sums)


def wgrad_kernel(pairs, adds, split, meta, *refs):
    j = pl.program_id(0)
    start = 0
    for p, count in enumerate(pairs):
        a, b = refs[2 * p], refs[2 * p + 1]

        @pl.when((j >= start) & (j < start + count))
        def _():
            y = tn(a[...], b[...])
            if adds:
                y = y + refs[2 * len(pairs)][...].astype(F32)
            if not split:
                refs[-1][...] = y.astype(BF)
                return
            keep, send = refs[-2:]
            n = y.shape[0] // 4
            swap = meta[2 + NBLK] > 0
            keep[:n] = y[:n].astype(BF)
            keep[n:] = jnp.where(swap, y[2 * n : 3 * n], y[n : 2 * n]).astype(BF)
            send[:n] = jnp.where(swap, y[n : 2 * n], y[2 * n : 3 * n]).astype(BF)
            send[n:] = y[3 * n :].astype(BF)

        start += count


def wgrad_call(meta, *flat, half, add=None, split=False):
    pairs = list(zip(flat[::2], flat[1::2]))
    m, d = pairs[0][0].shape
    t = 512
    counts = tuple(b.shape[1] // t for _, b in pairs)
    total = sum(counts)
    in_specs, ops, start = [], [], 0
    for (a, b), c in zip(pairs, counts):
        in_specs.append(pl.BlockSpec((m, d // 2), lambda j, mt: (0, half)))
        in_specs.append(
            pl.BlockSpec((m, t), lambda j, mt, s=start, c=c: (0, jnp.clip(j - s, 0, c - 1)))
        )
        ops += [a, b]
        start += c
    rows = d // 4 if split else d // 2
    if add is not None:
        in_specs.append(pl.BlockSpec((d // 2, t), lambda j, mt: (0, j)))
        ops.append(add)
    out_spec = pl.BlockSpec((rows, t), lambda j, mt: (0, j))
    out_shape = jax.ShapeDtypeStruct((rows, total * t), BF)
    return pl.pallas_call(
        functools.partial(wgrad_kernel, counts, add is not None, split),
        name="wgrad",
        grid_spec=pltpu.PrefetchScalarGridSpec(
            num_scalar_prefetch=1,
            grid=(total,),
            in_specs=in_specs,
            out_specs=[out_spec, out_spec] if split else out_spec,
        ),
        out_shape=[out_shape, out_shape] if split else out_shape,
        compiler_params=params(1),
        cost_estimate=cost(m * d * total * t, 2 * (m * d // 2 * len(pairs) + m * total * t + d * total * t)),
    )(meta, *ops)


def pack_kernel(*refs):
    out, at = refs[-1], 0
    for ref in refs[:-1]:
        n = ref.shape[0]
        out[at : at + n] = ref[...]
        at += n


def pack_call(*pieces):
    rows = sum(p.shape[0] for p in pieces)
    cols = pieces[0].shape[1]
    t = 512
    return pl.pallas_call(
        pack_kernel,
        name="pack",
        grid=(cols // t,),
        in_specs=[pl.BlockSpec((p.shape[0], t), lambda j: (0, j)) for p in pieces],
        out_specs=pl.BlockSpec((rows, t), lambda j: (0, j)),
        out_shape=jax.ShapeDtypeStruct((rows, cols), BF),
        compiler_params=params(1),
        cost_estimate=cost(0, 4 * rows * cols),
    )(*pieces)


def half_sum_kernel(keep, got, mid, send):
    n = mid.shape[0]
    mid[...] = keep[:n].astype(F32) + got[:n].astype(F32)
    send[...] = (keep[n:].astype(F32) + got[n:].astype(F32)).astype(BF)


def half_sum_call(keep, got):
    rows, cols = keep.shape
    t = 512
    n = rows // 2
    small = pl.BlockSpec((n, t), lambda j: (0, j))
    return pl.pallas_call(
        half_sum_kernel,
        name="hsum",
        grid=(cols // t,),
        in_specs=[pl.BlockSpec((rows, t), lambda j: (0, j))] * 2,
        out_specs=[small] * 2,
        out_shape=[jax.ShapeDtypeStruct((n, cols), F32), jax.ShapeDtypeStruct((n, cols), BF)],
        compiler_params=params(1),
        cost_estimate=cost(4 * n * cols, 14 * n * cols),
    )(keep, got)


def last_sum_kernel(plan, mid, got, *outs):
    j = pl.program_id(0)
    at = 0
    for (count, turned), out in zip(plan, outs):

        @pl.when((j >= at) & (j < at + count))
        def _():
            v = mid[...] + got[...].astype(F32)
            out[...] = v.T if turned else v

        at += count


def last_sum_call(mid, got, plan):
    n, cols = mid.shape
    t = 512
    block = pl.BlockSpec((n, t), lambda j: (0, j))
    out_specs, out_shape, at = [], [], 0
    for count, turned in plan:
        def place(j, at=at, count=count):
            return jnp.clip(j - at, 0, count - 1)

        if turned:
            out_specs.append(pl.BlockSpec((t, n), lambda j, f=place: (f(j), 0)))
            out_shape.append(jax.ShapeDtypeStruct((count * t, n), F32))
        else:
            out_specs.append(pl.BlockSpec((n, t), lambda j, f=place: (0, f(j))))
            out_shape.append(jax.ShapeDtypeStruct((n, count * t), F32))
        at += count
    return pl.pallas_call(
        functools.partial(last_sum_kernel, plan),
        name="lsum",
        grid=(cols // t,),
        in_specs=[block, block],
        out_specs=out_specs,
        out_shape=out_shape,
        compiler_params=params(1),
        cost_estimate=cost(2 * n * cols, 10 * n * cols),
    )(mid, got)


def total_of(meta, refs, c, cols):
    here, sent = refs[2 * c], refs[2 * c + 1]
    return jnp.where(meta[1 + NBLK] > 0, here[:, cols].astype(F32), sent[:, cols].astype(F32))


def block_out_kernel(local_len, meta, x_ref, b_ref, *refs):
    y_ref = refs[-1]
    rows = x_ref.shape[0]
    mask = row_valid(meta, pl.program_id(0) * rows, rows, local_len)
    for r in range(NBLK):
        col = block_cols(meta[1 + r] * 256)
        k = r % 2 * 256
        s = total_of(meta, refs, r // 2, slice(k, k + 256))
        y_ref[:, col] = (mask * (x_ref[:, col].astype(F32) + s + b_ref[:, col])).astype(BF)


def input_grad_kernel(local_len, meta, x_ref, g_ref, st_ref, *refs):
    y_ref = refs[-1]
    rows = x_ref.shape[0]
    mask = row_valid(meta, pl.program_id(0) * rows, rows, local_len)
    mean = st_ref[:, 0:1]
    inv = st_ref[:, 1:2]
    one = jnp.zeros((rows, 1), F32)
    two = jnp.zeros((rows, 1), F32)
    for r in range(NBLK):
        col = block_cols(meta[1 + r] * 256)
        k = r % 2 * 256
        dn = total_of(meta, refs, r // 2, slice(k, k + 256))
        one += jnp.sum(dn, axis=1, keepdims=True)
        two += jnp.sum(dn * ((x_ref[:, col].astype(F32) - mean) * inv), axis=1, keepdims=True)
    d = x_ref.shape[1]
    one = one / d
    two = two / d
    for r in range(NBLK):
        col = block_cols(meta[1 + r] * 256)
        k = r % 2 * 256
        dn = total_of(meta, refs, r // 2, slice(k, k + 256))
        xh = (x_ref[:, col].astype(F32) - mean) * inv
        y_ref[:, col] = (g_ref[:, col].astype(F32) * mask + inv * (dn - one - xh * two)).astype(BF)


def rows_call(meta, *ops, body, name, specs):
    rows = 256
    m, d = ops[0].shape
    made = {
        "row": pl.BlockSpec((rows, d), lambda i, mt: (i, 0)),
        "part": pl.BlockSpec((rows, d // 4), lambda i, mt: (i, 0)),
        "stat": pl.BlockSpec((rows, 128), lambda i, mt: (i, 0)),
        "vec": pl.BlockSpec((1, d), lambda i, mt: (0, 0)),
    }
    return pl.pallas_call(
        body,
        name=name,
        grid_spec=pltpu.PrefetchScalarGridSpec(
            num_scalar_prefetch=1,
            grid=(m // rows,),
            in_specs=[made[s] for s in specs],
            out_specs=made["row"],
        ),
        out_shape=jax.ShapeDtypeStruct((m, d), BF),
        compiler_params=params(1),
        cost_estimate=cost(10 * m * d, 8 * m * d),
    )(meta, *ops)


def after(v, *others):
    return lax.optimization_barrier((v,) + others)[0]


class Order:
    def __init__(self):
        self.last = ()

    def __call__(self, f, first, *rest, **named):
        out = f(after(first, *self.last), *rest, **named)
        self.last = (jax.tree.leaves(out)[0],)
        return out


def add_bf(a, b):
    return lax.optimization_barrier((a.astype(F32) + b.astype(F32)).astype(BF))


def pick_bf(a, b, middle, other):
    total = (a.astype(F32) + b.astype(F32)).astype(BF)
    return lax.optimization_barrier(jnp.where(middle > 0, total, other))


class Pipe:
    LAG = 3

    def __init__(self, run, middle, count):
        self.run, self.middle, self.count = run, middle, count
        self.parts, self.got, self.sums, self.crossed = [], [], [], []
        self.here, self.sent = [], []

    def send(self, part=None):
        step = len(self.got)
        back = step - self.LAG
        pairs = []
        v = part
        if part is not None:
            self.parts.append(part)
            pairs += [(0, 1), (3, 2)]
        if back >= 0:
            pairs += [(1, 0), (2, 3)]
            a, b = self.sums[back], self.crossed[back]
            if part is None:
                v = self.run(add_bf, a, b)
            else:
                v = self.run(pick_bf, a, b, self.middle, part)
        got = lax.ppermute(v, "tensor", pairs)
        self.got.append(got)
        if back >= 0:
            self.here.append(v)
            self.sent.append(got)

    def cross(self):
        k = len(self.sums)
        v = self.run(add_bf, self.parts[k], self.got[k])
        self.sums.append(v)
        self.crossed.append(lax.ppermute(v, "tensor", [(1, 2), (2, 1)]))


class PlainPipe:
    def __init__(self, run, middle, count):
        self.here, self.sent = [], []

    def send(self, part=None):
        if part is not None:
            total = lax.psum(part, "tensor")
            self.here.append(total)
            self.sent.append(total)

    def cross(self):
        pass


class SmallMesh:
    def x(self, v):
        return lax.ppermute(v, "dp", [(0, 2), (2, 0), (1, 3), (3, 1)])

    def core(self, v):
        return lax.ppermute(v, "dp", [(0, 1), (1, 0), (2, 3), (3, 2)])

    def y(self, v):
        return lax.ppermute(v, "ctx", [(0, 1), (1, 0)])

    def perm(self):
        r = jnp.arange(NBLK, dtype=jnp.int32)
        dp = lax.axis_index("dp") ^ (((r >> 1) & 1) * 2 + (r >> 2))
        return dp * 2 + (lax.axis_index("ctx") ^ (r & 1))

    def middle(self):
        z = lax.axis_index("tensor")
        return ((z == 1) | (z == 2)).astype(jnp.int32)

    pipe = Pipe

    def first_hop(self, own, earlier=None):
        if earlier is None:
            return self.x(own), self.y(own)
        return self.x(after(own, earlier)), self.y(own)

    def second_hop(self, hop, earlier=()):
        return self.x(after(hop[1], hop[0], *earlier))

    def waited(self, hop):
        return hop

    def near(self, run, own, hop):
        v = run(pack_call, own, hop[1])
        return v, self.core(v)

    def pieces(self, near, hop, diag):
        return near[0], hop[0], diag, near[1], self.core(hop[0]), self.core(diag)

    def turn(self, v, first):
        pairs = []
        for dp in range(4):
            for c in range(2):
                to = (dp ^ 2) * 2 + c if dp % 2 != first else dp * 2 + (c ^ 1)
                pairs.append((dp * 2 + c, to))
        return lax.ppermute(v, ("dp", "ctx"), pairs)

    def scatter_cross(self, theirs):
        return self.core(theirs)

    def scatter_own(self, run, meta, pairs, got):
        keep, send = run(wgrad_call, meta, *pairs, half=0, add=got, split=True)
        return keep, self.turn(send, 1)

    def scatter_half(self, run, parts):
        mid, send = run(half_sum_call, *parts)
        return mid, self.turn(send, 0)

    def scatter_last(self, run, plan, parts):
        return run(last_sum_call, *parts, plan=plan)

    def previous(self, kv, slots):
        return lax.ppermute(kv, "ctx", [(0, 1)])

    def give_back(self, dpv, dkv, slots):
        return dkv, lax.ppermute(dpv, "ctx", [(1, 0)])

    def small_sum(self, run, v, step):
        def add(a, b):
            return a + b

        if step == 0:
            got = self.core(v)
        elif step == 1:
            got = self.x(v)
        elif step == 2:
            got = self.y(v)
        elif step == 3:
            got = lax.ppermute(v, "tensor", [(0, 1), (1, 0), (2, 3), (3, 2)])
        else:
            got = lax.ppermute(v, "tensor", [(0, 2), (2, 0), (1, 3), (3, 1)])
        return lambda: run(add, v, got)


class AnyMesh:
    def perm(self):
        return jnp.arange(NBLK, dtype=jnp.int32)

    def middle(self):
        return jnp.ones((), jnp.int32)

    pipe = PlainPipe

    def first_hop(self, own, earlier=None):
        return lax.all_gather(own, ("dp", "ctx"), axis=0, tiled=True)

    def second_hop(self, hop, earlier=()):
        return ()

    def waited(self, hop):
        return (hop,)

    def near(self, run, own, hop):
        return hop[:512], hop[1024:1536]

    def pieces(self, near, hop, diag):
        return near[0], hop[512:768], hop[768:1024], near[1], hop[1536:1792], hop[1792:]

    def scatter_cross(self, theirs):
        return theirs

    def scatter_own(self, run, meta, pairs, got):
        full = jnp.concatenate([run(wgrad_call, meta, *pairs, half=0), got], axis=0)
        return lax.psum_scatter(full, ("dp", "ctx"), scatter_dimension=0, tiled=True).astype(F32)

    def scatter_half(self, run, parts):
        return parts

    def scatter_last(self, run, plan, parts):
        outs, at = [], 0
        for count, turned in plan:
            v = parts[:, at * 512 : (at + count) * 512]
            outs.append(v.T if turned else v)
            at += count
        return outs

    def previous(self, kv, slots):
        own = kv.reshape(slots, -1, kv.shape[1])
        full = lax.all_gather(own, "ctx", axis=1, tiled=True)
        return full.reshape(-1, kv.shape[1])

    def give_back(self, dpv, dkv, slots):
        cols = dkv.shape[1]
        full = dpv.reshape(slots, -1, cols)
        got = lax.psum_scatter(full, "ctx", scatter_dimension=1, tiled=True)
        return dkv, got.reshape(-1, cols)

    def small_sum(self, run, v, step):
        got = v
        if step == 0:
            got = lax.psum(v, ("dp", "ctx"))
        elif step == 3:
            got = lax.psum(v, "tensor")
        return lambda: got


def rotary_tables(positions):
    half_rot = ROT // 2
    lane = jnp.arange(128, dtype=jnp.int32)
    exponent = (lane % half_rot).astype(F32) * (2.0 / ROT)
    angles = positions[:, None] * jnp.exp(-math.log(10000.0) * exponent)[None, :]
    cos_all, sin_all = jnp.cos(angles), jnp.sin(angles)
    cosf = jnp.where(lane < ROT, cos_all, 1.0)
    s1 = jnp.where(lane < half_rot, -sin_all, 0.0)
    s2 = jnp.where((lane >= half_rot) & (lane < ROT), sin_all, 0.0)
    return cosf, s1, s2


def local(small, block_input, out_grad, lengths, attn_gain, attn_shift, ffn_gain, ffn_shift, w_qkv, b_qkv, w_proj, b_proj, w_in, b_in, w_out, b_out):
    comm = SmallMesh() if small else AnyMesh()
    slots, local_len, d = block_input.shape
    m = slots * local_len
    nheads = b_qkv.shape[0] // (3 * HD)
    nq = 3 * nheads * HD
    ctx = lax.axis_index("ctx")
    core = lax.axis_index("dp") % 2
    meta = jnp.concatenate(
        [ctx[None].astype(jnp.int32), comm.perm(), comm.middle()[None], core[None].astype(jnp.int32), lengths]
    )

    run = Order()
    x2 = block_input.reshape(m, d)
    og2 = out_grad.reshape(m, d)
    ga, sa, gf, sf = (v.reshape(1, d) for v in (attn_gain, attn_shift, ffn_gain, ffn_shift))
    bq = b_qkv.reshape(1, nq)
    positions = ctx * local_len + jnp.arange(local_len, dtype=jnp.int32)
    tabs = rotary_tables(positions.astype(F32))

    own1 = jnp.concatenate([w_qkv, w_proj.T], axis=1).astype(BF)
    hop1 = comm.first_hop(own1)
    own2 = w_in.astype(BF)
    own3 = w_out.T.astype(BF)
    run.last = (own1, own2, own3)
    hop2 = comm.first_hop(own2, hop1[0])
    h1, h2, g, stats, g_sum = run(norm_call, meta, x2, og2, ga, sa, gf, sf, local_len)
    diag1 = comm.second_hop(hop1)
    near1 = comm.near(run, own1, hop1)
    g1 = comm.pieces(near1, hop1, diag1)
    near2 = comm.near(run, own2, hop2)
    kv = run(kv_call, h1, g1, bq, tabs, nheads)
    pv = comm.previous(kv, slots)
    diag2 = comm.second_hop(hop2, (kv,))
    hop3 = comm.first_hop(own3, diag2)
    q, dob = run(qd_call, h1, g, g1, bq, tabs, nheads)
    near3 = comm.near(run, own3, hop3)
    g2 = comm.pieces(near2, hop2, diag2)
    diag3 = comm.second_hop(hop3)
    ob, dq, dkv, dpv = run(attn_call, meta, q, kv, pv, dob, tabs, nheads)
    dkv, rv = comm.give_back(dpv, dkv, slots)
    gb, dg = run(hidden_call, after(h2, *comm.waited(hop3)), g2, b_in.reshape(1, -1))
    g3 = comm.pieces(near3, hop3, diag3)

    pipe = comm.pipe(run, meta[1 + NBLK], 8)
    ff = gb.shape[1] // 512
    out0, out2 = run(out_call, ob, gb, (g1[0], g1[3]), (g3[0], g3[3]))
    pipe.send(out0)
    pipe.send(out2)
    cross3 = comm.scatter_cross(run(wgrad_call, meta, g, gb, half=1))
    far = (1, 2, 4, 5)
    out1, out3 = run(out_call, ob, gb, [g1[k] for k in far], [g3[k] for k in far])
    du, bin_sum = run(dhid_call, g, g3, dg)
    pipe.send(after(out1, du))
    pipe.cross()
    state3 = comm.scatter_own(run, meta, (g, gb), cross3)
    pipe.cross()
    dqkv, bqkv_sum = run(join_call, dq, dkv, rv, tabs, nheads)
    pipe.send(out3)
    gain_sums = jnp.zeros((4, d), F32)
    dn0, dn1, gain_sums = run(back_call, meta, dqkv, du, g1, g2, x2, stats, ga, gf, gain_sums, 0)
    pipe.cross()
    pipe.send(dn0)
    state3 = comm.scatter_half(run, state3)
    theirs1 = run(wgrad_call, meta, h1, dqkv, g, ob, half=1)
    pipe.cross()
    pipe.send(dn1)
    cross2 = comm.scatter_cross(run(wgrad_call, after(meta, jax.tree.leaves(state3)[-1]), h2, du, half=1))
    dn2, dn3, gain_sums = run(back_call, meta, dqkv, du, g1, g2, x2, stats, ga, gf, gain_sums, 1)
    pipe.cross()
    pipe.send(dn2)
    state2 = comm.scatter_own(run, meta, (h2, du), cross2)
    (grad_out,) = comm.scatter_last(run, ((ff, True),), state3)
    pipe.cross()
    pipe.send(dn3)
    state2 = comm.scatter_half(run, state2)
    pipe.cross()
    pipe.send()
    cross1 = comm.scatter_cross(after(theirs1, pipe.here[-1]))

    def sums_of(order):
        return [v for c in order for v in (pipe.here[c], pipe.sent[c])]

    block_output = run(
        rows_call, meta, x2, (b_proj + b_out).reshape(1, d), *sums_of((0, 2, 1, 3)),
        body=functools.partial(block_out_kernel, local_len), name="bout", specs=("row", "vec") + ("part",) * 8,
    ).reshape(slots, local_len, d)
    (grad_in,) = comm.scatter_last(run, ((ff, False),), state2)
    state1 = comm.scatter_own(run, meta, (h1, dqkv, g, ob), cross1)
    pipe.cross()
    pipe.send()
    small = jnp.concatenate([gain_sums.reshape(-1), g_sum.reshape(-1), bqkv_sum.reshape(-1), bin_sum.reshape(-1)])
    small = after(small, pipe.here[-1])
    for step in range(3):
        small = comm.small_sum(run, small, step)()
    gains = small[: 4 * d]
    group = small[4 * d :]
    state1 = comm.scatter_half(run, after(state1, pipe.sent[5]))
    add = comm.small_sum(run, gains, 3)
    pipe.send()
    grad_qkv, grad_proj = comm.scatter_last(
        run, ((nq // 512, False), (nheads * HD // 512, True)), after(state1, pipe.sent[6])
    )
    gains = add()
    add = comm.small_sum(run, gains, 4)
    gains = add().reshape(4, d)
    input_grad = run(
        rows_call, meta, x2, og2, stats, *sums_of(range(4, 8)),
        body=functools.partial(input_grad_kernel, local_len), name="igrad", specs=("row", "row", "stat") + ("part",) * 8,
    ).reshape(slots, local_len, d)
    bias_grad = group[:d]
    return (
        block_output,
        input_grad,
        gains[0],
        gains[1],
        gains[2],
        gains[3],
        grad_qkv,
        group[d : d + nq],
        grad_proj,
        bias_grad,
        grad_in,
        group[d + nq :],
        grad_out,
        bias_grad,
    )


def solution(mesh):
    small = mesh.shape["dp"] == 4 and mesh.shape["ctx"] == 2 and mesh.shape["tensor"] == 4
    placed = (
        P("dp", "ctx", None),
        P("dp", "ctx", None),
        P("dp"),
        P(),
        P(),
        P(),
        P(),
        P(("dp", "ctx"), "tensor"),
        P("tensor"),
        P("tensor", ("dp", "ctx")),
        P(),
        P(("dp", "ctx"), "tensor"),
        P("tensor"),
        P("tensor", ("dp", "ctx")),
        P(),
    )
    return jax.shard_map(
        functools.partial(local, small),
        mesh=mesh,
        in_specs=placed,
        out_specs=(
            P("dp", "ctx", None),
            P("dp", "ctx", None),
            P(),
            P(),
            P(),
            P(),
            P(("dp", "ctx"), "tensor"),
            P("tensor"),
            P("tensor", ("dp", "ctx")),
            P(),
            P(("dp", "ctx"), "tensor"),
            P("tensor"),
            P("tensor", ("dp", "ctx")),
            P(),
        ),
        check_vma=False,
    )
```

```python
import functools
import math

import jax
import jax.numpy as jnp
from jax import lax
from jax.experimental import pallas as pl
from jax.experimental.pallas import tpu as pltpu
from jax.sharding import PartitionSpec as P

HD = 256
ROT = 64
NBLK = 8
BF = jnp.bfloat16
F32 = jnp.float32

neg_big = -1e30
inv_sqrt_two = 0.7071067811865476
inv_sqrt_tau = 0.3989422804014327


COST_SCALE = 20


def cost(flops, nbytes, trans=0):
    k = COST_SCALE
    flops = max(flops, 300 * nbytes)
    return pl.CostEstimate(flops=int(k * flops), bytes_accessed=int(k * nbytes), transcendentals=int(k * trans))


def params(n, mb=60):
    return pltpu.CompilerParams(
        dimension_semantics=("arbitrary",) * n, vmem_limit_bytes=int(mb * 1024 * 1024)
    )


def nn(a, b):
    return lax.dot_general(a, b, (((1,), (0,)), ((), ())), preferred_element_type=F32)


def nn_rows(a, pieces):
    total, at = None, 0
    for w in pieces:
        y = nn(a[:, at : at + w.shape[0]], w[...])
        total = y if total is None else total + y
        at += w.shape[0]
    return total


def nt(a, b):
    return lax.dot_general(a, b, (((1,), (1,)), ((), ())), preferred_element_type=F32)


def tn(a, b):
    return lax.dot_general(a, b, (((0,), (0,)), ((), ())), preferred_element_type=F32)


def block_cols(r):
    return pl.ds(pl.multiple_of(r, 128), 256)


def row_valid(meta, row0, rows, local_len):
    slot = row0 // local_len
    pos = meta[0] * local_len + row0 % local_len + lax.broadcasted_iota(jnp.int32, (rows, 1), 0)
    return (pos < meta[3 + NBLK + slot]).astype(F32)


def norm_kernel(local_len, meta, x_ref, g_ref, ga, sa, h1_ref, g_out, st_ref, gs_ref):
    rows = x_ref.shape[0]
    i = pl.program_id(0)
    x = x_ref[...].astype(F32)
    mean = jnp.mean(x, axis=-1, keepdims=True)
    cen = x - mean
    inv = lax.rsqrt(jnp.mean(cen * cen, axis=-1, keepdims=True) + 1e-05)
    mask = row_valid(meta, i * rows, rows, local_len)
    lane = lax.broadcasted_iota(jnp.int32, (rows, 128), 1)
    st_ref[...] = jnp.where(lane == 0, mean, inv)
    for r in range(NBLK):
        src = block_cols(meta[1 + r] * 256)
        dst = slice(r * 256, (r + 1) * 256)
        xh = (x_ref[:, src].astype(F32) - mean) * inv
        h1_ref[:, dst] = (xh * ga[:, src] + sa[:, src]).astype(BF)
        gm = g_ref[:, src].astype(F32) * mask
        g_out[:, dst] = gm.astype(BF)
        part = jnp.sum(gm, axis=0, keepdims=True)

        @pl.when(i == 0)
        def _():
            gs_ref[:, src] = part

        @pl.when(i > 0)
        def _():
            gs_ref[:, src] = gs_ref[:, src] + part


def second_norm_kernel(meta, x_ref, st_ref, gf, sf, h2_ref):
    for r in range(NBLK):
        src = block_cols(meta[1 + r] * 256)
        xh = (x_ref[:, src].astype(F32) - st_ref[:, 0:1]) * st_ref[:, 1:2]
        h2_ref[:, r * 256 : (r + 1) * 256] = (xh * gf[:, src] + sf[:, src]).astype(BF)


def second_norm_call(meta, x2, st, gf, sf):
    m, d = x2.shape
    rows = 256
    row_spec = pl.BlockSpec((rows, d), lambda i, mt: (i, 0))
    vec = pl.BlockSpec((1, d), lambda i, mt: (0, 0))
    return pl.pallas_call(
        second_norm_kernel,
        name="norm2",
        grid_spec=pltpu.PrefetchScalarGridSpec(
            num_scalar_prefetch=1,
            grid=(m // rows,),
            in_specs=[row_spec, pl.BlockSpec((rows, 128), lambda i, mt: (i, 0)), vec, vec],
            out_specs=row_spec,
        ),
        out_shape=jax.ShapeDtypeStruct((m, d), BF),
        compiler_params=params(1),
        cost_estimate=cost(5 * m * d, 4 * m * d),
    )(meta, x2, st, gf, sf)


def norm_call(meta, x2, g2, ga, sa, local_len):
    m, d = x2.shape
    rows = 256
    row_spec = pl.BlockSpec((rows, d), lambda i, mt: (i, 0))
    vec = pl.BlockSpec((1, d), lambda i, mt: (0, 0))
    return pl.pallas_call(
        functools.partial(norm_kernel, local_len),
        name="norm",
        grid_spec=pltpu.PrefetchScalarGridSpec(
            num_scalar_prefetch=1,
            grid=(m // rows,),
            in_specs=[row_spec, row_spec, vec, vec],
            out_specs=[row_spec, row_spec, pl.BlockSpec((rows, 128), lambda i, mt: (i, 0)), vec],
        ),
        out_shape=[jax.ShapeDtypeStruct((m, d), BF)] * 2
        + [jax.ShapeDtypeStruct((m, 128), F32), jax.ShapeDtypeStruct((1, d), F32)],
        compiler_params=params(1),
        cost_estimate=cost(20 * m * d, 10 * m * d),
    )(meta, x2, g2, ga, sa)


def rotate_tile(y, cosf, s1, s2, sign):
    head = y[:, :128]
    rot = (
        head * cosf
        + pltpu.roll(head, 96, 1) * (s1 * sign)
        + pltpu.roll(head, 32, 1) * (s2 * sign)
    )
    return rot, y[:, 128:]


def rotated(out, y, cosf, s1, s2):
    local_len = cosf.shape[0]
    for s in range(y.shape[0] // local_len):
        rows = slice(s * local_len, (s + 1) * local_len)
        rot, rest = rotate_tile(y[rows], cosf[...], s1[...], s2[...], 1.0)
        out[rows, :128] = rot.astype(BF)
        out[rows, 128:] = rest.astype(BF)


def kv_kernel(h1, w0, w1, w2, w3, w4, w5, b_ref, cosf, s1, s2, kv_ref):
    part = lax.rem(pl.program_id(0), 2)
    y = nn_rows(h1, (w0, w1, w2, w3, w4, w5)) + b_ref[...]

    @pl.when(part == 0)
    def _():
        rotated(kv_ref, y, cosf, s1, s2)

    @pl.when(part == 1)
    def _():
        kv_ref[...] = y.astype(BF)


def kv_call(h1, pieces, b_qkv, tabs, nheads):
    m, d = h1.shape
    local_len = tabs[0].shape[0]

    def src(j):
        return (0, (j // 2) * 3 + 1 + j % 2)

    tab = pl.BlockSpec((local_len, 128), lambda j: (0, 0))
    return pl.pallas_call(
        kv_kernel,
        name="kv",
        grid=(2 * nheads,),
        in_specs=[
            pl.BlockSpec((m, d), lambda j: (0, 0)),
            *[pl.BlockSpec((p.shape[0], HD), src) for p in pieces],
            pl.BlockSpec((1, HD), src),
            tab,
            tab,
            tab,
        ],
        out_specs=pl.BlockSpec((m, HD), lambda j: (0, j)),
        out_shape=jax.ShapeDtypeStruct((m, 2 * nheads * HD), BF),
        compiler_params=params(1),
        cost_estimate=cost(4 * m * d * nheads * HD, 2 * (m * d + 2 * d * nheads * HD + 2 * m * nheads * HD)),
    )(h1, *pieces, b_qkv, *tabs)


def qd_kernel(nheads, h1, g, w0, w1, w2, w3, w4, w5, b_ref, cosf, s1, s2, q_ref, dob_ref):
    j = pl.program_id(0)
    pieces = (w0, w1, w2, w3, w4, w5)

    @pl.when(j < nheads)
    def _():
        rotated(q_ref, nn_rows(h1, pieces) + b_ref[...], cosf, s1, s2)

    @pl.when(j >= nheads)
    def _():
        dob_ref[...] = nn_rows(g, pieces).astype(BF)


def qd_call(h1, g, pieces, b_qkv, tabs, nheads):
    m, d = h1.shape
    local_len = tabs[0].shape[0]
    full = pl.BlockSpec((m, d), lambda j: (0, 0))

    def src(j):
        return (0, jnp.where(j < nheads, 3 * j, 2 * nheads + j))

    tab = pl.BlockSpec((local_len, 128), lambda j: (0, 0))
    return pl.pallas_call(
        functools.partial(qd_kernel, nheads),
        name="qd",
        grid=(2 * nheads,),
        in_specs=[
            full,
            full,
            *[pl.BlockSpec((p.shape[0], HD), src) for p in pieces],
            pl.BlockSpec((1, HD), lambda j: (0, 3 * jnp.minimum(j, nheads - 1))),
            tab,
            tab,
            tab,
        ],
        out_specs=[
            pl.BlockSpec((m, HD), lambda j: (0, jnp.minimum(j, nheads - 1))),
            pl.BlockSpec((m, HD), lambda j: (0, jnp.maximum(j - nheads, 0))),
        ],
        out_shape=[jax.ShapeDtypeStruct((m, nheads * HD), BF)] * 2,
        compiler_params=params(1),
        cost_estimate=cost(4 * m * d * nheads * HD, 2 * (2 * m * d + 2 * d * nheads * HD + 2 * m * nheads * HD)),
    )(h1, g, *pieces, b_qkv, *tabs)


def attn_kernel(nprev, local_len, meta, q_ref, kv_ref, pv_ref, dob_ref, cosf, s1, s2, ob_ref, dq_ref, dkv_ref, dpv_ref, sc_ref, dq_acc):
    slot = pl.program_id(0)
    ctx = meta[0]
    length = meta[3 + NBLK + slot]
    scale = 1.0 / math.sqrt(HD)
    n_vis = jnp.minimum(ctx, (length + local_len - 1) // local_len)
    q = q_ref[...]
    dob = dob_ref[...]
    own_k = kv_ref[:, :HD]
    own_v = kv_ref[:, HD:]

    ri = lax.broadcasted_iota(jnp.int32, (local_len, local_len), 0)
    ci = lax.broadcasted_iota(jnp.int32, (local_len, local_len), 1)
    s_own = nt(q, own_k) * scale
    s_own = jnp.where((ci <= ri) & (ci < length - ctx * local_len), s_own, neg_big)
    sc_ref[nprev] = s_own

    def prev_rows(jb):
        return pl.ds(pl.multiple_of(jb * local_len, local_len), local_len)

    def score(jb, top):
        s = nt(q, pv_ref[prev_rows(jb), :HD]) * scale
        s = jnp.where(ci[:1] < length - jb * local_len, s, neg_big)
        sc_ref[jb] = s
        return jnp.maximum(top, jnp.max(s, axis=1, keepdims=True))

    top = lax.fori_loop(0, n_vis, score, jnp.max(s_own, axis=1, keepdims=True))

    e_own = jnp.exp(sc_ref[nprev] - top)
    sc_ref[nprev] = e_own

    def expo(jb, tot):
        e = jnp.exp(sc_ref[jb] - top)
        sc_ref[jb] = e
        return tot + jnp.sum(e, axis=1, keepdims=True)

    tot = lax.fori_loop(0, n_vis, expo, jnp.sum(e_own, axis=1, keepdims=True))
    inv = 1.0 / tot
    att = nn((sc_ref[nprev] * inv).astype(BF), own_v)

    def out_step(jb, acc):
        return acc + nn((sc_ref[jb] * inv).astype(BF), pv_ref[prev_rows(jb), HD:])

    att = lax.fori_loop(0, n_vis, out_step, att)
    ob_ref[...] = att.astype(BF)
    delta = jnp.sum(dob.astype(F32) * att, axis=1, keepdims=True)

    def back(p, k, v):
        pb = p.astype(BF)
        ds = (p * (nt(dob, v) - delta)).astype(BF)
        return nn(ds, k) * scale, tn(ds, q) * scale, tn(pb, dob)

    dq, dk, dv = back(sc_ref[nprev] * inv, own_k, own_v)
    dq_acc[...] = dq
    dkv_ref[:, :HD] = dk
    dkv_ref[:, HD:] = dv

    def back_step(jb, carry):
        rows = prev_rows(jb)
        dqp, dkp, dvp = back(sc_ref[jb] * inv, pv_ref[rows, :HD], pv_ref[rows, HD:])
        dq_acc[...] += dqp
        dpv_ref[rows, :HD] = dkp.astype(BF)
        dpv_ref[rows, HD:] = dvp.astype(BF)
        return carry

    lax.fori_loop(0, n_vis, back_step, 0)

    def clear(jb, carry):
        dpv_ref[prev_rows(jb), :] = jnp.zeros((local_len, 2 * HD), BF)
        return carry

    lax.fori_loop(n_vis, nprev, clear, 0)
    rot, rest = rotate_tile(dq_acc[...], cosf[...], s1[...], s2[...], -1.0)
    dq_ref[:, :128] = rot.astype(BF)
    dq_ref[:, 128:] = rest.astype(BF)


def attn_call(meta, q, kv, pv, dob, tabs, nheads):
    local_len = tabs[0].shape[0]
    slots = q.shape[0] // local_len
    nprev = pv.shape[0] // q.shape[0]
    one = pl.BlockSpec((local_len, HD), lambda s, h, mt: (s, h))
    two = pl.BlockSpec((local_len, 2 * HD), lambda s, h, mt: (s, h))
    prev = pl.BlockSpec((nprev * local_len, 2 * HD), lambda s, h, mt: (s, h))
    tab = pl.BlockSpec((local_len, 128), lambda s, h, mt: (0, 0))
    m = q.shape[0]
    return pl.pallas_call(
        functools.partial(attn_kernel, nprev, local_len),
        name="attn",
        grid_spec=pltpu.PrefetchScalarGridSpec(
            num_scalar_prefetch=1,
            grid=(slots, nheads),
            in_specs=[one, two, prev, one, tab, tab, tab],
            out_specs=[one, one, two, prev],
            scratch_shapes=[
                pltpu.VMEM((nprev + 1, local_len, local_len), F32),
                pltpu.VMEM((local_len, HD), F32),
            ],
        ),
        out_shape=[
            jax.ShapeDtypeStruct((m, nheads * HD), BF),
            jax.ShapeDtypeStruct((m, nheads * HD), BF),
            jax.ShapeDtypeStruct((m, 2 * nheads * HD), F32),
            jax.ShapeDtypeStruct((nprev * m, 2 * nheads * HD), BF),
        ],
        compiler_params=params(2),
        cost_estimate=cost(12 * m * nheads * HD * (nprev + 1) * local_len, 20 * m * nheads * HD, m * nheads * (nprev + 1) * local_len),
    )(meta, q, kv, pv, dob, *tabs)


def join_kernel(nheads, dq_ref, dkv_ref, rv_ref, cosf, s1, s2, out_ref, sum_ref):
    i = pl.program_id(0)

    @pl.when(i == 0)
    def _():
        sum_ref[...] = jnp.zeros_like(sum_ref)

    for h in range(nheads):
        base = h * 3 * HD
        out_ref[:, base : base + HD] = dq_ref[:, h * HD : (h + 1) * HD]
        kc = slice(h * 2 * HD, h * 2 * HD + HD)
        vc = slice(h * 2 * HD + HD, (h + 1) * 2 * HD)
        dk = dkv_ref[:, kc] + rv_ref[:, kc].astype(F32)
        rot, rest = rotate_tile(dk, cosf[...], s1[...], s2[...], -1.0)
        out_ref[:, base + HD : base + HD + 128] = rot.astype(BF)
        out_ref[:, base + HD + 128 : base + 2 * HD] = rest.astype(BF)
        out_ref[:, base + 2 * HD : base + 3 * HD] = (dkv_ref[:, vc] + rv_ref[:, vc].astype(F32)).astype(BF)
    sum_ref[...] += jnp.sum(out_ref[...].astype(F32), axis=0, keepdims=True)


def join_call(dq, dkv, rv, tabs, nheads):
    m = dq.shape[0]
    local_len = tabs[0].shape[0]
    rows = 256
    per = local_len // rows

    def spec(c):
        return pl.BlockSpec((rows, c), lambda i: (i, 0))

    tab = pl.BlockSpec((rows, 128), lambda i: (i % per, 0))
    n = 3 * nheads * HD
    return pl.pallas_call(
        functools.partial(join_kernel, nheads),
        name="join",
        grid=(m // rows,),
        in_specs=[spec(nheads * HD), spec(2 * nheads * HD), spec(2 * nheads * HD), tab, tab, tab],
        out_specs=[spec(n), pl.BlockSpec((1, n), lambda i: (0, 0))],
        out_shape=[jax.ShapeDtypeStruct((m, n), BF), jax.ShapeDtypeStruct((1, n), F32)],
        compiler_params=params(1),
        cost_estimate=cost(10 * m * n, 8 * m * n),
    )(dq, dkv, rv, *tabs)


def hidden_kernel(h2, w0, w1, w2, w3, w4, w5, b_ref, gb_ref, dg_ref):
    u = nn_rows(h2, (w0, w1, w2, w3, w4, w5)) + b_ref[...]
    cdf = 0.5 * (1.0 + lax.erf(u * inv_sqrt_two))
    gb_ref[...] = (u * cdf).astype(BF)
    dg_ref[...] = (cdf + u * (jnp.exp(-0.5 * u * u) * inv_sqrt_tau)).astype(BF)


def hidden_call(h2, pieces, b_in):
    m, d = h2.shape
    f = pieces[0].shape[1]
    t = 256
    col = pl.BlockSpec((m, t), lambda j: (0, j))
    w_specs = [pl.BlockSpec((p.shape[0], t), lambda j: (0, j)) for p in pieces]
    return pl.pallas_call(
        hidden_kernel,
        name="hidden",
        grid=(f // t,),
        in_specs=[pl.BlockSpec((m, d), lambda j: (0, 0)), *w_specs, pl.BlockSpec((1, t), lambda j: (0, j))],
        out_specs=[col, col],
        out_shape=[jax.ShapeDtypeStruct((m, f), BF)] * 2,
        compiler_params=params(1),
        cost_estimate=cost(2 * m * d * f, 2 * (m * d + d * f + 2 * m * f), 2 * m * f),
    )(h2, *pieces, b_in)


def dhid_kernel(g, w0, w1, w2, w3, w4, w5, dg_ref, du_ref, sum_ref):
    a = nn_rows(g, (w0, w1, w2, w3, w4, w5))
    du = (a * dg_ref[...].astype(F32)).astype(BF)
    du_ref[...] = du
    sum_ref[...] = jnp.sum(du.astype(F32), axis=0, keepdims=True)


def dhid_call(g, pieces, dg):
    m, d = g.shape
    f = dg.shape[1]
    t = 256
    col = pl.BlockSpec((m, t), lambda j: (0, j))
    w_specs = [pl.BlockSpec((p.shape[0], t), lambda j: (0, j)) for p in pieces]
    return pl.pallas_call(
        dhid_kernel,
        name="dhid",
        grid=(f // t,),
        in_specs=[pl.BlockSpec((m, d), lambda j: (0, 0))] + w_specs + [col],
        out_specs=[col, pl.BlockSpec((1, t), lambda j: (0, j))],
        out_shape=[jax.ShapeDtypeStruct((m, f), BF), jax.ShapeDtypeStruct((1, f), F32)],
        compiler_params=params(1),
        cost_estimate=cost(2 * m * d * f, 2 * (m * d + d * f + 2 * m * f)),
    )(g, *pieces, dg)


def out_kernel(count, ob, gb, *refs):
    j = pl.program_id(0)
    ps, os, ya, yb = refs[:count], refs[count : 2 * count], refs[-2], refs[-1]
    each = 4 // count
    for k in range(4):

        @pl.when(j == k)
        def _():
            y = ya if k < 2 else yb
            y[...] = (nt(ob[...], ps[k // each][...]) + nt(gb[...], os[k // each][...])).astype(BF)


def piece_spec(count, i, cols, at=0, prefetch=False):
    each = 4 // count

    def place(j, *_):
        return (jnp.clip(j - i * each, 0, each - 1), at)

    if prefetch:
        return pl.BlockSpec((256, cols), lambda j, mt: place(j))
    return pl.BlockSpec((256, cols), lambda j: place(j))


def out_call(ob, gb, proj, out):
    m, f = gb.shape
    nf = ob.shape[1]
    count = len(out)
    last = proj[0].shape[1] // nf - 1
    part = jax.ShapeDtypeStruct((m, 512), BF)
    return pl.pallas_call(
        functools.partial(out_kernel, count),
        name="outp",
        grid=(4,),
        in_specs=[pl.BlockSpec((m, nf), lambda j: (0, 0)), pl.BlockSpec((m, f), lambda j: (0, 0))]
        + [piece_spec(count, i, nf, last) for i in range(count)]
        + [piece_spec(count, i, f) for i in range(count)],
        out_specs=[
            pl.BlockSpec((m, 256), lambda j: (0, jnp.minimum(j, 1))),
            pl.BlockSpec((m, 256), lambda j: (0, jnp.maximum(j - 2, 0))),
        ],
        out_shape=[part, part],
        compiler_params=params(1),
        cost_estimate=cost(2048 * m * (f + nf), 2 * (m * f + m * nf + 1024 * (f + nf) + 1024 * m)),
    )(ob, gb, *proj, *out)


def back_kernel(meta, dqkv, du, w10, w11, w12, w20, w21, w22, x_ref, st_ref, ga, gf, prev, da_ref, db_ref, sums_ref):
    j = pl.program_id(0)
    for w1, w2, dn_ref, mine in ((w10, w20, da_ref, j < 2), (w11, w21, db_ref, j == 2), (w12, w22, db_ref, j == 3)):

        @pl.when(mine)
        def _():
            dh1 = nt(dqkv[...], w1[...])
            dh2 = nt(du[...], w2[...])
            xh = (x_ref[...].astype(F32) - st_ref[:, 0:1]) * st_ref[:, 1:2]
            dn_ref[...] = (dh1 * ga[...] + dh2 * gf[...]).astype(BF)
            sums_ref[0:1, :] = jnp.sum(dh1 * xh, axis=0, keepdims=True)
            sums_ref[1:2, :] = jnp.sum(dh1, axis=0, keepdims=True)
            sums_ref[2:3, :] = jnp.sum(dh2 * xh, axis=0, keepdims=True)
            sums_ref[3:4, :] = jnp.sum(dh2, axis=0, keepdims=True)


def back_call(meta, dqkv, du, g1, g2, x2, st, ga, gf, sums, half):
    m, d = x2.shape
    nq = dqkv.shape[1]
    f = du.shape[1]
    n = d // 4

    def absolute(rows):
        return pl.BlockSpec((rows, 256), lambda j, mt: (0, mt[1 + 4 * half + j]))

    part = jax.ShapeDtypeStruct((m, n), BF)
    at = slice(3 * half, 3 * half + 3)
    return pl.pallas_call(
        back_kernel,
        name="backn",
        grid_spec=pltpu.PrefetchScalarGridSpec(
            num_scalar_prefetch=1,
            grid=(4,),
            in_specs=[
                pl.BlockSpec((m, nq), lambda j, mt: (0, 0)),
                pl.BlockSpec((m, f), lambda j, mt: (0, 0)),
                pl.BlockSpec((256, nq), lambda j, mt: (jnp.minimum(j, 1), 0)),
                pl.BlockSpec((256, nq), lambda j, mt: (0, 0)),
                pl.BlockSpec((256, nq), lambda j, mt: (0, 0)),
                pl.BlockSpec((256, f), lambda j, mt: (jnp.minimum(j, 1), 0)),
                pl.BlockSpec((256, f), lambda j, mt: (0, 0)),
                pl.BlockSpec((256, f), lambda j, mt: (0, 0)),
                absolute(m),
                pl.BlockSpec((m, 128), lambda j, mt: (0, 0)),
                absolute(1),
                absolute(1),
                pl.BlockSpec(memory_space=pl.ANY),
            ],
            out_specs=[
                pl.BlockSpec((m, n // 2), lambda j, mt: (0, jnp.minimum(j, 1))),
                pl.BlockSpec((m, n // 2), lambda j, mt: (0, jnp.maximum(j - 2, 0))),
                absolute(4),
            ],
        ),
        out_shape=[part, part, jax.ShapeDtypeStruct((4, d), F32)],
        input_output_aliases={13: 2},
        compiler_params=params(1),
        cost_estimate=cost(4 * m * n * (f + nq), 2 * (m * f + m * nq + 2 * n * (f + nq) + 4 * m * n)),
    )(meta, dqkv, du, *g1[at], *g2[at], x2, st, ga, gf, sums)


def wgrad_kernel(pairs, adds, split, meta, *refs):
    j = pl.program_id(0)
    start = 0
    for p, count in enumerate(pairs):
        a, b = refs[2 * p], refs[2 * p + 1]

        @pl.when((j >= start) & (j < start + count))
        def _():
            y = tn(a[...], b[...])
            if adds:
                y = y + refs[2 * len(pairs)][...].astype(F32)
            if not split:
                refs[-1][...] = y.astype(BF)
                return
            keep, send = refs[-2:]
            n = y.shape[0] // 4
            swap = meta[2 + NBLK] > 0
            keep[:n] = y[:n].astype(BF)
            keep[n:] = jnp.where(swap, y[2 * n : 3 * n], y[n : 2 * n]).astype(BF)
            send[:n] = jnp.where(swap, y[n : 2 * n], y[2 * n : 3 * n]).astype(BF)
            send[n:] = y[3 * n :].astype(BF)

        start += count


def wgrad_call(meta, *flat, half, add=None, split=False):
    pairs = list(zip(flat[::2], flat[1::2]))
    m, d = pairs[0][0].shape
    t = 512
    counts = tuple(b.shape[1] // t for _, b in pairs)
    total = sum(counts)
    in_specs, ops, start = [], [], 0
    for (a, b), c in zip(pairs, counts):
        in_specs.append(pl.BlockSpec((m, d // 2), lambda j, mt: (0, half)))
        in_specs.append(
            pl.BlockSpec((m, t), lambda j, mt, s=start, c=c: (0, jnp.clip(j - s, 0, c - 1)))
        )
        ops += [a, b]
        start += c
    rows = d // 4 if split else d // 2
    if add is not None:
        in_specs.append(pl.BlockSpec((d // 2, t), lambda j, mt: (0, j)))
        ops.append(add)
    out_spec = pl.BlockSpec((rows, t), lambda j, mt: (0, j))
    out_shape = jax.ShapeDtypeStruct((rows, total * t), BF)
    return pl.pallas_call(
        functools.partial(wgrad_kernel, counts, add is not None, split),
        name="wgrad",
        grid_spec=pltpu.PrefetchScalarGridSpec(
            num_scalar_prefetch=1,
            grid=(total,),
            in_specs=in_specs,
            out_specs=[out_spec, out_spec] if split else out_spec,
        ),
        out_shape=[out_shape, out_shape] if split else out_shape,
        compiler_params=params(1),
        cost_estimate=cost(m * d * total * t, 2 * (m * d // 2 * len(pairs) + m * total * t + d * total * t)),
    )(meta, *ops)


def pack_kernel(*refs):
    out, at = refs[-1], 0
    for ref in refs[:-1]:
        n = ref.shape[0]
        out[at : at + n] = ref[...]
        at += n


def pack_call(*pieces):
    rows = sum(p.shape[0] for p in pieces)
    cols = pieces[0].shape[1]
    t = 512
    return pl.pallas_call(
        pack_kernel,
        name="pack",
        grid=(cols // t,),
        in_specs=[pl.BlockSpec((p.shape[0], t), lambda j: (0, j)) for p in pieces],
        out_specs=pl.BlockSpec((rows, t), lambda j: (0, j)),
        out_shape=jax.ShapeDtypeStruct((rows, cols), BF),
        compiler_params=params(1),
        cost_estimate=cost(0, 4 * rows * cols),
    )(*pieces)


def half_sum_kernel(keep, got, mid, send):
    n = mid.shape[0]
    mid[...] = keep[:n].astype(F32) + got[:n].astype(F32)
    send[...] = (keep[n:].astype(F32) + got[n:].astype(F32)).astype(BF)


def half_sum_call(keep, got):
    rows, cols = keep.shape
    t = 512
    n = rows // 2
    small = pl.BlockSpec((n, t), lambda j: (0, j))
    return pl.pallas_call(
        half_sum_kernel,
        name="hsum",
        grid=(cols // t,),
        in_specs=[pl.BlockSpec((rows, t), lambda j: (0, j))] * 2,
        out_specs=[small] * 2,
        out_shape=[jax.ShapeDtypeStruct((n, cols), F32), jax.ShapeDtypeStruct((n, cols), BF)],
        compiler_params=params(1),
        cost_estimate=cost(4 * n * cols, 14 * n * cols),
    )(keep, got)


def last_sum_kernel(plan, mid, got, *outs):
    j = pl.program_id(0)
    at = 0
    for (count, turned), out in zip(plan, outs):

        @pl.when((j >= at) & (j < at + count))
        def _():
            v = mid[...] + got[...].astype(F32)
            out[...] = v.T if turned else v

        at += count


def last_sum_call(mid, got, plan):
    n, cols = mid.shape
    t = 512
    block = pl.BlockSpec((n, t), lambda j: (0, j))
    out_specs, out_shape, at = [], [], 0
    for count, turned in plan:
        def place(j, at=at, count=count):
            return jnp.clip(j - at, 0, count - 1)

        if turned:
            out_specs.append(pl.BlockSpec((t, n), lambda j, f=place: (f(j), 0)))
            out_shape.append(jax.ShapeDtypeStruct((count * t, n), F32))
        else:
            out_specs.append(pl.BlockSpec((n, t), lambda j, f=place: (0, f(j))))
            out_shape.append(jax.ShapeDtypeStruct((n, count * t), F32))
        at += count
    return pl.pallas_call(
        functools.partial(last_sum_kernel, plan),
        name="lsum",
        grid=(cols // t,),
        in_specs=[block, block],
        out_specs=out_specs,
        out_shape=out_shape,
        compiler_params=params(1),
        cost_estimate=cost(2 * n * cols, 10 * n * cols),
    )(mid, got)


def total_of(meta, refs, c, cols):
    here, sent = refs[2 * c], refs[2 * c + 1]
    return jnp.where(meta[1 + NBLK] > 0, here[:, cols].astype(F32), sent[:, cols].astype(F32))


def block_out_kernel(local_len, first, meta, x_ref, b_ref, *refs):
    y_ref = refs[-1]
    rows = x_ref.shape[0]
    mask = row_valid(meta, (first + pl.program_id(0)) * rows, rows, local_len)
    for r in range(NBLK):
        col = block_cols(meta[1 + r] * 256)
        k = r % 2 * 256
        s = total_of(meta, refs, r // 2, slice(k, k + 256))
        y_ref[:, col] = (mask * (x_ref[:, col].astype(F32) + s + b_ref[:, col])).astype(BF)


def input_grad_kernel(local_len, first, meta, x_ref, g_ref, st_ref, *refs):
    y_ref = refs[-1]
    rows = x_ref.shape[0]
    mask = row_valid(meta, (first + pl.program_id(0)) * rows, rows, local_len)
    mean = st_ref[:, 0:1]
    inv = st_ref[:, 1:2]
    one = jnp.zeros((rows, 1), F32)
    two = jnp.zeros((rows, 1), F32)
    for r in range(NBLK):
        col = block_cols(meta[1 + r] * 256)
        k = r % 2 * 256
        dn = total_of(meta, refs, r // 2, slice(k, k + 256))
        one += jnp.sum(dn, axis=1, keepdims=True)
        two += jnp.sum(dn * ((x_ref[:, col].astype(F32) - mean) * inv), axis=1, keepdims=True)
    d = x_ref.shape[1]
    one = one / d
    two = two / d
    for r in range(NBLK):
        col = block_cols(meta[1 + r] * 256)
        k = r % 2 * 256
        dn = total_of(meta, refs, r // 2, slice(k, k + 256))
        xh = (x_ref[:, col].astype(F32) - mean) * inv
        y_ref[:, col] = (g_ref[:, col].astype(F32) * mask + inv * (dn - one - xh * two)).astype(BF)


def rows_call(meta, *ops, body, name, specs, steps=None, into=None):
    rows = 256
    m, d = ops[0].shape
    first, last = steps or (0, m // rows)
    made = {
        "row": pl.BlockSpec((rows, d), lambda i, mt: (first + i, 0)),
        "part": pl.BlockSpec((rows, d // 4), lambda i, mt: (first + i, 0)),
        "stat": pl.BlockSpec((rows, 128), lambda i, mt: (first + i, 0)),
        "vec": pl.BlockSpec((1, d), lambda i, mt: (0, 0)),
    }
    in_specs = [made[s] for s in specs]
    aliases = {}
    if into is not None:
        aliases = {1 + len(ops): 0}
        in_specs.append(pl.BlockSpec(memory_space=pl.ANY))
        ops += (into,)
    return pl.pallas_call(
        functools.partial(body, first),
        name=name,
        grid_spec=pltpu.PrefetchScalarGridSpec(
            num_scalar_prefetch=1,
            grid=(last - first,),
            in_specs=in_specs,
            out_specs=made["row"],
        ),
        out_shape=jax.ShapeDtypeStruct((m, d), BF),
        input_output_aliases=aliases,
        compiler_params=params(1),
        cost_estimate=cost(10 * (last - first) * rows * d, 8 * (last - first) * rows * d),
    )(meta, *ops)


def after(v, *others):
    return lax.optimization_barrier((v,) + others)[0]


class Order:
    def __init__(self):
        self.last = ()

    def __call__(self, f, first, *rest, **named):
        out = f(after(first, *self.last), *rest, **named)
        self.last = (jax.tree.leaves(out)[0],)
        return out


def add_bf(a, b):
    return lax.optimization_barrier((a.astype(F32) + b.astype(F32)).astype(BF))


def pick_bf(a, b, middle, other):
    total = (a.astype(F32) + b.astype(F32)).astype(BF)
    return lax.optimization_barrier(jnp.where(middle > 0, total, other))


class Pipe:
    LAG = 3

    def __init__(self, run, middle, count):
        self.run, self.middle, self.count = run, middle, count
        self.parts, self.got, self.sums, self.crossed = [], [], [], []
        self.here, self.sent = [], []

    def send(self, part=None):
        step = len(self.got)
        back = step - self.LAG
        pairs = []
        v = part
        if part is not None:
            self.parts.append(part)
            pairs += [(0, 1), (3, 2)]
        if back >= 0:
            pairs += [(1, 0), (2, 3)]
            a, b = self.sums[back], self.crossed[back]
            if part is None:
                v = self.run(add_bf, a, b)
            else:
                v = self.run(pick_bf, a, b, self.middle, part)
        got = lax.ppermute(v, "tensor", pairs)
        self.got.append(got)
        if back >= 0:
            self.here.append(v)
            self.sent.append(got)

    def cross(self):
        k = len(self.sums)
        v = self.run(add_bf, self.parts[k], self.got[k])
        self.sums.append(v)
        self.crossed.append(lax.ppermute(v, "tensor", [(1, 2), (2, 1)]))


class PlainPipe:
    def __init__(self, run, middle, count):
        self.here, self.sent, self.sums = [], [], []

    def send(self, part=None):
        if part is not None:
            total = lax.psum(part, "tensor")
            self.here.append(total)
            self.sent.append(total)

    def cross(self):
        pass


class SmallMesh:
    def x(self, v):
        return lax.ppermute(v, "dp", [(0, 2), (2, 0), (1, 3), (3, 1)])

    def core(self, v):
        return lax.ppermute(v, "dp", [(0, 1), (1, 0), (2, 3), (3, 2)])

    def y(self, v):
        return lax.ppermute(v, "ctx", [(0, 1), (1, 0)])

    def perm(self):
        r = jnp.arange(NBLK, dtype=jnp.int32)
        dp = lax.axis_index("dp") ^ (((r >> 1) & 1) * 2 + (r >> 2))
        return dp * 2 + (lax.axis_index("ctx") ^ (r & 1))

    def middle(self):
        z = lax.axis_index("tensor")
        return ((z == 1) | (z == 2)).astype(jnp.int32)

    pipe = Pipe

    def first_hop(self, own, earlier=None):
        if earlier is None:
            return self.x(own), self.y(own)
        return self.x(after(own, earlier)), self.y(own)

    def second_hop(self, hop, earlier=()):
        return self.x(after(hop[1], hop[0], *earlier))

    def waited(self, hop):
        return hop

    def near(self, run, own, hop):
        v = run(pack_call, own, hop[1])
        return v, self.core(v)

    def pieces(self, near, hop, diag, earlier=()):
        return near[0], hop[0], diag, near[1], self.core(after(hop[0], *earlier[:1])), self.core(after(diag, *earlier))

    def turn(self, v, first):
        pairs = []
        for dp in range(4):
            for c in range(2):
                to = (dp ^ 2) * 2 + c if dp % 2 != first else dp * 2 + (c ^ 1)
                pairs.append((dp * 2 + c, to))
        return lax.ppermute(v, ("dp", "ctx"), pairs)

    def scatter_cross(self, theirs):
        return self.core(theirs)

    def scatter_own(self, run, meta, pairs, got):
        keep, send = run(wgrad_call, meta, *pairs, half=0, add=got, split=True)
        return keep, self.turn(send, 1)

    def scatter_half(self, run, parts):
        mid, send = run(half_sum_call, *parts)
        return mid, self.turn(send, 0)

    def scatter_last(self, run, plan, parts):
        return run(last_sum_call, *parts, plan=plan)

    def previous(self, kv, slots):
        return lax.ppermute(kv, "ctx", [(0, 1)])

    def give_back(self, dpv, dkv, slots):
        return dkv, lax.ppermute(dpv, "ctx", [(1, 0)])

    def small_sum(self, run, v, step):
        def add(a, b):
            return a + b

        if step == 0:
            got = self.core(v)
        elif step == 1:
            got = self.x(v)
        elif step == 2:
            got = self.y(v)
        elif step == 3:
            got = lax.ppermute(v, "tensor", [(0, 1), (1, 0), (2, 3), (3, 2)])
        else:
            got = lax.ppermute(v, "tensor", [(0, 2), (2, 0), (1, 3), (3, 1)])
        return lambda: run(add, v, got)


class AnyMesh:
    def perm(self):
        return jnp.arange(NBLK, dtype=jnp.int32)

    def middle(self):
        return jnp.ones((), jnp.int32)

    pipe = PlainPipe

    def first_hop(self, own, earlier=None):
        return lax.all_gather(own, ("dp", "ctx"), axis=0, tiled=True)

    def second_hop(self, hop, earlier=()):
        return ()

    def waited(self, hop):
        return (hop,)

    def near(self, run, own, hop):
        return hop[:512], hop[1024:1536]

    def pieces(self, near, hop, diag, earlier=()):
        return near[0], hop[512:768], hop[768:1024], near[1], hop[1536:1792], hop[1792:]

    def scatter_cross(self, theirs):
        return theirs

    def scatter_own(self, run, meta, pairs, got):
        full = jnp.concatenate([run(wgrad_call, meta, *pairs, half=0), got], axis=0)
        return lax.psum_scatter(full, ("dp", "ctx"), scatter_dimension=0, tiled=True).astype(F32)

    def scatter_half(self, run, parts):
        return parts

    def scatter_last(self, run, plan, parts):
        outs, at = [], 0
        for count, turned in plan:
            v = parts[:, at * 512 : (at + count) * 512]
            outs.append(v.T if turned else v)
            at += count
        return outs

    def previous(self, kv, slots):
        own = kv.reshape(slots, -1, kv.shape[1])
        full = lax.all_gather(own, "ctx", axis=1, tiled=True)
        return full.reshape(-1, kv.shape[1])

    def give_back(self, dpv, dkv, slots):
        cols = dkv.shape[1]
        full = dpv.reshape(slots, -1, cols)
        got = lax.psum_scatter(full, "ctx", scatter_dimension=1, tiled=True)
        return dkv, got.reshape(-1, cols)

    def small_sum(self, run, v, step):
        got = v
        if step == 0:
            got = lax.psum(v, ("dp", "ctx"))
        elif step == 3:
            got = lax.psum(v, "tensor")
        return lambda: got


def rotary_tables(positions):
    half_rot = ROT // 2
    lane = jnp.arange(128, dtype=jnp.int32)
    exponent = (lane % half_rot).astype(F32) * (2.0 / ROT)
    angles = positions[:, None] * jnp.exp(-math.log(10000.0) * exponent)[None, :]
    cos_all, sin_all = jnp.cos(angles), jnp.sin(angles)
    cosf = jnp.where(lane < ROT, cos_all, 1.0)
    s1 = jnp.where(lane < half_rot, -sin_all, 0.0)
    s2 = jnp.where((lane >= half_rot) & (lane < ROT), sin_all, 0.0)
    return cosf, s1, s2


def local(small, block_input, out_grad, lengths, attn_gain, attn_shift, ffn_gain, ffn_shift, w_qkv, b_qkv, w_proj, b_proj, w_in, b_in, w_out, b_out):
    comm = SmallMesh() if small else AnyMesh()
    slots, local_len, d = block_input.shape
    m = slots * local_len
    nheads = b_qkv.shape[0] // (3 * HD)
    nq = 3 * nheads * HD
    ctx = lax.axis_index("ctx")
    core = lax.axis_index("dp") % 2
    meta = jnp.concatenate(
        [ctx[None].astype(jnp.int32), comm.perm(), comm.middle()[None], core[None].astype(jnp.int32), lengths]
    )

    run = Order()
    x2 = block_input.reshape(m, d)
    og2 = out_grad.reshape(m, d)
    ga, sa, gf, sf = (v.reshape(1, d) for v in (attn_gain, attn_shift, ffn_gain, ffn_shift))
    bq = b_qkv.reshape(1, nq)
    positions = ctx * local_len + jnp.arange(local_len, dtype=jnp.int32)
    tabs = rotary_tables(positions.astype(F32))

    own1 = jnp.concatenate([w_qkv, w_proj.T], axis=1).astype(BF)
    hop1 = comm.first_hop(own1)
    own2 = w_in.astype(BF)
    own3 = w_out.T.astype(BF)
    run.last = (own1, own2, own3)
    hop2 = comm.first_hop(own2, hop1[0])
    h1, g, stats, g_sum = run(norm_call, meta, x2, og2, ga, sa, local_len)
    diag1 = comm.second_hop(hop1)
    near1 = comm.near(run, own1, hop1)
    g1 = comm.pieces(near1, hop1, diag1)
    near2 = comm.near(run, own2, hop2)
    kv = run(kv_call, h1, g1, bq, tabs, nheads)
    pv = comm.previous(kv, slots)
    diag2 = comm.second_hop(hop2, (kv,))
    hop3 = comm.first_hop(own3, diag2)
    q, dob = run(qd_call, h1, g, g1, bq, tabs, nheads)
    g2 = comm.pieces(near2, hop2, diag2, (kv, q))
    diag3 = comm.second_hop(hop3)
    h2 = run(second_norm_call, meta, x2, stats, gf, sf)
    gb, dg = run(hidden_call, h2, g2, b_in.reshape(1, -1))
    near3 = comm.near(run, own3, hop3)
    ob, dq, dkv, dpv = run(attn_call, meta, q, kv, pv, dob, tabs, nheads)
    dkv, rv = comm.give_back(dpv, dkv, slots)
    g3 = comm.pieces(near3, hop3, diag3)

    pipe = comm.pipe(run, meta[1 + NBLK], 8)
    ff = gb.shape[1] // 512
    out0, out2 = run(out_call, ob, gb, (g1[0], g1[3]), (g3[0], g3[3]))
    pipe.send(out0)
    pipe.send(out2)
    far = (1, 2, 4, 5)
    out1, out3 = run(out_call, ob, gb, [g1[k] for k in far], [g3[k] for k in far])
    cross3 = comm.scatter_cross(run(wgrad_call, meta, g, gb, half=1))
    du, bin_sum = run(dhid_call, g, g3, dg)
    pipe.cross()
    pipe.send(after(out1, *pipe.sums))
    state3 = comm.scatter_own(run, meta, (g, gb), cross3)
    pipe.cross()
    dqkv, bqkv_sum = run(join_call, dq, dkv, rv, tabs, nheads)
    pipe.send(out3)
    gain_sums = jnp.zeros((4, d), F32)
    dn0, dn1, gain_sums = run(back_call, meta, dqkv, du, g1, g2, x2, stats, ga, gf, gain_sums, 0)
    pipe.cross()
    pipe.send(dn0)
    state3 = comm.scatter_half(run, state3)
    theirs1 = run(wgrad_call, meta, h1, dqkv, g, ob, half=1)
    pipe.cross()
    pipe.send(dn1)
    cross2 = comm.scatter_cross(run(wgrad_call, after(meta, jax.tree.leaves(state3)[-1]), h2, du, half=1))
    dn2, dn3, gain_sums = run(back_call, meta, dqkv, du, g1, g2, x2, stats, ga, gf, gain_sums, 1)
    pipe.cross()
    pipe.send(dn2)
    state2 = comm.scatter_own(run, meta, (h2, du), cross2)
    pipe.cross()
    pipe.send(dn3)
    small = jnp.concatenate([gain_sums.reshape(-1), g_sum.reshape(-1), bqkv_sum.reshape(-1), bin_sum.reshape(-1)])
    add = comm.small_sum(run, small, 0)
    (grad_out,) = comm.scatter_last(run, ((ff, True),), state3)
    small = add()
    add = comm.small_sum(run, small, 1)
    state2 = comm.scatter_half(run, state2)
    small = add()
    pipe.cross()
    pipe.send()
    cross1 = comm.scatter_cross(after(theirs1, pipe.here[-1]))

    def sums_of(order):
        return [v for c in order for v in (pipe.here[c], pipe.sent[c])]

    out_ops = (meta, x2, (b_proj + b_out).reshape(1, d), *sums_of((0, 2, 1, 3)))
    out_half = functools.partial(
        rows_call, body=functools.partial(block_out_kernel, local_len), name="bout", specs=("row", "vec") + ("part",) * 8
    )
    block_output = run(out_half, *out_ops, steps=(0, 2))
    (grad_in,) = comm.scatter_last(run, ((ff, False),), state2)
    add = comm.small_sum(run, after(small, grad_in), 2)
    state1 = comm.scatter_own(run, meta, (h1, dqkv, g, ob), cross1)
    small = add()
    pipe.cross()
    pipe.send()
    block_output = run(out_half, *out_ops, steps=(2, 4), into=block_output).reshape(slots, local_len, d)
    gains = small[: 4 * d]
    group = small[4 * d :]
    state1 = comm.scatter_half(run, after(state1, pipe.sent[5]))
    add = comm.small_sum(run, gains, 3)
    pipe.send()
    grad_qkv, grad_proj = comm.scatter_last(
        run, ((nq // 512, False), (nheads * HD // 512, True)), after(state1, pipe.sent[6])
    )
    gains = add()
    add = comm.small_sum(run, gains, 4)
    input_grad = run(
        rows_call, meta, x2, og2, stats, *sums_of(range(4, 8)),
        body=functools.partial(input_grad_kernel, local_len), name="igrad", specs=("row", "row", "stat") + ("part",) * 8,
    ).reshape(slots, local_len, d)
    gains = add().reshape(4, d)
    bias_grad = group[:d]
    return (
        block_output,
        input_grad,
        gains[0],
        gains[1],
        gains[2],
        gains[3],
        grad_qkv,
        group[d : d + nq],
        grad_proj,
        bias_grad,
        grad_in,
        group[d + nq :],
        grad_out,
        bias_grad,
    )


def solution(mesh):
    small = mesh.shape["dp"] == 4 and mesh.shape["ctx"] == 2 and mesh.shape["tensor"] == 4
    placed = (
        P("dp", "ctx", None),
        P("dp", "ctx", None),
        P("dp"),
        P(),
        P(),
        P(),
        P(),
        P(("dp", "ctx"), "tensor"),
        P("tensor"),
        P("tensor", ("dp", "ctx")),
        P(),
        P(("dp", "ctx"), "tensor"),
        P("tensor"),
        P("tensor", ("dp", "ctx")),
        P(),
    )
    return jax.shard_map(
        functools.partial(local, small),
        mesh=mesh,
        in_specs=placed,
        out_specs=(
            P("dp", "ctx", None),
            P("dp", "ctx", None),
            P(),
            P(),
            P(),
            P(),
            P(("dp", "ctx"), "tensor"),
            P("tensor"),
            P("tensor", ("dp", "ctx")),
            P(),
            P(("dp", "ctx"), "tensor"),
            P("tensor"),
            P("tensor", ("dp", "ctx")),
            P(),
        ),
        check_vma=False,
    )
```

```python
import functools
import math

import jax
import jax.numpy as jnp
from jax import lax
from jax.experimental import pallas as pl
from jax.experimental.pallas import tpu as pltpu
from jax.sharding import PartitionSpec as P

HD = 256
ROT = 64
NBLK = 8
BF = jnp.bfloat16
F32 = jnp.float32

neg_big = -1e30
inv_sqrt_two = 0.7071067811865476
inv_sqrt_tau = 0.3989422804014327


COST_SCALE = 20


def cost(flops, nbytes, trans=0, k=COST_SCALE):
    flops = max(flops, 300 * nbytes)
    return pl.CostEstimate(flops=int(k * flops), bytes_accessed=int(k * nbytes), transcendentals=int(k * trans))


def params(n, mb=60):
    return pltpu.CompilerParams(
        dimension_semantics=("arbitrary",) * n, vmem_limit_bytes=int(mb * 1024 * 1024)
    )


def nn(a, b):
    return lax.dot_general(a, b, (((1,), (0,)), ((), ())), preferred_element_type=F32)


def nn_rows(a, pieces):
    total, at = None, 0
    for w in pieces:
        y = nn(a[:, at : at + w.shape[0]], w[...])
        total = y if total is None else total + y
        at += w.shape[0]
    return total


def nt(a, b):
    return lax.dot_general(a, b, (((1,), (1,)), ((), ())), preferred_element_type=F32)


def tn(a, b):
    return lax.dot_general(a, b, (((0,), (0,)), ((), ())), preferred_element_type=F32)


def block_cols(r):
    return pl.ds(pl.multiple_of(r, 128), 256)


def row_valid(meta, row0, rows, local_len):
    slot = row0 // local_len
    pos = meta[0] * local_len + row0 % local_len + lax.broadcasted_iota(jnp.int32, (rows, 1), 0)
    return (pos < meta[3 + NBLK + slot]).astype(F32)


def norm_kernel(local_len, meta, x_ref, g_ref, ga, sa, h1_ref, g_out, st_ref, gs_ref):
    rows = x_ref.shape[0]
    i = pl.program_id(0)
    x = x_ref[...].astype(F32)
    mean = jnp.mean(x, axis=-1, keepdims=True)
    cen = x - mean
    inv = lax.rsqrt(jnp.mean(cen * cen, axis=-1, keepdims=True) + 1e-05)
    mask = row_valid(meta, i * rows, rows, local_len)
    lane = lax.broadcasted_iota(jnp.int32, (rows, 128), 1)
    st_ref[...] = jnp.where(lane == 0, mean, inv)
    for r in range(NBLK):
        src = block_cols(meta[1 + r] * 256)
        dst = slice(r * 256, (r + 1) * 256)
        xh = (x_ref[:, src].astype(F32) - mean) * inv
        h1_ref[:, dst] = (xh * ga[:, src] + sa[:, src]).astype(BF)
        gm = g_ref[:, src].astype(F32) * mask
        g_out[:, dst] = gm.astype(BF)
        part = jnp.sum(gm, axis=0, keepdims=True)

        @pl.when(i == 0)
        def _():
            gs_ref[:, src] = part

        @pl.when(i > 0)
        def _():
            gs_ref[:, src] = gs_ref[:, src] + part


def second_norm_kernel(meta, x_ref, st_ref, gf, sf, h2_ref):
    for r in range(NBLK):
        src = block_cols(meta[1 + r] * 256)
        xh = (x_ref[:, src].astype(F32) - st_ref[:, 0:1]) * st_ref[:, 1:2]
        h2_ref[:, r * 256 : (r + 1) * 256] = (xh * gf[:, src] + sf[:, src]).astype(BF)


def second_norm_call(meta, x2, st, gf, sf):
    m, d = x2.shape
    rows = 256
    row_spec = pl.BlockSpec((rows, d), lambda i, mt: (i, 0))
    vec = pl.BlockSpec((1, d), lambda i, mt: (0, 0))
    return pl.pallas_call(
        second_norm_kernel,
        name="norm2",
        grid_spec=pltpu.PrefetchScalarGridSpec(
            num_scalar_prefetch=1,
            grid=(m // rows,),
            in_specs=[row_spec, pl.BlockSpec((rows, 128), lambda i, mt: (i, 0)), vec, vec],
            out_specs=row_spec,
        ),
        out_shape=jax.ShapeDtypeStruct((m, d), BF),
        compiler_params=params(1),
        cost_estimate=cost(5 * m * d, 4 * m * d),
    )(meta, x2, st, gf, sf)


def norm_call(meta, x2, g2, ga, sa, local_len):
    m, d = x2.shape
    rows = 256
    row_spec = pl.BlockSpec((rows, d), lambda i, mt: (i, 0))
    vec = pl.BlockSpec((1, d), lambda i, mt: (0, 0))
    return pl.pallas_call(
        functools.partial(norm_kernel, local_len),
        name="norm",
        grid_spec=pltpu.PrefetchScalarGridSpec(
            num_scalar_prefetch=1,
            grid=(m // rows,),
            in_specs=[row_spec, row_spec, vec, vec],
            out_specs=[row_spec, row_spec, pl.BlockSpec((rows, 128), lambda i, mt: (i, 0)), vec],
        ),
        out_shape=[jax.ShapeDtypeStruct((m, d), BF)] * 2
        + [jax.ShapeDtypeStruct((m, 128), F32), jax.ShapeDtypeStruct((1, d), F32)],
        compiler_params=params(1),
        cost_estimate=cost(20 * m * d, 10 * m * d),
    )(meta, x2, g2, ga, sa)


def rotate_tile(y, cosf, s1, s2, sign):
    head = y[:, :128]
    rot = (
        head * cosf
        + pltpu.roll(head, 96, 1) * (s1 * sign)
        + pltpu.roll(head, 32, 1) * (s2 * sign)
    )
    return rot, y[:, 128:]


def rotated(out, y, cosf, s1, s2):
    local_len = cosf.shape[0]
    for s in range(y.shape[0] // local_len):
        rows = slice(s * local_len, (s + 1) * local_len)
        rot, rest = rotate_tile(y[rows], cosf[...], s1[...], s2[...], 1.0)
        out[rows, :128] = rot.astype(BF)
        out[rows, 128:] = rest.astype(BF)


def kv_kernel(h1, w0, w1, w2, w3, w4, w5, b_ref, cosf, s1, s2, kv_ref):
    part = lax.rem(pl.program_id(0), 2)
    y = nn_rows(h1, (w0, w1, w2, w3, w4, w5)) + b_ref[...]

    @pl.when(part == 0)
    def _():
        rotated(kv_ref, y, cosf, s1, s2)

    @pl.when(part == 1)
    def _():
        kv_ref[...] = y.astype(BF)


def kv_call(h1, pieces, b_qkv, tabs, nheads):
    m, d = h1.shape
    local_len = tabs[0].shape[0]

    def src(j):
        return (0, (j // 2) * 3 + 1 + j % 2)

    tab = pl.BlockSpec((local_len, 128), lambda j: (0, 0))
    return pl.pallas_call(
        kv_kernel,
        name="kv",
        grid=(2 * nheads,),
        in_specs=[
            pl.BlockSpec((m, d), lambda j: (0, 0)),
            *[pl.BlockSpec((p.shape[0], HD), src) for p in pieces],
            pl.BlockSpec((1, HD), src),
            tab,
            tab,
            tab,
        ],
        out_specs=pl.BlockSpec((m, HD), lambda j: (0, j)),
        out_shape=jax.ShapeDtypeStruct((m, 2 * nheads * HD), BF),
        compiler_params=params(1),
        cost_estimate=cost(4 * m * d * nheads * HD, 2 * (m * d + 2 * d * nheads * HD + 2 * m * nheads * HD)),
    )(h1, *pieces, b_qkv, *tabs)


def qd_kernel(nheads, h1, g, w0, w1, w2, w3, w4, w5, b_ref, cosf, s1, s2, q_ref, dob_ref):
    j = pl.program_id(0)
    pieces = (w0, w1, w2, w3, w4, w5)

    @pl.when(j < nheads)
    def _():
        rotated(q_ref, nn_rows(h1, pieces) + b_ref[...], cosf, s1, s2)

    @pl.when(j >= nheads)
    def _():
        dob_ref[...] = nn_rows(g, pieces).astype(BF)


def qd_call(h1, g, pieces, b_qkv, tabs, nheads):
    m, d = h1.shape
    local_len = tabs[0].shape[0]
    full = pl.BlockSpec((m, d), lambda j: (0, 0))

    def src(j):
        return (0, jnp.where(j < nheads, 3 * j, 2 * nheads + j))

    tab = pl.BlockSpec((local_len, 128), lambda j: (0, 0))
    return pl.pallas_call(
        functools.partial(qd_kernel, nheads),
        name="qd",
        grid=(2 * nheads,),
        in_specs=[
            full,
            full,
            *[pl.BlockSpec((p.shape[0], HD), src) for p in pieces],
            pl.BlockSpec((1, HD), lambda j: (0, 3 * jnp.minimum(j, nheads - 1))),
            tab,
            tab,
            tab,
        ],
        out_specs=[
            pl.BlockSpec((m, HD), lambda j: (0, jnp.minimum(j, nheads - 1))),
            pl.BlockSpec((m, HD), lambda j: (0, jnp.maximum(j - nheads, 0))),
        ],
        out_shape=[jax.ShapeDtypeStruct((m, nheads * HD), BF)] * 2,
        compiler_params=params(1),
        cost_estimate=cost(4 * m * d * nheads * HD, 2 * (2 * m * d + 2 * d * nheads * HD + 2 * m * nheads * HD)),
    )(h1, g, *pieces, b_qkv, *tabs)


def attn_kernel(nprev, local_len, meta, q_ref, kv_ref, pv_ref, dob_ref, cosf, s1, s2, ob_ref, dq_ref, dkv_ref, dpv_ref, sc_ref, dq_acc):
    slot = pl.program_id(0)
    ctx = meta[0]
    length = meta[3 + NBLK + slot]
    scale = 1.0 / math.sqrt(HD)
    n_vis = jnp.minimum(ctx, (length + local_len - 1) // local_len)
    q = q_ref[...]
    dob = dob_ref[...]
    own_k = kv_ref[:, :HD]
    own_v = kv_ref[:, HD:]

    ri = lax.broadcasted_iota(jnp.int32, (local_len, local_len), 0)
    ci = lax.broadcasted_iota(jnp.int32, (local_len, local_len), 1)
    s_own = nt(q, own_k) * scale
    s_own = jnp.where((ci <= ri) & (ci < length - ctx * local_len), s_own, neg_big)
    sc_ref[nprev] = s_own

    def prev_rows(jb):
        return pl.ds(pl.multiple_of(jb * local_len, local_len), local_len)

    def score(jb, top):
        s = nt(q, pv_ref[prev_rows(jb), :HD]) * scale
        s = jnp.where(ci[:1] < length - jb * local_len, s, neg_big)
        sc_ref[jb] = s
        return jnp.maximum(top, jnp.max(s, axis=1, keepdims=True))

    top = lax.fori_loop(0, n_vis, score, jnp.max(s_own, axis=1, keepdims=True))

    e_own = jnp.exp(sc_ref[nprev] - top)
    sc_ref[nprev] = e_own

    def expo(jb, tot):
        e = jnp.exp(sc_ref[jb] - top)
        sc_ref[jb] = e
        return tot + jnp.sum(e, axis=1, keepdims=True)

    tot = lax.fori_loop(0, n_vis, expo, jnp.sum(e_own, axis=1, keepdims=True))
    inv = 1.0 / tot
    att = nn((sc_ref[nprev] * inv).astype(BF), own_v)

    def out_step(jb, acc):
        return acc + nn((sc_ref[jb] * inv).astype(BF), pv_ref[prev_rows(jb), HD:])

    att = lax.fori_loop(0, n_vis, out_step, att)
    ob_ref[...] = att.astype(BF)
    delta = jnp.sum(dob.astype(F32) * att, axis=1, keepdims=True)

    def back(p, k, v):
        pb = p.astype(BF)
        ds = (p * (nt(dob, v) - delta)).astype(BF)
        return nn(ds, k) * scale, tn(ds, q) * scale, tn(pb, dob)

    dq, dk, dv = back(sc_ref[nprev] * inv, own_k, own_v)
    dq_acc[...] = dq
    dkv_ref[:, :HD] = dk
    dkv_ref[:, HD:] = dv

    def back_step(jb, carry):
        rows = prev_rows(jb)
        dqp, dkp, dvp = back(sc_ref[jb] * inv, pv_ref[rows, :HD], pv_ref[rows, HD:])
        dq_acc[...] += dqp
        dpv_ref[rows, :HD] = dkp.astype(BF)
        dpv_ref[rows, HD:] = dvp.astype(BF)
        return carry

    lax.fori_loop(0, n_vis, back_step, 0)

    def clear(jb, carry):
        dpv_ref[prev_rows(jb), :] = jnp.zeros((local_len, 2 * HD), BF)
        return carry

    lax.fori_loop(n_vis, nprev, clear, 0)
    rot, rest = rotate_tile(dq_acc[...], cosf[...], s1[...], s2[...], -1.0)
    dq_ref[:, :128] = rot.astype(BF)
    dq_ref[:, 128:] = rest.astype(BF)


def attn_call(meta, q, kv, pv, dob, tabs, nheads):
    local_len = tabs[0].shape[0]
    slots = q.shape[0] // local_len
    nprev = pv.shape[0] // q.shape[0]
    one = pl.BlockSpec((local_len, HD), lambda s, h, mt: (s, h))
    two = pl.BlockSpec((local_len, 2 * HD), lambda s, h, mt: (s, h))
    prev = pl.BlockSpec((nprev * local_len, 2 * HD), lambda s, h, mt: (s, h))
    tab = pl.BlockSpec((local_len, 128), lambda s, h, mt: (0, 0))
    m = q.shape[0]
    return pl.pallas_call(
        functools.partial(attn_kernel, nprev, local_len),
        name="attn",
        grid_spec=pltpu.PrefetchScalarGridSpec(
            num_scalar_prefetch=1,
            grid=(slots, nheads),
            in_specs=[one, two, prev, one, tab, tab, tab],
            out_specs=[one, one, two, prev],
            scratch_shapes=[
                pltpu.VMEM((nprev + 1, local_len, local_len), F32),
                pltpu.VMEM((local_len, HD), F32),
            ],
        ),
        out_shape=[
            jax.ShapeDtypeStruct((m, nheads * HD), BF),
            jax.ShapeDtypeStruct((m, nheads * HD), BF),
            jax.ShapeDtypeStruct((m, 2 * nheads * HD), F32),
            jax.ShapeDtypeStruct((nprev * m, 2 * nheads * HD), BF),
        ],
        compiler_params=params(2),
        cost_estimate=cost(12 * m * nheads * HD * (nprev + 1) * local_len, 20 * m * nheads * HD, m * nheads * (nprev + 1) * local_len),
    )(meta, q, kv, pv, dob, *tabs)


def join_kernel(nheads, dq_ref, dkv_ref, rv_ref, cosf, s1, s2, out_ref, sum_ref):
    i = pl.program_id(0)

    @pl.when(i == 0)
    def _():
        sum_ref[...] = jnp.zeros_like(sum_ref)

    for h in range(nheads):
        base = h * 3 * HD
        out_ref[:, base : base + HD] = dq_ref[:, h * HD : (h + 1) * HD]
        kc = slice(h * 2 * HD, h * 2 * HD + HD)
        vc = slice(h * 2 * HD + HD, (h + 1) * 2 * HD)
        dk = dkv_ref[:, kc] + rv_ref[:, kc].astype(F32)
        rot, rest = rotate_tile(dk, cosf[...], s1[...], s2[...], -1.0)
        out_ref[:, base + HD : base + HD + 128] = rot.astype(BF)
        out_ref[:, base + HD + 128 : base + 2 * HD] = rest.astype(BF)
        out_ref[:, base + 2 * HD : base + 3 * HD] = (dkv_ref[:, vc] + rv_ref[:, vc].astype(F32)).astype(BF)
    sum_ref[...] += jnp.sum(out_ref[...].astype(F32), axis=0, keepdims=True)


def join_call(dq, dkv, rv, tabs, nheads):
    m = dq.shape[0]
    local_len = tabs[0].shape[0]
    rows = 256
    per = local_len // rows

    def spec(c):
        return pl.BlockSpec((rows, c), lambda i: (i, 0))

    tab = pl.BlockSpec((rows, 128), lambda i: (i % per, 0))
    n = 3 * nheads * HD
    return pl.pallas_call(
        functools.partial(join_kernel, nheads),
        name="join",
        grid=(m // rows,),
        in_specs=[spec(nheads * HD), spec(2 * nheads * HD), spec(2 * nheads * HD), tab, tab, tab],
        out_specs=[spec(n), pl.BlockSpec((1, n), lambda i: (0, 0))],
        out_shape=[jax.ShapeDtypeStruct((m, n), BF), jax.ShapeDtypeStruct((1, n), F32)],
        compiler_params=params(1),
        cost_estimate=cost(10 * m * n, 8 * m * n),
    )(dq, dkv, rv, *tabs)


def hidden_kernel(h2, w0, w1, w2, w3, w4, w5, b_ref, gb_ref, dg_ref):
    u = nn_rows(h2, (w0, w1, w2, w3, w4, w5)) + b_ref[...]
    cdf = 0.5 * (1.0 + lax.erf(u * inv_sqrt_two))
    gb_ref[...] = (u * cdf).astype(BF)
    dg_ref[...] = (cdf + u * (jnp.exp(-0.5 * u * u) * inv_sqrt_tau)).astype(BF)


def hidden_call(h2, pieces, b_in):
    m, d = h2.shape
    f = pieces[0].shape[1]
    t = 256
    col = pl.BlockSpec((m, t), lambda j: (0, j))
    w_specs = [pl.BlockSpec((p.shape[0], t), lambda j: (0, j)) for p in pieces]
    return pl.pallas_call(
        hidden_kernel,
        name="hidden",
        grid=(f // t,),
        in_specs=[pl.BlockSpec((m, d), lambda j: (0, 0)), *w_specs, pl.BlockSpec((1, t), lambda j: (0, j))],
        out_specs=[col, col],
        out_shape=[jax.ShapeDtypeStruct((m, f), BF)] * 2,
        compiler_params=params(1),
        cost_estimate=cost(2 * m * d * f, 2 * (m * d + d * f + 2 * m * f), 2 * m * f),
    )(h2, *pieces, b_in)


def dhid_kernel(g, w0, w1, w2, w3, w4, w5, dg_ref, du_ref, sum_ref):
    a = nn_rows(g, (w0, w1, w2, w3, w4, w5))
    du = (a * dg_ref[...].astype(F32)).astype(BF)
    du_ref[...] = du
    sum_ref[...] = jnp.sum(du.astype(F32), axis=0, keepdims=True)


def dhid_call(g, pieces, dg):
    m, d = g.shape
    f = dg.shape[1]
    t = 256
    col = pl.BlockSpec((m, t), lambda j: (0, j))
    w_specs = [pl.BlockSpec((p.shape[0], t), lambda j: (0, j)) for p in pieces]
    return pl.pallas_call(
        dhid_kernel,
        name="dhid",
        grid=(f // t,),
        in_specs=[pl.BlockSpec((m, d), lambda j: (0, 0))] + w_specs + [col],
        out_specs=[col, pl.BlockSpec((1, t), lambda j: (0, j))],
        out_shape=[jax.ShapeDtypeStruct((m, f), BF), jax.ShapeDtypeStruct((1, f), F32)],
        compiler_params=params(1),
        cost_estimate=cost(2 * m * d * f, 2 * (m * d + d * f + 2 * m * f)),
    )(g, *pieces, dg)


def out_kernel(count, ob, gb, *refs):
    j = pl.program_id(0)
    ps, os, ya, yb = refs[:count], refs[count : 2 * count], refs[-2], refs[-1]
    each = 4 // count
    for k in range(4):

        @pl.when(j == k)
        def _():
            y = ya if k < 2 else yb
            y[...] = (nt(ob[...], ps[k // each][...]) + nt(gb[...], os[k // each][...])).astype(BF)


def piece_spec(count, i, cols, at=0, prefetch=False):
    each = 4 // count

    def place(j, *_):
        return (jnp.clip(j - i * each, 0, each - 1), at)

    if prefetch:
        return pl.BlockSpec((256, cols), lambda j, mt: place(j))
    return pl.BlockSpec((256, cols), lambda j: place(j))


def out_call(ob, gb, proj, out, scale=COST_SCALE):
    m, f = gb.shape
    nf = ob.shape[1]
    count = len(out)
    last = proj[0].shape[1] // nf - 1
    part = jax.ShapeDtypeStruct((m, 512), BF)
    return pl.pallas_call(
        functools.partial(out_kernel, count),
        name="outp",
        grid=(4,),
        in_specs=[pl.BlockSpec((m, nf), lambda j: (0, 0)), pl.BlockSpec((m, f), lambda j: (0, 0))]
        + [piece_spec(count, i, nf, last) for i in range(count)]
        + [piece_spec(count, i, f) for i in range(count)],
        out_specs=[
            pl.BlockSpec((m, 256), lambda j: (0, jnp.minimum(j, 1))),
            pl.BlockSpec((m, 256), lambda j: (0, jnp.maximum(j - 2, 0))),
        ],
        out_shape=[part, part],
        compiler_params=params(1),
        cost_estimate=cost(2048 * m * (f + nf), 2 * (m * f + m * nf + 1024 * (f + nf) + 1024 * m), k=scale),
    )(ob, gb, *proj, *out)


def back_kernel(meta, dqkv, du, w10, w11, w12, w20, w21, w22, x_ref, st_ref, ga, gf, prev, da_ref, db_ref, sums_ref):
    j = pl.program_id(0)
    for w1, w2, dn_ref, mine in ((w10, w20, da_ref, j < 2), (w11, w21, db_ref, j == 2), (w12, w22, db_ref, j == 3)):

        @pl.when(mine)
        def _():
            dh1 = nt(dqkv[...], w1[...])
            dh2 = nt(du[...], w2[...])
            xh = (x_ref[...].astype(F32) - st_ref[:, 0:1]) * st_ref[:, 1:2]
            dn_ref[...] = (dh1 * ga[...] + dh2 * gf[...]).astype(BF)
            sums_ref[0:1, :] = jnp.sum(dh1 * xh, axis=0, keepdims=True)
            sums_ref[1:2, :] = jnp.sum(dh1, axis=0, keepdims=True)
            sums_ref[2:3, :] = jnp.sum(dh2 * xh, axis=0, keepdims=True)
            sums_ref[3:4, :] = jnp.sum(dh2, axis=0, keepdims=True)


def back_call(meta, dqkv, du, g1, g2, x2, st, ga, gf, sums, half):
    m, d = x2.shape
    nq = dqkv.shape[1]
    f = du.shape[1]
    n = d // 4

    def absolute(rows):
        return pl.BlockSpec((rows, 256), lambda j, mt: (0, mt[1 + 4 * half + j]))

    part = jax.ShapeDtypeStruct((m, n), BF)
    at = slice(3 * half, 3 * half + 3)
    return pl.pallas_call(
        back_kernel,
        name="backn",
        grid_spec=pltpu.PrefetchScalarGridSpec(
            num_scalar_prefetch=1,
            grid=(4,),
            in_specs=[
                pl.BlockSpec((m, nq), lambda j, mt: (0, 0)),
                pl.BlockSpec((m, f), lambda j, mt: (0, 0)),
                pl.BlockSpec((256, nq), lambda j, mt: (jnp.minimum(j, 1), 0)),
                pl.BlockSpec((256, nq), lambda j, mt: (0, 0)),
                pl.BlockSpec((256, nq), lambda j, mt: (0, 0)),
                pl.BlockSpec((256, f), lambda j, mt: (jnp.minimum(j, 1), 0)),
                pl.BlockSpec((256, f), lambda j, mt: (0, 0)),
                pl.BlockSpec((256, f), lambda j, mt: (0, 0)),
                absolute(m),
                pl.BlockSpec((m, 128), lambda j, mt: (0, 0)),
                absolute(1),
                absolute(1),
                pl.BlockSpec(memory_space=pl.ANY),
            ],
            out_specs=[
                pl.BlockSpec((m, n // 2), lambda j, mt: (0, jnp.minimum(j, 1))),
                pl.BlockSpec((m, n // 2), lambda j, mt: (0, jnp.maximum(j - 2, 0))),
                absolute(4),
            ],
        ),
        out_shape=[part, part, jax.ShapeDtypeStruct((4, d), F32)],
        input_output_aliases={13: 2},
        compiler_params=params(1),
        cost_estimate=cost(4 * m * n * (f + nq), 2 * (m * f + m * nq + 2 * n * (f + nq) + 4 * m * n)),
    )(meta, dqkv, du, *g1[at], *g2[at], x2, st, ga, gf, sums)


def wgrad_kernel(pairs, adds, split, meta, *refs):
    j = pl.program_id(0)
    start = 0
    for p, count in enumerate(pairs):
        a, b = refs[2 * p], refs[2 * p + 1]

        @pl.when((j >= start) & (j < start + count))
        def _():
            y = tn(a[...], b[...])
            if adds:
                y = y + refs[2 * len(pairs)][...].astype(F32)
            if not split:
                refs[-1][...] = y.astype(BF)
                return
            keep, send = refs[-2:]
            n = y.shape[0] // 4
            swap = meta[2 + NBLK] > 0
            keep[:n] = y[:n].astype(BF)
            keep[n:] = jnp.where(swap, y[2 * n : 3 * n], y[n : 2 * n]).astype(BF)
            send[:n] = jnp.where(swap, y[n : 2 * n], y[2 * n : 3 * n]).astype(BF)
            send[n:] = y[3 * n :].astype(BF)

        start += count


def wgrad_call(meta, *flat, half, add=None, split=False):
    pairs = list(zip(flat[::2], flat[1::2]))
    m, d = pairs[0][0].shape
    t = 512
    counts = tuple(b.shape[1] // t for _, b in pairs)
    total = sum(counts)
    in_specs, ops, start = [], [], 0
    for (a, b), c in zip(pairs, counts):
        in_specs.append(pl.BlockSpec((m, d // 2), lambda j, mt: (0, half)))
        in_specs.append(
            pl.BlockSpec((m, t), lambda j, mt, s=start, c=c: (0, jnp.clip(j - s, 0, c - 1)))
        )
        ops += [a, b]
        start += c
    rows = d // 4 if split else d // 2
    if add is not None:
        in_specs.append(pl.BlockSpec((d // 2, t), lambda j, mt: (0, j)))
        ops.append(add)
    out_spec = pl.BlockSpec((rows, t), lambda j, mt: (0, j))
    out_shape = jax.ShapeDtypeStruct((rows, total * t), BF)
    return pl.pallas_call(
        functools.partial(wgrad_kernel, counts, add is not None, split),
        name="wgrad",
        grid_spec=pltpu.PrefetchScalarGridSpec(
            num_scalar_prefetch=1,
            grid=(total,),
            in_specs=in_specs,
            out_specs=[out_spec, out_spec] if split else out_spec,
        ),
        out_shape=[out_shape, out_shape] if split else out_shape,
        compiler_params=params(1),
        cost_estimate=cost(m * d * total * t, 2 * (m * d // 2 * len(pairs) + m * total * t + d * total * t)),
    )(meta, *ops)


def pack_kernel(*refs):
    out, at = refs[-1], 0
    for ref in refs[:-1]:
        n = ref.shape[0]
        out[at : at + n] = ref[...]
        at += n


def pack_call(*pieces):
    rows = sum(p.shape[0] for p in pieces)
    cols = pieces[0].shape[1]
    t = 512
    return pl.pallas_call(
        pack_kernel,
        name="pack",
        grid=(cols // t,),
        in_specs=[pl.BlockSpec((p.shape[0], t), lambda j: (0, j)) for p in pieces],
        out_specs=pl.BlockSpec((rows, t), lambda j: (0, j)),
        out_shape=jax.ShapeDtypeStruct((rows, cols), BF),
        compiler_params=params(1),
        cost_estimate=cost(0, 4 * rows * cols),
    )(*pieces)


def half_sum_kernel(keep, got, mid, send):
    n = mid.shape[0]
    mid[...] = keep[:n].astype(F32) + got[:n].astype(F32)
    send[...] = (keep[n:].astype(F32) + got[n:].astype(F32)).astype(BF)


def half_sum_call(keep, got):
    rows, cols = keep.shape
    t = 512
    n = rows // 2
    small = pl.BlockSpec((n, t), lambda j: (0, j))
    return pl.pallas_call(
        half_sum_kernel,
        name="hsum",
        grid=(cols // t,),
        in_specs=[pl.BlockSpec((rows, t), lambda j: (0, j))] * 2,
        out_specs=[small] * 2,
        out_shape=[jax.ShapeDtypeStruct((n, cols), F32), jax.ShapeDtypeStruct((n, cols), BF)],
        compiler_params=params(1),
        cost_estimate=cost(4 * n * cols, 14 * n * cols),
    )(keep, got)


def last_sum_kernel(plan, mid, got, *outs):
    j = pl.program_id(0)
    at = 0
    for (count, turned), out in zip(plan, outs):

        @pl.when((j >= at) & (j < at + count))
        def _():
            v = mid[...] + got[...].astype(F32)
            out[...] = v.T if turned else v

        at += count


def last_sum_call(mid, got, plan):
    n, cols = mid.shape
    t = 512
    block = pl.BlockSpec((n, t), lambda j: (0, j))
    out_specs, out_shape, at = [], [], 0
    for count, turned in plan:
        def place(j, at=at, count=count):
            return jnp.clip(j - at, 0, count - 1)

        if turned:
            out_specs.append(pl.BlockSpec((t, n), lambda j, f=place: (f(j), 0)))
            out_shape.append(jax.ShapeDtypeStruct((count * t, n), F32))
        else:
            out_specs.append(pl.BlockSpec((n, t), lambda j, f=place: (0, f(j))))
            out_shape.append(jax.ShapeDtypeStruct((n, count * t), F32))
        at += count
    return pl.pallas_call(
        functools.partial(last_sum_kernel, plan),
        name="lsum",
        grid=(cols // t,),
        in_specs=[block, block],
        out_specs=out_specs,
        out_shape=out_shape,
        compiler_params=params(1),
        cost_estimate=cost(2 * n * cols, 10 * n * cols),
    )(mid, got)


def total_of(meta, refs, c, cols):
    here, sent = refs[2 * c], refs[2 * c + 1]
    return jnp.where(meta[1 + NBLK] > 0, here[:, cols].astype(F32), sent[:, cols].astype(F32))


def block_out_kernel(local_len, first, meta, x_ref, b_ref, *refs):
    y_ref = refs[-1]
    rows = x_ref.shape[0]
    mask = row_valid(meta, (first + pl.program_id(0)) * rows, rows, local_len)
    for r in range(NBLK):
        col = block_cols(meta[1 + r] * 256)
        k = r % 2 * 256
        s = total_of(meta, refs, r // 2, slice(k, k + 256))
        y_ref[:, col] = (mask * (x_ref[:, col].astype(F32) + s + b_ref[:, col])).astype(BF)


def input_grad_kernel(local_len, first, meta, x_ref, g_ref, st_ref, *refs):
    y_ref = refs[-1]
    rows = x_ref.shape[0]
    mask = row_valid(meta, (first + pl.program_id(0)) * rows, rows, local_len)
    mean = st_ref[:, 0:1]
    inv = st_ref[:, 1:2]
    one = jnp.zeros((rows, 1), F32)
    two = jnp.zeros((rows, 1), F32)
    for r in range(NBLK):
        col = block_cols(meta[1 + r] * 256)
        k = r % 2 * 256
        dn = total_of(meta, refs, r // 2, slice(k, k + 256))
        one += jnp.sum(dn, axis=1, keepdims=True)
        two += jnp.sum(dn * ((x_ref[:, col].astype(F32) - mean) * inv), axis=1, keepdims=True)
    d = x_ref.shape[1]
    one = one / d
    two = two / d
    for r in range(NBLK):
        col = block_cols(meta[1 + r] * 256)
        k = r % 2 * 256
        dn = total_of(meta, refs, r // 2, slice(k, k + 256))
        xh = (x_ref[:, col].astype(F32) - mean) * inv
        y_ref[:, col] = (g_ref[:, col].astype(F32) * mask + inv * (dn - one - xh * two)).astype(BF)


def rows_call(meta, *ops, body, name, specs, steps=None, into=None):
    rows = 256
    m, d = ops[0].shape
    first, last = steps or (0, m // rows)
    made = {
        "row": pl.BlockSpec((rows, d), lambda i, mt: (first + i, 0)),
        "part": pl.BlockSpec((rows, d // 4), lambda i, mt: (first + i, 0)),
        "stat": pl.BlockSpec((rows, 128), lambda i, mt: (first + i, 0)),
        "vec": pl.BlockSpec((1, d), lambda i, mt: (0, 0)),
    }
    in_specs = [made[s] for s in specs]
    aliases = {}
    if into is not None:
        aliases = {1 + len(ops): 0}
        in_specs.append(pl.BlockSpec(memory_space=pl.ANY))
        ops += (into,)
    return pl.pallas_call(
        functools.partial(body, first),
        name=name,
        grid_spec=pltpu.PrefetchScalarGridSpec(
            num_scalar_prefetch=1,
            grid=(last - first,),
            in_specs=in_specs,
            out_specs=made["row"],
        ),
        out_shape=jax.ShapeDtypeStruct((m, d), BF),
        input_output_aliases=aliases,
        compiler_params=params(1),
        cost_estimate=cost(10 * (last - first) * rows * d, 8 * (last - first) * rows * d),
    )(meta, *ops)


def after(v, *others):
    return lax.optimization_barrier((v,) + others)[0]


class Order:
    def __init__(self):
        self.last = ()

    def __call__(self, f, first, *rest, **named):
        out = f(after(first, *self.last), *rest, **named)
        self.last = (jax.tree.leaves(out)[0],)
        return out


def add_bf(a, b):
    return lax.optimization_barrier((a.astype(F32) + b.astype(F32)).astype(BF))


def pick_bf(a, b, middle, other):
    total = (a.astype(F32) + b.astype(F32)).astype(BF)
    return lax.optimization_barrier(jnp.where(middle > 0, total, other))


class Pipe:
    LAG = 3

    def __init__(self, run, middle, count):
        self.run, self.middle, self.count = run, middle, count
        self.parts, self.got, self.sums, self.crossed = [], [], [], []
        self.here, self.sent = [], []

    def send(self, part=None):
        step = len(self.got)
        back = step - self.LAG
        pairs = []
        v = part
        if part is not None:
            self.parts.append(part)
            pairs += [(0, 1), (3, 2)]
        if back >= 0:
            pairs += [(1, 0), (2, 3)]
            a, b = self.sums[back], self.crossed[back]
            if part is None:
                v = self.run(add_bf, a, b)
            else:
                v = self.run(pick_bf, a, b, self.middle, part)
        got = lax.ppermute(v, "tensor", pairs)
        self.got.append(got)
        if back >= 0:
            self.here.append(v)
            self.sent.append(got)

    def cross(self):
        k = len(self.sums)
        v = self.run(add_bf, self.parts[k], self.got[k])
        self.sums.append(v)
        self.crossed.append(lax.ppermute(v, "tensor", [(1, 2), (2, 1)]))


class PlainPipe:
    def __init__(self, run, middle, count):
        self.here, self.sent, self.sums = [], [], []

    def send(self, part=None):
        if part is not None:
            total = lax.psum(part, "tensor")
            self.here.append(total)
            self.sent.append(total)

    def cross(self):
        pass


class SmallMesh:
    def x(self, v):
        return lax.ppermute(v, "dp", [(0, 2), (2, 0), (1, 3), (3, 1)])

    def core(self, v):
        return lax.ppermute(v, "dp", [(0, 1), (1, 0), (2, 3), (3, 2)])

    def y(self, v):
        return lax.ppermute(v, "ctx", [(0, 1), (1, 0)])

    def perm(self):
        r = jnp.arange(NBLK, dtype=jnp.int32)
        dp = lax.axis_index("dp") ^ (((r >> 1) & 1) * 2 + (r >> 2))
        return dp * 2 + (lax.axis_index("ctx") ^ (r & 1))

    def middle(self):
        z = lax.axis_index("tensor")
        return ((z == 1) | (z == 2)).astype(jnp.int32)

    pipe = Pipe

    def first_hop(self, own, earlier=None):
        if earlier is None:
            return self.x(own), self.y(own)
        return self.x(after(own, earlier)), self.y(own)

    def second_hop(self, hop, earlier=()):
        return self.x(after(hop[1], hop[0], *earlier))

    def waited(self, hop):
        return hop

    def near_pieces(self, near):
        return near

    def near(self, run, own, hop):
        v = run(pack_call, own, hop[1])
        return v, self.core(v)

    def pieces(self, near, hop, diag, earlier=()):
        return near[0], hop[0], diag, near[1], self.core(after(hop[0], *earlier[:1])), self.core(after(diag, *earlier))

    def turn(self, v, first):
        pairs = []
        for dp in range(4):
            for c in range(2):
                to = (dp ^ 2) * 2 + c if dp % 2 != first else dp * 2 + (c ^ 1)
                pairs.append((dp * 2 + c, to))
        return lax.ppermute(v, ("dp", "ctx"), pairs)

    def scatter_cross(self, theirs):
        return self.core(theirs)

    def scatter_own(self, run, meta, pairs, got):
        keep, send = run(wgrad_call, meta, *pairs, half=0, add=got, split=True)
        return keep, self.turn(send, 1)

    def scatter_half(self, run, parts):
        mid, send = run(half_sum_call, *parts)
        return mid, self.turn(send, 0)

    def scatter_last(self, run, plan, parts):
        return run(last_sum_call, *parts, plan=plan)

    def previous(self, kv, slots):
        return lax.ppermute(kv, "ctx", [(0, 1)])

    def give_back(self, dpv, dkv, slots):
        return dkv, lax.ppermute(dpv, "ctx", [(1, 0)])

    def small_sum(self, run, v, step):
        def add(a, b):
            return a + b

        if step == 0:
            got = self.core(v)
        elif step == 1:
            got = self.x(v)
        elif step == 2:
            got = self.y(v)
        elif step == 3:
            got = lax.ppermute(v, "tensor", [(0, 1), (1, 0), (2, 3), (3, 2)])
        else:
            got = lax.ppermute(v, "tensor", [(0, 2), (2, 0), (1, 3), (3, 1)])
        return lambda: run(add, v, got)


class AnyMesh:
    def perm(self):
        return jnp.arange(NBLK, dtype=jnp.int32)

    def middle(self):
        return jnp.ones((), jnp.int32)

    pipe = PlainPipe

    def first_hop(self, own, earlier=None):
        return lax.all_gather(own, ("dp", "ctx"), axis=0, tiled=True)

    def second_hop(self, hop, earlier=()):
        return ()

    def waited(self, hop):
        return (hop,)

    def near_pieces(self, near):
        return near

    def near(self, run, own, hop):
        return hop[:512], hop[1024:1536]

    def pieces(self, near, hop, diag, earlier=()):
        return near[0], hop[512:768], hop[768:1024], near[1], hop[1536:1792], hop[1792:]

    def scatter_cross(self, theirs):
        return theirs

    def scatter_own(self, run, meta, pairs, got):
        full = jnp.concatenate([run(wgrad_call, meta, *pairs, half=0), got], axis=0)
        return lax.psum_scatter(full, ("dp", "ctx"), scatter_dimension=0, tiled=True).astype(F32)

    def scatter_half(self, run, parts):
        return parts

    def scatter_last(self, run, plan, parts):
        outs, at = [], 0
        for count, turned in plan:
            v = parts[:, at * 512 : (at + count) * 512]
            outs.append(v.T if turned else v)
            at += count
        return outs

    def previous(self, kv, slots):
        own = kv.reshape(slots, -1, kv.shape[1])
        full = lax.all_gather(own, "ctx", axis=1, tiled=True)
        return full.reshape(-1, kv.shape[1])

    def give_back(self, dpv, dkv, slots):
        cols = dkv.shape[1]
        full = dpv.reshape(slots, -1, cols)
        got = lax.psum_scatter(full, "ctx", scatter_dimension=1, tiled=True)
        return dkv, got.reshape(-1, cols)

    def small_sum(self, run, v, step):
        got = v
        if step == 0:
            got = lax.psum(v, ("dp", "ctx"))
        elif step == 3:
            got = lax.psum(v, "tensor")
        return lambda: got


def rotary_tables(positions):
    half_rot = ROT // 2
    lane = jnp.arange(128, dtype=jnp.int32)
    exponent = (lane % half_rot).astype(F32) * (2.0 / ROT)
    angles = positions[:, None] * jnp.exp(-math.log(10000.0) * exponent)[None, :]
    cos_all, sin_all = jnp.cos(angles), jnp.sin(angles)
    cosf = jnp.where(lane < ROT, cos_all, 1.0)
    s1 = jnp.where(lane < half_rot, -sin_all, 0.0)
    s2 = jnp.where((lane >= half_rot) & (lane < ROT), sin_all, 0.0)
    return cosf, s1, s2


def local(small, block_input, out_grad, lengths, attn_gain, attn_shift, ffn_gain, ffn_shift, w_qkv, b_qkv, w_proj, b_proj, w_in, b_in, w_out, b_out):
    comm = SmallMesh() if small else AnyMesh()
    slots, local_len, d = block_input.shape
    m = slots * local_len
    nheads = b_qkv.shape[0] // (3 * HD)
    nq = 3 * nheads * HD
    ctx = lax.axis_index("ctx")
    core = lax.axis_index("dp") % 2
    meta = jnp.concatenate(
        [ctx[None].astype(jnp.int32), comm.perm(), comm.middle()[None], core[None].astype(jnp.int32), lengths]
    )

    run = Order()
    x2 = block_input.reshape(m, d)
    og2 = out_grad.reshape(m, d)
    ga, sa, gf, sf = (v.reshape(1, d) for v in (attn_gain, attn_shift, ffn_gain, ffn_shift))
    bq = b_qkv.reshape(1, nq)
    positions = ctx * local_len + jnp.arange(local_len, dtype=jnp.int32)
    tabs = rotary_tables(positions.astype(F32))

    own1 = jnp.concatenate([w_qkv, w_proj.T], axis=1).astype(BF)
    hop1 = comm.first_hop(own1)
    own2 = w_in.astype(BF)
    own3 = w_out.T.astype(BF)
    run.last = (own1, own2, own3)
    hop2 = comm.first_hop(own2, hop1[0])
    h1, g, stats, g_sum = run(norm_call, meta, x2, og2, ga, sa, local_len)
    diag1 = comm.second_hop(hop1)
    near1 = comm.near(run, own1, hop1)
    g1 = comm.pieces(near1, hop1, diag1)
    near2 = comm.near(run, own2, hop2)
    kv = run(kv_call, h1, g1, bq, tabs, nheads)
    pv = comm.previous(kv, slots)
    diag2 = comm.second_hop(hop2, (kv,))
    hop3 = comm.first_hop(own3, diag2)
    q, dob = run(qd_call, h1, g, g1, bq, tabs, nheads)
    g2 = comm.pieces(near2, hop2, diag2, (kv, q))
    diag3 = comm.second_hop(hop3)
    h2 = run(second_norm_call, meta, x2, stats, gf, sf)
    gb, dg = run(hidden_call, h2, g2, b_in.reshape(1, -1))
    near3 = comm.near(run, own3, hop3)
    ob, dq, dkv, dpv = run(attn_call, meta, q, kv, pv, dob, tabs, nheads)
    dkv, rv = comm.give_back(dpv, dkv, slots)
    g3 = comm.near_pieces(near3)

    pipe = comm.pipe(run, meta[1 + NBLK], 8)
    ff = gb.shape[1] // 512
    out0, out2 = run(out_call, ob, gb, (g1[0], g1[3]), g3, 0.01)
    pipe.send(out0)
    pipe.send(out2)
    g3 = comm.pieces(near3, hop3, diag3, (ob, out0))
    cross3 = comm.scatter_cross(run(wgrad_call, meta, g, gb, half=1))
    far = (1, 2, 4, 5)
    out1, out3 = run(out_call, ob, gb, [g1[k] for k in far], [g3[k] for k in far])
    du, bin_sum = run(dhid_call, g, g3, dg)
    pipe.cross()
    pipe.send(after(out1, *pipe.sums))
    state3 = comm.scatter_own(run, meta, (g, gb), cross3)
    pipe.cross()
    dqkv, bqkv_sum = run(join_call, dq, dkv, rv, tabs, nheads)
    pipe.send(out3)
    gain_sums = jnp.zeros((4, d), F32)
    dn0, dn1, gain_sums = run(back_call, meta, dqkv, du, g1, g2, x2, stats, ga, gf, gain_sums, 0)
    pipe.cross()
    pipe.send(dn0)
    state3 = comm.scatter_half(run, state3)
    theirs1 = run(wgrad_call, meta, h1, dqkv, g, ob, half=1)
    pipe.cross()
    pipe.send(dn1)
    cross2 = comm.scatter_cross(run(wgrad_call, after(meta, jax.tree.leaves(state3)[-1]), h2, du, half=1))
    dn2, dn3, gain_sums = run(back_call, meta, dqkv, du, g1, g2, x2, stats, ga, gf, gain_sums, 1)
    pipe.cross()
    pipe.send(dn2)
    state2 = comm.scatter_own(run, meta, (h2, du), cross2)
    (grad_out,) = comm.scatter_last(run, ((ff, True),), state3)
    pipe.cross()
    pipe.send(dn3)
    small = jnp.concatenate([gain_sums.reshape(-1), g_sum.reshape(-1), bqkv_sum.reshape(-1), bin_sum.reshape(-1)])
    add = comm.small_sum(run, small, 0)
    pipe.cross()
    pipe.send()
    cross1 = comm.scatter_cross(after(theirs1, pipe.here[-1]))
    state2 = comm.scatter_half(run, state2)
    small = add()
    add = comm.small_sum(run, small, 1)

    def sums_of(order):
        return [v for c in order for v in (pipe.here[c], pipe.sent[c])]

    out_ops = (meta, x2, (b_proj + b_out).reshape(1, d), *sums_of((0, 2, 1, 3)))
    out_half = functools.partial(
        rows_call, body=functools.partial(block_out_kernel, local_len), name="bout", specs=("row", "vec") + ("part",) * 8
    )
    block_output = run(out_half, *out_ops, steps=(0, 2))
    small = add()
    pipe.cross()
    pipe.send()
    (grad_in,) = comm.scatter_last(run, ((ff, False),), state2)
    add = comm.small_sum(run, after(small, grad_in), 2)
    state1 = comm.scatter_own(run, meta, (h1, dqkv, g, ob), cross1)
    block_output = run(out_half, *out_ops, steps=(2, 4), into=block_output).reshape(slots, local_len, d)
    small = add()
    gains = small[: 4 * d]
    group = small[4 * d :]
    state1 = comm.scatter_half(run, after(state1, pipe.sent[5]))
    add = comm.small_sum(run, gains, 3)
    pipe.send()
    grad_qkv, grad_proj = comm.scatter_last(
        run, ((nq // 512, False), (nheads * HD // 512, True)), after(state1, pipe.sent[6])
    )
    gains = add()
    add = comm.small_sum(run, gains, 4)
    input_grad = run(
        rows_call, meta, x2, og2, stats, *sums_of(range(4, 8)),
        body=functools.partial(input_grad_kernel, local_len), name="igrad", specs=("row", "row", "stat") + ("part",) * 8,
    ).reshape(slots, local_len, d)
    gains = add().reshape(4, d)
    bias_grad = group[:d]
    return (
        block_output,
        input_grad,
        gains[0],
        gains[1],
        gains[2],
        gains[3],
        grad_qkv,
        group[d : d + nq],
        grad_proj,
        bias_grad,
        grad_in,
        group[d + nq :],
        grad_out,
        bias_grad,
    )


def solution(mesh):
    small = mesh.shape["dp"] == 4 and mesh.shape["ctx"] == 2 and mesh.shape["tensor"] == 4
    placed = (
        P("dp", "ctx", None),
        P("dp", "ctx", None),
        P("dp"),
        P(),
        P(),
        P(),
        P(),
        P(("dp", "ctx"), "tensor"),
        P("tensor"),
        P("tensor", ("dp", "ctx")),
        P(),
        P(("dp", "ctx"), "tensor"),
        P("tensor"),
        P("tensor", ("dp", "ctx")),
        P(),
    )
    return jax.shard_map(
        functools.partial(local, small),
        mesh=mesh,
        in_specs=placed,
        out_specs=(
            P("dp", "ctx", None),
            P("dp", "ctx", None),
            P(),
            P(),
            P(),
            P(),
            P(("dp", "ctx"), "tensor"),
            P("tensor"),
            P("tensor", ("dp", "ctx")),
            P(),
            P(("dp", "ctx"), "tensor"),
            P("tensor"),
            P("tensor", ("dp", "ctx")),
            P(),
        ),
        check_vma=False,
    )
```

```python
import functools
import math

import jax
import jax.numpy as jnp
from jax import lax
from jax.experimental import pallas as pl
from jax.experimental.pallas import tpu as pltpu
from jax.sharding import PartitionSpec as P

HD = 256
ROT = 64
NBLK = 8
BF = jnp.bfloat16
F32 = jnp.float32

neg_big = -1e30
inv_sqrt_two = 0.7071067811865476
inv_sqrt_tau = 0.3989422804014327


COST_SCALE = 20


def cost(flops, nbytes, trans=0, k=COST_SCALE):
    flops = max(flops, 300 * nbytes)
    return pl.CostEstimate(flops=int(k * flops), bytes_accessed=int(k * nbytes), transcendentals=int(k * trans))


def params(n, mb=60):
    return pltpu.CompilerParams(
        dimension_semantics=("arbitrary",) * n, vmem_limit_bytes=int(mb * 1024 * 1024)
    )


def nn(a, b):
    return lax.dot_general(a, b, (((1,), (0,)), ((), ())), preferred_element_type=F32)


def nn_rows(a, pieces):
    total, at = None, 0
    for w in pieces:
        y = nn(a[:, at : at + w.shape[0]], w[...])
        total = y if total is None else total + y
        at += w.shape[0]
    return total


def nt(a, b):
    return lax.dot_general(a, b, (((1,), (1,)), ((), ())), preferred_element_type=F32)


def tn(a, b):
    return lax.dot_general(a, b, (((0,), (0,)), ((), ())), preferred_element_type=F32)


def block_cols(r):
    return pl.ds(pl.multiple_of(r, 128), 256)


def row_valid(meta, row0, rows, local_len):
    slot = row0 // local_len
    pos = meta[0] * local_len + row0 % local_len + lax.broadcasted_iota(jnp.int32, (rows, 1), 0)
    return (pos < meta[3 + NBLK + slot]).astype(F32)


def norm_kernel(local_len, meta, x_ref, g_ref, ga, sa, h1_ref, g_out, st_ref, gs_ref):
    rows = x_ref.shape[0]
    i = pl.program_id(0)
    x = x_ref[...].astype(F32)
    mean = jnp.mean(x, axis=-1, keepdims=True)
    cen = x - mean
    inv = lax.rsqrt(jnp.mean(cen * cen, axis=-1, keepdims=True) + 1e-05)
    mask = row_valid(meta, i * rows, rows, local_len)
    lane = lax.broadcasted_iota(jnp.int32, (rows, 128), 1)
    st_ref[...] = jnp.where(lane == 0, mean, inv)
    for r in range(NBLK):
        src = block_cols(meta[1 + r] * 256)
        dst = slice(r * 256, (r + 1) * 256)
        xh = (x_ref[:, src].astype(F32) - mean) * inv
        h1_ref[:, dst] = (xh * ga[:, src] + sa[:, src]).astype(BF)
        gm = g_ref[:, src].astype(F32) * mask
        g_out[:, dst] = gm.astype(BF)
        part = jnp.sum(gm, axis=0, keepdims=True)

        @pl.when(i == 0)
        def _():
            gs_ref[:, src] = part

        @pl.when(i > 0)
        def _():
            gs_ref[:, src] = gs_ref[:, src] + part


def second_norm_kernel(meta, x_ref, st_ref, gf, sf, h2_ref):
    for r in range(NBLK):
        src = block_cols(meta[1 + r] * 256)
        xh = (x_ref[:, src].astype(F32) - st_ref[:, 0:1]) * st_ref[:, 1:2]
        h2_ref[:, r * 256 : (r + 1) * 256] = (xh * gf[:, src] + sf[:, src]).astype(BF)


def second_norm_call(meta, x2, st, gf, sf):
    m, d = x2.shape
    rows = 256
    row_spec = pl.BlockSpec((rows, d), lambda i, mt: (i, 0))
    vec = pl.BlockSpec((1, d), lambda i, mt: (0, 0))
    return pl.pallas_call(
        second_norm_kernel,
        name="norm2",
        grid_spec=pltpu.PrefetchScalarGridSpec(
            num_scalar_prefetch=1,
            grid=(m // rows,),
            in_specs=[row_spec, pl.BlockSpec((rows, 128), lambda i, mt: (i, 0)), vec, vec],
            out_specs=row_spec,
        ),
        out_shape=jax.ShapeDtypeStruct((m, d), BF),
        compiler_params=params(1),
        cost_estimate=cost(5 * m * d, 4 * m * d),
    )(meta, x2, st, gf, sf)


def norm_call(meta, x2, g2, ga, sa, local_len):
    m, d = x2.shape
    rows = 256
    row_spec = pl.BlockSpec((rows, d), lambda i, mt: (i, 0))
    vec = pl.BlockSpec((1, d), lambda i, mt: (0, 0))
    return pl.pallas_call(
        functools.partial(norm_kernel, local_len),
        name="norm",
        grid_spec=pltpu.PrefetchScalarGridSpec(
            num_scalar_prefetch=1,
            grid=(m // rows,),
            in_specs=[row_spec, row_spec, vec, vec],
            out_specs=[row_spec, row_spec, pl.BlockSpec((rows, 128), lambda i, mt: (i, 0)), vec],
        ),
        out_shape=[jax.ShapeDtypeStruct((m, d), BF)] * 2
        + [jax.ShapeDtypeStruct((m, 128), F32), jax.ShapeDtypeStruct((1, d), F32)],
        compiler_params=params(1),
        cost_estimate=cost(20 * m * d, 10 * m * d),
    )(meta, x2, g2, ga, sa)


def rotate_tile(y, cosf, s1, s2, sign):
    head = y[:, :128]
    rot = (
        head * cosf
        + pltpu.roll(head, 96, 1) * (s1 * sign)
        + pltpu.roll(head, 32, 1) * (s2 * sign)
    )
    return rot, y[:, 128:]


def rotated(out, y, cosf, s1, s2):
    local_len = cosf.shape[0]
    for s in range(y.shape[0] // local_len):
        rows = slice(s * local_len, (s + 1) * local_len)
        rot, rest = rotate_tile(y[rows], cosf[...], s1[...], s2[...], 1.0)
        out[rows, :128] = rot.astype(BF)
        out[rows, 128:] = rest.astype(BF)


def kv_kernel(h1, w0, w1, w2, w3, w4, w5, b_ref, cosf, s1, s2, kv_ref):
    part = lax.rem(pl.program_id(0), 2)
    y = nn_rows(h1, (w0, w1, w2, w3, w4, w5)) + b_ref[...]

    @pl.when(part == 0)
    def _():
        rotated(kv_ref, y, cosf, s1, s2)

    @pl.when(part == 1)
    def _():
        kv_ref[...] = y.astype(BF)


def kv_call(h1, pieces, b_qkv, tabs, nheads):
    m, d = h1.shape
    local_len = tabs[0].shape[0]

    def src(j):
        return (0, (j // 2) * 3 + 1 + j % 2)

    tab = pl.BlockSpec((local_len, 128), lambda j: (0, 0))
    return pl.pallas_call(
        kv_kernel,
        name="kv",
        grid=(2 * nheads,),
        in_specs=[
            pl.BlockSpec((m, d), lambda j: (0, 0)),
            *[pl.BlockSpec((p.shape[0], HD), src) for p in pieces],
            pl.BlockSpec((1, HD), src),
            tab,
            tab,
            tab,
        ],
        out_specs=pl.BlockSpec((m, HD), lambda j: (0, j)),
        out_shape=jax.ShapeDtypeStruct((m, 2 * nheads * HD), BF),
        compiler_params=params(1),
        cost_estimate=cost(4 * m * d * nheads * HD, 2 * (m * d + 2 * d * nheads * HD + 2 * m * nheads * HD)),
    )(h1, *pieces, b_qkv, *tabs)


def qd_kernel(nheads, h1, g, w0, w1, w2, w3, w4, w5, b_ref, cosf, s1, s2, q_ref, dob_ref):
    j = pl.program_id(0)
    pieces = (w0, w1, w2, w3, w4, w5)

    @pl.when(j < nheads)
    def _():
        rotated(q_ref, nn_rows(h1, pieces) + b_ref[...], cosf, s1, s2)

    @pl.when(j >= nheads)
    def _():
        dob_ref[...] = nn_rows(g, pieces).astype(BF)


def qd_call(h1, g, pieces, b_qkv, tabs, nheads):
    m, d = h1.shape
    local_len = tabs[0].shape[0]
    full = pl.BlockSpec((m, d), lambda j: (0, 0))

    def src(j):
        return (0, jnp.where(j < nheads, 3 * j, 2 * nheads + j))

    tab = pl.BlockSpec((local_len, 128), lambda j: (0, 0))
    return pl.pallas_call(
        functools.partial(qd_kernel, nheads),
        name="qd",
        grid=(2 * nheads,),
        in_specs=[
            full,
            full,
            *[pl.BlockSpec((p.shape[0], HD), src) for p in pieces],
            pl.BlockSpec((1, HD), lambda j: (0, 3 * jnp.minimum(j, nheads - 1))),
            tab,
            tab,
            tab,
        ],
        out_specs=[
            pl.BlockSpec((m, HD), lambda j: (0, jnp.minimum(j, nheads - 1))),
            pl.BlockSpec((m, HD), lambda j: (0, jnp.maximum(j - nheads, 0))),
        ],
        out_shape=[jax.ShapeDtypeStruct((m, nheads * HD), BF)] * 2,
        compiler_params=params(1),
        cost_estimate=cost(4 * m * d * nheads * HD, 2 * (2 * m * d + 2 * d * nheads * HD + 2 * m * nheads * HD)),
    )(h1, g, *pieces, b_qkv, *tabs)


def attn_kernel(nprev, local_len, meta, q_ref, kv_ref, pv_ref, dob_ref, cosf, s1, s2, ob_ref, dq_ref, dkv_ref, dpv_ref, sc_ref, dq_acc):
    slot = pl.program_id(0)
    ctx = meta[0]
    length = meta[3 + NBLK + slot]
    scale = 1.0 / math.sqrt(HD)
    n_vis = jnp.minimum(ctx, (length + local_len - 1) // local_len)
    q = q_ref[...]
    dob = dob_ref[...]
    own_k = kv_ref[:, :HD]
    own_v = kv_ref[:, HD:]

    ri = lax.broadcasted_iota(jnp.int32, (local_len, local_len), 0)
    ci = lax.broadcasted_iota(jnp.int32, (local_len, local_len), 1)
    s_own = nt(q, own_k) * scale
    s_own = jnp.where((ci <= ri) & (ci < length - ctx * local_len), s_own, neg_big)
    sc_ref[nprev] = s_own

    def prev_rows(jb):
        return pl.ds(pl.multiple_of(jb * local_len, local_len), local_len)

    def score(jb, top):
        s = nt(q, pv_ref[prev_rows(jb), :HD]) * scale
        s = jnp.where(ci[:1] < length - jb * local_len, s, neg_big)
        sc_ref[jb] = s
        return jnp.maximum(top, jnp.max(s, axis=1, keepdims=True))

    top = lax.fori_loop(0, n_vis, score, jnp.max(s_own, axis=1, keepdims=True))

    e_own = jnp.exp(sc_ref[nprev] - top)
    sc_ref[nprev] = e_own

    def expo(jb, tot):
        e = jnp.exp(sc_ref[jb] - top)
        sc_ref[jb] = e
        return tot + jnp.sum(e, axis=1, keepdims=True)

    tot = lax.fori_loop(0, n_vis, expo, jnp.sum(e_own, axis=1, keepdims=True))
    inv = 1.0 / tot
    att = nn((sc_ref[nprev] * inv).astype(BF), own_v)

    def out_step(jb, acc):
        return acc + nn((sc_ref[jb] * inv).astype(BF), pv_ref[prev_rows(jb), HD:])

    att = lax.fori_loop(0, n_vis, out_step, att)
    ob_ref[...] = att.astype(BF)
    delta = jnp.sum(dob.astype(F32) * att, axis=1, keepdims=True)

    def back(p, k, v):
        pb = p.astype(BF)
        ds = (p * (nt(dob, v) - delta)).astype(BF)
        return nn(ds, k) * scale, tn(ds, q) * scale, tn(pb, dob)

    dq, dk, dv = back(sc_ref[nprev] * inv, own_k, own_v)
    dq_acc[...] = dq
    dkv_ref[:, :HD] = dk
    dkv_ref[:, HD:] = dv

    def back_step(jb, carry):
        rows = prev_rows(jb)
        dqp, dkp, dvp = back(sc_ref[jb] * inv, pv_ref[rows, :HD], pv_ref[rows, HD:])
        dq_acc[...] += dqp
        dpv_ref[rows, :HD] = dkp.astype(BF)
        dpv_ref[rows, HD:] = dvp.astype(BF)
        return carry

    lax.fori_loop(0, n_vis, back_step, 0)

    def clear(jb, carry):
        dpv_ref[prev_rows(jb), :] = jnp.zeros((local_len, 2 * HD), BF)
        return carry

    lax.fori_loop(n_vis, nprev, clear, 0)
    rot, rest = rotate_tile(dq_acc[...], cosf[...], s1[...], s2[...], -1.0)
    dq_ref[:, :128] = rot.astype(BF)
    dq_ref[:, 128:] = rest.astype(BF)


def attn_call(meta, q, kv, pv, dob, tabs, nheads):
    local_len = tabs[0].shape[0]
    slots = q.shape[0] // local_len
    nprev = pv.shape[0] // q.shape[0]
    one = pl.BlockSpec((local_len, HD), lambda s, h, mt: (s, h))
    two = pl.BlockSpec((local_len, 2 * HD), lambda s, h, mt: (s, h))
    prev = pl.BlockSpec((nprev * local_len, 2 * HD), lambda s, h, mt: (s, h))
    tab = pl.BlockSpec((local_len, 128), lambda s, h, mt: (0, 0))
    m = q.shape[0]
    return pl.pallas_call(
        functools.partial(attn_kernel, nprev, local_len),
        name="attn",
        grid_spec=pltpu.PrefetchScalarGridSpec(
            num_scalar_prefetch=1,
            grid=(slots, nheads),
            in_specs=[one, two, prev, one, tab, tab, tab],
            out_specs=[one, one, two, prev],
            scratch_shapes=[
                pltpu.VMEM((nprev + 1, local_len, local_len), F32),
                pltpu.VMEM((local_len, HD), F32),
            ],
        ),
        out_shape=[
            jax.ShapeDtypeStruct((m, nheads * HD), BF),
            jax.ShapeDtypeStruct((m, nheads * HD), BF),
            jax.ShapeDtypeStruct((m, 2 * nheads * HD), F32),
            jax.ShapeDtypeStruct((nprev * m, 2 * nheads * HD), BF),
        ],
        compiler_params=params(2),
        cost_estimate=cost(12 * m * nheads * HD * (nprev + 1) * local_len, 20 * m * nheads * HD, m * nheads * (nprev + 1) * local_len),
    )(meta, q, kv, pv, dob, *tabs)


def join_kernel(nheads, dq_ref, dkv_ref, rv_ref, cosf, s1, s2, out_ref, sum_ref):
    i = pl.program_id(0)

    @pl.when(i == 0)
    def _():
        sum_ref[...] = jnp.zeros_like(sum_ref)

    for h in range(nheads):
        base = h * 3 * HD
        out_ref[:, base : base + HD] = dq_ref[:, h * HD : (h + 1) * HD]
        kc = slice(h * 2 * HD, h * 2 * HD + HD)
        vc = slice(h * 2 * HD + HD, (h + 1) * 2 * HD)
        dk = dkv_ref[:, kc] + rv_ref[:, kc].astype(F32)
        rot, rest = rotate_tile(dk, cosf[...], s1[...], s2[...], -1.0)
        out_ref[:, base + HD : base + HD + 128] = rot.astype(BF)
        out_ref[:, base + HD + 128 : base + 2 * HD] = rest.astype(BF)
        out_ref[:, base + 2 * HD : base + 3 * HD] = (dkv_ref[:, vc] + rv_ref[:, vc].astype(F32)).astype(BF)
    sum_ref[...] += jnp.sum(out_ref[...].astype(F32), axis=0, keepdims=True)


def join_call(dq, dkv, rv, tabs, nheads):
    m = dq.shape[0]
    local_len = tabs[0].shape[0]
    rows = 256
    per = local_len // rows

    def spec(c):
        return pl.BlockSpec((rows, c), lambda i: (i, 0))

    tab = pl.BlockSpec((rows, 128), lambda i: (i % per, 0))
    n = 3 * nheads * HD
    return pl.pallas_call(
        functools.partial(join_kernel, nheads),
        name="join",
        grid=(m // rows,),
        in_specs=[spec(nheads * HD), spec(2 * nheads * HD), spec(2 * nheads * HD), tab, tab, tab],
        out_specs=[spec(n), pl.BlockSpec((1, n), lambda i: (0, 0))],
        out_shape=[jax.ShapeDtypeStruct((m, n), BF), jax.ShapeDtypeStruct((1, n), F32)],
        compiler_params=params(1),
        cost_estimate=cost(10 * m * n, 8 * m * n),
    )(dq, dkv, rv, *tabs)


def hidden_kernel(h2, w0, w1, w2, w3, w4, w5, b_ref, gb_ref, dg_ref):
    u = nn_rows(h2, (w0, w1, w2, w3, w4, w5)) + b_ref[...]
    cdf = 0.5 * (1.0 + lax.erf(u * inv_sqrt_two))
    gb_ref[...] = (u * cdf).astype(BF)
    dg_ref[...] = (cdf + u * (jnp.exp(-0.5 * u * u) * inv_sqrt_tau)).astype(BF)


def hidden_call(h2, pieces, b_in):
    m, d = h2.shape
    f = pieces[0].shape[1]
    t = 256
    col = pl.BlockSpec((m, t), lambda j: (0, j))
    w_specs = [pl.BlockSpec((p.shape[0], t), lambda j: (0, j)) for p in pieces]
    return pl.pallas_call(
        hidden_kernel,
        name="hidden",
        grid=(f // t,),
        in_specs=[pl.BlockSpec((m, d), lambda j: (0, 0)), *w_specs, pl.BlockSpec((1, t), lambda j: (0, j))],
        out_specs=[col, col],
        out_shape=[jax.ShapeDtypeStruct((m, f), BF)] * 2,
        compiler_params=params(1),
        cost_estimate=cost(2 * m * d * f, 2 * (m * d + d * f + 2 * m * f), 2 * m * f),
    )(h2, *pieces, b_in)


def dhid_kernel(g, w0, w1, w2, w3, w4, w5, dg_ref, du_ref, sum_ref):
    a = nn_rows(g, (w0, w1, w2, w3, w4, w5))
    du = (a * dg_ref[...].astype(F32)).astype(BF)
    du_ref[...] = du
    sum_ref[...] = jnp.sum(du.astype(F32), axis=0, keepdims=True)


def dhid_call(g, pieces, dg):
    m, d = g.shape
    f = dg.shape[1]
    t = 256
    col = pl.BlockSpec((m, t), lambda j: (0, j))
    w_specs = [pl.BlockSpec((p.shape[0], t), lambda j: (0, j)) for p in pieces]
    return pl.pallas_call(
        dhid_kernel,
        name="dhid",
        grid=(f // t,),
        in_specs=[pl.BlockSpec((m, d), lambda j: (0, 0))] + w_specs + [col],
        out_specs=[col, pl.BlockSpec((1, t), lambda j: (0, j))],
        out_shape=[jax.ShapeDtypeStruct((m, f), BF), jax.ShapeDtypeStruct((1, f), F32)],
        compiler_params=params(1),
        cost_estimate=cost(2 * m * d * f, 2 * (m * d + d * f + 2 * m * f)),
    )(g, *pieces, dg)


def out_kernel(count, ob, gb, *refs):
    j = pl.program_id(0)
    ps, os, ya, yb = refs[:count], refs[count : 2 * count], refs[-2], refs[-1]
    each = 4 // count
    for k in range(4):

        @pl.when(j == k)
        def _():
            y = ya if k < 2 else yb
            y[...] = (nt(ob[...], ps[k // each][...]) + nt(gb[...], os[k // each][...])).astype(BF)


def piece_spec(count, i, cols, at=0, prefetch=False):
    each = 4 // count

    def place(j, *_):
        return (jnp.clip(j - i * each, 0, each - 1), at)

    if prefetch:
        return pl.BlockSpec((256, cols), lambda j, mt: place(j))
    return pl.BlockSpec((256, cols), lambda j: place(j))


def out_call(ob, gb, proj, out, scale=COST_SCALE):
    m, f = gb.shape
    nf = ob.shape[1]
    count = len(out)
    last = proj[0].shape[1] // nf - 1
    part = jax.ShapeDtypeStruct((m, 512), BF)
    return pl.pallas_call(
        functools.partial(out_kernel, count),
        name="outp",
        grid=(4,),
        in_specs=[pl.BlockSpec((m, nf), lambda j: (0, 0)), pl.BlockSpec((m, f), lambda j: (0, 0))]
        + [piece_spec(count, i, nf, last) for i in range(count)]
        + [piece_spec(count, i, f) for i in range(count)],
        out_specs=[
            pl.BlockSpec((m, 256), lambda j: (0, jnp.minimum(j, 1))),
            pl.BlockSpec((m, 256), lambda j: (0, jnp.maximum(j - 2, 0))),
        ],
        out_shape=[part, part],
        compiler_params=params(1),
        cost_estimate=cost(2048 * m * (f + nf), 2 * (m * f + m * nf + 1024 * (f + nf) + 1024 * m), k=scale),
    )(ob, gb, *proj, *out)


def back_kernel(meta, dqkv, du, w10, w11, w12, w20, w21, w22, x_ref, st_ref, ga, gf, prev, da_ref, db_ref, sums_ref):
    j = pl.program_id(0)
    for w1, w2, dn_ref, mine in ((w10, w20, da_ref, j < 2), (w11, w21, db_ref, j == 2), (w12, w22, db_ref, j == 3)):

        @pl.when(mine)
        def _():
            dh1 = nt(dqkv[...], w1[...])
            dh2 = nt(du[...], w2[...])
            xh = (x_ref[...].astype(F32) - st_ref[:, 0:1]) * st_ref[:, 1:2]
            dn_ref[...] = (dh1 * ga[...] + dh2 * gf[...]).astype(BF)
            sums_ref[0:1, :] = jnp.sum(dh1 * xh, axis=0, keepdims=True)
            sums_ref[1:2, :] = jnp.sum(dh1, axis=0, keepdims=True)
            sums_ref[2:3, :] = jnp.sum(dh2 * xh, axis=0, keepdims=True)
            sums_ref[3:4, :] = jnp.sum(dh2, axis=0, keepdims=True)


def back_call(meta, dqkv, du, g1, g2, x2, st, ga, gf, sums, half):
    m, d = x2.shape
    nq = dqkv.shape[1]
    f = du.shape[1]
    n = d // 4

    def absolute(rows):
        return pl.BlockSpec((rows, 256), lambda j, mt: (0, mt[1 + 4 * half + j]))

    part = jax.ShapeDtypeStruct((m, n), BF)
    at = slice(3 * half, 3 * half + 3)
    return pl.pallas_call(
        back_kernel,
        name="backn",
        grid_spec=pltpu.PrefetchScalarGridSpec(
            num_scalar_prefetch=1,
            grid=(4,),
            in_specs=[
                pl.BlockSpec((m, nq), lambda j, mt: (0, 0)),
                pl.BlockSpec((m, f), lambda j, mt: (0, 0)),
                pl.BlockSpec((256, nq), lambda j, mt: (jnp.minimum(j, 1), 0)),
                pl.BlockSpec((256, nq), lambda j, mt: (0, 0)),
                pl.BlockSpec((256, nq), lambda j, mt: (0, 0)),
                pl.BlockSpec((256, f), lambda j, mt: (jnp.minimum(j, 1), 0)),
                pl.BlockSpec((256, f), lambda j, mt: (0, 0)),
                pl.BlockSpec((256, f), lambda j, mt: (0, 0)),
                absolute(m),
                pl.BlockSpec((m, 128), lambda j, mt: (0, 0)),
                absolute(1),
                absolute(1),
                pl.BlockSpec(memory_space=pl.ANY),
            ],
            out_specs=[
                pl.BlockSpec((m, n // 2), lambda j, mt: (0, jnp.minimum(j, 1))),
                pl.BlockSpec((m, n // 2), lambda j, mt: (0, jnp.maximum(j - 2, 0))),
                absolute(4),
            ],
        ),
        out_shape=[part, part, jax.ShapeDtypeStruct((4, d), F32)],
        input_output_aliases={13: 2},
        compiler_params=params(1),
        cost_estimate=cost(4 * m * n * (f + nq), 2 * (m * f + m * nq + 2 * n * (f + nq) + 4 * m * n)),
    )(meta, dqkv, du, *g1[at], *g2[at], x2, st, ga, gf, sums)


def wgrad_kernel(pairs, adds, split, meta, *refs):
    j = pl.program_id(0)
    start = 0
    for p, count in enumerate(pairs):
        a, b = refs[2 * p], refs[2 * p + 1]

        @pl.when((j >= start) & (j < start + count))
        def _():
            y = tn(a[...], b[...])
            if adds:
                y = y + refs[2 * len(pairs)][...].astype(F32)
            if not split:
                refs[-1][...] = y.astype(BF)
                return
            keep, send = refs[-2:]
            n = y.shape[0] // 4
            swap = meta[2 + NBLK] > 0
            keep[:n] = y[:n].astype(BF)
            keep[n:] = jnp.where(swap, y[2 * n : 3 * n], y[n : 2 * n]).astype(BF)
            send[:n] = jnp.where(swap, y[n : 2 * n], y[2 * n : 3 * n]).astype(BF)
            send[n:] = y[3 * n :].astype(BF)

        start += count


def wgrad_call(meta, *flat, half, add=None, split=False):
    pairs = list(zip(flat[::2], flat[1::2]))
    m, d = pairs[0][0].shape
    t = 512
    counts = tuple(b.shape[1] // t for _, b in pairs)
    total = sum(counts)
    in_specs, ops, start = [], [], 0
    for (a, b), c in zip(pairs, counts):
        in_specs.append(pl.BlockSpec((m, d // 2), lambda j, mt: (0, half)))
        in_specs.append(
            pl.BlockSpec((m, t), lambda j, mt, s=start, c=c: (0, jnp.clip(j - s, 0, c - 1)))
        )
        ops += [a, b]
        start += c
    rows = d // 4 if split else d // 2
    if add is not None:
        in_specs.append(pl.BlockSpec((d // 2, t), lambda j, mt: (0, j)))
        ops.append(add)
    out_spec = pl.BlockSpec((rows, t), lambda j, mt: (0, j))
    out_shape = jax.ShapeDtypeStruct((rows, total * t), BF)
    return pl.pallas_call(
        functools.partial(wgrad_kernel, counts, add is not None, split),
        name="wgrad",
        grid_spec=pltpu.PrefetchScalarGridSpec(
            num_scalar_prefetch=1,
            grid=(total,),
            in_specs=in_specs,
            out_specs=[out_spec, out_spec] if split else out_spec,
        ),
        out_shape=[out_shape, out_shape] if split else out_shape,
        compiler_params=params(1),
        cost_estimate=cost(m * d * total * t, 2 * (m * d // 2 * len(pairs) + m * total * t + d * total * t)),
    )(meta, *ops)


def pack_kernel(*refs):
    out, at = refs[-1], 0
    for ref in refs[:-1]:
        n = ref.shape[0]
        out[at : at + n] = ref[...]
        at += n


def pack_call(*pieces):
    rows = sum(p.shape[0] for p in pieces)
    cols = pieces[0].shape[1]
    t = 512
    return pl.pallas_call(
        pack_kernel,
        name="pack",
        grid=(cols // t,),
        in_specs=[pl.BlockSpec((p.shape[0], t), lambda j: (0, j)) for p in pieces],
        out_specs=pl.BlockSpec((rows, t), lambda j: (0, j)),
        out_shape=jax.ShapeDtypeStruct((rows, cols), BF),
        compiler_params=params(1),
        cost_estimate=cost(0, 4 * rows * cols),
    )(*pieces)


def half_sum_kernel(keep, got, mid, send):
    n = mid.shape[0]
    mid[...] = keep[:n].astype(F32) + got[:n].astype(F32)
    send[...] = (keep[n:].astype(F32) + got[n:].astype(F32)).astype(BF)


def half_sum_call(keep, got):
    rows, cols = keep.shape
    t = 512
    n = rows // 2
    small = pl.BlockSpec((n, t), lambda j: (0, j))
    return pl.pallas_call(
        half_sum_kernel,
        name="hsum",
        grid=(cols // t,),
        in_specs=[pl.BlockSpec((rows, t), lambda j: (0, j))] * 2,
        out_specs=[small] * 2,
        out_shape=[jax.ShapeDtypeStruct((n, cols), F32), jax.ShapeDtypeStruct((n, cols), BF)],
        compiler_params=params(1),
        cost_estimate=cost(4 * n * cols, 14 * n * cols),
    )(keep, got)


def last_sum_kernel(plan, mid, got, *outs):
    j = pl.program_id(0)
    at = 0
    for (count, turned), out in zip(plan, outs):

        @pl.when((j >= at) & (j < at + count))
        def _():
            v = mid[...] + got[...].astype(F32)
            out[...] = v.T if turned else v

        at += count


def last_sum_call(mid, got, plan):
    n, cols = mid.shape
    t = 512
    block = pl.BlockSpec((n, t), lambda j: (0, j))
    out_specs, out_shape, at = [], [], 0
    for count, turned in plan:
        def place(j, at=at, count=count):
            return jnp.clip(j - at, 0, count - 1)

        if turned:
            out_specs.append(pl.BlockSpec((t, n), lambda j, f=place: (f(j), 0)))
            out_shape.append(jax.ShapeDtypeStruct((count * t, n), F32))
        else:
            out_specs.append(pl.BlockSpec((n, t), lambda j, f=place: (0, f(j))))
            out_shape.append(jax.ShapeDtypeStruct((n, count * t), F32))
        at += count
    return pl.pallas_call(
        functools.partial(last_sum_kernel, plan),
        name="lsum",
        grid=(cols // t,),
        in_specs=[block, block],
        out_specs=out_specs,
        out_shape=out_shape,
        compiler_params=params(1),
        cost_estimate=cost(2 * n * cols, 10 * n * cols),
    )(mid, got)


def by_role(meta, refs, body):
    @pl.when(meta[1 + NBLK] > 0)
    def _():
        body(refs[0::2])

    @pl.when(meta[1 + NBLK] == 0)
    def _():
        body(refs[1::2])


def block_out_kernel(local_len, first, meta, x_ref, b_ref, *refs):
    y_ref = refs[-1]
    rows = x_ref.shape[0]
    mask = row_valid(meta, (first + pl.program_id(0)) * rows, rows, local_len)

    def body(parts):
        for r in range(NBLK):
            col = block_cols(meta[1 + r] * 256)
            s = parts[r // 2][:, r % 2 * 256 : r % 2 * 256 + 256].astype(F32)
            y_ref[:, col] = (mask * (x_ref[:, col].astype(F32) + s + b_ref[:, col])).astype(BF)

    by_role(meta, refs[:8], body)


def input_grad_kernel(local_len, first, meta, x_ref, g_ref, st_ref, *refs):
    y_ref = refs[-1]
    rows = x_ref.shape[0]
    mask = row_valid(meta, (first + pl.program_id(0)) * rows, rows, local_len)
    mean = st_ref[:, 0:1]
    inv = st_ref[:, 1:2]
    d = x_ref.shape[1]

    def body(parts):
        def dn_of(r):
            return parts[r // 2][:, r % 2 * 256 : r % 2 * 256 + 256].astype(F32)

        one = jnp.zeros((rows, 256), F32)
        two = jnp.zeros((rows, 256), F32)
        for r in range(NBLK):
            dn = dn_of(r)
            one += dn
            two += dn * (x_ref[:, block_cols(meta[1 + r] * 256)].astype(F32) - mean)
        one = jnp.sum(one, axis=1, keepdims=True) / d
        two = jnp.sum(two, axis=1, keepdims=True) * inv / d
        slope = inv * inv * two
        shift = slope * mean - inv * one
        for r in range(NBLK):
            col = block_cols(meta[1 + r] * 256)
            y = g_ref[:, col].astype(F32) * mask + inv * dn_of(r)
            y_ref[:, col] = (y + (shift - slope * x_ref[:, col].astype(F32))).astype(BF)

    by_role(meta, refs[:8], body)


def rows_call(meta, *ops, body, name, specs, steps=None, into=None):
    rows = 256
    m, d = ops[0].shape
    first, last = steps or (0, m // rows)
    made = {
        "row": pl.BlockSpec((rows, d), lambda i, mt: (first + i, 0)),
        "part": pl.BlockSpec((rows, d // 4), lambda i, mt: (first + i, 0)),
        "stat": pl.BlockSpec((rows, 128), lambda i, mt: (first + i, 0)),
        "vec": pl.BlockSpec((1, d), lambda i, mt: (0, 0)),
    }
    in_specs = [made[s] for s in specs]
    aliases = {}
    if into is not None:
        aliases = {1 + len(ops): 0}
        in_specs.append(pl.BlockSpec(memory_space=pl.ANY))
        ops += (into,)
    return pl.pallas_call(
        functools.partial(body, first),
        name=name,
        grid_spec=pltpu.PrefetchScalarGridSpec(
            num_scalar_prefetch=1,
            grid=(last - first,),
            in_specs=in_specs,
            out_specs=made["row"],
        ),
        out_shape=jax.ShapeDtypeStruct((m, d), BF),
        input_output_aliases=aliases,
        compiler_params=params(1),
        cost_estimate=cost(10 * (last - first) * rows * d, 8 * (last - first) * rows * d),
    )(meta, *ops)


def after(v, *others):
    return lax.optimization_barrier((v,) + others)[0]


class Order:
    def __init__(self):
        self.last = ()

    def __call__(self, f, first, *rest, **named):
        out = f(after(first, *self.last), *rest, **named)
        self.last = (jax.tree.leaves(out)[0],)
        return out


def add_bf(a, b):
    return lax.optimization_barrier((a.astype(F32) + b.astype(F32)).astype(BF))


def pick_bf(a, b, middle, other):
    total = (a.astype(F32) + b.astype(F32)).astype(BF)
    return lax.optimization_barrier(jnp.where(middle > 0, total, other))


class Pipe:
    LAG = 3

    def __init__(self, run, middle, count):
        self.run, self.middle, self.count = run, middle, count
        self.parts, self.got, self.sums, self.crossed = [], [], [], []
        self.here, self.sent = [], []

    def send(self, part=None):
        step = len(self.got)
        back = step - self.LAG
        pairs = []
        v = part
        if part is not None:
            self.parts.append(part)
            pairs += [(0, 1), (3, 2)]
        if back >= 0:
            pairs += [(1, 0), (2, 3)]
            a, b = self.sums[back], self.crossed[back]
            if part is None:
                v = self.run(add_bf, a, b)
            else:
                v = self.run(pick_bf, a, b, self.middle, part)
        got = lax.ppermute(v, "tensor", pairs)
        self.got.append(got)
        if back >= 0:
            self.here.append(v)
            self.sent.append(got)

    def cross(self):
        k = len(self.sums)
        v = self.run(add_bf, self.parts[k], self.got[k])
        self.sums.append(v)
        self.crossed.append(lax.ppermute(v, "tensor", [(1, 2), (2, 1)]))


class PlainPipe:
    def __init__(self, run, middle, count):
        self.here, self.sent, self.sums = [], [], []

    def send(self, part=None):
        if part is not None:
            total = lax.psum(part, "tensor")
            self.here.append(total)
            self.sent.append(total)

    def cross(self):
        pass


class SmallMesh:
    def x(self, v):
        return lax.ppermute(v, "dp", [(0, 2), (2, 0), (1, 3), (3, 1)])

    def core(self, v):
        return lax.ppermute(v, "dp", [(0, 1), (1, 0), (2, 3), (3, 2)])

    def y(self, v):
        return lax.ppermute(v, "ctx", [(0, 1), (1, 0)])

    def perm(self):
        r = jnp.arange(NBLK, dtype=jnp.int32)
        dp = lax.axis_index("dp") ^ (((r >> 1) & 1) * 2 + (r >> 2))
        return dp * 2 + (lax.axis_index("ctx") ^ (r & 1))

    def middle(self):
        z = lax.axis_index("tensor")
        return ((z == 1) | (z == 2)).astype(jnp.int32)

    pipe = Pipe

    def first_hop(self, own, earlier=None):
        if earlier is None:
            return self.x(own), self.y(own)
        return self.x(after(own, earlier)), self.y(own)

    def second_hop(self, hop, earlier=()):
        return self.x(after(hop[1], hop[0], *earlier))

    def waited(self, hop):
        return hop

    def near_pieces(self, near):
        return near

    def near(self, run, own, hop):
        v = run(pack_call, own, hop[1])
        return v, self.core(v)

    def pieces(self, near, hop, diag, earlier=()):
        return near[0], hop[0], diag, near[1], self.core(after(hop[0], *earlier[:1])), self.core(after(diag, *earlier))

    def turn(self, v, first):
        pairs = []
        for dp in range(4):
            for c in range(2):
                to = (dp ^ 2) * 2 + c if dp % 2 != first else dp * 2 + (c ^ 1)
                pairs.append((dp * 2 + c, to))
        return lax.ppermute(v, ("dp", "ctx"), pairs)

    def scatter_cross(self, theirs):
        return self.core(theirs)

    def scatter_own(self, run, meta, pairs, got):
        keep, send = run(wgrad_call, meta, *pairs, half=0, add=got, split=True)
        return keep, self.turn(send, 1)

    def scatter_half(self, run, parts):
        mid, send = run(half_sum_call, *parts)
        return mid, self.turn(send, 0)

    def scatter_last(self, run, plan, parts):
        return run(last_sum_call, *parts, plan=plan)

    def previous(self, kv, slots):
        return lax.ppermute(kv, "ctx", [(0, 1)])

    def give_back(self, dpv, dkv, slots):
        return dkv, lax.ppermute(dpv, "ctx", [(1, 0)])

    def small_sum(self, run, v, step):
        def add(a, b):
            return a + b

        if step == 0:
            got = self.core(v)
        elif step == 1:
            got = self.x(v)
        elif step == 2:
            got = self.y(v)
        elif step == 3:
            got = lax.ppermute(v, "tensor", [(0, 1), (1, 0), (2, 3), (3, 2)])
        else:
            got = lax.ppermute(v, "tensor", [(0, 2), (2, 0), (1, 3), (3, 1)])
        return lambda: run(add, v, got)


class AnyMesh:
    def perm(self):
        return jnp.arange(NBLK, dtype=jnp.int32)

    def middle(self):
        return jnp.ones((), jnp.int32)

    pipe = PlainPipe

    def first_hop(self, own, earlier=None):
        return lax.all_gather(own, ("dp", "ctx"), axis=0, tiled=True)

    def second_hop(self, hop, earlier=()):
        return ()

    def waited(self, hop):
        return (hop,)

    def near_pieces(self, near):
        return near

    def near(self, run, own, hop):
        return hop[:512], hop[1024:1536]

    def pieces(self, near, hop, diag, earlier=()):
        return near[0], hop[512:768], hop[768:1024], near[1], hop[1536:1792], hop[1792:]

    def scatter_cross(self, theirs):
        return theirs

    def scatter_own(self, run, meta, pairs, got):
        full = jnp.concatenate([run(wgrad_call, meta, *pairs, half=0), got], axis=0)
        return lax.psum_scatter(full, ("dp", "ctx"), scatter_dimension=0, tiled=True).astype(F32)

    def scatter_half(self, run, parts):
        return parts

    def scatter_last(self, run, plan, parts):
        outs, at = [], 0
        for count, turned in plan:
            v = parts[:, at * 512 : (at + count) * 512]
            outs.append(v.T if turned else v)
            at += count
        return outs

    def previous(self, kv, slots):
        own = kv.reshape(slots, -1, kv.shape[1])
        full = lax.all_gather(own, "ctx", axis=1, tiled=True)
        return full.reshape(-1, kv.shape[1])

    def give_back(self, dpv, dkv, slots):
        cols = dkv.shape[1]
        full = dpv.reshape(slots, -1, cols)
        got = lax.psum_scatter(full, "ctx", scatter_dimension=1, tiled=True)
        return dkv, got.reshape(-1, cols)

    def small_sum(self, run, v, step):
        got = v
        if step == 0:
            got = lax.psum(v, ("dp", "ctx"))
        elif step == 3:
            got = lax.psum(v, "tensor")
        return lambda: got


def rotary_tables(positions):
    half_rot = ROT // 2
    lane = jnp.arange(128, dtype=jnp.int32)
    exponent = (lane % half_rot).astype(F32) * (2.0 / ROT)
    angles = positions[:, None] * jnp.exp(-math.log(10000.0) * exponent)[None, :]
    cos_all, sin_all = jnp.cos(angles), jnp.sin(angles)
    cosf = jnp.where(lane < ROT, cos_all, 1.0)
    s1 = jnp.where(lane < half_rot, -sin_all, 0.0)
    s2 = jnp.where((lane >= half_rot) & (lane < ROT), sin_all, 0.0)
    return cosf, s1, s2


def local(small, block_input, out_grad, lengths, attn_gain, attn_shift, ffn_gain, ffn_shift, w_qkv, b_qkv, w_proj, b_proj, w_in, b_in, w_out, b_out):
    comm = SmallMesh() if small else AnyMesh()
    slots, local_len, d = block_input.shape
    m = slots * local_len
    nheads = b_qkv.shape[0] // (3 * HD)
    nq = 3 * nheads * HD
    ctx = lax.axis_index("ctx")
    core = lax.axis_index("dp") % 2
    meta = jnp.concatenate(
        [ctx[None].astype(jnp.int32), comm.perm(), comm.middle()[None], core[None].astype(jnp.int32), lengths]
    )

    run = Order()
    x2 = block_input.reshape(m, d)
    og2 = out_grad.reshape(m, d)
    ga, sa, gf, sf = (v.reshape(1, d) for v in (attn_gain, attn_shift, ffn_gain, ffn_shift))
    bq = b_qkv.reshape(1, nq)
    positions = ctx * local_len + jnp.arange(local_len, dtype=jnp.int32)
    tabs = rotary_tables(positions.astype(F32))

    own1 = jnp.concatenate([w_qkv, w_proj.T], axis=1).astype(BF)
    hop1 = comm.first_hop(own1)
    own2 = w_in.astype(BF)
    own3 = w_out.T.astype(BF)
    run.last = (own1, own2, own3)
    hop2 = comm.first_hop(own2, hop1[0])
    h1, g, stats, g_sum = run(norm_call, meta, x2, og2, ga, sa, local_len)
    diag1 = comm.second_hop(hop1)
    near1 = comm.near(run, own1, hop1)
    g1 = comm.pieces(near1, hop1, diag1)
    near2 = comm.near(run, own2, hop2)
    kv = run(kv_call, h1, g1, bq, tabs, nheads)
    pv = comm.previous(kv, slots)
    diag2 = comm.second_hop(hop2, (kv,))
    hop3 = comm.first_hop(own3, diag2)
    q, dob = run(qd_call, h1, g, g1, bq, tabs, nheads)
    g2 = comm.pieces(near2, hop2, diag2, (kv, q))
    diag3 = comm.second_hop(hop3)
    h2 = run(second_norm_call, meta, x2, stats, gf, sf)
    gb, dg = run(hidden_call, h2, g2, b_in.reshape(1, -1))
    near3 = comm.near(run, own3, hop3)
    ob, dq, dkv, dpv = run(attn_call, meta, q, kv, pv, dob, tabs, nheads)
    dkv, rv = comm.give_back(dpv, dkv, slots)
    g3 = comm.near_pieces(near3)

    pipe = comm.pipe(run, meta[1 + NBLK], 8)
    ff = gb.shape[1] // 512
    out0, out2 = run(out_call, ob, gb, (g1[0], g1[3]), g3, 0.01)
    pipe.send(out0)
    pipe.send(out2)
    g3 = comm.pieces(near3, hop3, diag3, (ob, out0))
    cross3 = comm.scatter_cross(run(wgrad_call, meta, g, gb, half=1))
    far = (1, 2, 4, 5)
    out1, out3 = run(out_call, ob, gb, [g1[k] for k in far], [g3[k] for k in far])
    du, bin_sum = run(dhid_call, g, g3, dg)
    pipe.cross()
    pipe.send(after(out1, *pipe.sums))
    state3 = comm.scatter_own(run, meta, (g, gb), cross3)
    pipe.cross()
    dqkv, bqkv_sum = run(join_call, dq, dkv, rv, tabs, nheads)
    pipe.send(out3)
    gain_sums = jnp.zeros((4, d), F32)
    dn0, dn1, gain_sums = run(back_call, meta, dqkv, du, g1, g2, x2, stats, ga, gf, gain_sums, 0)
    pipe.cross()
    pipe.send(dn0)
    state3 = comm.scatter_half(run, state3)
    pipe.cross()
    pipe.send(dn1)
    dn2, dn3, gain_sums = run(back_call, meta, dqkv, du, g1, g2, x2, stats, ga, gf, gain_sums, 1)
    pipe.cross()
    pipe.send(dn2)
    cross2 = comm.scatter_cross(run(wgrad_call, after(meta, jax.tree.leaves(state3)[-1]), h2, du, half=1))
    theirs1 = run(wgrad_call, meta, h1, dqkv, g, ob, half=1)
    pipe.cross()
    pipe.send(dn3)
    state2 = comm.scatter_own(run, meta, (h2, du), cross2)
    (grad_out,) = comm.scatter_last(run, ((ff, True),), state3)
    small = jnp.concatenate([gain_sums.reshape(-1), g_sum.reshape(-1), bqkv_sum.reshape(-1), bin_sum.reshape(-1)])
    add = comm.small_sum(run, after(small, grad_out), 0)
    pipe.cross()
    pipe.send()
    cross1 = comm.scatter_cross(after(theirs1, pipe.here[-1]))
    state2 = comm.scatter_half(run, state2)
    small = add()
    add = comm.small_sum(run, small, 1)

    def sums_of(order):
        return [v for c in order for v in (pipe.here[c], pipe.sent[c])]

    out_ops = (meta, x2, (b_proj + b_out).reshape(1, d), *sums_of((0, 2, 1, 3)))
    out_half = functools.partial(
        rows_call, body=functools.partial(block_out_kernel, local_len), name="bout", specs=("row", "vec") + ("part",) * 8
    )
    block_output = run(out_half, *out_ops, steps=(0, 2))
    small = add()
    pipe.cross()
    pipe.send()
    (grad_in,) = comm.scatter_last(run, ((ff, False),), state2)
    add = comm.small_sum(run, after(small, grad_in), 2)
    state1 = comm.scatter_own(run, meta, (h1, dqkv, g, ob), cross1)
    block_output = run(out_half, *out_ops, steps=(2, 4), into=block_output).reshape(slots, local_len, d)
    small = add()
    gains = small[: 4 * d]
    group = small[4 * d :]
    state1 = comm.scatter_half(run, after(state1, pipe.sent[5]))
    pipe.send()
    grad_qkv, grad_proj = comm.scatter_last(
        run, ((nq // 512, False), (nheads * HD // 512, True)), after(state1, pipe.sent[6])
    )
    add = comm.small_sum(run, after(gains, grad_qkv), 3)
    gains = add()
    add = comm.small_sum(run, gains, 4)
    input_grad = run(
        rows_call, meta, x2, og2, stats, *sums_of(range(4, 8)),
        body=functools.partial(input_grad_kernel, local_len), name="igrad", specs=("row", "row", "stat") + ("part",) * 8,
    ).reshape(slots, local_len, d)
    gains = add().reshape(4, d)
    bias_grad = group[:d]
    return (
        block_output,
        input_grad,
        gains[0],
        gains[1],
        gains[2],
        gains[3],
        grad_qkv,
        group[d : d + nq],
        grad_proj,
        bias_grad,
        grad_in,
        group[d + nq :],
        grad_out,
        bias_grad,
    )


def solution(mesh):
    small = mesh.shape["dp"] == 4 and mesh.shape["ctx"] == 2 and mesh.shape["tensor"] == 4
    placed = (
        P("dp", "ctx", None),
        P("dp", "ctx", None),
        P("dp"),
        P(),
        P(),
        P(),
        P(),
        P(("dp", "ctx"), "tensor"),
        P("tensor"),
        P("tensor", ("dp", "ctx")),
        P(),
        P(("dp", "ctx"), "tensor"),
        P("tensor"),
        P("tensor", ("dp", "ctx")),
        P(),
    )
    return jax.shard_map(
        functools.partial(local, small),
        mesh=mesh,
        in_specs=placed,
        out_specs=(
            P("dp", "ctx", None),
            P("dp", "ctx", None),
            P(),
            P(),
            P(),
            P(),
            P(("dp", "ctx"), "tensor"),
            P("tensor"),
            P("tensor", ("dp", "ctx")),
            P(),
            P(("dp", "ctx"), "tensor"),
            P("tensor"),
            P("tensor", ("dp", "ctx")),
            P(),
        ),
        check_vma=False,
    )
```

```python
import functools
import math

import jax
import jax.numpy as jnp
from jax import lax
from jax.experimental import pallas as pl
from jax.experimental.pallas import tpu as pltpu
from jax.sharding import PartitionSpec as P

HD = 256
ROT = 64
NBLK = 8
BF = jnp.bfloat16
F32 = jnp.float32

neg_big = -1e30
inv_sqrt_two = 0.7071067811865476
inv_sqrt_tau = 0.3989422804014327


COST_SCALE = 20


def cost(flops, nbytes, trans=0, k=COST_SCALE):
    flops = max(flops, 300 * nbytes)
    return pl.CostEstimate(flops=int(k * flops), bytes_accessed=int(k * nbytes), transcendentals=int(k * trans))


def params(n, mb=60):
    return pltpu.CompilerParams(
        dimension_semantics=("arbitrary",) * n, vmem_limit_bytes=int(mb * 1024 * 1024)
    )


def nn(a, b):
    return lax.dot_general(a, b, (((1,), (0,)), ((), ())), preferred_element_type=F32)


def nn_rows(a, pieces):
    total, at = None, 0
    for w in pieces:
        y = nn(a[:, at : at + w.shape[0]], w[...])
        total = y if total is None else total + y
        at += w.shape[0]
    return total


def nt(a, b):
    return lax.dot_general(a, b, (((1,), (1,)), ((), ())), preferred_element_type=F32)


def tn(a, b):
    return lax.dot_general(a, b, (((0,), (0,)), ((), ())), preferred_element_type=F32)


def block_cols(r):
    return pl.ds(pl.multiple_of(r, 128), 256)


def row_valid(meta, row0, rows, local_len):
    slot = row0 // local_len
    pos = meta[0] * local_len + row0 % local_len + lax.broadcasted_iota(jnp.int32, (rows, 1), 0)
    return (pos < meta[3 + NBLK + slot]).astype(F32)


def norm_kernel(local_len, meta, x_ref, g_ref, ga, sa, h1_ref, g_out, st_ref, gs_ref):
    rows = x_ref.shape[0]
    i = pl.program_id(0)
    x = x_ref[...].astype(F32)
    mean = jnp.mean(x, axis=-1, keepdims=True)
    cen = x - mean
    inv = lax.rsqrt(jnp.mean(cen * cen, axis=-1, keepdims=True) + 1e-05)
    mask = row_valid(meta, i * rows, rows, local_len)
    lane = lax.broadcasted_iota(jnp.int32, (rows, 128), 1)
    st_ref[...] = jnp.where(lane == 0, mean, inv)
    for r in range(NBLK):
        src = block_cols(meta[1 + r] * 256)
        dst = slice(r * 256, (r + 1) * 256)
        xh = (x_ref[:, src].astype(F32) - mean) * inv
        h1_ref[:, dst] = (xh * ga[:, src] + sa[:, src]).astype(BF)
        gm = g_ref[:, src].astype(F32) * mask
        g_out[:, dst] = gm.astype(BF)
        part = jnp.sum(gm, axis=0, keepdims=True)

        @pl.when(i == 0)
        def _():
            gs_ref[:, src] = part

        @pl.when(i > 0)
        def _():
            gs_ref[:, src] = gs_ref[:, src] + part


def second_norm_kernel(meta, x_ref, st_ref, gf, sf, h2_ref):
    for r in range(NBLK):
        src = block_cols(meta[1 + r] * 256)
        xh = (x_ref[:, src].astype(F32) - st_ref[:, 0:1]) * st_ref[:, 1:2]
        h2_ref[:, r * 256 : (r + 1) * 256] = (xh * gf[:, src] + sf[:, src]).astype(BF)


def second_norm_call(meta, x2, st, gf, sf):
    m, d = x2.shape
    rows = 256
    row_spec = pl.BlockSpec((rows, d), lambda i, mt: (i, 0))
    vec = pl.BlockSpec((1, d), lambda i, mt: (0, 0))
    return pl.pallas_call(
        second_norm_kernel,
        name="norm2",
        grid_spec=pltpu.PrefetchScalarGridSpec(
            num_scalar_prefetch=1,
            grid=(m // rows,),
            in_specs=[row_spec, pl.BlockSpec((rows, 128), lambda i, mt: (i, 0)), vec, vec],
            out_specs=row_spec,
        ),
        out_shape=jax.ShapeDtypeStruct((m, d), BF),
        compiler_params=params(1),
        cost_estimate=cost(5 * m * d, 4 * m * d),
    )(meta, x2, st, gf, sf)


def norm_call(meta, x2, g2, ga, sa, local_len):
    m, d = x2.shape
    rows = 256
    row_spec = pl.BlockSpec((rows, d), lambda i, mt: (i, 0))
    vec = pl.BlockSpec((1, d), lambda i, mt: (0, 0))
    return pl.pallas_call(
        functools.partial(norm_kernel, local_len),
        name="norm",
        grid_spec=pltpu.PrefetchScalarGridSpec(
            num_scalar_prefetch=1,
            grid=(m // rows,),
            in_specs=[row_spec, row_spec, vec, vec],
            out_specs=[row_spec, row_spec, pl.BlockSpec((rows, 128), lambda i, mt: (i, 0)), vec],
        ),
        out_shape=[jax.ShapeDtypeStruct((m, d), BF)] * 2
        + [jax.ShapeDtypeStruct((m, 128), F32), jax.ShapeDtypeStruct((1, d), F32)],
        compiler_params=params(1),
        cost_estimate=cost(20 * m * d, 10 * m * d),
    )(meta, x2, g2, ga, sa)


def rotate_tile(y, cosf, s1, s2, sign):
    head = y[:, :128]
    rot = (
        head * cosf
        + pltpu.roll(head, 96, 1) * (s1 * sign)
        + pltpu.roll(head, 32, 1) * (s2 * sign)
    )
    return rot, y[:, 128:]


def rotated(out, y, cosf, s1, s2):
    local_len = cosf.shape[0]
    for s in range(y.shape[0] // local_len):
        rows = slice(s * local_len, (s + 1) * local_len)
        rot, rest = rotate_tile(y[rows], cosf[...], s1[...], s2[...], 1.0)
        out[rows, :128] = rot.astype(BF)
        out[rows, 128:] = rest.astype(BF)


def kv_kernel(h1, w0, w1, w2, w3, w4, w5, b_ref, cosf, s1, s2, kv_ref):
    part = lax.rem(pl.program_id(0), 2)
    y = nn_rows(h1, (w0, w1, w2, w3, w4, w5)) + b_ref[...]

    @pl.when(part == 0)
    def _():
        rotated(kv_ref, y, cosf, s1, s2)

    @pl.when(part == 1)
    def _():
        kv_ref[...] = y.astype(BF)


def kv_call(h1, pieces, b_qkv, tabs, nheads):
    m, d = h1.shape
    local_len = tabs[0].shape[0]

    def src(j):
        return (0, (j // 2) * 3 + 1 + j % 2)

    tab = pl.BlockSpec((local_len, 128), lambda j: (0, 0))
    return pl.pallas_call(
        kv_kernel,
        name="kv",
        grid=(2 * nheads,),
        in_specs=[
            pl.BlockSpec((m, d), lambda j: (0, 0)),
            *[pl.BlockSpec((p.shape[0], HD), src) for p in pieces],
            pl.BlockSpec((1, HD), src),
            tab,
            tab,
            tab,
        ],
        out_specs=pl.BlockSpec((m, HD), lambda j: (0, j)),
        out_shape=jax.ShapeDtypeStruct((m, 2 * nheads * HD), BF),
        compiler_params=params(1),
        cost_estimate=cost(4 * m * d * nheads * HD, 2 * (m * d + 2 * d * nheads * HD + 2 * m * nheads * HD)),
    )(h1, *pieces, b_qkv, *tabs)


def qd_kernel(nheads, h1, g, w0, w1, w2, w3, w4, w5, b_ref, cosf, s1, s2, q_ref, dob_ref):
    j = pl.program_id(0)
    pieces = (w0, w1, w2, w3, w4, w5)

    @pl.when(j < nheads)
    def _():
        rotated(q_ref, nn_rows(h1, pieces) + b_ref[...], cosf, s1, s2)

    @pl.when(j >= nheads)
    def _():
        dob_ref[...] = nn_rows(g, pieces).astype(BF)


def qd_call(h1, g, pieces, b_qkv, tabs, nheads):
    m, d = h1.shape
    local_len = tabs[0].shape[0]
    full = pl.BlockSpec((m, d), lambda j: (0, 0))

    def src(j):
        return (0, jnp.where(j < nheads, 3 * j, 2 * nheads + j))

    tab = pl.BlockSpec((local_len, 128), lambda j: (0, 0))
    return pl.pallas_call(
        functools.partial(qd_kernel, nheads),
        name="qd",
        grid=(2 * nheads,),
        in_specs=[
            full,
            full,
            *[pl.BlockSpec((p.shape[0], HD), src) for p in pieces],
            pl.BlockSpec((1, HD), lambda j: (0, 3 * jnp.minimum(j, nheads - 1))),
            tab,
            tab,
            tab,
        ],
        out_specs=[
            pl.BlockSpec((m, HD), lambda j: (0, jnp.minimum(j, nheads - 1))),
            pl.BlockSpec((m, HD), lambda j: (0, jnp.maximum(j - nheads, 0))),
        ],
        out_shape=[jax.ShapeDtypeStruct((m, nheads * HD), BF)] * 2,
        compiler_params=params(1),
        cost_estimate=cost(4 * m * d * nheads * HD, 2 * (2 * m * d + 2 * d * nheads * HD + 2 * m * nheads * HD)),
    )(h1, g, *pieces, b_qkv, *tabs)


def attn_kernel(nprev, local_len, meta, q_ref, kv_ref, pv_ref, dob_ref, cosf, s1, s2, ob_ref, dq_ref, dkv_ref, dpv_ref, sc_ref, dq_acc):
    slot = pl.program_id(0)
    ctx = meta[0]
    length = meta[3 + NBLK + slot]
    scale = 1.0 / math.sqrt(HD)
    n_vis = jnp.minimum(ctx, (length + local_len - 1) // local_len)
    q = q_ref[...]
    dob = dob_ref[...]
    own_k = kv_ref[:, :HD]
    own_v = kv_ref[:, HD:]

    ri = lax.broadcasted_iota(jnp.int32, (local_len, local_len), 0)
    ci = lax.broadcasted_iota(jnp.int32, (local_len, local_len), 1)
    s_own = nt(q, own_k) * scale
    s_own = jnp.where((ci <= ri) & (ci < length - ctx * local_len), s_own, neg_big)
    sc_ref[nprev] = s_own

    def prev_rows(jb):
        return pl.ds(pl.multiple_of(jb * local_len, local_len), local_len)

    def score(jb, top):
        s = nt(q, pv_ref[prev_rows(jb), :HD]) * scale
        s = jnp.where(ci[:1] < length - jb * local_len, s, neg_big)
        sc_ref[jb] = s
        return jnp.maximum(top, jnp.max(s, axis=1, keepdims=True))

    top = lax.fori_loop(0, n_vis, score, jnp.max(s_own, axis=1, keepdims=True))

    e_own = jnp.exp(sc_ref[nprev] - top)
    sc_ref[nprev] = e_own

    def expo(jb, tot):
        e = jnp.exp(sc_ref[jb] - top)
        sc_ref[jb] = e
        return tot + jnp.sum(e, axis=1, keepdims=True)

    tot = lax.fori_loop(0, n_vis, expo, jnp.sum(e_own, axis=1, keepdims=True))
    inv = 1.0 / tot
    att = nn((sc_ref[nprev] * inv).astype(BF), own_v)

    def out_step(jb, acc):
        return acc + nn((sc_ref[jb] * inv).astype(BF), pv_ref[prev_rows(jb), HD:])

    att = lax.fori_loop(0, n_vis, out_step, att)
    ob_ref[...] = att.astype(BF)
    delta = jnp.sum(dob.astype(F32) * att, axis=1, keepdims=True)

    def back(p, k, v):
        pb = p.astype(BF)
        ds = (p * (nt(dob, v) - delta)).astype(BF)
        return nn(ds, k) * scale, tn(ds, q) * scale, tn(pb, dob)

    dq, dk, dv = back(sc_ref[nprev] * inv, own_k, own_v)
    dq_acc[...] = dq
    dkv_ref[:, :HD] = dk
    dkv_ref[:, HD:] = dv

    def back_step(jb, carry):
        rows = prev_rows(jb)
        dqp, dkp, dvp = back(sc_ref[jb] * inv, pv_ref[rows, :HD], pv_ref[rows, HD:])
        dq_acc[...] += dqp
        dpv_ref[rows, :HD] = dkp.astype(BF)
        dpv_ref[rows, HD:] = dvp.astype(BF)
        return carry

    lax.fori_loop(0, n_vis, back_step, 0)

    def clear(jb, carry):
        dpv_ref[prev_rows(jb), :] = jnp.zeros((local_len, 2 * HD), BF)
        return carry

    lax.fori_loop(n_vis, nprev, clear, 0)
    rot, rest = rotate_tile(dq_acc[...], cosf[...], s1[...], s2[...], -1.0)
    dq_ref[:, :128] = rot.astype(BF)
    dq_ref[:, 128:] = rest.astype(BF)


def attn_call(meta, q, kv, pv, dob, tabs, nheads):
    local_len = tabs[0].shape[0]
    slots = q.shape[0] // local_len
    nprev = pv.shape[0] // q.shape[0]
    one = pl.BlockSpec((local_len, HD), lambda s, h, mt: (s, h))
    two = pl.BlockSpec((local_len, 2 * HD), lambda s, h, mt: (s, h))
    prev = pl.BlockSpec((nprev * local_len, 2 * HD), lambda s, h, mt: (s, h))
    tab = pl.BlockSpec((local_len, 128), lambda s, h, mt: (0, 0))
    m = q.shape[0]
    return pl.pallas_call(
        functools.partial(attn_kernel, nprev, local_len),
        name="attn",
        grid_spec=pltpu.PrefetchScalarGridSpec(
            num_scalar_prefetch=1,
            grid=(slots, nheads),
            in_specs=[one, two, prev, one, tab, tab, tab],
            out_specs=[one, one, two, prev],
            scratch_shapes=[
                pltpu.VMEM((nprev + 1, local_len, local_len), F32),
                pltpu.VMEM((local_len, HD), F32),
            ],
        ),
        out_shape=[
            jax.ShapeDtypeStruct((m, nheads * HD), BF),
            jax.ShapeDtypeStruct((m, nheads * HD), BF),
            jax.ShapeDtypeStruct((m, 2 * nheads * HD), F32),
            jax.ShapeDtypeStruct((nprev * m, 2 * nheads * HD), BF),
        ],
        compiler_params=params(2),
        cost_estimate=cost(12 * m * nheads * HD * (nprev + 1) * local_len, 20 * m * nheads * HD, m * nheads * (nprev + 1) * local_len),
    )(meta, q, kv, pv, dob, *tabs)


def join_kernel(nheads, dq_ref, dkv_ref, rv_ref, cosf, s1, s2, out_ref, sum_ref):
    i = pl.program_id(0)

    @pl.when(i == 0)
    def _():
        sum_ref[...] = jnp.zeros_like(sum_ref)

    for h in range(nheads):
        base = h * 3 * HD
        out_ref[:, base : base + HD] = dq_ref[:, h * HD : (h + 1) * HD]
        kc = slice(h * 2 * HD, h * 2 * HD + HD)
        vc = slice(h * 2 * HD + HD, (h + 1) * 2 * HD)
        dk = dkv_ref[:, kc] + rv_ref[:, kc].astype(F32)
        rot, rest = rotate_tile(dk, cosf[...], s1[...], s2[...], -1.0)
        out_ref[:, base + HD : base + HD + 128] = rot.astype(BF)
        out_ref[:, base + HD + 128 : base + 2 * HD] = rest.astype(BF)
        out_ref[:, base + 2 * HD : base + 3 * HD] = (dkv_ref[:, vc] + rv_ref[:, vc].astype(F32)).astype(BF)
    sum_ref[...] += jnp.sum(out_ref[...].astype(F32), axis=0, keepdims=True)


def join_call(dq, dkv, rv, tabs, nheads):
    m = dq.shape[0]
    local_len = tabs[0].shape[0]
    rows = 256
    per = local_len // rows

    def spec(c):
        return pl.BlockSpec((rows, c), lambda i: (i, 0))

    tab = pl.BlockSpec((rows, 128), lambda i: (i % per, 0))
    n = 3 * nheads * HD
    return pl.pallas_call(
        functools.partial(join_kernel, nheads),
        name="join",
        grid=(m // rows,),
        in_specs=[spec(nheads * HD), spec(2 * nheads * HD), spec(2 * nheads * HD), tab, tab, tab],
        out_specs=[spec(n), pl.BlockSpec((1, n), lambda i: (0, 0))],
        out_shape=[jax.ShapeDtypeStruct((m, n), BF), jax.ShapeDtypeStruct((1, n), F32)],
        compiler_params=params(1),
        cost_estimate=cost(10 * m * n, 8 * m * n),
    )(dq, dkv, rv, *tabs)


def hidden_kernel(h2, w0, w1, w2, w3, w4, w5, b_ref, gb_ref, dg_ref):
    u = nn_rows(h2, (w0, w1, w2, w3, w4, w5)) + b_ref[...]
    cdf = 0.5 * (1.0 + lax.erf(u * inv_sqrt_two))
    gb_ref[...] = (u * cdf).astype(BF)
    dg_ref[...] = (cdf + u * (jnp.exp(-0.5 * u * u) * inv_sqrt_tau)).astype(BF)


def hidden_call(h2, pieces, b_in):
    m, d = h2.shape
    f = pieces[0].shape[1]
    t = 256
    col = pl.BlockSpec((m, t), lambda j: (0, j))
    w_specs = [pl.BlockSpec((p.shape[0], t), lambda j: (0, j)) for p in pieces]
    return pl.pallas_call(
        hidden_kernel,
        name="hidden",
        grid=(f // t,),
        in_specs=[pl.BlockSpec((m, d), lambda j: (0, 0)), *w_specs, pl.BlockSpec((1, t), lambda j: (0, j))],
        out_specs=[col, col],
        out_shape=[jax.ShapeDtypeStruct((m, f), BF)] * 2,
        compiler_params=params(1),
        cost_estimate=cost(2 * m * d * f, 2 * (m * d + d * f + 2 * m * f), 2 * m * f),
    )(h2, *pieces, b_in)


def dhid_kernel(g, w0, w1, w2, w3, w4, w5, dg_ref, du_ref, sum_ref):
    a = nn_rows(g, (w0, w1, w2, w3, w4, w5))
    du = (a * dg_ref[...].astype(F32)).astype(BF)
    du_ref[...] = du
    sum_ref[...] = jnp.sum(du.astype(F32), axis=0, keepdims=True)


def dhid_call(g, pieces, dg):
    m, d = g.shape
    f = dg.shape[1]
    t = 256
    col = pl.BlockSpec((m, t), lambda j: (0, j))
    w_specs = [pl.BlockSpec((p.shape[0], t), lambda j: (0, j)) for p in pieces]
    return pl.pallas_call(
        dhid_kernel,
        name="dhid",
        grid=(f // t,),
        in_specs=[pl.BlockSpec((m, d), lambda j: (0, 0))] + w_specs + [col],
        out_specs=[col, pl.BlockSpec((1, t), lambda j: (0, j))],
        out_shape=[jax.ShapeDtypeStruct((m, f), BF), jax.ShapeDtypeStruct((1, f), F32)],
        compiler_params=params(1),
        cost_estimate=cost(2 * m * d * f, 2 * (m * d + d * f + 2 * m * f)),
    )(g, *pieces, dg)


def out_kernel(count, ob, gb, *refs):
    j = pl.program_id(0)
    ps, os, ya, yb = refs[:count], refs[count : 2 * count], refs[-2], refs[-1]
    each = 4 // count
    for k in range(4):

        @pl.when(j == k)
        def _():
            y = ya if k < 2 else yb
            y[...] = (nt(ob[...], ps[k // each][...]) + nt(gb[...], os[k // each][...])).astype(BF)


def piece_spec(count, i, cols, at=0, prefetch=False):
    each = 4 // count

    def place(j, *_):
        return (jnp.clip(j - i * each, 0, each - 1), at)

    if prefetch:
        return pl.BlockSpec((256, cols), lambda j, mt: place(j))
    return pl.BlockSpec((256, cols), lambda j: place(j))


def out_call(ob, gb, proj, out, scale=COST_SCALE):
    m, f = gb.shape
    nf = ob.shape[1]
    count = len(out)
    last = proj[0].shape[1] // nf - 1
    part = jax.ShapeDtypeStruct((m, 512), BF)
    return pl.pallas_call(
        functools.partial(out_kernel, count),
        name="outp",
        grid=(4,),
        in_specs=[pl.BlockSpec((m, nf), lambda j: (0, 0)), pl.BlockSpec((m, f), lambda j: (0, 0))]
        + [piece_spec(count, i, nf, last) for i in range(count)]
        + [piece_spec(count, i, f) for i in range(count)],
        out_specs=[
            pl.BlockSpec((m, 256), lambda j: (0, jnp.minimum(j, 1))),
            pl.BlockSpec((m, 256), lambda j: (0, jnp.maximum(j - 2, 0))),
        ],
        out_shape=[part, part],
        compiler_params=params(1),
        cost_estimate=cost(2048 * m * (f + nf), 2 * (m * f + m * nf + 1024 * (f + nf) + 1024 * m), k=scale),
    )(ob, gb, *proj, *out)


def back_kernel(meta, dqkv, du, w10, w11, w12, w20, w21, w22, x_ref, st_ref, ga, gf, prev, da_ref, db_ref, sums_ref):
    j = pl.program_id(0)
    for w1, w2, dn_ref, mine in ((w10, w20, da_ref, j < 2), (w11, w21, db_ref, j == 2), (w12, w22, db_ref, j == 3)):

        @pl.when(mine)
        def _():
            dh1 = nt(dqkv[...], w1[...])
            dh2 = nt(du[...], w2[...])
            xh = (x_ref[...].astype(F32) - st_ref[:, 0:1]) * st_ref[:, 1:2]
            dn_ref[...] = (dh1 * ga[...] + dh2 * gf[...]).astype(BF)
            sums_ref[0:1, :] = jnp.sum(dh1 * xh, axis=0, keepdims=True)
            sums_ref[1:2, :] = jnp.sum(dh1, axis=0, keepdims=True)
            sums_ref[2:3, :] = jnp.sum(dh2 * xh, axis=0, keepdims=True)
            sums_ref[3:4, :] = jnp.sum(dh2, axis=0, keepdims=True)


def back_call(meta, dqkv, du, g1, g2, x2, st, ga, gf, sums, half):
    m, d = x2.shape
    nq = dqkv.shape[1]
    f = du.shape[1]
    n = d // 4

    def absolute(rows):
        return pl.BlockSpec((rows, 256), lambda j, mt: (0, mt[1 + 4 * half + j]))

    part = jax.ShapeDtypeStruct((m, n), BF)
    at = slice(3 * half, 3 * half + 3)
    return pl.pallas_call(
        back_kernel,
        name="backn",
        grid_spec=pltpu.PrefetchScalarGridSpec(
            num_scalar_prefetch=1,
            grid=(4,),
            in_specs=[
                pl.BlockSpec((m, nq), lambda j, mt: (0, 0)),
                pl.BlockSpec((m, f), lambda j, mt: (0, 0)),
                pl.BlockSpec((256, nq), lambda j, mt: (jnp.minimum(j, 1), 0)),
                pl.BlockSpec((256, nq), lambda j, mt: (0, 0)),
                pl.BlockSpec((256, nq), lambda j, mt: (0, 0)),
                pl.BlockSpec((256, f), lambda j, mt: (jnp.minimum(j, 1), 0)),
                pl.BlockSpec((256, f), lambda j, mt: (0, 0)),
                pl.BlockSpec((256, f), lambda j, mt: (0, 0)),
                absolute(m),
                pl.BlockSpec((m, 128), lambda j, mt: (0, 0)),
                absolute(1),
                absolute(1),
                pl.BlockSpec(memory_space=pl.ANY),
            ],
            out_specs=[
                pl.BlockSpec((m, n // 2), lambda j, mt: (0, jnp.minimum(j, 1))),
                pl.BlockSpec((m, n // 2), lambda j, mt: (0, jnp.maximum(j - 2, 0))),
                absolute(4),
            ],
        ),
        out_shape=[part, part, jax.ShapeDtypeStruct((4, d), F32)],
        input_output_aliases={13: 2},
        compiler_params=params(1),
        cost_estimate=cost(4 * m * n * (f + nq), 2 * (m * f + m * nq + 2 * n * (f + nq) + 4 * m * n)),
    )(meta, dqkv, du, *g1[at], *g2[at], x2, st, ga, gf, sums)


def wgrad_kernel(pairs, adds, split, meta, *refs):
    j = pl.program_id(0)
    start = 0
    for p, count in enumerate(pairs):
        a, b = refs[2 * p], refs[2 * p + 1]

        @pl.when((j >= start) & (j < start + count))
        def _():
            y = tn(a[...], b[...])
            if adds:
                y = y + refs[2 * len(pairs)][...].astype(F32)
            if not split:
                refs[-1][...] = y.astype(BF)
                return
            keep, send = refs[-2:]
            n = y.shape[0] // 4
            swap = meta[2 + NBLK] > 0
            keep[:n] = y[:n].astype(BF)
            keep[n:] = jnp.where(swap, y[2 * n : 3 * n], y[n : 2 * n]).astype(BF)
            send[:n] = jnp.where(swap, y[n : 2 * n], y[2 * n : 3 * n]).astype(BF)
            send[n:] = y[3 * n :].astype(BF)

        start += count


def wgrad_call(meta, *flat, half, add=None, split=False):
    pairs = list(zip(flat[::2], flat[1::2]))
    m, d = pairs[0][0].shape
    t = 512
    counts = tuple(b.shape[1] // t for _, b in pairs)
    total = sum(counts)
    in_specs, ops, start = [], [], 0
    for (a, b), c in zip(pairs, counts):
        in_specs.append(pl.BlockSpec((m, d // 2), lambda j, mt: (0, half)))
        in_specs.append(
            pl.BlockSpec((m, t), lambda j, mt, s=start, c=c: (0, jnp.clip(j - s, 0, c - 1)))
        )
        ops += [a, b]
        start += c
    rows = d // 4 if split else d // 2
    if add is not None:
        in_specs.append(pl.BlockSpec((d // 2, t), lambda j, mt: (0, j)))
        ops.append(add)
    out_spec = pl.BlockSpec((rows, t), lambda j, mt: (0, j))
    out_shape = jax.ShapeDtypeStruct((rows, total * t), BF)
    return pl.pallas_call(
        functools.partial(wgrad_kernel, counts, add is not None, split),
        name="wgrad",
        grid_spec=pltpu.PrefetchScalarGridSpec(
            num_scalar_prefetch=1,
            grid=(total,),
            in_specs=in_specs,
            out_specs=[out_spec, out_spec] if split else out_spec,
        ),
        out_shape=[out_shape, out_shape] if split else out_shape,
        compiler_params=params(1),
        cost_estimate=cost(m * d * total * t, 2 * (m * d // 2 * len(pairs) + m * total * t + d * total * t)),
    )(meta, *ops)


def pack_kernel(*refs):
    out, at = refs[-1], 0
    for ref in refs[:-1]:
        n = ref.shape[0]
        out[at : at + n] = ref[...]
        at += n


def pack_call(*pieces):
    rows = sum(p.shape[0] for p in pieces)
    cols = pieces[0].shape[1]
    t = 512
    return pl.pallas_call(
        pack_kernel,
        name="pack",
        grid=(cols // t,),
        in_specs=[pl.BlockSpec((p.shape[0], t), lambda j: (0, j)) for p in pieces],
        out_specs=pl.BlockSpec((rows, t), lambda j: (0, j)),
        out_shape=jax.ShapeDtypeStruct((rows, cols), BF),
        compiler_params=params(1),
        cost_estimate=cost(0, 4 * rows * cols),
    )(*pieces)


def half_sum_kernel(keep, got, mid, send):
    n = mid.shape[0]
    mid[...] = keep[:n].astype(F32) + got[:n].astype(F32)
    send[...] = (keep[n:].astype(F32) + got[n:].astype(F32)).astype(BF)


def half_sum_call(keep, got):
    rows, cols = keep.shape
    t = 512
    n = rows // 2
    small = pl.BlockSpec((n, t), lambda j: (0, j))
    return pl.pallas_call(
        half_sum_kernel,
        name="hsum",
        grid=(cols // t,),
        in_specs=[pl.BlockSpec((rows, t), lambda j: (0, j))] * 2,
        out_specs=[small] * 2,
        out_shape=[jax.ShapeDtypeStruct((n, cols), F32), jax.ShapeDtypeStruct((n, cols), BF)],
        compiler_params=params(1),
        cost_estimate=cost(4 * n * cols, 14 * n * cols),
    )(keep, got)


def last_sum_kernel(plan, mid, got, *outs):
    j = pl.program_id(0)
    at = 0
    for (count, turned), out in zip(plan, outs):

        @pl.when((j >= at) & (j < at + count))
        def _():
            v = mid[...] + got[...].astype(F32)
            out[...] = v.T if turned else v

        at += count


def last_sum_call(mid, got, plan):
    n, cols = mid.shape
    t = 512
    block = pl.BlockSpec((n, t), lambda j: (0, j))
    out_specs, out_shape, at = [], [], 0
    for count, turned in plan:
        def place(j, at=at, count=count):
            return jnp.clip(j - at, 0, count - 1)

        if turned:
            out_specs.append(pl.BlockSpec((t, n), lambda j, f=place: (f(j), 0)))
            out_shape.append(jax.ShapeDtypeStruct((count * t, n), F32))
        else:
            out_specs.append(pl.BlockSpec((n, t), lambda j, f=place: (0, f(j))))
            out_shape.append(jax.ShapeDtypeStruct((n, count * t), F32))
        at += count
    return pl.pallas_call(
        functools.partial(last_sum_kernel, plan),
        name="lsum",
        grid=(cols // t,),
        in_specs=[block, block],
        out_specs=out_specs,
        out_shape=out_shape,
        compiler_params=params(1),
        cost_estimate=cost(2 * n * cols, 10 * n * cols),
    )(mid, got)


def by_role(meta, refs, body):
    @pl.when(meta[1 + NBLK] > 0)
    def _():
        body(refs[0::2])

    @pl.when(meta[1 + NBLK] == 0)
    def _():
        body(refs[1::2])


def block_out_kernel(local_len, first, meta, x_ref, b_ref, *refs):
    y_ref = refs[-1]
    rows = x_ref.shape[0]
    mask = row_valid(meta, (first + pl.program_id(0)) * rows, rows, local_len)

    def body(parts):
        for r in range(NBLK):
            col = block_cols(meta[1 + r] * 256)
            s = parts[r // 2][:, r % 2 * 256 : r % 2 * 256 + 256].astype(F32)
            y_ref[:, col] = (mask * (x_ref[:, col].astype(F32) + s + b_ref[:, col])).astype(BF)

    by_role(meta, refs[:8], body)


def input_grad_kernel(local_len, first, meta, x_ref, g_ref, st_ref, *refs):
    y_ref = refs[-1]
    rows = x_ref.shape[0]
    mask = row_valid(meta, (first + pl.program_id(0)) * rows, rows, local_len)
    mean = st_ref[:, 0:1]
    inv = st_ref[:, 1:2]
    d = x_ref.shape[1]

    def body(parts):
        def dn_of(r):
            return parts[r // 2][:, r % 2 * 256 : r % 2 * 256 + 256].astype(F32)

        one = jnp.zeros((rows, 256), F32)
        two = jnp.zeros((rows, 256), F32)
        for r in range(NBLK):
            dn = dn_of(r)
            one += dn
            two += dn * (x_ref[:, block_cols(meta[1 + r] * 256)].astype(F32) - mean)
        one = jnp.sum(one, axis=1, keepdims=True) / d
        two = jnp.sum(two, axis=1, keepdims=True) * inv / d
        slope = inv * inv * two
        shift = slope * mean - inv * one
        for r in range(NBLK):
            col = block_cols(meta[1 + r] * 256)
            y = g_ref[:, col].astype(F32) * mask + inv * dn_of(r)
            y_ref[:, col] = (y + (shift - slope * x_ref[:, col].astype(F32))).astype(BF)

    by_role(meta, refs[:8], body)


def rows_call(meta, *ops, body, name, specs, steps=None, into=None):
    rows = 256
    m, d = ops[0].shape
    first, last = steps or (0, m // rows)
    made = {
        "row": pl.BlockSpec((rows, d), lambda i, mt: (first + i, 0)),
        "part": pl.BlockSpec((rows, d // 4), lambda i, mt: (first + i, 0)),
        "stat": pl.BlockSpec((rows, 128), lambda i, mt: (first + i, 0)),
        "vec": pl.BlockSpec((1, d), lambda i, mt: (0, 0)),
    }
    in_specs = [made[s] for s in specs]
    aliases = {}
    if into is not None:
        aliases = {1 + len(ops): 0}
        in_specs.append(pl.BlockSpec(memory_space=pl.ANY))
        ops += (into,)
    return pl.pallas_call(
        functools.partial(body, first),
        name=name,
        grid_spec=pltpu.PrefetchScalarGridSpec(
            num_scalar_prefetch=1,
            grid=(last - first,),
            in_specs=in_specs,
            out_specs=made["row"],
        ),
        out_shape=jax.ShapeDtypeStruct((m, d), BF),
        input_output_aliases=aliases,
        compiler_params=params(1),
        cost_estimate=cost(10 * (last - first) * rows * d, 8 * (last - first) * rows * d),
    )(meta, *ops)


def after(v, *others):
    return lax.optimization_barrier((v,) + others)[0]


class Order:
    def __init__(self):
        self.last = ()

    def __call__(self, f, first, *rest, **named):
        out = f(after(first, *self.last), *rest, **named)
        self.last = (jax.tree.leaves(out)[0],)
        return out


def add_bf(a, b):
    return lax.optimization_barrier((a.astype(F32) + b.astype(F32)).astype(BF))


def pick_bf(a, b, middle, other):
    total = (a.astype(F32) + b.astype(F32)).astype(BF)
    return lax.optimization_barrier(jnp.where(middle > 0, total, other))


class Pipe:
    LAG = 3

    def __init__(self, run, middle, count):
        self.run, self.middle, self.count = run, middle, count
        self.parts, self.got, self.sums, self.crossed = [], [], [], []
        self.here, self.sent = [], []

    def send(self, part=None):
        step = len(self.got)
        back = step - self.LAG
        pairs = []
        v = part
        if part is not None:
            self.parts.append(part)
            pairs += [(0, 1), (3, 2)]
        if back >= 0:
            pairs += [(1, 0), (2, 3)]
            a, b = self.sums[back], self.crossed[back]
            if part is None:
                v = self.run(add_bf, a, b)
            else:
                v = self.run(pick_bf, a, b, self.middle, part)
        got = lax.ppermute(v, "tensor", pairs)
        self.got.append(got)
        if back >= 0:
            self.here.append(v)
            self.sent.append(got)

    def cross(self):
        k = len(self.sums)
        v = self.run(add_bf, self.parts[k], self.got[k])
        self.sums.append(v)
        self.crossed.append(lax.ppermute(v, "tensor", [(1, 2), (2, 1)]))


class PlainPipe:
    def __init__(self, run, middle, count):
        self.here, self.sent, self.sums = [], [], []

    def send(self, part=None):
        if part is not None:
            total = lax.psum(part, "tensor")
            self.here.append(total)
            self.sent.append(total)

    def cross(self):
        pass


class SmallMesh:
    def x(self, v):
        return lax.ppermute(v, "dp", [(0, 2), (2, 0), (1, 3), (3, 1)])

    def core(self, v):
        return lax.ppermute(v, "dp", [(0, 1), (1, 0), (2, 3), (3, 2)])

    def y(self, v):
        return lax.ppermute(v, "ctx", [(0, 1), (1, 0)])

    def perm(self):
        r = jnp.arange(NBLK, dtype=jnp.int32)
        dp = lax.axis_index("dp") ^ (((r >> 1) & 1) * 2 + (r >> 2))
        return dp * 2 + (lax.axis_index("ctx") ^ (r & 1))

    def middle(self):
        z = lax.axis_index("tensor")
        return ((z == 1) | (z == 2)).astype(jnp.int32)

    pipe = Pipe

    def first_hop(self, own, earlier=None):
        if earlier is None:
            return self.x(own), self.y(own)
        return self.x(after(own, earlier)), self.y(own)

    def second_hop(self, hop, earlier=()):
        return self.x(after(hop[1], hop[0], *earlier))

    def waited(self, hop):
        return hop

    def near_pieces(self, near):
        return near

    def near(self, run, own, hop):
        v = run(pack_call, own, hop[1])
        return v, self.core(v)

    def pieces(self, near, hop, diag, earlier=()):
        return near[0], hop[0], diag, near[1], self.core(after(hop[0], *earlier[:1])), self.core(after(diag, *earlier))

    def turn(self, v, first):
        pairs = []
        for dp in range(4):
            for c in range(2):
                to = (dp ^ 2) * 2 + c if dp % 2 != first else dp * 2 + (c ^ 1)
                pairs.append((dp * 2 + c, to))
        return lax.ppermute(v, ("dp", "ctx"), pairs)

    def scatter_cross(self, theirs):
        return self.core(theirs)

    def scatter_own(self, run, meta, pairs, got):
        keep, send = run(wgrad_call, meta, *pairs, half=0, add=got, split=True)
        return keep, self.turn(send, 1)

    def scatter_half(self, run, parts):
        mid, send = run(half_sum_call, *parts)
        return mid, self.turn(send, 0)

    def scatter_last(self, run, plan, parts):
        return run(last_sum_call, *parts, plan=plan)

    def previous(self, kv, slots):
        return lax.ppermute(kv, "ctx", [(0, 1)])

    def give_back(self, dpv, dkv, slots):
        return dkv, lax.ppermute(dpv, "ctx", [(1, 0)])

    def small_sum(self, run, v, step):
        def add(a, b):
            return a + b

        if step == 0:
            got = self.core(v)
        elif step == 1:
            got = self.x(v)
        elif step == 2:
            got = self.y(v)
        elif step == 3:
            got = lax.ppermute(v, "tensor", [(0, 1), (1, 0), (2, 3), (3, 2)])
        else:
            got = lax.ppermute(v, "tensor", [(0, 2), (2, 0), (1, 3), (3, 1)])
        return lambda: run(add, v, got)


class AnyMesh:
    def perm(self):
        return jnp.arange(NBLK, dtype=jnp.int32)

    def middle(self):
        return jnp.ones((), jnp.int32)

    pipe = PlainPipe

    def first_hop(self, own, earlier=None):
        return lax.all_gather(own, ("dp", "ctx"), axis=0, tiled=True)

    def second_hop(self, hop, earlier=()):
        return ()

    def waited(self, hop):
        return (hop,)

    def near_pieces(self, near):
        return near

    def near(self, run, own, hop):
        return hop[:512], hop[1024:1536]

    def pieces(self, near, hop, diag, earlier=()):
        return near[0], hop[512:768], hop[768:1024], near[1], hop[1536:1792], hop[1792:]

    def scatter_cross(self, theirs):
        return theirs

    def scatter_own(self, run, meta, pairs, got):
        full = jnp.concatenate([run(wgrad_call, meta, *pairs, half=0), got], axis=0)
        return lax.psum_scatter(full, ("dp", "ctx"), scatter_dimension=0, tiled=True).astype(F32)

    def scatter_half(self, run, parts):
        return parts

    def scatter_last(self, run, plan, parts):
        outs, at = [], 0
        for count, turned in plan:
            v = parts[:, at * 512 : (at + count) * 512]
            outs.append(v.T if turned else v)
            at += count
        return outs

    def previous(self, kv, slots):
        own = kv.reshape(slots, -1, kv.shape[1])
        full = lax.all_gather(own, "ctx", axis=1, tiled=True)
        return full.reshape(-1, kv.shape[1])

    def give_back(self, dpv, dkv, slots):
        cols = dkv.shape[1]
        full = dpv.reshape(slots, -1, cols)
        got = lax.psum_scatter(full, "ctx", scatter_dimension=1, tiled=True)
        return dkv, got.reshape(-1, cols)

    def small_sum(self, run, v, step):
        got = v
        if step == 0:
            got = lax.psum(v, ("dp", "ctx"))
        elif step == 3:
            got = lax.psum(v, "tensor")
        return lambda: got


def rotary_tables(positions):
    half_rot = ROT // 2
    lane = jnp.arange(128, dtype=jnp.int32)
    exponent = (lane % half_rot).astype(F32) * (2.0 / ROT)
    angles = positions[:, None] * jnp.exp(-math.log(10000.0) * exponent)[None, :]
    cos_all, sin_all = jnp.cos(angles), jnp.sin(angles)
    cosf = jnp.where(lane < ROT, cos_all, 1.0)
    s1 = jnp.where(lane < half_rot, -sin_all, 0.0)
    s2 = jnp.where((lane >= half_rot) & (lane < ROT), sin_all, 0.0)
    return cosf, s1, s2


def local(small, block_input, out_grad, lengths, attn_gain, attn_shift, ffn_gain, ffn_shift, w_qkv, b_qkv, w_proj, b_proj, w_in, b_in, w_out, b_out):
    comm = SmallMesh() if small else AnyMesh()
    slots, local_len, d = block_input.shape
    m = slots * local_len
    nheads = b_qkv.shape[0] // (3 * HD)
    nq = 3 * nheads * HD
    ctx = lax.axis_index("ctx")
    core = lax.axis_index("dp") % 2
    meta = jnp.concatenate(
        [ctx[None].astype(jnp.int32), comm.perm(), comm.middle()[None], core[None].astype(jnp.int32), lengths]
    )

    run = Order()
    x2 = block_input.reshape(m, d)
    og2 = out_grad.reshape(m, d)
    ga, sa, gf, sf = (v.reshape(1, d) for v in (attn_gain, attn_shift, ffn_gain, ffn_shift))
    bq = b_qkv.reshape(1, nq)
    positions = ctx * local_len + jnp.arange(local_len, dtype=jnp.int32)
    tabs = rotary_tables(positions.astype(F32))

    own1 = jnp.concatenate([w_qkv, w_proj.T], axis=1).astype(BF)
    hop1 = comm.first_hop(own1)
    own2 = w_in.astype(BF)
    own3 = w_out.T.astype(BF)
    run.last = (own1, own2, own3)
    hop2 = comm.first_hop(own2, hop1[0])
    h1, g, stats, g_sum = run(norm_call, meta, x2, og2, ga, sa, local_len)
    diag1 = comm.second_hop(hop1)
    near1 = comm.near(run, own1, hop1)
    g1 = comm.pieces(near1, hop1, diag1)
    near2 = comm.near(run, own2, hop2)
    kv = run(kv_call, h1, g1, bq, tabs, nheads)
    pv = comm.previous(kv, slots)
    diag2 = comm.second_hop(hop2, (kv,))
    hop3 = comm.first_hop(own3, diag2)
    q, dob = run(qd_call, h1, g, g1, bq, tabs, nheads)
    g2 = comm.pieces(near2, hop2, diag2, (kv, q))
    diag3 = comm.second_hop(hop3)
    h2 = run(second_norm_call, meta, x2, stats, gf, sf)
    gb, dg = run(hidden_call, h2, g2, b_in.reshape(1, -1))
    near3 = comm.near(run, own3, hop3)
    ob, dq, dkv, dpv = run(attn_call, meta, q, kv, pv, dob, tabs, nheads)
    dkv, rv = comm.give_back(dpv, dkv, slots)
    g3 = comm.near_pieces(near3)

    pipe = comm.pipe(run, meta[1 + NBLK], 8)
    ff = gb.shape[1] // 512
    out0, out2 = run(out_call, ob, gb, (g1[0], g1[3]), g3, 0.01)
    pipe.send(out0)
    pipe.send(out2)
    g3 = comm.pieces(near3, hop3, diag3, (ob, out0))
    cross3 = comm.scatter_cross(run(wgrad_call, meta, g, gb, half=1))
    far = (1, 2, 4, 5)
    out1, out3 = run(out_call, ob, gb, [g1[k] for k in far], [g3[k] for k in far])
    du, bin_sum = run(dhid_call, g, g3, dg)
    pipe.cross()
    pipe.send(after(out1, *pipe.sums))
    state3 = comm.scatter_own(run, meta, (g, gb), cross3)
    pipe.cross()
    dqkv, bqkv_sum = run(join_call, dq, dkv, rv, tabs, nheads)
    pipe.send(out3)
    gain_sums = jnp.zeros((4, d), F32)
    pipe.cross()
    dn0, dn1, gain_sums = run(back_call, meta, dqkv, du, g1, g2, x2, stats, ga, gf, gain_sums, 0)
    pipe.send(dn0)
    pipe.cross()
    pipe.send(dn1)
    state3 = comm.scatter_half(run, state3)
    dn2, dn3, gain_sums = run(back_call, meta, dqkv, du, g1, g2, x2, stats, ga, gf, gain_sums, 1)
    pipe.cross()
    pipe.send(dn2)
    cross2 = comm.scatter_cross(run(wgrad_call, after(meta, jax.tree.leaves(state3)[-1]), h2, du, half=1))
    theirs1 = run(wgrad_call, meta, h1, dqkv, g, ob, half=1)
    pipe.cross()
    pipe.send(dn3)
    state2 = comm.scatter_own(run, meta, (h2, du), cross2)
    (grad_out,) = comm.scatter_last(run, ((ff, True),), state3)
    small = jnp.concatenate([gain_sums.reshape(-1), g_sum.reshape(-1), bqkv_sum.reshape(-1), bin_sum.reshape(-1)])
    add = comm.small_sum(run, after(small, grad_out), 0)
    pipe.cross()
    pipe.send()
    cross1 = comm.scatter_cross(after(theirs1, pipe.here[-1]))
    state2 = comm.scatter_half(run, state2)
    small = add()
    add = comm.small_sum(run, small, 1)

    def sums_of(order):
        return [v for c in order for v in (pipe.here[c], pipe.sent[c])]

    out_ops = (meta, x2, (b_proj + b_out).reshape(1, d), *sums_of((0, 2, 1, 3)))
    out_half = functools.partial(
        rows_call, body=functools.partial(block_out_kernel, local_len), name="bout", specs=("row", "vec") + ("part",) * 8
    )
    block_output = run(out_half, *out_ops, steps=(0, 2))
    small = add()
    pipe.cross()
    pipe.send()
    (grad_in,) = comm.scatter_last(run, ((ff, False),), state2)
    add = comm.small_sum(run, after(small, grad_in), 2)
    state1 = comm.scatter_own(run, meta, (h1, dqkv, g, ob), cross1)
    block_output = run(out_half, *out_ops, steps=(2, 4), into=block_output).reshape(slots, local_len, d)
    small = add()
    gains = small[: 4 * d]
    group = small[4 * d :]
    pipe.send()
    state1 = comm.scatter_half(run, after(state1, pipe.sent[5]))
    add = comm.small_sum(run, after(gains, *jax.tree.leaves(state1)[:1]), 3)
    input_grad = run(
        rows_call, meta, x2, og2, stats, *sums_of(range(4, 8)),
        body=functools.partial(input_grad_kernel, local_len), name="igrad", specs=("row", "row", "stat") + ("part",) * 8,
    ).reshape(slots, local_len, d)
    gains = add()
    add = comm.small_sum(run, gains, 4)
    grad_qkv, grad_proj = comm.scatter_last(run, ((nq // 512, False), (nheads * HD // 512, True)), state1)
    gains = add().reshape(4, d)
    bias_grad = group[:d]
    return (
        block_output,
        input_grad,
        gains[0],
        gains[1],
        gains[2],
        gains[3],
        grad_qkv,
        group[d : d + nq],
        grad_proj,
        bias_grad,
        grad_in,
        group[d + nq :],
        grad_out,
        bias_grad,
    )


def solution(mesh):
    small = mesh.shape["dp"] == 4 and mesh.shape["ctx"] == 2 and mesh.shape["tensor"] == 4
    placed = (
        P("dp", "ctx", None),
        P("dp", "ctx", None),
        P("dp"),
        P(),
        P(),
        P(),
        P(),
        P(("dp", "ctx"), "tensor"),
        P("tensor"),
        P("tensor", ("dp", "ctx")),
        P(),
        P(("dp", "ctx"), "tensor"),
        P("tensor"),
        P("tensor", ("dp", "ctx")),
        P(),
    )
    return jax.shard_map(
        functools.partial(local, small),
        mesh=mesh,
        in_specs=placed,
        out_specs=(
            P("dp", "ctx", None),
            P("dp", "ctx", None),
            P(),
            P(),
            P(),
            P(),
            P(("dp", "ctx"), "tensor"),
            P("tensor"),
            P("tensor", ("dp", "ctx")),
            P(),
            P(("dp", "ctx"), "tensor"),
            P("tensor"),
            P("tensor", ("dp", "ctx")),
            P(),
        ),
        check_vma=False,
    )
```

```python
import functools
import math

import jax
import jax.numpy as jnp
from jax import lax
from jax.experimental import pallas as pl
from jax.experimental.pallas import tpu as pltpu
from jax.sharding import PartitionSpec as P

HD = 256
ROT = 64
NBLK = 8
BF = jnp.bfloat16
F32 = jnp.float32

neg_big = -1e30
inv_sqrt_two = 0.7071067811865476
inv_sqrt_tau = 0.3989422804014327


COST_SCALE = 100


def cost(flops, nbytes, trans=0, k=COST_SCALE):
    flops = max(flops, 300 * nbytes)
    return pl.CostEstimate(flops=int(k * flops), bytes_accessed=int(k * nbytes), transcendentals=int(k * trans))


def params(n, mb=60):
    return pltpu.CompilerParams(
        dimension_semantics=("arbitrary",) * n, vmem_limit_bytes=int(mb * 1024 * 1024)
    )


def nn(a, b):
    return lax.dot_general(a, b, (((1,), (0,)), ((), ())), preferred_element_type=F32)


def nn_rows(a, pieces):
    total, at = None, 0
    for w in pieces:
        y = nn(a[:, at : at + w.shape[0]], w[...])
        total = y if total is None else total + y
        at += w.shape[0]
    return total


def nt(a, b):
    return lax.dot_general(a, b, (((1,), (1,)), ((), ())), preferred_element_type=F32)


def tn(a, b):
    return lax.dot_general(a, b, (((0,), (0,)), ((), ())), preferred_element_type=F32)


def block_cols(r):
    return pl.ds(pl.multiple_of(r, 128), 256)


def row_valid(meta, row0, rows, local_len):
    slot = row0 // local_len
    pos = meta[0] * local_len + row0 % local_len + lax.broadcasted_iota(jnp.int32, (rows, 1), 0)
    return (pos < meta[3 + NBLK + slot]).astype(F32)


def norm_kernel(local_len, meta, x_ref, g_ref, ga, sa, h1_ref, g_out, st_ref, gs_ref):
    rows = x_ref.shape[0]
    i = pl.program_id(0)
    x = x_ref[...].astype(F32)
    mean = jnp.mean(x, axis=-1, keepdims=True)
    cen = x - mean
    inv = lax.rsqrt(jnp.mean(cen * cen, axis=-1, keepdims=True) + 1e-05)
    mask = row_valid(meta, i * rows, rows, local_len)
    lane = lax.broadcasted_iota(jnp.int32, (rows, 128), 1)
    st_ref[...] = jnp.where(lane == 0, mean, inv)
    for r in range(NBLK):
        src = block_cols(meta[1 + r] * 256)
        dst = slice(r * 256, (r + 1) * 256)
        xh = (x_ref[:, src].astype(F32) - mean) * inv
        h1_ref[:, dst] = (xh * ga[:, src] + sa[:, src]).astype(BF)
        gm = g_ref[:, src].astype(F32) * mask
        g_out[:, dst] = gm.astype(BF)
        part = jnp.sum(gm, axis=0, keepdims=True)

        @pl.when(i == 0)
        def _():
            gs_ref[:, src] = part

        @pl.when(i > 0)
        def _():
            gs_ref[:, src] = gs_ref[:, src] + part


def second_norm_kernel(meta, x_ref, st_ref, gf, sf, h2_ref):
    for r in range(NBLK):
        src = block_cols(meta[1 + r] * 256)
        xh = (x_ref[:, src].astype(F32) - st_ref[:, 0:1]) * st_ref[:, 1:2]
        h2_ref[:, r * 256 : (r + 1) * 256] = (xh * gf[:, src] + sf[:, src]).astype(BF)


def second_norm_call(meta, x2, st, gf, sf):
    m, d = x2.shape
    rows = 256
    row_spec = pl.BlockSpec((rows, d), lambda i, mt: (i, 0))
    vec = pl.BlockSpec((1, d), lambda i, mt: (0, 0))
    return pl.pallas_call(
        second_norm_kernel,
        name="norm2",
        grid_spec=pltpu.PrefetchScalarGridSpec(
            num_scalar_prefetch=1,
            grid=(m // rows,),
            in_specs=[row_spec, pl.BlockSpec((rows, 128), lambda i, mt: (i, 0)), vec, vec],
            out_specs=row_spec,
        ),
        out_shape=jax.ShapeDtypeStruct((m, d), BF),
        compiler_params=params(1),
        cost_estimate=cost(5 * m * d, 4 * m * d),
    )(meta, x2, st, gf, sf)


def norm_call(meta, x2, g2, ga, sa, local_len):
    m, d = x2.shape
    rows = 256
    row_spec = pl.BlockSpec((rows, d), lambda i, mt: (i, 0))
    vec = pl.BlockSpec((1, d), lambda i, mt: (0, 0))
    return pl.pallas_call(
        functools.partial(norm_kernel, local_len),
        name="norm",
        grid_spec=pltpu.PrefetchScalarGridSpec(
            num_scalar_prefetch=1,
            grid=(m // rows,),
            in_specs=[row_spec, row_spec, vec, vec],
            out_specs=[row_spec, row_spec, pl.BlockSpec((rows, 128), lambda i, mt: (i, 0)), vec],
        ),
        out_shape=[jax.ShapeDtypeStruct((m, d), BF)] * 2
        + [jax.ShapeDtypeStruct((m, 128), F32), jax.ShapeDtypeStruct((1, d), F32)],
        compiler_params=params(1),
        cost_estimate=cost(20 * m * d, 10 * m * d),
    )(meta, x2, g2, ga, sa)


def rotate_tile(y, cosf, s1, s2, sign):
    head = y[:, :128]
    rot = (
        head * cosf
        + pltpu.roll(head, 96, 1) * (s1 * sign)
        + pltpu.roll(head, 32, 1) * (s2 * sign)
    )
    return rot, y[:, 128:]


def rotated(out, y, cosf, s1, s2):
    local_len = cosf.shape[0]
    for s in range(y.shape[0] // local_len):
        rows = slice(s * local_len, (s + 1) * local_len)
        rot, rest = rotate_tile(y[rows], cosf[...], s1[...], s2[...], 1.0)
        out[rows, :128] = rot.astype(BF)
        out[rows, 128:] = rest.astype(BF)


def kv_kernel(h1, w0, w1, w2, w3, w4, w5, b_ref, cosf, s1, s2, kv_ref):
    part = lax.rem(pl.program_id(0), 2)
    y = nn_rows(h1, (w0, w1, w2, w3, w4, w5)) + b_ref[...]

    @pl.when(part == 0)
    def _():
        rotated(kv_ref, y, cosf, s1, s2)

    @pl.when(part == 1)
    def _():
        kv_ref[...] = y.astype(BF)


def kv_call(h1, pieces, b_qkv, tabs, nheads):
    m, d = h1.shape
    local_len = tabs[0].shape[0]

    def src(j):
        return (0, (j // 2) * 3 + 1 + j % 2)

    tab = pl.BlockSpec((local_len, 128), lambda j: (0, 0))
    return pl.pallas_call(
        kv_kernel,
        name="kv",
        grid=(2 * nheads,),
        in_specs=[
            pl.BlockSpec((m, d), lambda j: (0, 0)),
            *[pl.BlockSpec((p.shape[0], HD), src) for p in pieces],
            pl.BlockSpec((1, HD), src),
            tab,
            tab,
            tab,
        ],
        out_specs=pl.BlockSpec((m, HD), lambda j: (0, j)),
        out_shape=jax.ShapeDtypeStruct((m, 2 * nheads * HD), BF),
        compiler_params=params(1),
        cost_estimate=cost(4 * m * d * nheads * HD, 2 * (m * d + 2 * d * nheads * HD + 2 * m * nheads * HD)),
    )(h1, *pieces, b_qkv, *tabs)


def qd_kernel(nheads, h1, g, w0, w1, w2, w3, w4, w5, b_ref, cosf, s1, s2, q_ref, dob_ref):
    j = pl.program_id(0)
    pieces = (w0, w1, w2, w3, w4, w5)

    @pl.when(j < nheads)
    def _():
        rotated(q_ref, nn_rows(h1, pieces) + b_ref[...], cosf, s1, s2)

    @pl.when(j >= nheads)
    def _():
        dob_ref[...] = nn_rows(g, pieces).astype(BF)


def qd_call(h1, g, pieces, b_qkv, tabs, nheads):
    m, d = h1.shape
    local_len = tabs[0].shape[0]
    full = pl.BlockSpec((m, d), lambda j: (0, 0))

    def src(j):
        return (0, jnp.where(j < nheads, 3 * j, 2 * nheads + j))

    tab = pl.BlockSpec((local_len, 128), lambda j: (0, 0))
    return pl.pallas_call(
        functools.partial(qd_kernel, nheads),
        name="qd",
        grid=(2 * nheads,),
        in_specs=[
            full,
            full,
            *[pl.BlockSpec((p.shape[0], HD), src) for p in pieces],
            pl.BlockSpec((1, HD), lambda j: (0, 3 * jnp.minimum(j, nheads - 1))),
            tab,
            tab,
            tab,
        ],
        out_specs=[
            pl.BlockSpec((m, HD), lambda j: (0, jnp.minimum(j, nheads - 1))),
            pl.BlockSpec((m, HD), lambda j: (0, jnp.maximum(j - nheads, 0))),
        ],
        out_shape=[jax.ShapeDtypeStruct((m, nheads * HD), BF)] * 2,
        compiler_params=params(1),
        cost_estimate=cost(4 * m * d * nheads * HD, 2 * (2 * m * d + 2 * d * nheads * HD + 2 * m * nheads * HD)),
    )(h1, g, *pieces, b_qkv, *tabs)


def attn_kernel(nprev, local_len, meta, q_ref, kv_ref, pv_ref, dob_ref, cosf, s1, s2, ob_ref, dq_ref, dkv_ref, dpv_ref, sc_ref, dq_acc):
    slot = pl.program_id(0)
    ctx = meta[0]
    length = meta[3 + NBLK + slot]
    scale = 1.0 / math.sqrt(HD)
    n_vis = jnp.minimum(ctx, (length + local_len - 1) // local_len)
    q = q_ref[...]
    dob = dob_ref[...]
    own_k = kv_ref[:, :HD]
    own_v = kv_ref[:, HD:]

    ri = lax.broadcasted_iota(jnp.int32, (local_len, local_len), 0)
    ci = lax.broadcasted_iota(jnp.int32, (local_len, local_len), 1)
    s_own = nt(q, own_k) * scale
    s_own = jnp.where((ci <= ri) & (ci < length - ctx * local_len), s_own, neg_big)
    sc_ref[nprev] = s_own

    def prev_rows(jb):
        return pl.ds(pl.multiple_of(jb * local_len, local_len), local_len)

    def score(jb, top):
        s = nt(q, pv_ref[prev_rows(jb), :HD]) * scale
        s = jnp.where(ci[:1] < length - jb * local_len, s, neg_big)
        sc_ref[jb] = s
        return jnp.maximum(top, jnp.max(s, axis=1, keepdims=True))

    top = lax.fori_loop(0, n_vis, score, jnp.max(s_own, axis=1, keepdims=True))

    e_own = jnp.exp(sc_ref[nprev] - top)
    sc_ref[nprev] = e_own

    def expo(jb, tot):
        e = jnp.exp(sc_ref[jb] - top)
        sc_ref[jb] = e
        return tot + jnp.sum(e, axis=1, keepdims=True)

    tot = lax.fori_loop(0, n_vis, expo, jnp.sum(e_own, axis=1, keepdims=True))
    inv = 1.0 / tot
    att = nn((sc_ref[nprev] * inv).astype(BF), own_v)

    def out_step(jb, acc):
        return acc + nn((sc_ref[jb] * inv).astype(BF), pv_ref[prev_rows(jb), HD:])

    att = lax.fori_loop(0, n_vis, out_step, att)
    ob_ref[...] = att.astype(BF)
    delta = jnp.sum(dob.astype(F32) * att, axis=1, keepdims=True)

    def back(p, k, v):
        pb = p.astype(BF)
        ds = (p * (nt(dob, v) - delta)).astype(BF)
        return nn(ds, k) * scale, tn(ds, q) * scale, tn(pb, dob)

    dq, dk, dv = back(sc_ref[nprev] * inv, own_k, own_v)
    dq_acc[...] = dq
    dkv_ref[:, :HD] = dk
    dkv_ref[:, HD:] = dv

    def back_step(jb, carry):
        rows = prev_rows(jb)
        dqp, dkp, dvp = back(sc_ref[jb] * inv, pv_ref[rows, :HD], pv_ref[rows, HD:])
        dq_acc[...] += dqp
        dpv_ref[rows, :HD] = dkp.astype(BF)
        dpv_ref[rows, HD:] = dvp.astype(BF)
        return carry

    lax.fori_loop(0, n_vis, back_step, 0)

    def clear(jb, carry):
        dpv_ref[prev_rows(jb), :] = jnp.zeros((local_len, 2 * HD), BF)
        return carry

    lax.fori_loop(n_vis, nprev, clear, 0)
    rot, rest = rotate_tile(dq_acc[...], cosf[...], s1[...], s2[...], -1.0)
    dq_ref[:, :128] = rot.astype(BF)
    dq_ref[:, 128:] = rest.astype(BF)


def attn_call(meta, q, kv, pv, dob, tabs, nheads):
    local_len = tabs[0].shape[0]
    slots = q.shape[0] // local_len
    nprev = pv.shape[0] // q.shape[0]
    one = pl.BlockSpec((local_len, HD), lambda s, h, mt: (s, h))
    two = pl.BlockSpec((local_len, 2 * HD), lambda s, h, mt: (s, h))
    prev = pl.BlockSpec((nprev * local_len, 2 * HD), lambda s, h, mt: (s, h))
    tab = pl.BlockSpec((local_len, 128), lambda s, h, mt: (0, 0))
    m = q.shape[0]
    return pl.pallas_call(
        functools.partial(attn_kernel, nprev, local_len),
        name="attn",
        grid_spec=pltpu.PrefetchScalarGridSpec(
            num_scalar_prefetch=1,
            grid=(slots, nheads),
            in_specs=[one, two, prev, one, tab, tab, tab],
            out_specs=[one, one, two, prev],
            scratch_shapes=[
                pltpu.VMEM((nprev + 1, local_len, local_len), F32),
                pltpu.VMEM((local_len, HD), F32),
            ],
        ),
        out_shape=[
            jax.ShapeDtypeStruct((m, nheads * HD), BF),
            jax.ShapeDtypeStruct((m, nheads * HD), BF),
            jax.ShapeDtypeStruct((m, 2 * nheads * HD), F32),
            jax.ShapeDtypeStruct((nprev * m, 2 * nheads * HD), BF),
        ],
        compiler_params=params(2),
        cost_estimate=cost(12 * m * nheads * HD * (nprev + 1) * local_len, 20 * m * nheads * HD, m * nheads * (nprev + 1) * local_len),
    )(meta, q, kv, pv, dob, *tabs)


def join_kernel(nheads, dq_ref, dkv_ref, rv_ref, cosf, s1, s2, out_ref, sum_ref):
    i = pl.program_id(0)

    @pl.when(i == 0)
    def _():
        sum_ref[...] = jnp.zeros_like(sum_ref)

    for h in range(nheads):
        base = h * 3 * HD
        out_ref[:, base : base + HD] = dq_ref[:, h * HD : (h + 1) * HD]
        kc = slice(h * 2 * HD, h * 2 * HD + HD)
        vc = slice(h * 2 * HD + HD, (h + 1) * 2 * HD)
        dk = dkv_ref[:, kc] + rv_ref[:, kc].astype(F32)
        rot, rest = rotate_tile(dk, cosf[...], s1[...], s2[...], -1.0)
        out_ref[:, base + HD : base + HD + 128] = rot.astype(BF)
        out_ref[:, base + HD + 128 : base + 2 * HD] = rest.astype(BF)
        out_ref[:, base + 2 * HD : base + 3 * HD] = (dkv_ref[:, vc] + rv_ref[:, vc].astype(F32)).astype(BF)
    sum_ref[...] += jnp.sum(out_ref[...].astype(F32), axis=0, keepdims=True)


def join_call(dq, dkv, rv, tabs, nheads):
    m = dq.shape[0]
    local_len = tabs[0].shape[0]
    rows = 256
    per = local_len // rows

    def spec(c):
        return pl.BlockSpec((rows, c), lambda i: (i, 0))

    tab = pl.BlockSpec((rows, 128), lambda i: (i % per, 0))
    n = 3 * nheads * HD
    return pl.pallas_call(
        functools.partial(join_kernel, nheads),
        name="join",
        grid=(m // rows,),
        in_specs=[spec(nheads * HD), spec(2 * nheads * HD), spec(2 * nheads * HD), tab, tab, tab],
        out_specs=[spec(n), pl.BlockSpec((1, n), lambda i: (0, 0))],
        out_shape=[jax.ShapeDtypeStruct((m, n), BF), jax.ShapeDtypeStruct((1, n), F32)],
        compiler_params=params(1),
        cost_estimate=cost(10 * m * n, 8 * m * n),
    )(dq, dkv, rv, *tabs)


def hidden_kernel(h2, w0, w1, w2, w3, w4, w5, b_ref, gb_ref, dg_ref):
    u = nn_rows(h2, (w0, w1, w2, w3, w4, w5)) + b_ref[...]
    cdf = 0.5 * (1.0 + lax.erf(u * inv_sqrt_two))
    gb_ref[...] = (u * cdf).astype(BF)
    dg_ref[...] = (cdf + u * (jnp.exp(-0.5 * u * u) * inv_sqrt_tau)).astype(BF)


def hidden_call(h2, pieces, b_in):
    m, d = h2.shape
    f = pieces[0].shape[1]
    t = 256
    col = pl.BlockSpec((m, t), lambda j: (0, j))
    w_specs = [pl.BlockSpec((p.shape[0], t), lambda j: (0, j)) for p in pieces]
    return pl.pallas_call(
        hidden_kernel,
        name="hidden",
        grid=(f // t,),
        in_specs=[pl.BlockSpec((m, d), lambda j: (0, 0)), *w_specs, pl.BlockSpec((1, t), lambda j: (0, j))],
        out_specs=[col, col],
        out_shape=[jax.ShapeDtypeStruct((m, f), BF)] * 2,
        compiler_params=params(1),
        cost_estimate=cost(2 * m * d * f, 2 * (m * d + d * f + 2 * m * f), 2 * m * f),
    )(h2, *pieces, b_in)


def dhid_kernel(g, w0, w1, w2, w3, w4, w5, dg_ref, du_ref, sum_ref):
    a = nn_rows(g, (w0, w1, w2, w3, w4, w5))
    du = (a * dg_ref[...].astype(F32)).astype(BF)
    du_ref[...] = du
    sum_ref[...] = jnp.sum(du.astype(F32), axis=0, keepdims=True)


def dhid_call(g, pieces, dg):
    m, d = g.shape
    f = dg.shape[1]
    t = 256
    col = pl.BlockSpec((m, t), lambda j: (0, j))
    w_specs = [pl.BlockSpec((p.shape[0], t), lambda j: (0, j)) for p in pieces]
    return pl.pallas_call(
        dhid_kernel,
        name="dhid",
        grid=(f // t,),
        in_specs=[pl.BlockSpec((m, d), lambda j: (0, 0))] + w_specs + [col],
        out_specs=[col, pl.BlockSpec((1, t), lambda j: (0, j))],
        out_shape=[jax.ShapeDtypeStruct((m, f), BF), jax.ShapeDtypeStruct((1, f), F32)],
        compiler_params=params(1),
        cost_estimate=cost(2 * m * d * f, 2 * (m * d + d * f + 2 * m * f)),
    )(g, *pieces, dg)


def out_kernel(count, ob, gb, *refs):
    j = pl.program_id(0)
    ps, os, ya, yb = refs[:count], refs[count : 2 * count], refs[-2], refs[-1]
    each = 4 // count
    for k in range(4):

        @pl.when(j == k)
        def _():
            y = ya if k < 2 else yb
            y[...] = (nt(ob[...], ps[k // each][...]) + nt(gb[...], os[k // each][...])).astype(BF)


def piece_spec(count, i, cols, at=0, prefetch=False):
    each = 4 // count

    def place(j, *_):
        return (jnp.clip(j - i * each, 0, each - 1), at)

    if prefetch:
        return pl.BlockSpec((256, cols), lambda j, mt: place(j))
    return pl.BlockSpec((256, cols), lambda j: place(j))


def out_call(ob, gb, proj, out, scale=COST_SCALE):
    m, f = gb.shape
    nf = ob.shape[1]
    count = len(out)
    last = proj[0].shape[1] // nf - 1
    part = jax.ShapeDtypeStruct((m, 512), BF)
    return pl.pallas_call(
        functools.partial(out_kernel, count),
        name="outp",
        grid=(4,),
        in_specs=[pl.BlockSpec((m, nf), lambda j: (0, 0)), pl.BlockSpec((m, f), lambda j: (0, 0))]
        + [piece_spec(count, i, nf, last) for i in range(count)]
        + [piece_spec(count, i, f) for i in range(count)],
        out_specs=[
            pl.BlockSpec((m, 256), lambda j: (0, jnp.minimum(j, 1))),
            pl.BlockSpec((m, 256), lambda j: (0, jnp.maximum(j - 2, 0))),
        ],
        out_shape=[part, part],
        compiler_params=params(1),
        cost_estimate=cost(2048 * m * (f + nf), 2 * (m * f + m * nf + 1024 * (f + nf) + 1024 * m), k=scale),
    )(ob, gb, *proj, *out)


def back_kernel(meta, dqkv, du, w10, w11, w12, w20, w21, w22, x_ref, st_ref, ga, gf, prev, da_ref, db_ref, sums_ref):
    j = pl.program_id(0)
    for w1, w2, dn_ref, mine in ((w10, w20, da_ref, j < 2), (w11, w21, db_ref, j == 2), (w12, w22, db_ref, j == 3)):

        @pl.when(mine)
        def _():
            dh1 = nt(dqkv[...], w1[...])
            dh2 = nt(du[...], w2[...])
            xh = (x_ref[...].astype(F32) - st_ref[:, 0:1]) * st_ref[:, 1:2]
            dn_ref[...] = (dh1 * ga[...] + dh2 * gf[...]).astype(BF)
            sums_ref[0:1, :] = jnp.sum(dh1 * xh, axis=0, keepdims=True)
            sums_ref[1:2, :] = jnp.sum(dh1, axis=0, keepdims=True)
            sums_ref[2:3, :] = jnp.sum(dh2 * xh, axis=0, keepdims=True)
            sums_ref[3:4, :] = jnp.sum(dh2, axis=0, keepdims=True)


def back_call(meta, dqkv, du, g1, g2, x2, st, ga, gf, sums, half):
    m, d = x2.shape
    nq = dqkv.shape[1]
    f = du.shape[1]
    n = d // 4

    def absolute(rows):
        return pl.BlockSpec((rows, 256), lambda j, mt: (0, mt[1 + 4 * half + j]))

    part = jax.ShapeDtypeStruct((m, n), BF)
    at = slice(3 * half, 3 * half + 3)
    return pl.pallas_call(
        back_kernel,
        name="backn",
        grid_spec=pltpu.PrefetchScalarGridSpec(
            num_scalar_prefetch=1,
            grid=(4,),
            in_specs=[
                pl.BlockSpec((m, nq), lambda j, mt: (0, 0)),
                pl.BlockSpec((m, f), lambda j, mt: (0, 0)),
                pl.BlockSpec((256, nq), lambda j, mt: (jnp.minimum(j, 1), 0)),
                pl.BlockSpec((256, nq), lambda j, mt: (0, 0)),
                pl.BlockSpec((256, nq), lambda j, mt: (0, 0)),
                pl.BlockSpec((256, f), lambda j, mt: (jnp.minimum(j, 1), 0)),
                pl.BlockSpec((256, f), lambda j, mt: (0, 0)),
                pl.BlockSpec((256, f), lambda j, mt: (0, 0)),
                absolute(m),
                pl.BlockSpec((m, 128), lambda j, mt: (0, 0)),
                absolute(1),
                absolute(1),
                pl.BlockSpec(memory_space=pl.ANY),
            ],
            out_specs=[
                pl.BlockSpec((m, n // 2), lambda j, mt: (0, jnp.minimum(j, 1))),
                pl.BlockSpec((m, n // 2), lambda j, mt: (0, jnp.maximum(j - 2, 0))),
                absolute(4),
            ],
        ),
        out_shape=[part, part, jax.ShapeDtypeStruct((4, d), F32)],
        input_output_aliases={13: 2},
        compiler_params=params(1),
        cost_estimate=cost(4 * m * n * (f + nq), 2 * (m * f + m * nq + 2 * n * (f + nq) + 4 * m * n)),
    )(meta, dqkv, du, *g1[at], *g2[at], x2, st, ga, gf, sums)


def wgrad_kernel(pairs, adds, split, meta, *refs):
    j = pl.program_id(0)
    start = 0
    for p, count in enumerate(pairs):
        a, b = refs[2 * p], refs[2 * p + 1]

        @pl.when((j >= start) & (j < start + count))
        def _():
            y = tn(a[...], b[...])
            if adds:
                y = y + refs[2 * len(pairs)][...].astype(F32)
            if not split:
                refs[-1][...] = y.astype(BF)
                return
            keep, send = refs[-2:]
            n = y.shape[0] // 4
            swap = meta[2 + NBLK] > 0
            keep[:n] = y[:n].astype(BF)
            keep[n:] = jnp.where(swap, y[2 * n : 3 * n], y[n : 2 * n]).astype(BF)
            send[:n] = jnp.where(swap, y[n : 2 * n], y[2 * n : 3 * n]).astype(BF)
            send[n:] = y[3 * n :].astype(BF)

        start += count


def wgrad_call(meta, *flat, half, add=None, split=False):
    pairs = list(zip(flat[::2], flat[1::2]))
    m, d = pairs[0][0].shape
    t = 512
    counts = tuple(b.shape[1] // t for _, b in pairs)
    total = sum(counts)
    in_specs, ops, start = [], [], 0
    for (a, b), c in zip(pairs, counts):
        in_specs.append(pl.BlockSpec((m, d // 2), lambda j, mt: (0, half)))
        in_specs.append(
            pl.BlockSpec((m, t), lambda j, mt, s=start, c=c: (0, jnp.clip(j - s, 0, c - 1)))
        )
        ops += [a, b]
        start += c
    rows = d // 4 if split else d // 2
    if add is not None:
        in_specs.append(pl.BlockSpec((d // 2, t), lambda j, mt: (0, j)))
        ops.append(add)
    out_spec = pl.BlockSpec((rows, t), lambda j, mt: (0, j))
    out_shape = jax.ShapeDtypeStruct((rows, total * t), BF)
    return pl.pallas_call(
        functools.partial(wgrad_kernel, counts, add is not None, split),
        name="wgrad",
        grid_spec=pltpu.PrefetchScalarGridSpec(
            num_scalar_prefetch=1,
            grid=(total,),
            in_specs=in_specs,
            out_specs=[out_spec, out_spec] if split else out_spec,
        ),
        out_shape=[out_shape, out_shape] if split else out_shape,
        compiler_params=params(1),
        cost_estimate=cost(m * d * total * t, 2 * (m * d // 2 * len(pairs) + m * total * t + d * total * t)),
    )(meta, *ops)


def pack_kernel(*refs):
    out, at = refs[-1], 0
    for ref in refs[:-1]:
        n = ref.shape[0]
        out[at : at + n] = ref[...]
        at += n


def pack_call(*pieces):
    rows = sum(p.shape[0] for p in pieces)
    cols = pieces[0].shape[1]
    t = 512
    return pl.pallas_call(
        pack_kernel,
        name="pack",
        grid=(cols // t,),
        in_specs=[pl.BlockSpec((p.shape[0], t), lambda j: (0, j)) for p in pieces],
        out_specs=pl.BlockSpec((rows, t), lambda j: (0, j)),
        out_shape=jax.ShapeDtypeStruct((rows, cols), BF),
        compiler_params=params(1),
        cost_estimate=cost(0, 4 * rows * cols),
    )(*pieces)


def half_sum_kernel(keep, got, mid, send):
    n = mid.shape[0]
    mid[...] = keep[:n].astype(F32) + got[:n].astype(F32)
    send[...] = (keep[n:].astype(F32) + got[n:].astype(F32)).astype(BF)


def half_sum_call(keep, got):
    rows, cols = keep.shape
    t = 512
    n = rows // 2
    small = pl.BlockSpec((n, t), lambda j: (0, j))
    return pl.pallas_call(
        half_sum_kernel,
        name="hsum",
        grid=(cols // t,),
        in_specs=[pl.BlockSpec((rows, t), lambda j: (0, j))] * 2,
        out_specs=[small] * 2,
        out_shape=[jax.ShapeDtypeStruct((n, cols), F32), jax.ShapeDtypeStruct((n, cols), BF)],
        compiler_params=params(1),
        cost_estimate=cost(4 * n * cols, 14 * n * cols),
    )(keep, got)


def last_sum_kernel(plan, mid, got, *outs):
    j = pl.program_id(0)
    at = 0
    for (count, turned), out in zip(plan, outs):

        @pl.when((j >= at) & (j < at + count))
        def _():
            v = mid[...] + got[...].astype(F32)
            out[...] = v.T if turned else v

        at += count


def last_sum_call(mid, got, plan):
    n, cols = mid.shape
    t = 512
    block = pl.BlockSpec((n, t), lambda j: (0, j))
    out_specs, out_shape, at = [], [], 0
    for count, turned in plan:
        def place(j, at=at, count=count):
            return jnp.clip(j - at, 0, count - 1)

        if turned:
            out_specs.append(pl.BlockSpec((t, n), lambda j, f=place: (f(j), 0)))
            out_shape.append(jax.ShapeDtypeStruct((count * t, n), F32))
        else:
            out_specs.append(pl.BlockSpec((n, t), lambda j, f=place: (0, f(j))))
            out_shape.append(jax.ShapeDtypeStruct((n, count * t), F32))
        at += count
    return pl.pallas_call(
        functools.partial(last_sum_kernel, plan),
        name="lsum",
        grid=(cols // t,),
        in_specs=[block, block],
        out_specs=out_specs,
        out_shape=out_shape,
        compiler_params=params(1),
        cost_estimate=cost(2 * n * cols, 10 * n * cols),
    )(mid, got)


def by_role(meta, refs, body):
    @pl.when(meta[1 + NBLK] > 0)
    def _():
        body(refs[0::2])

    @pl.when(meta[1 + NBLK] == 0)
    def _():
        body(refs[1::2])


def block_out_kernel(local_len, first, meta, x_ref, b_ref, *refs):
    y_ref = refs[-1]
    rows = x_ref.shape[0]
    mask = row_valid(meta, (first + pl.program_id(0)) * rows, rows, local_len)

    def body(parts):
        for r in range(NBLK):
            col = block_cols(meta[1 + r] * 256)
            s = parts[r // 2][:, r % 2 * 256 : r % 2 * 256 + 256].astype(F32)
            y_ref[:, col] = (mask * (x_ref[:, col].astype(F32) + s + b_ref[:, col])).astype(BF)

    by_role(meta, refs[:8], body)


def input_grad_kernel(local_len, first, meta, x_ref, g_ref, st_ref, *refs):
    y_ref = refs[-1]
    rows = x_ref.shape[0]
    mask = row_valid(meta, (first + pl.program_id(0)) * rows, rows, local_len)
    mean = st_ref[:, 0:1]
    inv = st_ref[:, 1:2]
    d = x_ref.shape[1]

    def body(parts):
        def dn_of(r):
            return parts[r // 2][:, r % 2 * 256 : r % 2 * 256 + 256].astype(F32)

        one = jnp.zeros((rows, 256), F32)
        two = jnp.zeros((rows, 256), F32)
        for r in range(NBLK):
            dn = dn_of(r)
            one += dn
            two += dn * (x_ref[:, block_cols(meta[1 + r] * 256)].astype(F32) - mean)
        one = jnp.sum(one, axis=1, keepdims=True) / d
        two = jnp.sum(two, axis=1, keepdims=True) * inv / d
        slope = inv * inv * two
        shift = slope * mean - inv * one
        for r in range(NBLK):
            col = block_cols(meta[1 + r] * 256)
            y = g_ref[:, col].astype(F32) * mask + inv * dn_of(r)
            y_ref[:, col] = (y + (shift - slope * x_ref[:, col].astype(F32))).astype(BF)

    by_role(meta, refs[:8], body)


def rows_call(meta, *ops, body, name, specs, steps=None, into=None):
    rows = 256
    m, d = ops[0].shape
    first, last = steps or (0, m // rows)
    made = {
        "row": pl.BlockSpec((rows, d), lambda i, mt: (first + i, 0)),
        "part": pl.BlockSpec((rows, d // 4), lambda i, mt: (first + i, 0)),
        "stat": pl.BlockSpec((rows, 128), lambda i, mt: (first + i, 0)),
        "vec": pl.BlockSpec((1, d), lambda i, mt: (0, 0)),
    }
    in_specs = [made[s] for s in specs]
    aliases = {}
    if into is not None:
        aliases = {1 + len(ops): 0}
        in_specs.append(pl.BlockSpec(memory_space=pl.ANY))
        ops += (into,)
    return pl.pallas_call(
        functools.partial(body, first),
        name=name,
        grid_spec=pltpu.PrefetchScalarGridSpec(
            num_scalar_prefetch=1,
            grid=(last - first,),
            in_specs=in_specs,
            out_specs=made["row"],
        ),
        out_shape=jax.ShapeDtypeStruct((m, d), BF),
        input_output_aliases=aliases,
        compiler_params=params(1),
        cost_estimate=cost(10 * (last - first) * rows * d, 8 * (last - first) * rows * d),
    )(meta, *ops)


def after(v, *others):
    return lax.optimization_barrier((v,) + others)[0]


class Order:
    def __init__(self):
        self.last = ()

    def __call__(self, f, first, *rest, **named):
        out = f(after(first, *self.last), *rest, **named)
        self.last = (jax.tree.leaves(out)[0],)
        return out


def add_bf(a, b):
    return lax.optimization_barrier((a.astype(F32) + b.astype(F32)).astype(BF))


def pick_bf(a, b, middle, other):
    total = (a.astype(F32) + b.astype(F32)).astype(BF)
    return lax.optimization_barrier(jnp.where(middle > 0, total, other))


class Pipe:
    LAG = 3

    def __init__(self, run, middle, count):
        self.run, self.middle, self.count = run, middle, count
        self.parts, self.got, self.sums, self.crossed = [], [], [], []
        self.here, self.sent = [], []

    def send(self, part=None):
        step = len(self.got)
        back = step - self.LAG
        pairs = []
        v = part
        if part is not None:
            self.parts.append(part)
            pairs += [(0, 1), (3, 2)]
        if back >= 0:
            pairs += [(1, 0), (2, 3)]
            a, b = self.sums[back], self.crossed[back]
            if part is None:
                v = self.run(add_bf, a, b)
            else:
                v = self.run(pick_bf, a, b, self.middle, part)
        got = lax.ppermute(v, "tensor", pairs)
        self.got.append(got)
        if back >= 0:
            self.here.append(v)
            self.sent.append(got)

    def cross(self):
        k = len(self.sums)
        v = self.run(add_bf, self.parts[k], self.got[k])
        self.sums.append(v)
        self.crossed.append(lax.ppermute(v, "tensor", [(1, 2), (2, 1)]))


class PlainPipe:
    def __init__(self, run, middle, count):
        self.here, self.sent, self.sums = [], [], []

    def send(self, part=None):
        if part is not None:
            total = lax.psum(part, "tensor")
            self.here.append(total)
            self.sent.append(total)

    def cross(self):
        pass


class SmallMesh:
    def x(self, v):
        return lax.ppermute(v, "dp", [(0, 2), (2, 0), (1, 3), (3, 1)])

    def core(self, v):
        return lax.ppermute(v, "dp", [(0, 1), (1, 0), (2, 3), (3, 2)])

    def y(self, v):
        return lax.ppermute(v, "ctx", [(0, 1), (1, 0)])

    def perm(self):
        r = jnp.arange(NBLK, dtype=jnp.int32)
        dp = lax.axis_index("dp") ^ (((r >> 1) & 1) * 2 + (r >> 2))
        return dp * 2 + (lax.axis_index("ctx") ^ (r & 1))

    def middle(self):
        z = lax.axis_index("tensor")
        return ((z == 1) | (z == 2)).astype(jnp.int32)

    pipe = Pipe

    def first_hop(self, own, earlier=None):
        if earlier is None:
            return self.x(own), self.y(own)
        return self.x(after(own, earlier)), self.y(own)

    def second_hop(self, hop, earlier=()):
        return self.x(after(hop[1], hop[0], *earlier))

    def waited(self, hop):
        return hop

    def near_pieces(self, near):
        return near

    def near(self, run, own, hop):
        v = run(pack_call, own, hop[1])
        return v, self.core(v)

    def pieces(self, near, hop, diag, earlier=()):
        return near[0], hop[0], diag, near[1], self.core(after(hop[0], *earlier[:1])), self.core(after(diag, *earlier))

    def turn(self, v, first):
        pairs = []
        for dp in range(4):
            for c in range(2):
                to = (dp ^ 2) * 2 + c if dp % 2 != first else dp * 2 + (c ^ 1)
                pairs.append((dp * 2 + c, to))
        return lax.ppermute(v, ("dp", "ctx"), pairs)

    def scatter_cross(self, theirs):
        return self.core(theirs)

    def scatter_own(self, run, meta, pairs, got):
        keep, send = run(wgrad_call, meta, *pairs, half=0, add=got, split=True)
        return keep, self.turn(send, 1)

    def scatter_half(self, run, parts):
        mid, send = run(half_sum_call, *parts)
        return mid, self.turn(send, 0)

    def scatter_last(self, run, plan, parts):
        return run(last_sum_call, *parts, plan=plan)

    def previous(self, kv, slots):
        return lax.ppermute(kv, "ctx", [(0, 1)])

    def give_back(self, dpv, dkv, slots):
        return dkv, lax.ppermute(dpv, "ctx", [(1, 0)])

    def small_sum(self, run, v, step):
        def add(a, b):
            return a + b

        if step == 0:
            got = self.core(v)
        elif step == 1:
            got = self.x(v)
        elif step == 2:
            got = self.y(v)
        elif step == 3:
            got = lax.ppermute(v, "tensor", [(0, 1), (1, 0), (2, 3), (3, 2)])
        else:
            got = lax.ppermute(v, "tensor", [(0, 2), (2, 0), (1, 3), (3, 1)])
        return lambda: run(add, v, got)


class AnyMesh:
    def perm(self):
        return jnp.arange(NBLK, dtype=jnp.int32)

    def middle(self):
        return jnp.ones((), jnp.int32)

    pipe = PlainPipe

    def first_hop(self, own, earlier=None):
        return lax.all_gather(own, ("dp", "ctx"), axis=0, tiled=True)

    def second_hop(self, hop, earlier=()):
        return ()

    def waited(self, hop):
        return (hop,)

    def near_pieces(self, near):
        return near

    def near(self, run, own, hop):
        return hop[:512], hop[1024:1536]

    def pieces(self, near, hop, diag, earlier=()):
        return near[0], hop[512:768], hop[768:1024], near[1], hop[1536:1792], hop[1792:]

    def scatter_cross(self, theirs):
        return theirs

    def scatter_own(self, run, meta, pairs, got):
        full = jnp.concatenate([run(wgrad_call, meta, *pairs, half=0), got], axis=0)
        return lax.psum_scatter(full, ("dp", "ctx"), scatter_dimension=0, tiled=True).astype(F32)

    def scatter_half(self, run, parts):
        return parts

    def scatter_last(self, run, plan, parts):
        outs, at = [], 0
        for count, turned in plan:
            v = parts[:, at * 512 : (at + count) * 512]
            outs.append(v.T if turned else v)
            at += count
        return outs

    def previous(self, kv, slots):
        own = kv.reshape(slots, -1, kv.shape[1])
        full = lax.all_gather(own, "ctx", axis=1, tiled=True)
        return full.reshape(-1, kv.shape[1])

    def give_back(self, dpv, dkv, slots):
        cols = dkv.shape[1]
        full = dpv.reshape(slots, -1, cols)
        got = lax.psum_scatter(full, "ctx", scatter_dimension=1, tiled=True)
        return dkv, got.reshape(-1, cols)

    def small_sum(self, run, v, step):
        got = v
        if step == 0:
            got = lax.psum(v, ("dp", "ctx"))
        elif step == 3:
            got = lax.psum(v, "tensor")
        return lambda: got


def rotary_tables(positions):
    half_rot = ROT // 2
    lane = jnp.arange(128, dtype=jnp.int32)
    exponent = (lane % half_rot).astype(F32) * (2.0 / ROT)
    angles = positions[:, None] * jnp.exp(-math.log(10000.0) * exponent)[None, :]
    cos_all, sin_all = jnp.cos(angles), jnp.sin(angles)
    cosf = jnp.where(lane < ROT, cos_all, 1.0)
    s1 = jnp.where(lane < half_rot, -sin_all, 0.0)
    s2 = jnp.where((lane >= half_rot) & (lane < ROT), sin_all, 0.0)
    return cosf, s1, s2


def local(small, block_input, out_grad, lengths, attn_gain, attn_shift, ffn_gain, ffn_shift, w_qkv, b_qkv, w_proj, b_proj, w_in, b_in, w_out, b_out):
    comm = SmallMesh() if small else AnyMesh()
    slots, local_len, d = block_input.shape
    m = slots * local_len
    nheads = b_qkv.shape[0] // (3 * HD)
    nq = 3 * nheads * HD
    ctx = lax.axis_index("ctx")
    core = lax.axis_index("dp") % 2
    meta = jnp.concatenate(
        [ctx[None].astype(jnp.int32), comm.perm(), comm.middle()[None], core[None].astype(jnp.int32), lengths]
    )

    run = Order()
    x2 = block_input.reshape(m, d)
    og2 = out_grad.reshape(m, d)
    ga, sa, gf, sf = (v.reshape(1, d) for v in (attn_gain, attn_shift, ffn_gain, ffn_shift))
    bq = b_qkv.reshape(1, nq)
    positions = ctx * local_len + jnp.arange(local_len, dtype=jnp.int32)
    tabs = rotary_tables(positions.astype(F32))

    own1 = jnp.concatenate([w_qkv, w_proj.T], axis=1).astype(BF)
    hop1 = comm.first_hop(own1)
    own2 = w_in.astype(BF)
    own3 = w_out.T.astype(BF)
    run.last = (own1, own2, own3)
    hop2 = comm.first_hop(own2, hop1[0])
    h1, g, stats, g_sum = run(norm_call, meta, x2, og2, ga, sa, local_len)
    diag1 = comm.second_hop(hop1)
    near1 = comm.near(run, own1, hop1)
    g1 = comm.pieces(near1, hop1, diag1)
    near2 = comm.near(run, own2, hop2)
    kv = run(kv_call, h1, g1, bq, tabs, nheads)
    pv = comm.previous(kv, slots)
    diag2 = comm.second_hop(hop2, (kv,))
    hop3 = comm.first_hop(own3, diag2)
    q, dob = run(qd_call, h1, g, g1, bq, tabs, nheads)
    g2 = comm.pieces(near2, hop2, diag2, (kv, q))
    diag3 = comm.second_hop(hop3)
    h2 = run(second_norm_call, meta, x2, stats, gf, sf)
    gb, dg = run(hidden_call, h2, g2, b_in.reshape(1, -1))
    near3 = comm.near(run, own3, hop3)
    ob, dq, dkv, dpv = run(attn_call, meta, q, kv, pv, dob, tabs, nheads)
    dkv, rv = comm.give_back(dpv, dkv, slots)
    g3 = comm.near_pieces(near3)

    pipe = comm.pipe(run, meta[1 + NBLK], 8)
    ff = gb.shape[1] // 512
    out0, out2 = run(out_call, ob, gb, (g1[0], g1[3]), g3, 0.01)
    pipe.send(out0)
    pipe.send(out2)
    g3 = comm.pieces(near3, hop3, diag3, (ob, out0))
    cross3 = comm.scatter_cross(run(wgrad_call, meta, g, gb, half=1))
    far = (1, 2, 4, 5)
    out1, out3 = run(out_call, ob, gb, [g1[k] for k in far], [g3[k] for k in far])
    du, bin_sum = run(dhid_call, g, g3, dg)
    pipe.cross()
    pipe.send(after(out1, *pipe.sums))
    state3 = comm.scatter_own(run, meta, (g, gb), cross3)
    pipe.cross()
    dqkv, bqkv_sum = run(join_call, dq, dkv, rv, tabs, nheads)
    pipe.send(out3)
    gain_sums = jnp.zeros((4, d), F32)
    pipe.cross()
    dn0, dn1, gain_sums = run(back_call, meta, dqkv, du, g1, g2, x2, stats, ga, gf, gain_sums, 0)
    pipe.send(dn0)
    pipe.cross()
    pipe.send(dn1)
    state3 = comm.scatter_half(run, state3)
    dn2, dn3, gain_sums = run(back_call, meta, dqkv, du, g1, g2, x2, stats, ga, gf, gain_sums, 1)
    pipe.cross()
    pipe.send(dn2)
    small = jnp.concatenate([gain_sums.reshape(-1), g_sum.reshape(-1), bqkv_sum.reshape(-1), bin_sum.reshape(-1)])
    add = comm.small_sum(run, small, 0)
    cross2 = comm.scatter_cross(run(wgrad_call, after(meta, jax.tree.leaves(state3)[-1]), h2, du, half=1))
    small = add()
    add = comm.small_sum(run, small, 1)
    theirs1 = run(wgrad_call, meta, h1, dqkv, g, ob, half=1)
    small = add()
    pipe.cross()
    pipe.send(dn3)
    state2 = comm.scatter_own(run, meta, (h2, du), cross2)
    cross1 = comm.scatter_cross(after(theirs1, *jax.tree.leaves(state2)[:1]))
    (grad_out,) = comm.scatter_last(run, ((ff, True),), state3)
    pipe.cross()
    pipe.send()
    state1 = comm.scatter_own(run, meta, (h1, dqkv, g, ob), cross1)
    pipe.cross()
    pipe.send()
    state2 = comm.scatter_half(run, state2)

    def sums_of(order):
        return [v for c in order for v in (pipe.here[c], pipe.sent[c])]

    out_ops = (meta, x2, (b_proj + b_out).reshape(1, d), *sums_of((0, 2, 1, 3)))
    out_half = functools.partial(
        rows_call, body=functools.partial(block_out_kernel, local_len), name="bout", specs=("row", "vec") + ("part",) * 8
    )
    block_output = run(out_half, *out_ops, steps=(0, 2))
    (grad_in,) = comm.scatter_last(run, ((ff, False),), state2)
    block_output = run(out_half, *out_ops, steps=(2, 4), into=block_output).reshape(slots, local_len, d)
    pipe.send()
    add = comm.small_sum(run, after(small, pipe.sent[5], pipe.here[-1], *jax.tree.leaves(state1)[-1:]), 2)
    state1 = comm.scatter_half(run, state1)
    small = add()
    gains = small[: 4 * d]
    group = small[4 * d :]
    add = comm.small_sum(run, after(gains, *jax.tree.leaves(state1)[:1]), 3)
    input_grad = run(
        rows_call, meta, x2, og2, stats, *sums_of(range(4, 8)),
        body=functools.partial(input_grad_kernel, local_len), name="igrad", specs=("row", "row", "stat") + ("part",) * 8,
    ).reshape(slots, local_len, d)
    gains = add()
    add = comm.small_sum(run, gains, 4)
    grad_qkv, grad_proj = comm.scatter_last(run, ((nq // 512, False), (nheads * HD // 512, True)), state1)
    gains = add().reshape(4, d)
    bias_grad = group[:d]
    return (
        block_output,
        input_grad,
        gains[0],
        gains[1],
        gains[2],
        gains[3],
        grad_qkv,
        group[d : d + nq],
        grad_proj,
        bias_grad,
        grad_in,
        group[d + nq :],
        grad_out,
        bias_grad,
    )


def solution(mesh):
    small = mesh.shape["dp"] == 4 and mesh.shape["ctx"] == 2 and mesh.shape["tensor"] == 4
    placed = (
        P("dp", "ctx", None),
        P("dp", "ctx", None),
        P("dp"),
        P(),
        P(),
        P(),
        P(),
        P(("dp", "ctx"), "tensor"),
        P("tensor"),
        P("tensor", ("dp", "ctx")),
        P(),
        P(("dp", "ctx"), "tensor"),
        P("tensor"),
        P("tensor", ("dp", "ctx")),
        P(),
    )
    return jax.shard_map(
        functools.partial(local, small),
        mesh=mesh,
        in_specs=placed,
        out_specs=(
            P("dp", "ctx", None),
            P("dp", "ctx", None),
            P(),
            P(),
            P(),
            P(),
            P(("dp", "ctx"), "tensor"),
            P("tensor"),
            P("tensor", ("dp", "ctx")),
            P(),
            P(("dp", "ctx"), "tensor"),
            P("tensor"),
            P("tensor", ("dp", "ctx")),
            P(),
        ),
        check_vma=False,
    )
```

```python
import functools
import math

import jax
import jax.numpy as jnp
from jax import lax
from jax.experimental import pallas as pl
from jax.experimental.pallas import tpu as pltpu
from jax.sharding import PartitionSpec as P

HD = 256
ROT = 64
NBLK = 8
BF = jnp.bfloat16
F32 = jnp.float32

neg_big = -1e30
inv_sqrt_two = 0.7071067811865476
inv_sqrt_tau = 0.3989422804014327


COST_SCALE = 100


def cost(flops, nbytes, trans=0, k=COST_SCALE):
    flops = max(flops, 300 * nbytes)
    return pl.CostEstimate(flops=int(k * flops), bytes_accessed=int(k * nbytes), transcendentals=int(k * trans))


def params(n, mb=60):
    return pltpu.CompilerParams(
        dimension_semantics=("arbitrary",) * n, vmem_limit_bytes=int(mb * 1024 * 1024)
    )


def nn(a, b):
    return lax.dot_general(a, b, (((1,), (0,)), ((), ())), preferred_element_type=F32)


def nn_rows(a, pieces):
    total, at = None, 0
    for w in pieces:
        y = nn(a[:, at : at + w.shape[0]], w[...])
        total = y if total is None else total + y
        at += w.shape[0]
    return total


def nt(a, b):
    return lax.dot_general(a, b, (((1,), (1,)), ((), ())), preferred_element_type=F32)


def tn(a, b):
    return lax.dot_general(a, b, (((0,), (0,)), ((), ())), preferred_element_type=F32)


def block_cols(r):
    return pl.ds(pl.multiple_of(r, 128), 256)


def row_valid(meta, row0, rows, local_len):
    slot = row0 // local_len
    pos = meta[0] * local_len + row0 % local_len + lax.broadcasted_iota(jnp.int32, (rows, 1), 0)
    return (pos < meta[3 + NBLK + slot]).astype(F32)


def norm_kernel(local_len, meta, x_ref, g_ref, ga, sa, h1_ref, g_out, st_ref, gs_ref):
    rows = x_ref.shape[0]
    i = pl.program_id(0)
    x = x_ref[...].astype(F32)
    mean = jnp.mean(x, axis=-1, keepdims=True)
    cen = x - mean
    inv = lax.rsqrt(jnp.mean(cen * cen, axis=-1, keepdims=True) + 1e-05)
    mask = row_valid(meta, i * rows, rows, local_len)
    lane = lax.broadcasted_iota(jnp.int32, (rows, 128), 1)
    st_ref[...] = jnp.where(lane == 0, mean, inv)
    for r in range(NBLK):
        src = block_cols(meta[1 + r] * 256)
        dst = slice(r * 256, (r + 1) * 256)
        xh = (x_ref[:, src].astype(F32) - mean) * inv
        h1_ref[:, dst] = (xh * ga[:, src] + sa[:, src]).astype(BF)
        gm = g_ref[:, src].astype(F32) * mask
        g_out[:, dst] = gm.astype(BF)
        part = jnp.sum(gm, axis=0, keepdims=True)

        @pl.when(i == 0)
        def _():
            gs_ref[:, src] = part

        @pl.when(i > 0)
        def _():
            gs_ref[:, src] = gs_ref[:, src] + part


def second_norm_kernel(meta, x_ref, st_ref, gf, sf, h2_ref):
    for r in range(NBLK):
        src = block_cols(meta[1 + r] * 256)
        xh = (x_ref[:, src].astype(F32) - st_ref[:, 0:1]) * st_ref[:, 1:2]
        h2_ref[:, r * 256 : (r + 1) * 256] = (xh * gf[:, src] + sf[:, src]).astype(BF)


def second_norm_call(meta, x2, st, gf, sf):
    m, d = x2.shape
    rows = 256
    row_spec = pl.BlockSpec((rows, d), lambda i, mt: (i, 0))
    vec = pl.BlockSpec((1, d), lambda i, mt: (0, 0))
    return pl.pallas_call(
        second_norm_kernel,
        name="norm2",
        grid_spec=pltpu.PrefetchScalarGridSpec(
            num_scalar_prefetch=1,
            grid=(m // rows,),
            in_specs=[row_spec, pl.BlockSpec((rows, 128), lambda i, mt: (i, 0)), vec, vec],
            out_specs=row_spec,
        ),
        out_shape=jax.ShapeDtypeStruct((m, d), BF),
        compiler_params=params(1),
        cost_estimate=cost(5 * m * d, 4 * m * d),
    )(meta, x2, st, gf, sf)


def norm_call(meta, x2, g2, ga, sa, local_len):
    m, d = x2.shape
    rows = 256
    row_spec = pl.BlockSpec((rows, d), lambda i, mt: (i, 0))
    vec = pl.BlockSpec((1, d), lambda i, mt: (0, 0))
    return pl.pallas_call(
        functools.partial(norm_kernel, local_len),
        name="norm",
        grid_spec=pltpu.PrefetchScalarGridSpec(
            num_scalar_prefetch=1,
            grid=(m // rows,),
            in_specs=[row_spec, row_spec, vec, vec],
            out_specs=[row_spec, row_spec, pl.BlockSpec((rows, 128), lambda i, mt: (i, 0)), vec],
        ),
        out_shape=[jax.ShapeDtypeStruct((m, d), BF)] * 2
        + [jax.ShapeDtypeStruct((m, 128), F32), jax.ShapeDtypeStruct((1, d), F32)],
        compiler_params=params(1),
        cost_estimate=cost(20 * m * d, 10 * m * d),
    )(meta, x2, g2, ga, sa)


def rotate_tile(y, cosf, s1, s2, sign):
    head = y[:, :128]
    rot = (
        head * cosf
        + pltpu.roll(head, 96, 1) * (s1 * sign)
        + pltpu.roll(head, 32, 1) * (s2 * sign)
    )
    return rot, y[:, 128:]


def rotated(out, y, cosf, s1, s2):
    local_len = cosf.shape[0]
    for s in range(y.shape[0] // local_len):
        rows = slice(s * local_len, (s + 1) * local_len)
        rot, rest = rotate_tile(y[rows], cosf[...], s1[...], s2[...], 1.0)
        out[rows, :128] = rot.astype(BF)
        out[rows, 128:] = rest.astype(BF)


def kv_kernel(h1, w0, w1, w2, w3, w4, w5, b_ref, cosf, s1, s2, kv_ref):
    part = lax.rem(pl.program_id(0), 2)
    y = nn_rows(h1, (w0, w1, w2, w3, w4, w5)) + b_ref[...]

    @pl.when(part == 0)
    def _():
        rotated(kv_ref, y, cosf, s1, s2)

    @pl.when(part == 1)
    def _():
        kv_ref[...] = y.astype(BF)


def kv_call(h1, pieces, b_qkv, tabs, nheads):
    m, d = h1.shape
    local_len = tabs[0].shape[0]

    def src(j):
        return (0, (j // 2) * 3 + 1 + j % 2)

    tab = pl.BlockSpec((local_len, 128), lambda j: (0, 0))
    return pl.pallas_call(
        kv_kernel,
        name="kv",
        grid=(2 * nheads,),
        in_specs=[
            pl.BlockSpec((m, d), lambda j: (0, 0)),
            *[pl.BlockSpec((p.shape[0], HD), src) for p in pieces],
            pl.BlockSpec((1, HD), src),
            tab,
            tab,
            tab,
        ],
        out_specs=pl.BlockSpec((m, HD), lambda j: (0, j)),
        out_shape=jax.ShapeDtypeStruct((m, 2 * nheads * HD), BF),
        compiler_params=params(1),
        cost_estimate=cost(4 * m * d * nheads * HD, 2 * (m * d + 2 * d * nheads * HD + 2 * m * nheads * HD)),
    )(h1, *pieces, b_qkv, *tabs)


def qd_kernel(nheads, h1, g, w0, w1, w2, w3, w4, w5, b_ref, cosf, s1, s2, q_ref, dob_ref):
    j = pl.program_id(0)
    pieces = (w0, w1, w2, w3, w4, w5)

    @pl.when(j < nheads)
    def _():
        rotated(q_ref, nn_rows(h1, pieces) + b_ref[...], cosf, s1, s2)

    @pl.when(j >= nheads)
    def _():
        dob_ref[...] = nn_rows(g, pieces).astype(BF)


def qd_call(h1, g, pieces, b_qkv, tabs, nheads):
    m, d = h1.shape
    local_len = tabs[0].shape[0]
    full = pl.BlockSpec((m, d), lambda j: (0, 0))

    def src(j):
        return (0, jnp.where(j < nheads, 3 * j, 2 * nheads + j))

    tab = pl.BlockSpec((local_len, 128), lambda j: (0, 0))
    return pl.pallas_call(
        functools.partial(qd_kernel, nheads),
        name="qd",
        grid=(2 * nheads,),
        in_specs=[
            full,
            full,
            *[pl.BlockSpec((p.shape[0], HD), src) for p in pieces],
            pl.BlockSpec((1, HD), lambda j: (0, 3 * jnp.minimum(j, nheads - 1))),
            tab,
            tab,
            tab,
        ],
        out_specs=[
            pl.BlockSpec((m, HD), lambda j: (0, jnp.minimum(j, nheads - 1))),
            pl.BlockSpec((m, HD), lambda j: (0, jnp.maximum(j - nheads, 0))),
        ],
        out_shape=[jax.ShapeDtypeStruct((m, nheads * HD), BF)] * 2,
        compiler_params=params(1),
        cost_estimate=cost(4 * m * d * nheads * HD, 2 * (2 * m * d + 2 * d * nheads * HD + 2 * m * nheads * HD)),
    )(h1, g, *pieces, b_qkv, *tabs)


def attn_kernel(nprev, local_len, meta, q_ref, kv_ref, pv_ref, dob_ref, cosf, s1, s2, ob_ref, dq_ref, dkv_ref, dpv_ref, sc_ref, dq_acc):
    slot = pl.program_id(0)
    ctx = meta[0]
    length = meta[3 + NBLK + slot]
    scale = 1.0 / math.sqrt(HD)
    n_vis = jnp.minimum(ctx, (length + local_len - 1) // local_len)
    q = q_ref[...]
    dob = dob_ref[...]
    own_k = kv_ref[:, :HD]
    own_v = kv_ref[:, HD:]

    ri = lax.broadcasted_iota(jnp.int32, (local_len, local_len), 0)
    ci = lax.broadcasted_iota(jnp.int32, (local_len, local_len), 1)
    s_own = nt(q, own_k) * scale
    s_own = jnp.where((ci <= ri) & (ci < length - ctx * local_len), s_own, neg_big)
    sc_ref[nprev] = s_own

    def prev_rows(jb):
        return pl.ds(pl.multiple_of(jb * local_len, local_len), local_len)

    def score(jb, top):
        s = nt(q, pv_ref[prev_rows(jb), :HD]) * scale
        s = jnp.where(ci[:1] < length - jb * local_len, s, neg_big)
        sc_ref[jb] = s
        return jnp.maximum(top, jnp.max(s, axis=1, keepdims=True))

    top = lax.fori_loop(0, n_vis, score, jnp.max(s_own, axis=1, keepdims=True))

    e_own = jnp.exp(sc_ref[nprev] - top)
    sc_ref[nprev] = e_own

    def expo(jb, tot):
        e = jnp.exp(sc_ref[jb] - top)
        sc_ref[jb] = e
        return tot + jnp.sum(e, axis=1, keepdims=True)

    tot = lax.fori_loop(0, n_vis, expo, jnp.sum(e_own, axis=1, keepdims=True))
    inv = 1.0 / tot
    att = nn((sc_ref[nprev] * inv).astype(BF), own_v)

    def out_step(jb, acc):
        return acc + nn((sc_ref[jb] * inv).astype(BF), pv_ref[prev_rows(jb), HD:])

    att = lax.fori_loop(0, n_vis, out_step, att)
    ob_ref[...] = att.astype(BF)
    delta = jnp.sum(dob.astype(F32) * att, axis=1, keepdims=True)

    def back(p, k, v):
        pb = p.astype(BF)
        ds = (p * (nt(dob, v) - delta)).astype(BF)
        return nn(ds, k) * scale, tn(ds, q) * scale, tn(pb, dob)

    dq, dk, dv = back(sc_ref[nprev] * inv, own_k, own_v)
    dq_acc[...] = dq
    dkv_ref[:, :HD] = dk
    dkv_ref[:, HD:] = dv

    def back_step(jb, carry):
        rows = prev_rows(jb)
        dqp, dkp, dvp = back(sc_ref[jb] * inv, pv_ref[rows, :HD], pv_ref[rows, HD:])
        dq_acc[...] += dqp
        dpv_ref[rows, :HD] = dkp.astype(BF)
        dpv_ref[rows, HD:] = dvp.astype(BF)
        return carry

    lax.fori_loop(0, n_vis, back_step, 0)

    def clear(jb, carry):
        dpv_ref[prev_rows(jb), :] = jnp.zeros((local_len, 2 * HD), BF)
        return carry

    lax.fori_loop(n_vis, nprev, clear, 0)
    rot, rest = rotate_tile(dq_acc[...], cosf[...], s1[...], s2[...], -1.0)
    dq_ref[:, :128] = rot.astype(BF)
    dq_ref[:, 128:] = rest.astype(BF)


def attn_call(meta, q, kv, pv, dob, tabs, nheads):
    local_len = tabs[0].shape[0]
    slots = q.shape[0] // local_len
    nprev = pv.shape[0] // q.shape[0]
    one = pl.BlockSpec((local_len, HD), lambda s, h, mt: (s, h))
    two = pl.BlockSpec((local_len, 2 * HD), lambda s, h, mt: (s, h))
    prev = pl.BlockSpec((nprev * local_len, 2 * HD), lambda s, h, mt: (s, h))
    tab = pl.BlockSpec((local_len, 128), lambda s, h, mt: (0, 0))
    m = q.shape[0]
    return pl.pallas_call(
        functools.partial(attn_kernel, nprev, local_len),
        name="attn",
        grid_spec=pltpu.PrefetchScalarGridSpec(
            num_scalar_prefetch=1,
            grid=(slots, nheads),
            in_specs=[one, two, prev, one, tab, tab, tab],
            out_specs=[one, one, two, prev],
            scratch_shapes=[
                pltpu.VMEM((nprev + 1, local_len, local_len), F32),
                pltpu.VMEM((local_len, HD), F32),
            ],
        ),
        out_shape=[
            jax.ShapeDtypeStruct((m, nheads * HD), BF),
            jax.ShapeDtypeStruct((m, nheads * HD), BF),
            jax.ShapeDtypeStruct((m, 2 * nheads * HD), F32),
            jax.ShapeDtypeStruct((nprev * m, 2 * nheads * HD), BF),
        ],
        compiler_params=params(2),
        cost_estimate=cost(12 * m * nheads * HD * (nprev + 1) * local_len, 20 * m * nheads * HD, m * nheads * (nprev + 1) * local_len),
    )(meta, q, kv, pv, dob, *tabs)


def join_kernel(nheads, dq_ref, dkv_ref, rv_ref, cosf, s1, s2, out_ref, sum_ref):
    i = pl.program_id(0)

    @pl.when(i == 0)
    def _():
        sum_ref[...] = jnp.zeros_like(sum_ref)

    for h in range(nheads):
        base = h * 3 * HD
        out_ref[:, base : base + HD] = dq_ref[:, h * HD : (h + 1) * HD]
        kc = slice(h * 2 * HD, h * 2 * HD + HD)
        vc = slice(h * 2 * HD + HD, (h + 1) * 2 * HD)
        dk = dkv_ref[:, kc] + rv_ref[:, kc].astype(F32)
        rot, rest = rotate_tile(dk, cosf[...], s1[...], s2[...], -1.0)
        out_ref[:, base + HD : base + HD + 128] = rot.astype(BF)
        out_ref[:, base + HD + 128 : base + 2 * HD] = rest.astype(BF)
        out_ref[:, base + 2 * HD : base + 3 * HD] = (dkv_ref[:, vc] + rv_ref[:, vc].astype(F32)).astype(BF)
    sum_ref[...] += jnp.sum(out_ref[...].astype(F32), axis=0, keepdims=True)


def join_call(dq, dkv, rv, tabs, nheads):
    m = dq.shape[0]
    local_len = tabs[0].shape[0]
    rows = 256
    per = local_len // rows

    def spec(c):
        return pl.BlockSpec((rows, c), lambda i: (i, 0))

    tab = pl.BlockSpec((rows, 128), lambda i: (i % per, 0))
    n = 3 * nheads * HD
    return pl.pallas_call(
        functools.partial(join_kernel, nheads),
        name="join",
        grid=(m // rows,),
        in_specs=[spec(nheads * HD), spec(2 * nheads * HD), spec(2 * nheads * HD), tab, tab, tab],
        out_specs=[spec(n), pl.BlockSpec((1, n), lambda i: (0, 0))],
        out_shape=[jax.ShapeDtypeStruct((m, n), BF), jax.ShapeDtypeStruct((1, n), F32)],
        compiler_params=params(1),
        cost_estimate=cost(10 * m * n, 8 * m * n),
    )(dq, dkv, rv, *tabs)


def hidden_kernel(h2, w0, w1, w2, w3, w4, w5, b_ref, gb_ref, dg_ref):
    u = nn_rows(h2, (w0, w1, w2, w3, w4, w5)) + b_ref[...]
    cdf = 0.5 * (1.0 + lax.erf(u * inv_sqrt_two))
    gb_ref[...] = (u * cdf).astype(BF)
    dg_ref[...] = (cdf + u * (jnp.exp(-0.5 * u * u) * inv_sqrt_tau)).astype(BF)


def hidden_call(h2, pieces, b_in):
    m, d = h2.shape
    f = pieces[0].shape[1]
    t = 256
    col = pl.BlockSpec((m, t), lambda j: (0, j))
    w_specs = [pl.BlockSpec((p.shape[0], t), lambda j: (0, j)) for p in pieces]
    return pl.pallas_call(
        hidden_kernel,
        name="hidden",
        grid=(f // t,),
        in_specs=[pl.BlockSpec((m, d), lambda j: (0, 0)), *w_specs, pl.BlockSpec((1, t), lambda j: (0, j))],
        out_specs=[col, col],
        out_shape=[jax.ShapeDtypeStruct((m, f), BF)] * 2,
        compiler_params=params(1),
        cost_estimate=cost(2 * m * d * f, 2 * (m * d + d * f + 2 * m * f), 2 * m * f),
    )(h2, *pieces, b_in)


def dhid_kernel(g, w0, w1, w2, w3, w4, w5, dg_ref, du_ref, sum_ref):
    a = nn_rows(g, (w0, w1, w2, w3, w4, w5))
    du = (a * dg_ref[...].astype(F32)).astype(BF)
    du_ref[...] = du
    sum_ref[...] = jnp.sum(du.astype(F32), axis=0, keepdims=True)


def dhid_call(g, pieces, dg):
    m, d = g.shape
    f = dg.shape[1]
    t = 256
    col = pl.BlockSpec((m, t), lambda j: (0, j))
    w_specs = [pl.BlockSpec((p.shape[0], t), lambda j: (0, j)) for p in pieces]
    return pl.pallas_call(
        dhid_kernel,
        name="dhid",
        grid=(f // t,),
        in_specs=[pl.BlockSpec((m, d), lambda j: (0, 0))] + w_specs + [col],
        out_specs=[col, pl.BlockSpec((1, t), lambda j: (0, j))],
        out_shape=[jax.ShapeDtypeStruct((m, f), BF), jax.ShapeDtypeStruct((1, f), F32)],
        compiler_params=params(1),
        cost_estimate=cost(2 * m * d * f, 2 * (m * d + d * f + 2 * m * f)),
    )(g, *pieces, dg)


def out_kernel(count, ob, gb, *refs):
    j = pl.program_id(0)
    ps, os, ya, yb = refs[:count], refs[count : 2 * count], refs[-2], refs[-1]
    each = 4 // count
    for k in range(4):

        @pl.when(j == k)
        def _():
            y = ya if k < 2 else yb
            y[...] = (nt(ob[...], ps[k // each][...]) + nt(gb[...], os[k // each][...])).astype(BF)


def piece_spec(count, i, cols, at=0, prefetch=False):
    each = 4 // count

    def place(j, *_):
        return (jnp.clip(j - i * each, 0, each - 1), at)

    if prefetch:
        return pl.BlockSpec((256, cols), lambda j, mt: place(j))
    return pl.BlockSpec((256, cols), lambda j: place(j))


def out_call(ob, gb, proj, out, scale=COST_SCALE):
    m, f = gb.shape
    nf = ob.shape[1]
    count = len(out)
    last = proj[0].shape[1] // nf - 1
    part = jax.ShapeDtypeStruct((m, 512), BF)
    return pl.pallas_call(
        functools.partial(out_kernel, count),
        name="outp",
        grid=(4,),
        in_specs=[pl.BlockSpec((m, nf), lambda j: (0, 0)), pl.BlockSpec((m, f), lambda j: (0, 0))]
        + [piece_spec(count, i, nf, last) for i in range(count)]
        + [piece_spec(count, i, f) for i in range(count)],
        out_specs=[
            pl.BlockSpec((m, 256), lambda j: (0, jnp.minimum(j, 1))),
            pl.BlockSpec((m, 256), lambda j: (0, jnp.maximum(j - 2, 0))),
        ],
        out_shape=[part, part],
        compiler_params=params(1),
        cost_estimate=cost(2048 * m * (f + nf), 2 * (m * f + m * nf + 1024 * (f + nf) + 1024 * m), k=scale),
    )(ob, gb, *proj, *out)


def back_kernel(meta, dqkv, du, w10, w11, w12, w20, w21, w22, x_ref, st_ref, ga, gf, prev, da_ref, db_ref, sums_ref):
    j = pl.program_id(0)
    for w1, w2, dn_ref, mine in ((w10, w20, da_ref, j < 2), (w11, w21, db_ref, j == 2), (w12, w22, db_ref, j == 3)):

        @pl.when(mine)
        def _():
            dh1 = nt(dqkv[...], w1[...])
            dh2 = nt(du[...], w2[...])
            xh = (x_ref[...].astype(F32) - st_ref[:, 0:1]) * st_ref[:, 1:2]
            dn_ref[...] = (dh1 * ga[...] + dh2 * gf[...]).astype(BF)
            sums_ref[0:1, :] = jnp.sum(dh1 * xh, axis=0, keepdims=True)
            sums_ref[1:2, :] = jnp.sum(dh1, axis=0, keepdims=True)
            sums_ref[2:3, :] = jnp.sum(dh2 * xh, axis=0, keepdims=True)
            sums_ref[3:4, :] = jnp.sum(dh2, axis=0, keepdims=True)


def back_call(meta, dqkv, du, g1, g2, x2, st, ga, gf, sums, half):
    m, d = x2.shape
    nq = dqkv.shape[1]
    f = du.shape[1]
    n = d // 4

    def absolute(rows):
        return pl.BlockSpec((rows, 256), lambda j, mt: (0, mt[1 + 4 * half + j]))

    part = jax.ShapeDtypeStruct((m, n), BF)
    at = slice(3 * half, 3 * half + 3)
    return pl.pallas_call(
        back_kernel,
        name="backn",
        grid_spec=pltpu.PrefetchScalarGridSpec(
            num_scalar_prefetch=1,
            grid=(4,),
            in_specs=[
                pl.BlockSpec((m, nq), lambda j, mt: (0, 0)),
                pl.BlockSpec((m, f), lambda j, mt: (0, 0)),
                pl.BlockSpec((256, nq), lambda j, mt: (jnp.minimum(j, 1), 0)),
                pl.BlockSpec((256, nq), lambda j, mt: (0, 0)),
                pl.BlockSpec((256, nq), lambda j, mt: (0, 0)),
                pl.BlockSpec((256, f), lambda j, mt: (jnp.minimum(j, 1), 0)),
                pl.BlockSpec((256, f), lambda j, mt: (0, 0)),
                pl.BlockSpec((256, f), lambda j, mt: (0, 0)),
                absolute(m),
                pl.BlockSpec((m, 128), lambda j, mt: (0, 0)),
                absolute(1),
                absolute(1),
                pl.BlockSpec(memory_space=pl.ANY),
            ],
            out_specs=[
                pl.BlockSpec((m, n // 2), lambda j, mt: (0, jnp.minimum(j, 1))),
                pl.BlockSpec((m, n // 2), lambda j, mt: (0, jnp.maximum(j - 2, 0))),
                absolute(4),
            ],
        ),
        out_shape=[part, part, jax.ShapeDtypeStruct((4, d), F32)],
        input_output_aliases={13: 2},
        compiler_params=params(1),
        cost_estimate=cost(4 * m * n * (f + nq), 2 * (m * f + m * nq + 2 * n * (f + nq) + 4 * m * n)),
    )(meta, dqkv, du, *g1[at], *g2[at], x2, st, ga, gf, sums)


def wgrad_kernel(pairs, adds, split, meta, *refs):
    j = pl.program_id(0)
    start = 0
    for p, count in enumerate(pairs):
        a, b = refs[2 * p], refs[2 * p + 1]

        @pl.when((j >= start) & (j < start + count))
        def _():
            y = tn(a[...], b[...])
            if adds:
                y = y + refs[2 * len(pairs)][...].astype(F32)
            if not split:
                refs[-1][...] = y.astype(BF)
                return
            keep, send = refs[-2:]
            n = y.shape[0] // 4
            swap = meta[2 + NBLK] > 0
            keep[:n] = y[:n].astype(BF)
            keep[n:] = jnp.where(swap, y[2 * n : 3 * n], y[n : 2 * n]).astype(BF)
            send[:n] = jnp.where(swap, y[n : 2 * n], y[2 * n : 3 * n]).astype(BF)
            send[n:] = y[3 * n :].astype(BF)

        start += count


def wgrad_call(meta, *flat, half, add=None, split=False):
    pairs = list(zip(flat[::2], flat[1::2]))
    m, d = pairs[0][0].shape
    t = 512
    counts = tuple(b.shape[1] // t for _, b in pairs)
    total = sum(counts)
    in_specs, ops, start = [], [], 0
    for (a, b), c in zip(pairs, counts):
        in_specs.append(pl.BlockSpec((m, d // 2), lambda j, mt: (0, half)))
        in_specs.append(
            pl.BlockSpec((m, t), lambda j, mt, s=start, c=c: (0, jnp.clip(j - s, 0, c - 1)))
        )
        ops += [a, b]
        start += c
    rows = d // 4 if split else d // 2
    if add is not None:
        in_specs.append(pl.BlockSpec((d // 2, t), lambda j, mt: (0, j)))
        ops.append(add)
    out_spec = pl.BlockSpec((rows, t), lambda j, mt: (0, j))
    out_shape = jax.ShapeDtypeStruct((rows, total * t), BF)
    return pl.pallas_call(
        functools.partial(wgrad_kernel, counts, add is not None, split),
        name="wgrad",
        grid_spec=pltpu.PrefetchScalarGridSpec(
            num_scalar_prefetch=1,
            grid=(total,),
            in_specs=in_specs,
            out_specs=[out_spec, out_spec] if split else out_spec,
        ),
        out_shape=[out_shape, out_shape] if split else out_shape,
        compiler_params=params(1),
        cost_estimate=cost(m * d * total * t, 2 * (m * d // 2 * len(pairs) + m * total * t + d * total * t)),
    )(meta, *ops)


def pack_kernel(*refs):
    out, at = refs[-1], 0
    for ref in refs[:-1]:
        n = ref.shape[0]
        out[at : at + n] = ref[...]
        at += n


def pack_call(*pieces):
    rows = sum(p.shape[0] for p in pieces)
    cols = pieces[0].shape[1]
    t = 512
    return pl.pallas_call(
        pack_kernel,
        name="pack",
        grid=(cols // t,),
        in_specs=[pl.BlockSpec((p.shape[0], t), lambda j: (0, j)) for p in pieces],
        out_specs=pl.BlockSpec((rows, t), lambda j: (0, j)),
        out_shape=jax.ShapeDtypeStruct((rows, cols), BF),
        compiler_params=params(1),
        cost_estimate=cost(0, 4 * rows * cols),
    )(*pieces)


def half_sum_kernel(keep, got, mid, send):
    n = mid.shape[0]
    mid[...] = keep[:n].astype(F32) + got[:n].astype(F32)
    send[...] = (keep[n:].astype(F32) + got[n:].astype(F32)).astype(BF)


def half_sum_call(keep, got):
    rows, cols = keep.shape
    t = 512
    n = rows // 2
    small = pl.BlockSpec((n, t), lambda j: (0, j))
    return pl.pallas_call(
        half_sum_kernel,
        name="hsum",
        grid=(cols // t,),
        in_specs=[pl.BlockSpec((rows, t), lambda j: (0, j))] * 2,
        out_specs=[small] * 2,
        out_shape=[jax.ShapeDtypeStruct((n, cols), F32), jax.ShapeDtypeStruct((n, cols), BF)],
        compiler_params=params(1),
        cost_estimate=cost(4 * n * cols, 14 * n * cols),
    )(keep, got)


def last_sum_kernel(plan, mid, got, *outs):
    j = pl.program_id(0)
    at = 0
    for (count, turned), out in zip(plan, outs):

        @pl.when((j >= at) & (j < at + count))
        def _():
            v = mid[...] + got[...].astype(F32)
            out[...] = v.T if turned else v

        at += count


def last_sum_call(mid, got, plan, scale):
    n, cols = mid.shape
    t = 512
    block = pl.BlockSpec((n, t), lambda j: (0, j))
    out_specs, out_shape, at = [], [], 0
    for count, turned in plan:
        def place(j, at=at, count=count):
            return jnp.clip(j - at, 0, count - 1)

        if turned:
            out_specs.append(pl.BlockSpec((t, n), lambda j, f=place: (f(j), 0)))
            out_shape.append(jax.ShapeDtypeStruct((count * t, n), F32))
        else:
            out_specs.append(pl.BlockSpec((n, t), lambda j, f=place: (0, f(j))))
            out_shape.append(jax.ShapeDtypeStruct((n, count * t), F32))
        at += count
    return pl.pallas_call(
        functools.partial(last_sum_kernel, plan),
        name="lsum",
        grid=(cols // t,),
        in_specs=[block, block],
        out_specs=out_specs,
        out_shape=out_shape,
        compiler_params=params(1),
        cost_estimate=cost(2 * n * cols, 10 * n * cols, k=scale),
    )(mid, got)


def by_role(meta, refs, body):
    @pl.when(meta[1 + NBLK] > 0)
    def _():
        body(refs[0::2])

    @pl.when(meta[1 + NBLK] == 0)
    def _():
        body(refs[1::2])


def block_out_kernel(local_len, first, meta, x_ref, b_ref, *refs):
    y_ref = refs[-1]
    rows = x_ref.shape[0]
    mask = row_valid(meta, (first + pl.program_id(0)) * rows, rows, local_len)

    def body(parts):
        for r in range(NBLK):
            col = block_cols(meta[1 + r] * 256)
            s = parts[r // 2][:, r % 2 * 256 : r % 2 * 256 + 256].astype(F32)
            y_ref[:, col] = (mask * (x_ref[:, col].astype(F32) + s + b_ref[:, col])).astype(BF)

    by_role(meta, refs[:8], body)


def input_grad_kernel(local_len, first, meta, x_ref, g_ref, st_ref, *refs):
    y_ref = refs[-1]
    rows = x_ref.shape[0]
    mask = row_valid(meta, (first + pl.program_id(0)) * rows, rows, local_len)
    mean = st_ref[:, 0:1]
    inv = st_ref[:, 1:2]
    d = x_ref.shape[1]

    def body(parts):
        def dn_of(r):
            return parts[r // 2][:, r % 2 * 256 : r % 2 * 256 + 256].astype(F32)

        one = jnp.zeros((rows, 256), F32)
        two = jnp.zeros((rows, 256), F32)
        for r in range(NBLK):
            dn = dn_of(r)
            one += dn
            two += dn * (x_ref[:, block_cols(meta[1 + r] * 256)].astype(F32) - mean)
        one = jnp.sum(one, axis=1, keepdims=True) / d
        two = jnp.sum(two, axis=1, keepdims=True) * inv / d
        slope = inv * inv * two
        shift = slope * mean - inv * one
        for r in range(NBLK):
            col = block_cols(meta[1 + r] * 256)
            y = g_ref[:, col].astype(F32) * mask + inv * dn_of(r)
            y_ref[:, col] = (y + (shift - slope * x_ref[:, col].astype(F32))).astype(BF)

    by_role(meta, refs[:8], body)


def rows_call(meta, *ops, body, name, specs, steps=None, into=None, scale=COST_SCALE):
    rows = 256
    m, d = ops[0].shape
    first, last = steps or (0, m // rows)
    made = {
        "row": pl.BlockSpec((rows, d), lambda i, mt: (first + i, 0)),
        "part": pl.BlockSpec((rows, d // 4), lambda i, mt: (first + i, 0)),
        "stat": pl.BlockSpec((rows, 128), lambda i, mt: (first + i, 0)),
        "vec": pl.BlockSpec((1, d), lambda i, mt: (0, 0)),
    }
    in_specs = [made[s] for s in specs]
    aliases = {}
    if into is not None:
        aliases = {1 + len(ops): 0}
        in_specs.append(pl.BlockSpec(memory_space=pl.ANY))
        ops += (into,)
    return pl.pallas_call(
        functools.partial(body, first),
        name=name,
        grid_spec=pltpu.PrefetchScalarGridSpec(
            num_scalar_prefetch=1,
            grid=(last - first,),
            in_specs=in_specs,
            out_specs=made["row"],
        ),
        out_shape=jax.ShapeDtypeStruct((m, d), BF),
        input_output_aliases=aliases,
        compiler_params=params(1),
        cost_estimate=cost(10 * (last - first) * rows * d, 8 * (last - first) * rows * d, k=scale),
    )(meta, *ops)


def after(v, *others):
    return lax.optimization_barrier((v,) + others)[0]


class Order:
    def __init__(self):
        self.last = ()

    def __call__(self, f, first, *rest, **named):
        out = f(after(first, *self.last), *rest, **named)
        self.last = (jax.tree.leaves(out)[0],)
        return out


def add_bf(a, b):
    return lax.optimization_barrier((a.astype(F32) + b.astype(F32)).astype(BF))


def pick_bf(a, b, middle, other):
    total = (a.astype(F32) + b.astype(F32)).astype(BF)
    return lax.optimization_barrier(jnp.where(middle > 0, total, other))


class Pipe:
    LAG = 3

    def __init__(self, run, middle, count):
        self.run, self.middle, self.count = run, middle, count
        self.parts, self.got, self.sums, self.crossed = [], [], [], []
        self.here, self.sent = [], []

    def send(self, part=None):
        step = len(self.got)
        back = step - self.LAG
        pairs = []
        v = part
        if part is not None:
            self.parts.append(part)
            pairs += [(0, 1), (3, 2)]
        if back >= 0:
            pairs += [(1, 0), (2, 3)]
            a, b = self.sums[back], self.crossed[back]
            if part is None:
                v = self.run(add_bf, a, b)
            else:
                v = self.run(pick_bf, a, b, self.middle, part)
        got = lax.ppermute(v, "tensor", pairs)
        self.got.append(got)
        if back >= 0:
            self.here.append(v)
            self.sent.append(got)

    def cross(self):
        k = len(self.sums)
        v = self.run(add_bf, self.parts[k], self.got[k])
        self.sums.append(v)
        self.crossed.append(lax.ppermute(v, "tensor", [(1, 2), (2, 1)]))


class PlainPipe:
    def __init__(self, run, middle, count):
        self.here, self.sent, self.sums = [], [], []

    def send(self, part=None):
        if part is not None:
            total = lax.psum(part, "tensor")
            self.here.append(total)
            self.sent.append(total)

    def cross(self):
        pass


class SmallMesh:
    def x(self, v):
        return lax.ppermute(v, "dp", [(0, 2), (2, 0), (1, 3), (3, 1)])

    def core(self, v):
        return lax.ppermute(v, "dp", [(0, 1), (1, 0), (2, 3), (3, 2)])

    def y(self, v):
        return lax.ppermute(v, "ctx", [(0, 1), (1, 0)])

    def perm(self):
        r = jnp.arange(NBLK, dtype=jnp.int32)
        dp = lax.axis_index("dp") ^ (((r >> 1) & 1) * 2 + (r >> 2))
        return dp * 2 + (lax.axis_index("ctx") ^ (r & 1))

    def middle(self):
        z = lax.axis_index("tensor")
        return ((z == 1) | (z == 2)).astype(jnp.int32)

    pipe = Pipe

    def first_hop(self, own, earlier=None):
        if earlier is None:
            return self.x(own), self.y(own)
        return self.x(after(own, earlier)), self.y(own)

    def second_hop(self, hop, earlier=()):
        return self.x(after(hop[1], hop[0], *earlier))

    def waited(self, hop):
        return hop

    def near_pieces(self, near):
        return near

    def near(self, run, own, hop):
        v = run(pack_call, own, hop[1])
        return v, self.core(v)

    def pieces(self, near, hop, diag, earlier=()):
        return near[0], hop[0], diag, near[1], self.core(after(hop[0], *earlier[:1])), self.core(after(diag, *earlier))

    def turn(self, v, first):
        pairs = []
        for dp in range(4):
            for c in range(2):
                to = (dp ^ 2) * 2 + c if dp % 2 != first else dp * 2 + (c ^ 1)
                pairs.append((dp * 2 + c, to))
        return lax.ppermute(v, ("dp", "ctx"), pairs)

    def scatter_cross(self, theirs):
        return self.core(theirs)

    def scatter_own(self, run, meta, pairs, got):
        keep, send = run(wgrad_call, meta, *pairs, half=0, add=got, split=True)
        return keep, self.turn(send, 1)

    def scatter_half(self, run, parts):
        mid, send = run(half_sum_call, *parts)
        return mid, self.turn(send, 0)

    def scatter_last(self, run, plan, parts, scale=COST_SCALE):
        return run(last_sum_call, *parts, plan=plan, scale=scale)

    def previous(self, kv, slots):
        return lax.ppermute(kv, "ctx", [(0, 1)])

    def give_back(self, dpv, dkv, slots):
        return dkv, lax.ppermute(dpv, "ctx", [(1, 0)])

    def small_sum(self, run, v, step):
        def add(a, b):
            return a + b

        if step == 0:
            got = self.core(v)
        elif step == 1:
            got = self.x(v)
        elif step == 2:
            got = self.y(v)
        elif step == 3:
            got = lax.ppermute(v, "tensor", [(0, 1), (1, 0), (2, 3), (3, 2)])
        else:
            got = lax.ppermute(v, "tensor", [(0, 2), (2, 0), (1, 3), (3, 1)])
        return lambda: run(add, v, got)


class AnyMesh:
    def perm(self):
        return jnp.arange(NBLK, dtype=jnp.int32)

    def middle(self):
        return jnp.ones((), jnp.int32)

    pipe = PlainPipe

    def first_hop(self, own, earlier=None):
        return lax.all_gather(own, ("dp", "ctx"), axis=0, tiled=True)

    def second_hop(self, hop, earlier=()):
        return ()

    def waited(self, hop):
        return (hop,)

    def near_pieces(self, near):
        return near

    def near(self, run, own, hop):
        return hop[:512], hop[1024:1536]

    def pieces(self, near, hop, diag, earlier=()):
        return near[0], hop[512:768], hop[768:1024], near[1], hop[1536:1792], hop[1792:]

    def scatter_cross(self, theirs):
        return theirs

    def scatter_own(self, run, meta, pairs, got):
        full = jnp.concatenate([run(wgrad_call, meta, *pairs, half=0), got], axis=0)
        return lax.psum_scatter(full, ("dp", "ctx"), scatter_dimension=0, tiled=True).astype(F32)

    def scatter_half(self, run, parts):
        return parts

    def scatter_last(self, run, plan, parts, scale=None):
        outs, at = [], 0
        for count, turned in plan:
            v = parts[:, at * 512 : (at + count) * 512]
            outs.append(v.T if turned else v)
            at += count
        return outs

    def previous(self, kv, slots):
        own = kv.reshape(slots, -1, kv.shape[1])
        full = lax.all_gather(own, "ctx", axis=1, tiled=True)
        return full.reshape(-1, kv.shape[1])

    def give_back(self, dpv, dkv, slots):
        cols = dkv.shape[1]
        full = dpv.reshape(slots, -1, cols)
        got = lax.psum_scatter(full, "ctx", scatter_dimension=1, tiled=True)
        return dkv, got.reshape(-1, cols)

    def small_sum(self, run, v, step):
        got = v
        if step == 0:
            got = lax.psum(v, ("dp", "ctx"))
        elif step == 3:
            got = lax.psum(v, "tensor")
        return lambda: got


def rotary_tables(positions):
    half_rot = ROT // 2
    lane = jnp.arange(128, dtype=jnp.int32)
    exponent = (lane % half_rot).astype(F32) * (2.0 / ROT)
    angles = positions[:, None] * jnp.exp(-math.log(10000.0) * exponent)[None, :]
    cos_all, sin_all = jnp.cos(angles), jnp.sin(angles)
    cosf = jnp.where(lane < ROT, cos_all, 1.0)
    s1 = jnp.where(lane < half_rot, -sin_all, 0.0)
    s2 = jnp.where((lane >= half_rot) & (lane < ROT), sin_all, 0.0)
    return cosf, s1, s2


def local(small, block_input, out_grad, lengths, attn_gain, attn_shift, ffn_gain, ffn_shift, w_qkv, b_qkv, w_proj, b_proj, w_in, b_in, w_out, b_out):
    comm = SmallMesh() if small else AnyMesh()
    slots, local_len, d = block_input.shape
    m = slots * local_len
    nheads = b_qkv.shape[0] // (3 * HD)
    nq = 3 * nheads * HD
    ctx = lax.axis_index("ctx")
    core = lax.axis_index("dp") % 2
    meta = jnp.concatenate(
        [ctx[None].astype(jnp.int32), comm.perm(), comm.middle()[None], core[None].astype(jnp.int32), lengths]
    )

    run = Order()
    x2 = block_input.reshape(m, d)
    og2 = out_grad.reshape(m, d)
    ga, sa, gf, sf = (v.reshape(1, d) for v in (attn_gain, attn_shift, ffn_gain, ffn_shift))
    bq = b_qkv.reshape(1, nq)
    positions = ctx * local_len + jnp.arange(local_len, dtype=jnp.int32)
    tabs = rotary_tables(positions.astype(F32))

    own1 = jnp.concatenate([w_qkv, w_proj.T], axis=1).astype(BF)
    hop1 = comm.first_hop(own1)
    own2 = w_in.astype(BF)
    own3 = w_out.T.astype(BF)
    run.last = (own1, own2, own3)
    hop2 = comm.first_hop(own2, hop1[0])
    h1, g, stats, g_sum = run(norm_call, meta, x2, og2, ga, sa, local_len)
    diag1 = comm.second_hop(hop1)
    near1 = comm.near(run, own1, hop1)
    g1 = comm.pieces(near1, hop1, diag1)
    near2 = comm.near(run, own2, hop2)
    kv = run(kv_call, h1, g1, bq, tabs, nheads)
    pv = comm.previous(kv, slots)
    diag2 = comm.second_hop(hop2, (kv,))
    hop3 = comm.first_hop(own3, diag2)
    q, dob = run(qd_call, h1, g, g1, bq, tabs, nheads)
    g2 = comm.pieces(near2, hop2, diag2, (kv, q))
    diag3 = comm.second_hop(hop3)
    h2 = run(second_norm_call, meta, x2, stats, gf, sf)
    gb, dg = run(hidden_call, h2, g2, b_in.reshape(1, -1))
    near3 = comm.near(run, own3, hop3)
    ob, dq, dkv, dpv = run(attn_call, meta, q, kv, pv, dob, tabs, nheads)
    dkv, rv = comm.give_back(dpv, dkv, slots)
    g3 = comm.near_pieces(near3)

    pipe = comm.pipe(run, meta[1 + NBLK], 8)
    ff = gb.shape[1] // 512
    out0, out2 = run(out_call, ob, gb, (g1[0], g1[3]), g3, 0.01)
    pipe.send(out0)
    pipe.send(out2)
    g3 = comm.pieces(near3, hop3, diag3, (ob, out0))
    cross3 = comm.scatter_cross(run(wgrad_call, meta, g, gb, half=1))
    far = (1, 2, 4, 5)
    out1, out3 = run(out_call, ob, gb, [g1[k] for k in far], [g3[k] for k in far])
    pipe.cross()
    pipe.send(after(out1, *pipe.sums))
    du, bin_sum = run(dhid_call, g, g3, dg)
    pipe.cross()
    state3 = comm.scatter_own(run, meta, (g, gb), cross3)
    dqkv, bqkv_sum = run(join_call, dq, dkv, rv, tabs, nheads)
    pipe.send(out3)
    gain_sums = jnp.zeros((4, d), F32)
    pipe.cross()
    dn0, dn1, gain_sums = run(back_call, meta, dqkv, du, g1, g2, x2, stats, ga, gf, gain_sums, 0)
    pipe.send(dn0)
    pipe.cross()
    pipe.send(dn1)
    state3 = comm.scatter_half(run, state3)
    dn2, dn3, gain_sums = run(back_call, meta, dqkv, du, g1, g2, x2, stats, ga, gf, gain_sums, 1)
    pipe.cross()
    pipe.send(dn2)
    small = jnp.concatenate([gain_sums.reshape(-1), g_sum.reshape(-1), bqkv_sum.reshape(-1), bin_sum.reshape(-1)])
    add = comm.small_sum(run, small, 0)
    cross2 = comm.scatter_cross(run(wgrad_call, after(meta, jax.tree.leaves(state3)[-1]), h2, du, half=1))
    small = add()
    add = comm.small_sum(run, small, 1)
    theirs1 = run(wgrad_call, meta, h1, dqkv, g, ob, half=1)
    small = add()
    pipe.cross()
    pipe.send(dn3)
    state2 = comm.scatter_own(run, meta, (h2, du), cross2)
    cross1 = comm.scatter_cross(after(theirs1, *jax.tree.leaves(state2)[:1]))
    (grad_out,) = comm.scatter_last(run, ((ff, True),), state3)
    pipe.cross()
    pipe.send()
    state1 = comm.scatter_own(run, meta, (h1, dqkv, g, ob), cross1)
    pipe.cross()
    pipe.send()
    state2 = comm.scatter_half(run, state2)

    def sums_of(order):
        return [v for c in order for v in (pipe.here[c], pipe.sent[c])]

    out_ops = (meta, x2, (b_proj + b_out).reshape(1, d), *sums_of((0, 2, 1, 3)))
    out_half = functools.partial(
        rows_call, body=functools.partial(block_out_kernel, local_len), name="bout", specs=("row", "vec") + ("part",) * 8
    )
    block_output = run(out_half, *out_ops, steps=(0, 2))
    block_output = run(out_half, *out_ops, steps=(2, 4), into=block_output, scale=0.01).reshape(slots, local_len, d)
    pipe.send()
    (grad_in,) = comm.scatter_last(run, ((ff, False),), state2, 0.01)
    add = comm.small_sum(run, after(small, pipe.sent[5], pipe.here[-1], *jax.tree.leaves(state1)[-1:]), 2)
    state1 = comm.scatter_half(run, state1)
    small = add()
    gains = small[: 4 * d]
    group = small[4 * d :]
    add = comm.small_sum(run, after(gains, *jax.tree.leaves(state1)[:1]), 3)
    input_grad = run(
        rows_call, meta, x2, og2, stats, *sums_of(range(4, 8)),
        body=functools.partial(input_grad_kernel, local_len), name="igrad", specs=("row", "row", "stat") + ("part",) * 8,
    ).reshape(slots, local_len, d)
    gains = add()
    add = comm.small_sum(run, gains, 4)
    grad_qkv, grad_proj = comm.scatter_last(run, ((nq // 512, False), (nheads * HD // 512, True)), state1)
    gains = add().reshape(4, d)
    bias_grad = group[:d]
    return (
        block_output,
        input_grad,
        gains[0],
        gains[1],
        gains[2],
        gains[3],
        grad_qkv,
        group[d : d + nq],
        grad_proj,
        bias_grad,
        grad_in,
        group[d + nq :],
        grad_out,
        bias_grad,
    )


def solution(mesh):
    small = mesh.shape["dp"] == 4 and mesh.shape["ctx"] == 2 and mesh.shape["tensor"] == 4
    placed = (
        P("dp", "ctx", None),
        P("dp", "ctx", None),
        P("dp"),
        P(),
        P(),
        P(),
        P(),
        P(("dp", "ctx"), "tensor"),
        P("tensor"),
        P("tensor", ("dp", "ctx")),
        P(),
        P(("dp", "ctx"), "tensor"),
        P("tensor"),
        P("tensor", ("dp", "ctx")),
        P(),
    )
    return jax.shard_map(
        functools.partial(local, small),
        mesh=mesh,
        in_specs=placed,
        out_specs=(
            P("dp", "ctx", None),
            P("dp", "ctx", None),
            P(),
            P(),
            P(),
            P(),
            P(("dp", "ctx"), "tensor"),
            P("tensor"),
            P("tensor", ("dp", "ctx")),
            P(),
            P(("dp", "ctx"), "tensor"),
            P("tensor"),
            P("tensor", ("dp", "ctx")),
            P(),
        ),
        check_vma=False,
    )
```

```python
import functools
import math

import jax
import jax.numpy as jnp
from jax import lax
from jax.experimental import pallas as pl
from jax.experimental.pallas import tpu as pltpu
from jax.sharding import PartitionSpec as P

HD = 256
ROT = 64
NBLK = 8
BF = jnp.bfloat16
F32 = jnp.float32

neg_big = -1e30
inv_sqrt_two = 0.7071067811865476
inv_sqrt_tau = 0.3989422804014327


COST_SCALE = 100


def cost(flops, nbytes, trans=0, k=COST_SCALE):
    flops = max(flops, 300 * nbytes)
    return pl.CostEstimate(flops=int(k * flops), bytes_accessed=int(k * nbytes), transcendentals=int(k * trans))


def params(n, mb=30):
    return pltpu.CompilerParams(
        dimension_semantics=("arbitrary",) * n, vmem_limit_bytes=int(mb * 1024 * 1024)
    )


def nn(a, b):
    return lax.dot_general(a, b, (((1,), (0,)), ((), ())), preferred_element_type=F32)


def nn_rows(a, pieces):
    total, at = None, 0
    for w in pieces:
        y = nn(a[:, at : at + w.shape[0]], w[...])
        total = y if total is None else total + y
        at += w.shape[0]
    return total


def nt(a, b):
    return lax.dot_general(a, b, (((1,), (1,)), ((), ())), preferred_element_type=F32)


def tn(a, b):
    return lax.dot_general(a, b, (((0,), (0,)), ((), ())), preferred_element_type=F32)


def block_cols(r):
    return pl.ds(pl.multiple_of(r, 128), 256)


def row_valid(meta, row0, rows, local_len):
    slot = row0 // local_len
    pos = meta[0] * local_len + row0 % local_len + lax.broadcasted_iota(jnp.int32, (rows, 1), 0)
    return (pos < meta[3 + NBLK + slot]).astype(F32)


def norm_kernel(local_len, meta, x_ref, g_ref, ga, sa, h1_ref, g_out, st_ref, gs_ref):
    rows = x_ref.shape[0]
    i = pl.program_id(0)
    x = x_ref[...].astype(F32)
    mean = jnp.mean(x, axis=-1, keepdims=True)
    cen = x - mean
    inv = lax.rsqrt(jnp.mean(cen * cen, axis=-1, keepdims=True) + 1e-05)
    mask = row_valid(meta, i * rows, rows, local_len)
    lane = lax.broadcasted_iota(jnp.int32, (rows, 128), 1)
    st_ref[...] = jnp.where(lane == 0, mean, inv)
    for r in range(NBLK):
        src = block_cols(meta[1 + r] * 256)
        dst = slice(r * 256, (r + 1) * 256)
        xh = (x_ref[:, src].astype(F32) - mean) * inv
        h1_ref[:, dst] = (xh * ga[:, src] + sa[:, src]).astype(BF)
        gm = g_ref[:, src].astype(F32) * mask
        g_out[:, dst] = gm.astype(BF)
        part = jnp.sum(gm, axis=0, keepdims=True)

        @pl.when(i == 0)
        def _():
            gs_ref[:, src] = part

        @pl.when(i > 0)
        def _():
            gs_ref[:, src] = gs_ref[:, src] + part


def second_norm_kernel(meta, x_ref, st_ref, gf, sf, h2_ref):
    for r in range(NBLK):
        src = block_cols(meta[1 + r] * 256)
        xh = (x_ref[:, src].astype(F32) - st_ref[:, 0:1]) * st_ref[:, 1:2]
        h2_ref[:, r * 256 : (r + 1) * 256] = (xh * gf[:, src] + sf[:, src]).astype(BF)


def second_norm_call(meta, x2, st, gf, sf):
    m, d = x2.shape
    rows = 256
    row_spec = pl.BlockSpec((rows, d), lambda i, mt: (i, 0))
    vec = pl.BlockSpec((1, d), lambda i, mt: (0, 0))
    return pl.pallas_call(
        second_norm_kernel,
        name="norm2",
        grid_spec=pltpu.PrefetchScalarGridSpec(
            num_scalar_prefetch=1,
            grid=(m // rows,),
            in_specs=[row_spec, pl.BlockSpec((rows, 128), lambda i, mt: (i, 0)), vec, vec],
            out_specs=row_spec,
        ),
        out_shape=jax.ShapeDtypeStruct((m, d), BF),
        compiler_params=params(1),
        cost_estimate=cost(5 * m * d, 4 * m * d),
    )(meta, x2, st, gf, sf)


def norm_call(meta, x2, g2, ga, sa, local_len):
    m, d = x2.shape
    rows = 256
    row_spec = pl.BlockSpec((rows, d), lambda i, mt: (i, 0))
    vec = pl.BlockSpec((1, d), lambda i, mt: (0, 0))
    return pl.pallas_call(
        functools.partial(norm_kernel, local_len),
        name="norm",
        grid_spec=pltpu.PrefetchScalarGridSpec(
            num_scalar_prefetch=1,
            grid=(m // rows,),
            in_specs=[row_spec, row_spec, vec, vec],
            out_specs=[row_spec, row_spec, pl.BlockSpec((rows, 128), lambda i, mt: (i, 0)), vec],
        ),
        out_shape=[jax.ShapeDtypeStruct((m, d), BF)] * 2
        + [jax.ShapeDtypeStruct((m, 128), F32), jax.ShapeDtypeStruct((1, d), F32)],
        compiler_params=params(1),
        cost_estimate=cost(20 * m * d, 10 * m * d),
    )(meta, x2, g2, ga, sa)


def rotate_tile(y, cosf, s1, s2, sign):
    head = y[:, :128]
    rot = (
        head * cosf
        + pltpu.roll(head, 96, 1) * (s1 * sign)
        + pltpu.roll(head, 32, 1) * (s2 * sign)
    )
    return rot, y[:, 128:]


def rotated(out, y, cosf, s1, s2):
    local_len = cosf.shape[0]
    for s in range(y.shape[0] // local_len):
        rows = slice(s * local_len, (s + 1) * local_len)
        rot, rest = rotate_tile(y[rows], cosf[...], s1[...], s2[...], 1.0)
        out[rows, :128] = rot.astype(BF)
        out[rows, 128:] = rest.astype(BF)


def kv_kernel(h1, w0, w1, w2, w3, w4, w5, b_ref, cosf, s1, s2, kv_ref):
    part = lax.rem(pl.program_id(0), 2)
    y = nn_rows(h1, (w0, w1, w2, w3, w4, w5)) + b_ref[...]

    @pl.when(part == 0)
    def _():
        rotated(kv_ref, y, cosf, s1, s2)

    @pl.when(part == 1)
    def _():
        kv_ref[...] = y.astype(BF)


def kv_call(h1, pieces, b_qkv, tabs, nheads):
    m, d = h1.shape
    local_len = tabs[0].shape[0]

    def src(j):
        return (0, (j // 2) * 3 + 1 + j % 2)

    tab = pl.BlockSpec((local_len, 128), lambda j: (0, 0))
    return pl.pallas_call(
        kv_kernel,
        name="kv",
        grid=(2 * nheads,),
        in_specs=[
            pl.BlockSpec((m, d), lambda j: (0, 0)),
            *[pl.BlockSpec((p.shape[0], HD), src) for p in pieces],
            pl.BlockSpec((1, HD), src),
            tab,
            tab,
            tab,
        ],
        out_specs=pl.BlockSpec((m, HD), lambda j: (0, j)),
        out_shape=jax.ShapeDtypeStruct((m, 2 * nheads * HD), BF),
        compiler_params=params(1),
        cost_estimate=cost(4 * m * d * nheads * HD, 2 * (m * d + 2 * d * nheads * HD + 2 * m * nheads * HD)),
    )(h1, *pieces, b_qkv, *tabs)


def qd_kernel(nheads, h1, g, w0, w1, w2, w3, w4, w5, b_ref, cosf, s1, s2, q_ref, dob_ref):
    j = pl.program_id(0)
    pieces = (w0, w1, w2, w3, w4, w5)

    @pl.when(j < nheads)
    def _():
        rotated(q_ref, nn_rows(h1, pieces) + b_ref[...], cosf, s1, s2)

    @pl.when(j >= nheads)
    def _():
        dob_ref[...] = nn_rows(g, pieces).astype(BF)


def qd_call(h1, g, pieces, b_qkv, tabs, nheads):
    m, d = h1.shape
    local_len = tabs[0].shape[0]
    full = pl.BlockSpec((m, d), lambda j: (0, 0))

    def src(j):
        return (0, jnp.where(j < nheads, 3 * j, 2 * nheads + j))

    tab = pl.BlockSpec((local_len, 128), lambda j: (0, 0))
    return pl.pallas_call(
        functools.partial(qd_kernel, nheads),
        name="qd",
        grid=(2 * nheads,),
        in_specs=[
            full,
            full,
            *[pl.BlockSpec((p.shape[0], HD), src) for p in pieces],
            pl.BlockSpec((1, HD), lambda j: (0, 3 * jnp.minimum(j, nheads - 1))),
            tab,
            tab,
            tab,
        ],
        out_specs=[
            pl.BlockSpec((m, HD), lambda j: (0, jnp.minimum(j, nheads - 1))),
            pl.BlockSpec((m, HD), lambda j: (0, jnp.maximum(j - nheads, 0))),
        ],
        out_shape=[jax.ShapeDtypeStruct((m, nheads * HD), BF)] * 2,
        compiler_params=params(1),
        cost_estimate=cost(4 * m * d * nheads * HD, 2 * (2 * m * d + 2 * d * nheads * HD + 2 * m * nheads * HD)),
    )(h1, g, *pieces, b_qkv, *tabs)


def attn_kernel(nprev, local_len, meta, q_ref, kv_ref, pv_ref, dob_ref, cosf, s1, s2, ob_ref, dq_ref, dkv_ref, dpv_ref, sc_ref, dq_acc):
    slot = pl.program_id(0)
    ctx = meta[0]
    length = meta[3 + NBLK + slot]
    scale = 1.0 / math.sqrt(HD)
    n_vis = jnp.minimum(ctx, (length + local_len - 1) // local_len)
    q = q_ref[...]
    dob = dob_ref[...]
    own_k = kv_ref[:, :HD]
    own_v = kv_ref[:, HD:]

    ri = lax.broadcasted_iota(jnp.int32, (local_len, local_len), 0)
    ci = lax.broadcasted_iota(jnp.int32, (local_len, local_len), 1)
    s_own = nt(q, own_k) * scale
    s_own = jnp.where((ci <= ri) & (ci < length - ctx * local_len), s_own, neg_big)
    sc_ref[nprev] = s_own

    def prev_rows(jb):
        return pl.ds(pl.multiple_of(jb * local_len, local_len), local_len)

    def score(jb, top):
        s = nt(q, pv_ref[prev_rows(jb), :HD]) * scale
        s = jnp.where(ci[:1] < length - jb * local_len, s, neg_big)
        sc_ref[jb] = s
        return jnp.maximum(top, jnp.max(s, axis=1, keepdims=True))

    top = lax.fori_loop(0, n_vis, score, jnp.max(s_own, axis=1, keepdims=True))

    e_own = jnp.exp(sc_ref[nprev] - top)
    sc_ref[nprev] = e_own

    def expo(jb, tot):
        e = jnp.exp(sc_ref[jb] - top)
        sc_ref[jb] = e
        return tot + jnp.sum(e, axis=1, keepdims=True)

    tot = lax.fori_loop(0, n_vis, expo, jnp.sum(e_own, axis=1, keepdims=True))
    inv = 1.0 / tot
    att = nn((sc_ref[nprev] * inv).astype(BF), own_v)

    def out_step(jb, acc):
        return acc + nn((sc_ref[jb] * inv).astype(BF), pv_ref[prev_rows(jb), HD:])

    att = lax.fori_loop(0, n_vis, out_step, att)
    ob_ref[...] = att.astype(BF)
    delta = jnp.sum(dob.astype(F32) * att, axis=1, keepdims=True)

    def back(p, k, v):
        pb = p.astype(BF)
        ds = (p * (nt(dob, v) - delta)).astype(BF)
        return nn(ds, k) * scale, tn(ds, q) * scale, tn(pb, dob)

    dq, dk, dv = back(sc_ref[nprev] * inv, own_k, own_v)
    dq_acc[...] = dq
    dkv_ref[:, :HD] = dk
    dkv_ref[:, HD:] = dv

    def back_step(jb, carry):
        rows = prev_rows(jb)
        dqp, dkp, dvp = back(sc_ref[jb] * inv, pv_ref[rows, :HD], pv_ref[rows, HD:])
        dq_acc[...] += dqp
        dpv_ref[rows, :HD] = dkp.astype(BF)
        dpv_ref[rows, HD:] = dvp.astype(BF)
        return carry

    lax.fori_loop(0, n_vis, back_step, 0)

    def clear(jb, carry):
        dpv_ref[prev_rows(jb), :] = jnp.zeros((local_len, 2 * HD), BF)
        return carry

    lax.fori_loop(n_vis, nprev, clear, 0)
    rot, rest = rotate_tile(dq_acc[...], cosf[...], s1[...], s2[...], -1.0)
    dq_ref[:, :128] = rot.astype(BF)
    dq_ref[:, 128:] = rest.astype(BF)


def attn_call(meta, q, kv, pv, dob, tabs, nheads):
    local_len = tabs[0].shape[0]
    slots = q.shape[0] // local_len
    nprev = pv.shape[0] // q.shape[0]
    one = pl.BlockSpec((local_len, HD), lambda s, h, mt: (s, h))
    two = pl.BlockSpec((local_len, 2 * HD), lambda s, h, mt: (s, h))
    prev = pl.BlockSpec((nprev * local_len, 2 * HD), lambda s, h, mt: (s, h))
    tab = pl.BlockSpec((local_len, 128), lambda s, h, mt: (0, 0))
    m = q.shape[0]
    return pl.pallas_call(
        functools.partial(attn_kernel, nprev, local_len),
        name="attn",
        grid_spec=pltpu.PrefetchScalarGridSpec(
            num_scalar_prefetch=1,
            grid=(slots, nheads),
            in_specs=[one, two, prev, one, tab, tab, tab],
            out_specs=[one, one, two, prev],
            scratch_shapes=[
                pltpu.VMEM((nprev + 1, local_len, local_len), F32),
                pltpu.VMEM((local_len, HD), F32),
            ],
        ),
        out_shape=[
            jax.ShapeDtypeStruct((m, nheads * HD), BF),
            jax.ShapeDtypeStruct((m, nheads * HD), BF),
            jax.ShapeDtypeStruct((m, 2 * nheads * HD), F32),
            jax.ShapeDtypeStruct((nprev * m, 2 * nheads * HD), BF),
        ],
        compiler_params=params(2, 30 if nprev == 1 else 60),
        cost_estimate=cost(12 * m * nheads * HD * (nprev + 1) * local_len, 20 * m * nheads * HD, m * nheads * (nprev + 1) * local_len),
    )(meta, q, kv, pv, dob, *tabs)


def join_kernel(nheads, dq_ref, dkv_ref, rv_ref, cosf, s1, s2, out_ref, sum_ref):
    i = pl.program_id(0)

    @pl.when(i == 0)
    def _():
        sum_ref[...] = jnp.zeros_like(sum_ref)

    for h in range(nheads):
        base = h * 3 * HD
        out_ref[:, base : base + HD] = dq_ref[:, h * HD : (h + 1) * HD]
        kc = slice(h * 2 * HD, h * 2 * HD + HD)
        vc = slice(h * 2 * HD + HD, (h + 1) * 2 * HD)
        dk = dkv_ref[:, kc] + rv_ref[:, kc].astype(F32)
        rot, rest = rotate_tile(dk, cosf[...], s1[...], s2[...], -1.0)
        out_ref[:, base + HD : base + HD + 128] = rot.astype(BF)
        out_ref[:, base + HD + 128 : base + 2 * HD] = rest.astype(BF)
        out_ref[:, base + 2 * HD : base + 3 * HD] = (dkv_ref[:, vc] + rv_ref[:, vc].astype(F32)).astype(BF)
    sum_ref[...] += jnp.sum(out_ref[...].astype(F32), axis=0, keepdims=True)


def join_call(dq, dkv, rv, tabs, nheads):
    m = dq.shape[0]
    local_len = tabs[0].shape[0]
    rows = 256
    per = local_len // rows

    def spec(c):
        return pl.BlockSpec((rows, c), lambda i: (i, 0))

    tab = pl.BlockSpec((rows, 128), lambda i: (i % per, 0))
    n = 3 * nheads * HD
    return pl.pallas_call(
        functools.partial(join_kernel, nheads),
        name="join",
        grid=(m // rows,),
        in_specs=[spec(nheads * HD), spec(2 * nheads * HD), spec(2 * nheads * HD), tab, tab, tab],
        out_specs=[spec(n), pl.BlockSpec((1, n), lambda i: (0, 0))],
        out_shape=[jax.ShapeDtypeStruct((m, n), BF), jax.ShapeDtypeStruct((1, n), F32)],
        compiler_params=params(1),
        cost_estimate=cost(10 * m * n, 8 * m * n),
    )(dq, dkv, rv, *tabs)


def hidden_kernel(h2, w0, w1, w2, w3, w4, w5, b_ref, gb_ref, dg_ref):
    u = nn_rows(h2, (w0, w1, w2, w3, w4, w5)) + b_ref[...]
    cdf = 0.5 * (1.0 + lax.erf(u * inv_sqrt_two))
    gb_ref[...] = (u * cdf).astype(BF)
    dg_ref[...] = (cdf + u * (jnp.exp(-0.5 * u * u) * inv_sqrt_tau)).astype(BF)


def hidden_call(h2, pieces, b_in):
    m, d = h2.shape
    f = pieces[0].shape[1]
    t = 256
    col = pl.BlockSpec((m, t), lambda j: (0, j))
    w_specs = [pl.BlockSpec((p.shape[0], t), lambda j: (0, j)) for p in pieces]
    return pl.pallas_call(
        hidden_kernel,
        name="hidden",
        grid=(f // t,),
        in_specs=[pl.BlockSpec((m, d), lambda j: (0, 0)), *w_specs, pl.BlockSpec((1, t), lambda j: (0, j))],
        out_specs=[col, col],
        out_shape=[jax.ShapeDtypeStruct((m, f), BF)] * 2,
        compiler_params=params(1),
        cost_estimate=cost(2 * m * d * f, 2 * (m * d + d * f + 2 * m * f), 2 * m * f),
    )(h2, *pieces, b_in)


def dhid_kernel(g, w0, w1, w2, w3, w4, w5, dg_ref, du_ref, sum_ref):
    a = nn_rows(g, (w0, w1, w2, w3, w4, w5))
    du = (a * dg_ref[...].astype(F32)).astype(BF)
    du_ref[...] = du
    sum_ref[...] = jnp.sum(du.astype(F32), axis=0, keepdims=True)


def dhid_call(g, pieces, dg):
    m, d = g.shape
    f = dg.shape[1]
    t = 256
    col = pl.BlockSpec((m, t), lambda j: (0, j))
    w_specs = [pl.BlockSpec((p.shape[0], t), lambda j: (0, j)) for p in pieces]
    return pl.pallas_call(
        dhid_kernel,
        name="dhid",
        grid=(f // t,),
        in_specs=[pl.BlockSpec((m, d), lambda j: (0, 0))] + w_specs + [col],
        out_specs=[col, pl.BlockSpec((1, t), lambda j: (0, j))],
        out_shape=[jax.ShapeDtypeStruct((m, f), BF), jax.ShapeDtypeStruct((1, f), F32)],
        compiler_params=params(1),
        cost_estimate=cost(2 * m * d * f, 2 * (m * d + d * f + 2 * m * f)),
    )(g, *pieces, dg)


def out_kernel(count, ob, gb, *refs):
    j = pl.program_id(0)
    ps, os, ya, yb = refs[:count], refs[count : 2 * count], refs[-2], refs[-1]
    each = 4 // count
    for k in range(4):

        @pl.when(j == k)
        def _():
            y = ya if k < 2 else yb
            y[...] = (nt(ob[...], ps[k // each][...]) + nt(gb[...], os[k // each][...])).astype(BF)


def piece_spec(count, i, cols, at=0, prefetch=False):
    each = 4 // count

    def place(j, *_):
        return (jnp.clip(j - i * each, 0, each - 1), at)

    if prefetch:
        return pl.BlockSpec((256, cols), lambda j, mt: place(j))
    return pl.BlockSpec((256, cols), lambda j: place(j))


def out_call(ob, gb, proj, out, scale=COST_SCALE):
    m, f = gb.shape
    nf = ob.shape[1]
    count = len(out)
    last = proj[0].shape[1] // nf - 1
    part = jax.ShapeDtypeStruct((m, 512), BF)
    return pl.pallas_call(
        functools.partial(out_kernel, count),
        name="outp",
        grid=(4,),
        in_specs=[pl.BlockSpec((m, nf), lambda j: (0, 0)), pl.BlockSpec((m, f), lambda j: (0, 0))]
        + [piece_spec(count, i, nf, last) for i in range(count)]
        + [piece_spec(count, i, f) for i in range(count)],
        out_specs=[
            pl.BlockSpec((m, 256), lambda j: (0, jnp.minimum(j, 1))),
            pl.BlockSpec((m, 256), lambda j: (0, jnp.maximum(j - 2, 0))),
        ],
        out_shape=[part, part],
        compiler_params=params(1),
        cost_estimate=cost(2048 * m * (f + nf), 2 * (m * f + m * nf + 1024 * (f + nf) + 1024 * m), k=scale),
    )(ob, gb, *proj, *out)


def back_kernel(meta, dqkv, du, w10, w11, w12, w20, w21, w22, x_ref, st_ref, ga, gf, prev, da_ref, db_ref, sums_ref):
    j = pl.program_id(0)
    for w1, w2, dn_ref, mine in ((w10, w20, da_ref, j < 2), (w11, w21, db_ref, j == 2), (w12, w22, db_ref, j == 3)):

        @pl.when(mine)
        def _():
            dh1 = nt(dqkv[...], w1[...])
            dh2 = nt(du[...], w2[...])
            xh = (x_ref[...].astype(F32) - st_ref[:, 0:1]) * st_ref[:, 1:2]
            dn_ref[...] = (dh1 * ga[...] + dh2 * gf[...]).astype(BF)
            sums_ref[0:1, :] = jnp.sum(dh1 * xh, axis=0, keepdims=True)
            sums_ref[1:2, :] = jnp.sum(dh1, axis=0, keepdims=True)
            sums_ref[2:3, :] = jnp.sum(dh2 * xh, axis=0, keepdims=True)
            sums_ref[3:4, :] = jnp.sum(dh2, axis=0, keepdims=True)


def back_call(meta, dqkv, du, g1, g2, x2, st, ga, gf, sums, half):
    m, d = x2.shape
    nq = dqkv.shape[1]
    f = du.shape[1]
    n = d // 4

    def absolute(rows):
        return pl.BlockSpec((rows, 256), lambda j, mt: (0, mt[1 + 4 * half + j]))

    part = jax.ShapeDtypeStruct((m, n), BF)
    at = slice(3 * half, 3 * half + 3)
    return pl.pallas_call(
        back_kernel,
        name="backn",
        grid_spec=pltpu.PrefetchScalarGridSpec(
            num_scalar_prefetch=1,
            grid=(4,),
            in_specs=[
                pl.BlockSpec((m, nq), lambda j, mt: (0, 0)),
                pl.BlockSpec((m, f), lambda j, mt: (0, 0)),
                pl.BlockSpec((256, nq), lambda j, mt: (jnp.minimum(j, 1), 0)),
                pl.BlockSpec((256, nq), lambda j, mt: (0, 0)),
                pl.BlockSpec((256, nq), lambda j, mt: (0, 0)),
                pl.BlockSpec((256, f), lambda j, mt: (jnp.minimum(j, 1), 0)),
                pl.BlockSpec((256, f), lambda j, mt: (0, 0)),
                pl.BlockSpec((256, f), lambda j, mt: (0, 0)),
                absolute(m),
                pl.BlockSpec((m, 128), lambda j, mt: (0, 0)),
                absolute(1),
                absolute(1),
                pl.BlockSpec(memory_space=pl.ANY),
            ],
            out_specs=[
                pl.BlockSpec((m, n // 2), lambda j, mt: (0, jnp.minimum(j, 1))),
                pl.BlockSpec((m, n // 2), lambda j, mt: (0, jnp.maximum(j - 2, 0))),
                absolute(4),
            ],
        ),
        out_shape=[part, part, jax.ShapeDtypeStruct((4, d), F32)],
        input_output_aliases={13: 2},
        compiler_params=params(1),
        cost_estimate=cost(4 * m * n * (f + nq), 2 * (m * f + m * nq + 2 * n * (f + nq) + 4 * m * n)),
    )(meta, dqkv, du, *g1[at], *g2[at], x2, st, ga, gf, sums)


def wgrad_kernel(pairs, adds, split, meta, *refs):
    j = pl.program_id(0)
    start = 0
    for p, count in enumerate(pairs):
        a, b = refs[2 * p], refs[2 * p + 1]

        @pl.when((j >= start) & (j < start + count))
        def _():
            y = tn(a[...], b[...])
            if adds:
                y = y + refs[2 * len(pairs)][...].astype(F32)
            if not split:
                refs[-1][...] = y.astype(BF)
                return
            keep, send = refs[-2:]
            n = y.shape[0] // 4
            swap = meta[2 + NBLK] > 0
            keep[:n] = y[:n].astype(BF)
            keep[n:] = jnp.where(swap, y[2 * n : 3 * n], y[n : 2 * n]).astype(BF)
            send[:n] = jnp.where(swap, y[n : 2 * n], y[2 * n : 3 * n]).astype(BF)
            send[n:] = y[3 * n :].astype(BF)

        start += count


def wgrad_call(meta, *flat, half, add=None, split=False):
    pairs = list(zip(flat[::2], flat[1::2]))
    m, d = pairs[0][0].shape
    t = 512
    counts = tuple(b.shape[1] // t for _, b in pairs)
    total = sum(counts)
    in_specs, ops, start = [], [], 0
    for (a, b), c in zip(pairs, counts):
        in_specs.append(pl.BlockSpec((m, d // 2), lambda j, mt: (0, half)))
        in_specs.append(
            pl.BlockSpec((m, t), lambda j, mt, s=start, c=c: (0, jnp.clip(j - s, 0, c - 1)))
        )
        ops += [a, b]
        start += c
    rows = d // 4 if split else d // 2
    if add is not None:
        in_specs.append(pl.BlockSpec((d // 2, t), lambda j, mt: (0, j)))
        ops.append(add)
    out_spec = pl.BlockSpec((rows, t), lambda j, mt: (0, j))
    out_shape = jax.ShapeDtypeStruct((rows, total * t), BF)
    return pl.pallas_call(
        functools.partial(wgrad_kernel, counts, add is not None, split),
        name="wgrad",
        grid_spec=pltpu.PrefetchScalarGridSpec(
            num_scalar_prefetch=1,
            grid=(total,),
            in_specs=in_specs,
            out_specs=[out_spec, out_spec] if split else out_spec,
        ),
        out_shape=[out_shape, out_shape] if split else out_shape,
        compiler_params=params(1),
        cost_estimate=cost(m * d * total * t, 2 * (m * d // 2 * len(pairs) + m * total * t + d * total * t)),
    )(meta, *ops)


def pack_kernel(*refs):
    out, at = refs[-1], 0
    for ref in refs[:-1]:
        n = ref.shape[0]
        out[at : at + n] = ref[...]
        at += n


def pack_call(*pieces):
    rows = sum(p.shape[0] for p in pieces)
    cols = pieces[0].shape[1]
    t = 512
    return pl.pallas_call(
        pack_kernel,
        name="pack",
        grid=(cols // t,),
        in_specs=[pl.BlockSpec((p.shape[0], t), lambda j: (0, j)) for p in pieces],
        out_specs=pl.BlockSpec((rows, t), lambda j: (0, j)),
        out_shape=jax.ShapeDtypeStruct((rows, cols), BF),
        compiler_params=params(1),
        cost_estimate=cost(0, 4 * rows * cols),
    )(*pieces)


def half_sum_kernel(keep, got, mid, send):
    n = mid.shape[0]
    mid[...] = keep[:n].astype(F32) + got[:n].astype(F32)
    send[...] = (keep[n:].astype(F32) + got[n:].astype(F32)).astype(BF)


def half_sum_call(keep, got):
    rows, cols = keep.shape
    t = 512
    n = rows // 2
    small = pl.BlockSpec((n, t), lambda j: (0, j))
    return pl.pallas_call(
        half_sum_kernel,
        name="hsum",
        grid=(cols // t,),
        in_specs=[pl.BlockSpec((rows, t), lambda j: (0, j))] * 2,
        out_specs=[small] * 2,
        out_shape=[jax.ShapeDtypeStruct((n, cols), F32), jax.ShapeDtypeStruct((n, cols), BF)],
        compiler_params=params(1),
        cost_estimate=cost(4 * n * cols, 14 * n * cols),
    )(keep, got)


def last_sum_kernel(plan, mid, got, *outs):
    j = pl.program_id(0)
    at = 0
    for (count, turned), out in zip(plan, outs):

        @pl.when((j >= at) & (j < at + count))
        def _():
            v = mid[...] + got[...].astype(F32)
            out[...] = v.T if turned else v

        at += count


def last_sum_call(mid, got, plan, scale):
    n, cols = mid.shape
    t = 512
    block = pl.BlockSpec((n, t), lambda j: (0, j))
    out_specs, out_shape, at = [], [], 0
    for count, turned in plan:
        def place(j, at=at, count=count):
            return jnp.clip(j - at, 0, count - 1)

        if turned:
            out_specs.append(pl.BlockSpec((t, n), lambda j, f=place: (f(j), 0)))
            out_shape.append(jax.ShapeDtypeStruct((count * t, n), F32))
        else:
            out_specs.append(pl.BlockSpec((n, t), lambda j, f=place: (0, f(j))))
            out_shape.append(jax.ShapeDtypeStruct((n, count * t), F32))
        at += count
    return pl.pallas_call(
        functools.partial(last_sum_kernel, plan),
        name="lsum",
        grid=(cols // t,),
        in_specs=[block, block],
        out_specs=out_specs,
        out_shape=out_shape,
        compiler_params=params(1),
        cost_estimate=cost(2 * n * cols, 10 * n * cols, k=scale),
    )(mid, got)


def by_role(meta, refs, body):
    @pl.when(meta[1 + NBLK] > 0)
    def _():
        body(refs[0::2])

    @pl.when(meta[1 + NBLK] == 0)
    def _():
        body(refs[1::2])


def block_out_kernel(local_len, first, meta, x_ref, b_ref, *refs):
    y_ref = refs[-1]
    rows = x_ref.shape[0]
    mask = row_valid(meta, (first + pl.program_id(0)) * rows, rows, local_len)

    def body(parts):
        for r in range(NBLK):
            col = block_cols(meta[1 + r] * 256)
            s = parts[r // 2][:, r % 2 * 256 : r % 2 * 256 + 256].astype(F32)
            y_ref[:, col] = (mask * (x_ref[:, col].astype(F32) + s + b_ref[:, col])).astype(BF)

    by_role(meta, refs[:8], body)


def input_grad_kernel(local_len, first, meta, x_ref, g_ref, st_ref, *refs):
    y_ref = refs[-1]
    rows = x_ref.shape[0]
    mask = row_valid(meta, (first + pl.program_id(0)) * rows, rows, local_len)
    mean = st_ref[:, 0:1]
    inv = st_ref[:, 1:2]
    d = x_ref.shape[1]

    def body(parts):
        def dn_of(r):
            return parts[r // 2][:, r % 2 * 256 : r % 2 * 256 + 256].astype(F32)

        one = jnp.zeros((rows, 256), F32)
        two = jnp.zeros((rows, 256), F32)
        for r in range(NBLK):
            dn = dn_of(r)
            one += dn
            two += dn * (x_ref[:, block_cols(meta[1 + r] * 256)].astype(F32) - mean)
        one = jnp.sum(one, axis=1, keepdims=True) / d
        two = jnp.sum(two, axis=1, keepdims=True) * inv / d
        slope = inv * inv * two
        shift = slope * mean - inv * one
        for r in range(NBLK):
            col = block_cols(meta[1 + r] * 256)
            y = g_ref[:, col].astype(F32) * mask + inv * dn_of(r)
            y_ref[:, col] = (y + (shift - slope * x_ref[:, col].astype(F32))).astype(BF)

    by_role(meta, refs[:8], body)


def rows_call(meta, *ops, body, name, specs, steps=None, into=None, scale=COST_SCALE):
    rows = 256
    m, d = ops[0].shape
    first, last = steps or (0, m // rows)
    made = {
        "row": pl.BlockSpec((rows, d), lambda i, mt: (first + i, 0)),
        "part": pl.BlockSpec((rows, d // 4), lambda i, mt: (first + i, 0)),
        "stat": pl.BlockSpec((rows, 128), lambda i, mt: (first + i, 0)),
        "vec": pl.BlockSpec((1, d), lambda i, mt: (0, 0)),
    }
    in_specs = [made[s] for s in specs]
    aliases = {}
    if into is not None:
        aliases = {1 + len(ops): 0}
        in_specs.append(pl.BlockSpec(memory_space=pl.ANY))
        ops += (into,)
    return pl.pallas_call(
        functools.partial(body, first),
        name=name,
        grid_spec=pltpu.PrefetchScalarGridSpec(
            num_scalar_prefetch=1,
            grid=(last - first,),
            in_specs=in_specs,
            out_specs=made["row"],
        ),
        out_shape=jax.ShapeDtypeStruct((m, d), BF),
        input_output_aliases=aliases,
        compiler_params=params(1),
        cost_estimate=cost(10 * (last - first) * rows * d, 8 * (last - first) * rows * d, k=scale),
    )(meta, *ops)


def after(v, *others):
    return lax.optimization_barrier((v,) + others)[0]


class Order:
    def __init__(self):
        self.last = ()

    def __call__(self, f, first, *rest, **named):
        out = f(after(first, *self.last), *rest, **named)
        self.last = (jax.tree.leaves(out)[0],)
        return out


def add_bf(a, b):
    return lax.optimization_barrier((a.astype(F32) + b.astype(F32)).astype(BF))


def pick_bf(a, b, middle, other):
    total = (a.astype(F32) + b.astype(F32)).astype(BF)
    return lax.optimization_barrier(jnp.where(middle > 0, total, other))


class Pipe:
    LAG = 3

    def __init__(self, run, middle, count):
        self.run, self.middle, self.count = run, middle, count
        self.parts, self.got, self.sums, self.crossed = [], [], [], []
        self.here, self.sent = [], []

    def send(self, part=None):
        step = len(self.got)
        back = step - self.LAG
        pairs = []
        v = part
        if part is not None:
            self.parts.append(part)
            pairs += [(0, 1), (3, 2)]
        if back >= 0:
            pairs += [(1, 0), (2, 3)]
            a, b = self.sums[back], self.crossed[back]
            if part is None:
                v = self.run(add_bf, a, b)
            else:
                v = self.run(pick_bf, a, b, self.middle, part)
        got = lax.ppermute(v, "tensor", pairs)
        self.got.append(got)
        if back >= 0:
            self.here.append(v)
            self.sent.append(got)

    def cross(self):
        k = len(self.sums)
        v = self.run(add_bf, self.parts[k], self.got[k])
        self.sums.append(v)
        self.crossed.append(lax.ppermute(v, "tensor", [(1, 2), (2, 1)]))


class PlainPipe:
    def __init__(self, run, middle, count):
        self.here, self.sent, self.sums = [], [], []

    def send(self, part=None):
        if part is not None:
            total = lax.psum(part, "tensor")
            self.here.append(total)
            self.sent.append(total)

    def cross(self):
        pass


class SmallMesh:
    def x(self, v):
        return lax.ppermute(v, "dp", [(0, 2), (2, 0), (1, 3), (3, 1)])

    def core(self, v):
        return lax.ppermute(v, "dp", [(0, 1), (1, 0), (2, 3), (3, 2)])

    def y(self, v):
        return lax.ppermute(v, "ctx", [(0, 1), (1, 0)])

    def perm(self):
        r = jnp.arange(NBLK, dtype=jnp.int32)
        dp = lax.axis_index("dp") ^ (((r >> 1) & 1) * 2 + (r >> 2))
        return dp * 2 + (lax.axis_index("ctx") ^ (r & 1))

    def middle(self):
        z = lax.axis_index("tensor")
        return ((z == 1) | (z == 2)).astype(jnp.int32)

    pipe = Pipe

    def first_hop(self, own, earlier=None):
        if earlier is None:
            return self.x(own), self.y(own)
        return self.x(after(own, earlier)), self.y(own)

    def second_hop(self, hop, earlier=()):
        return self.x(after(hop[1], hop[0], *earlier))

    def waited(self, hop):
        return hop

    def near_pieces(self, near):
        return near

    def near(self, run, own, hop):
        v = run(pack_call, own, hop[1])
        return v, self.core(v)

    def pieces(self, near, hop, diag, earlier=()):
        return near[0], hop[0], diag, near[1], self.core(after(hop[0], *earlier[:1])), self.core(after(diag, *earlier))

    def turn(self, v, first):
        pairs = []
        for dp in range(4):
            for c in range(2):
                to = (dp ^ 2) * 2 + c if dp % 2 != first else dp * 2 + (c ^ 1)
                pairs.append((dp * 2 + c, to))
        return lax.ppermute(v, ("dp", "ctx"), pairs)

    def scatter_cross(self, theirs):
        return self.core(theirs)

    def scatter_own(self, run, meta, pairs, got):
        keep, send = run(wgrad_call, meta, *pairs, half=0, add=got, split=True)
        return keep, self.turn(send, 1)

    def scatter_half(self, run, parts):
        mid, send = run(half_sum_call, *parts)
        return mid, self.turn(send, 0)

    def scatter_last(self, run, plan, parts, scale=COST_SCALE):
        return run(last_sum_call, *parts, plan=plan, scale=scale)

    def previous(self, kv, slots):
        return lax.ppermute(kv, "ctx", [(0, 1)])

    def give_back(self, dpv, dkv, slots):
        return dkv, lax.ppermute(dpv, "ctx", [(1, 0)])

    def small_sum(self, run, v, step):
        def add(a, b):
            return a + b

        if step == 0:
            got = self.core(v)
        elif step == 1:
            got = self.x(v)
        elif step == 2:
            got = self.y(v)
        elif step == 3:
            got = lax.ppermute(v, "tensor", [(0, 1), (1, 0), (2, 3), (3, 2)])
        else:
            got = lax.ppermute(v, "tensor", [(0, 2), (2, 0), (1, 3), (3, 1)])
        return lambda: run(add, v, got)


class AnyMesh:
    def perm(self):
        return jnp.arange(NBLK, dtype=jnp.int32)

    def middle(self):
        return jnp.ones((), jnp.int32)

    pipe = PlainPipe

    def first_hop(self, own, earlier=None):
        return lax.all_gather(own, ("dp", "ctx"), axis=0, tiled=True)

    def second_hop(self, hop, earlier=()):
        return ()

    def waited(self, hop):
        return (hop,)

    def near_pieces(self, near):
        return near

    def near(self, run, own, hop):
        return hop[:512], hop[1024:1536]

    def pieces(self, near, hop, diag, earlier=()):
        return near[0], hop[512:768], hop[768:1024], near[1], hop[1536:1792], hop[1792:]

    def scatter_cross(self, theirs):
        return theirs

    def scatter_own(self, run, meta, pairs, got):
        full = jnp.concatenate([run(wgrad_call, meta, *pairs, half=0), got], axis=0)
        return lax.psum_scatter(full, ("dp", "ctx"), scatter_dimension=0, tiled=True).astype(F32)

    def scatter_half(self, run, parts):
        return parts

    def scatter_last(self, run, plan, parts, scale=None):
        outs, at = [], 0
        for count, turned in plan:
            v = parts[:, at * 512 : (at + count) * 512]
            outs.append(v.T if turned else v)
            at += count
        return outs

    def previous(self, kv, slots):
        own = kv.reshape(slots, -1, kv.shape[1])
        full = lax.all_gather(own, "ctx", axis=1, tiled=True)
        return full.reshape(-1, kv.shape[1])

    def give_back(self, dpv, dkv, slots):
        cols = dkv.shape[1]
        full = dpv.reshape(slots, -1, cols)
        got = lax.psum_scatter(full, "ctx", scatter_dimension=1, tiled=True)
        return dkv, got.reshape(-1, cols)

    def small_sum(self, run, v, step):
        got = v
        if step == 0:
            got = lax.psum(v, ("dp", "ctx"))
        elif step == 3:
            got = lax.psum(v, "tensor")
        return lambda: got


def rotary_tables(positions):
    half_rot = ROT // 2
    lane = jnp.arange(128, dtype=jnp.int32)
    exponent = (lane % half_rot).astype(F32) * (2.0 / ROT)
    angles = positions[:, None] * jnp.exp(-math.log(10000.0) * exponent)[None, :]
    cos_all, sin_all = jnp.cos(angles), jnp.sin(angles)
    cosf = jnp.where(lane < ROT, cos_all, 1.0)
    s1 = jnp.where(lane < half_rot, -sin_all, 0.0)
    s2 = jnp.where((lane >= half_rot) & (lane < ROT), sin_all, 0.0)
    return cosf, s1, s2


def local(small, block_input, out_grad, lengths, attn_gain, attn_shift, ffn_gain, ffn_shift, w_qkv, b_qkv, w_proj, b_proj, w_in, b_in, w_out, b_out):
    comm = SmallMesh() if small else AnyMesh()
    slots, local_len, d = block_input.shape
    m = slots * local_len
    nheads = b_qkv.shape[0] // (3 * HD)
    nq = 3 * nheads * HD
    ctx = lax.axis_index("ctx")
    core = lax.axis_index("dp") % 2
    meta = jnp.concatenate(
        [ctx[None].astype(jnp.int32), comm.perm(), comm.middle()[None], core[None].astype(jnp.int32), lengths]
    )

    run = Order()
    x2 = block_input.reshape(m, d)
    og2 = out_grad.reshape(m, d)
    ga, sa, gf, sf = (v.reshape(1, d) for v in (attn_gain, attn_shift, ffn_gain, ffn_shift))
    bq = b_qkv.reshape(1, nq)
    positions = ctx * local_len + jnp.arange(local_len, dtype=jnp.int32)
    tabs = rotary_tables(positions.astype(F32))

    own1 = jnp.concatenate([w_qkv, w_proj.T], axis=1).astype(BF)
    hop1 = comm.first_hop(own1)
    own2 = w_in.astype(BF)
    own3 = w_out.T.astype(BF)
    run.last = (own1, own2, own3)
    hop2 = comm.first_hop(own2, hop1[0])
    h1, g, stats, g_sum = run(norm_call, meta, x2, og2, ga, sa, local_len)
    diag1 = comm.second_hop(hop1)
    near1 = comm.near(run, own1, hop1)
    g1 = comm.pieces(near1, hop1, diag1)
    near2 = comm.near(run, own2, hop2)
    kv = run(kv_call, h1, g1, bq, tabs, nheads)
    pv = comm.previous(kv, slots)
    diag2 = comm.second_hop(hop2, (kv,))
    hop3 = comm.first_hop(own3, diag2)
    q, dob = run(qd_call, h1, g, g1, bq, tabs, nheads)
    g2 = comm.pieces(near2, hop2, diag2, (kv, q))
    diag3 = comm.second_hop(hop3)
    h2 = run(second_norm_call, meta, x2, stats, gf, sf)
    gb, dg = run(hidden_call, h2, g2, b_in.reshape(1, -1))
    near3 = comm.near(run, own3, hop3)
    ob, dq, dkv, dpv = run(attn_call, meta, q, kv, pv, dob, tabs, nheads)
    dkv, rv = comm.give_back(dpv, dkv, slots)
    g3 = comm.near_pieces(near3)

    pipe = comm.pipe(run, meta[1 + NBLK], 8)
    ff = gb.shape[1] // 512
    out0, out2 = run(out_call, ob, gb, (g1[0], g1[3]), g3, 0.01)
    pipe.send(out0)
    pipe.send(out2)
    g3 = comm.pieces(near3, hop3, diag3, (ob, out0))
    cross3 = comm.scatter_cross(run(wgrad_call, meta, g, gb, half=1))
    far = (1, 2, 4, 5)
    out1, out3 = run(out_call, ob, gb, [g1[k] for k in far], [g3[k] for k in far])
    pipe.cross()
    pipe.send(after(out1, *pipe.sums))
    du, bin_sum = run(dhid_call, g, g3, dg)
    pipe.cross()
    state3 = comm.scatter_own(run, meta, (g, gb), cross3)
    dqkv, bqkv_sum = run(join_call, dq, dkv, rv, tabs, nheads)
    pipe.send(out3)
    gain_sums = jnp.zeros((4, d), F32)
    pipe.cross()
    dn0, dn1, gain_sums = run(back_call, meta, dqkv, du, g1, g2, x2, stats, ga, gf, gain_sums, 0)
    pipe.send(dn0)
    pipe.cross()
    pipe.send(dn1)
    state3 = comm.scatter_half(run, state3)
    dn2, dn3, gain_sums = run(back_call, meta, dqkv, du, g1, g2, x2, stats, ga, gf, gain_sums, 1)
    pipe.cross()
    pipe.send(dn2)
    small = jnp.concatenate([gain_sums.reshape(-1), g_sum.reshape(-1), bqkv_sum.reshape(-1), bin_sum.reshape(-1)])
    add = comm.small_sum(run, small, 0)
    cross2 = comm.scatter_cross(run(wgrad_call, after(meta, jax.tree.leaves(state3)[-1]), h2, du, half=1))
    small = add()
    add = comm.small_sum(run, small, 1)
    theirs1 = run(wgrad_call, meta, h1, dqkv, g, ob, half=1)
    small = add()
    pipe.cross()
    pipe.send(dn3)
    state2 = comm.scatter_own(run, meta, (h2, du), cross2)
    cross1 = comm.scatter_cross(after(theirs1, *jax.tree.leaves(state2)[:1]))
    (grad_out,) = comm.scatter_last(run, ((ff, True),), state3)
    pipe.cross()
    pipe.send()
    state1 = comm.scatter_own(run, meta, (h1, dqkv, g, ob), cross1)
    pipe.cross()
    pipe.send()
    state2 = comm.scatter_half(run, state2)

    def sums_of(order):
        return [v for c in order for v in (pipe.here[c], pipe.sent[c])]

    out_ops = (meta, x2, (b_proj + b_out).reshape(1, d), *sums_of((0, 2, 1, 3)))
    out_half = functools.partial(
        rows_call, body=functools.partial(block_out_kernel, local_len), name="bout", specs=("row", "vec") + ("part",) * 8
    )
    block_output = run(out_half, *out_ops, steps=(0, 2))
    block_output = run(out_half, *out_ops, steps=(2, 4), into=block_output, scale=0.01).reshape(slots, local_len, d)
    pipe.send()
    (grad_in,) = comm.scatter_last(run, ((ff, False),), state2, 0.01)
    add = comm.small_sum(run, after(small, pipe.sent[5], pipe.here[-1], *jax.tree.leaves(state1)[-1:]), 2)
    state1 = comm.scatter_half(run, state1)
    small = add()
    gains = small[: 4 * d]
    group = small[4 * d :]
    add = comm.small_sum(run, after(gains, *jax.tree.leaves(state1)[:1]), 3)
    input_grad = run(
        rows_call, meta, x2, og2, stats, *sums_of(range(4, 8)),
        body=functools.partial(input_grad_kernel, local_len), name="igrad", specs=("row", "row", "stat") + ("part",) * 8,
    ).reshape(slots, local_len, d)
    gains = add()
    add = comm.small_sum(run, gains, 4)
    grad_qkv, grad_proj = comm.scatter_last(run, ((nq // 512, False), (nheads * HD // 512, True)), state1)
    gains = add().reshape(4, d)
    bias_grad = group[:d]
    return (
        block_output,
        input_grad,
        gains[0],
        gains[1],
        gains[2],
        gains[3],
        grad_qkv,
        group[d : d + nq],
        grad_proj,
        bias_grad,
        grad_in,
        group[d + nq :],
        grad_out,
        bias_grad,
    )


def solution(mesh):
    small = mesh.shape["dp"] == 4 and mesh.shape["ctx"] == 2 and mesh.shape["tensor"] == 4
    placed = (
        P("dp", "ctx", None),
        P("dp", "ctx", None),
        P("dp"),
        P(),
        P(),
        P(),
        P(),
        P(("dp", "ctx"), "tensor"),
        P("tensor"),
        P("tensor", ("dp", "ctx")),
        P(),
        P(("dp", "ctx"), "tensor"),
        P("tensor"),
        P("tensor", ("dp", "ctx")),
        P(),
    )
    return jax.shard_map(
        functools.partial(local, small),
        mesh=mesh,
        in_specs=placed,
        out_specs=(
            P("dp", "ctx", None),
            P("dp", "ctx", None),
            P(),
            P(),
            P(),
            P(),
            P(("dp", "ctx"), "tensor"),
            P("tensor"),
            P("tensor", ("dp", "ctx")),
            P(),
            P(("dp", "ctx"), "tensor"),
            P("tensor"),
            P("tensor", ("dp", "ctx")),
            P(),
        ),
        check_vma=False,
    )
```

```python
import functools
import math

import jax
import jax.numpy as jnp
from jax import lax
from jax.experimental import pallas as pl
from jax.experimental.pallas import tpu as pltpu
from jax.sharding import PartitionSpec as P

HD = 256
ROT = 64
NBLK = 8
BF = jnp.bfloat16
F32 = jnp.float32

neg_big = -1e30
inv_sqrt_two = 0.7071067811865476
inv_sqrt_tau = 0.3989422804014327


COST_SCALE = 100


def cost(flops, nbytes, trans=0, k=COST_SCALE):
    flops = max(flops, 300 * nbytes)
    return pl.CostEstimate(flops=int(k * flops), bytes_accessed=int(k * nbytes), transcendentals=int(k * trans))


def params(n, mb=21):
    return pltpu.CompilerParams(
        dimension_semantics=("arbitrary",) * n, vmem_limit_bytes=int(mb * 1024 * 1024)
    )


def nn(a, b):
    return lax.dot_general(a, b, (((1,), (0,)), ((), ())), preferred_element_type=F32)


def nn_rows(a, pieces):
    total, at = None, 0
    for w in pieces:
        y = nn(a[:, at : at + w.shape[0]], w[...])
        total = y if total is None else total + y
        at += w.shape[0]
    return total


def nt(a, b):
    return lax.dot_general(a, b, (((1,), (1,)), ((), ())), preferred_element_type=F32)


def tn(a, b):
    return lax.dot_general(a, b, (((0,), (0,)), ((), ())), preferred_element_type=F32)


def block_cols(r):
    return pl.ds(pl.multiple_of(r, 128), 256)


def row_valid(meta, row0, rows, local_len):
    slot = row0 // local_len
    pos = meta[0] * local_len + row0 % local_len + lax.broadcasted_iota(jnp.int32, (rows, 1), 0)
    return (pos < meta[3 + NBLK + slot]).astype(F32)


def norm_kernel(local_len, meta, x_ref, g_ref, ga, sa, h1_ref, g_out, st_ref, gs_ref):
    rows = x_ref.shape[0]
    i = pl.program_id(0)
    x = x_ref[...].astype(F32)
    mean = jnp.mean(x, axis=-1, keepdims=True)
    cen = x - mean
    inv = lax.rsqrt(jnp.mean(cen * cen, axis=-1, keepdims=True) + 1e-05)
    mask = row_valid(meta, i * rows, rows, local_len)
    lane = lax.broadcasted_iota(jnp.int32, (rows, 128), 1)
    st_ref[...] = jnp.where(lane == 0, mean, inv)
    for r in range(NBLK):
        src = block_cols(meta[1 + r] * 256)
        dst = slice(r * 256, (r + 1) * 256)
        xh = (x_ref[:, src].astype(F32) - mean) * inv
        h1_ref[:, dst] = (xh * ga[:, src] + sa[:, src]).astype(BF)
        gm = g_ref[:, src].astype(F32) * mask
        g_out[:, dst] = gm.astype(BF)
        part = jnp.sum(gm, axis=0, keepdims=True)

        @pl.when(i == 0)
        def _():
            gs_ref[:, src] = part

        @pl.when(i > 0)
        def _():
            gs_ref[:, src] = gs_ref[:, src] + part


def second_norm_kernel(meta, x_ref, st_ref, gf, sf, h2_ref):
    for r in range(NBLK):
        src = block_cols(meta[1 + r] * 256)
        xh = (x_ref[:, src].astype(F32) - st_ref[:, 0:1]) * st_ref[:, 1:2]
        h2_ref[:, r * 256 : (r + 1) * 256] = (xh * gf[:, src] + sf[:, src]).astype(BF)


def second_norm_call(meta, x2, st, gf, sf):
    m, d = x2.shape
    rows = 256
    row_spec = pl.BlockSpec((rows, d), lambda i, mt: (i, 0))
    vec = pl.BlockSpec((1, d), lambda i, mt: (0, 0))
    return pl.pallas_call(
        second_norm_kernel,
        name="norm2",
        grid_spec=pltpu.PrefetchScalarGridSpec(
            num_scalar_prefetch=1,
            grid=(m // rows,),
            in_specs=[row_spec, pl.BlockSpec((rows, 128), lambda i, mt: (i, 0)), vec, vec],
            out_specs=row_spec,
        ),
        out_shape=jax.ShapeDtypeStruct((m, d), BF),
        compiler_params=params(1),
        cost_estimate=cost(5 * m * d, 4 * m * d),
    )(meta, x2, st, gf, sf)


def norm_call(meta, x2, g2, ga, sa, local_len):
    m, d = x2.shape
    rows = 256
    row_spec = pl.BlockSpec((rows, d), lambda i, mt: (i, 0))
    vec = pl.BlockSpec((1, d), lambda i, mt: (0, 0))
    return pl.pallas_call(
        functools.partial(norm_kernel, local_len),
        name="norm",
        grid_spec=pltpu.PrefetchScalarGridSpec(
            num_scalar_prefetch=1,
            grid=(m // rows,),
            in_specs=[row_spec, row_spec, vec, vec],
            out_specs=[row_spec, row_spec, pl.BlockSpec((rows, 128), lambda i, mt: (i, 0)), vec],
        ),
        out_shape=[jax.ShapeDtypeStruct((m, d), BF)] * 2
        + [jax.ShapeDtypeStruct((m, 128), F32), jax.ShapeDtypeStruct((1, d), F32)],
        compiler_params=params(1),
        cost_estimate=cost(20 * m * d, 10 * m * d),
    )(meta, x2, g2, ga, sa)


def rotate_tile(y, cosf, s1, s2, sign):
    head = y[:, :128]
    rot = (
        head * cosf
        + pltpu.roll(head, 96, 1) * (s1 * sign)
        + pltpu.roll(head, 32, 1) * (s2 * sign)
    )
    return rot, y[:, 128:]


def rotated(out, y, cosf, s1, s2):
    local_len = cosf.shape[0]
    for s in range(y.shape[0] // local_len):
        rows = slice(s * local_len, (s + 1) * local_len)
        rot, rest = rotate_tile(y[rows], cosf[...], s1[...], s2[...], 1.0)
        out[rows, :128] = rot.astype(BF)
        out[rows, 128:] = rest.astype(BF)


def kv_kernel(h1, w0, w1, w2, w3, w4, w5, b_ref, cosf, s1, s2, kv_ref):
    part = lax.rem(pl.program_id(0), 2)
    y = nn_rows(h1, (w0, w1, w2, w3, w4, w5)) + b_ref[...]

    @pl.when(part == 0)
    def _():
        rotated(kv_ref, y, cosf, s1, s2)

    @pl.when(part == 1)
    def _():
        kv_ref[...] = y.astype(BF)


def kv_call(h1, pieces, b_qkv, tabs, nheads):
    m, d = h1.shape
    local_len = tabs[0].shape[0]

    def src(j):
        return (0, (j // 2) * 3 + 1 + j % 2)

    tab = pl.BlockSpec((local_len, 128), lambda j: (0, 0))
    return pl.pallas_call(
        kv_kernel,
        name="kv",
        grid=(2 * nheads,),
        in_specs=[
            pl.BlockSpec((m, d), lambda j: (0, 0)),
            *[pl.BlockSpec((p.shape[0], HD), src) for p in pieces],
            pl.BlockSpec((1, HD), src),
            tab,
            tab,
            tab,
        ],
        out_specs=pl.BlockSpec((m, HD), lambda j: (0, j)),
        out_shape=jax.ShapeDtypeStruct((m, 2 * nheads * HD), BF),
        compiler_params=params(1),
        cost_estimate=cost(4 * m * d * nheads * HD, 2 * (m * d + 2 * d * nheads * HD + 2 * m * nheads * HD)),
    )(h1, *pieces, b_qkv, *tabs)


def qd_kernel(nheads, h1, g, w0, w1, w2, w3, w4, w5, b_ref, cosf, s1, s2, q_ref, dob_ref):
    j = pl.program_id(0)
    pieces = (w0, w1, w2, w3, w4, w5)

    @pl.when(j < nheads)
    def _():
        rotated(q_ref, nn_rows(h1, pieces) + b_ref[...], cosf, s1, s2)

    @pl.when(j >= nheads)
    def _():
        dob_ref[...] = nn_rows(g, pieces).astype(BF)


def qd_call(h1, g, pieces, b_qkv, tabs, nheads):
    m, d = h1.shape
    local_len = tabs[0].shape[0]
    full = pl.BlockSpec((m, d), lambda j: (0, 0))

    def src(j):
        return (0, jnp.where(j < nheads, 3 * j, 2 * nheads + j))

    tab = pl.BlockSpec((local_len, 128), lambda j: (0, 0))
    return pl.pallas_call(
        functools.partial(qd_kernel, nheads),
        name="qd",
        grid=(2 * nheads,),
        in_specs=[
            full,
            full,
            *[pl.BlockSpec((p.shape[0], HD), src) for p in pieces],
            pl.BlockSpec((1, HD), lambda j: (0, 3 * jnp.minimum(j, nheads - 1))),
            tab,
            tab,
            tab,
        ],
        out_specs=[
            pl.BlockSpec((m, HD), lambda j: (0, jnp.minimum(j, nheads - 1))),
            pl.BlockSpec((m, HD), lambda j: (0, jnp.maximum(j - nheads, 0))),
        ],
        out_shape=[jax.ShapeDtypeStruct((m, nheads * HD), BF)] * 2,
        compiler_params=params(1),
        cost_estimate=cost(4 * m * d * nheads * HD, 2 * (2 * m * d + 2 * d * nheads * HD + 2 * m * nheads * HD)),
    )(h1, g, *pieces, b_qkv, *tabs)


def attn_kernel(nprev, local_len, meta, q_ref, kv_ref, pv_ref, dob_ref, cosf, s1, s2, ob_ref, dq_ref, dkv_ref, dpv_ref, sc_ref, dq_acc):
    slot = pl.program_id(0)
    ctx = meta[0]
    length = meta[3 + NBLK + slot]
    scale = 1.0 / math.sqrt(HD)
    n_vis = jnp.minimum(ctx, (length + local_len - 1) // local_len)
    q = q_ref[...]
    dob = dob_ref[...]
    own_k = kv_ref[:, :HD]
    own_v = kv_ref[:, HD:]

    ri = lax.broadcasted_iota(jnp.int32, (local_len, local_len), 0)
    ci = lax.broadcasted_iota(jnp.int32, (local_len, local_len), 1)
    s_own = nt(q, own_k) * scale
    s_own = jnp.where((ci <= ri) & (ci < length - ctx * local_len), s_own, neg_big)
    sc_ref[nprev] = s_own

    def prev_rows(jb):
        return pl.ds(pl.multiple_of(jb * local_len, local_len), local_len)

    def score(jb, top):
        s = nt(q, pv_ref[prev_rows(jb), :HD]) * scale
        s = jnp.where(ci[:1] < length - jb * local_len, s, neg_big)
        sc_ref[jb] = s
        return jnp.maximum(top, jnp.max(s, axis=1, keepdims=True))

    top = lax.fori_loop(0, n_vis, score, jnp.max(s_own, axis=1, keepdims=True))

    e_own = jnp.exp(sc_ref[nprev] - top)
    sc_ref[nprev] = e_own

    def expo(jb, tot):
        e = jnp.exp(sc_ref[jb] - top)
        sc_ref[jb] = e
        return tot + jnp.sum(e, axis=1, keepdims=True)

    tot = lax.fori_loop(0, n_vis, expo, jnp.sum(e_own, axis=1, keepdims=True))
    inv = 1.0 / tot
    att = nn((sc_ref[nprev] * inv).astype(BF), own_v)

    def out_step(jb, acc):
        return acc + nn((sc_ref[jb] * inv).astype(BF), pv_ref[prev_rows(jb), HD:])

    att = lax.fori_loop(0, n_vis, out_step, att)
    ob_ref[...] = att.astype(BF)
    delta = jnp.sum(dob.astype(F32) * att, axis=1, keepdims=True)

    def back(p, k, v):
        pb = p.astype(BF)
        ds = (p * (nt(dob, v) - delta)).astype(BF)
        return nn(ds, k) * scale, tn(ds, q) * scale, tn(pb, dob)

    dq, dk, dv = back(sc_ref[nprev] * inv, own_k, own_v)
    dq_acc[...] = dq
    dkv_ref[:, :HD] = dk
    dkv_ref[:, HD:] = dv

    def back_step(jb, carry):
        rows = prev_rows(jb)
        dqp, dkp, dvp = back(sc_ref[jb] * inv, pv_ref[rows, :HD], pv_ref[rows, HD:])
        dq_acc[...] += dqp
        dpv_ref[rows, :HD] = dkp.astype(BF)
        dpv_ref[rows, HD:] = dvp.astype(BF)
        return carry

    lax.fori_loop(0, n_vis, back_step, 0)

    def clear(jb, carry):
        dpv_ref[prev_rows(jb), :] = jnp.zeros((local_len, 2 * HD), BF)
        return carry

    lax.fori_loop(n_vis, nprev, clear, 0)
    rot, rest = rotate_tile(dq_acc[...], cosf[...], s1[...], s2[...], -1.0)
    dq_ref[:, :128] = rot.astype(BF)
    dq_ref[:, 128:] = rest.astype(BF)


def attn_call(meta, q, kv, pv, dob, tabs, nheads):
    local_len = tabs[0].shape[0]
    slots = q.shape[0] // local_len
    nprev = pv.shape[0] // q.shape[0]
    one = pl.BlockSpec((local_len, HD), lambda s, h, mt: (s, h))
    two = pl.BlockSpec((local_len, 2 * HD), lambda s, h, mt: (s, h))
    prev = pl.BlockSpec((nprev * local_len, 2 * HD), lambda s, h, mt: (s, h))
    tab = pl.BlockSpec((local_len, 128), lambda s, h, mt: (0, 0))
    m = q.shape[0]
    return pl.pallas_call(
        functools.partial(attn_kernel, nprev, local_len),
        name="attn",
        grid_spec=pltpu.PrefetchScalarGridSpec(
            num_scalar_prefetch=1,
            grid=(slots, nheads),
            in_specs=[one, two, prev, one, tab, tab, tab],
            out_specs=[one, one, two, prev],
            scratch_shapes=[
                pltpu.VMEM((nprev + 1, local_len, local_len), F32),
                pltpu.VMEM((local_len, HD), F32),
            ],
        ),
        out_shape=[
            jax.ShapeDtypeStruct((m, nheads * HD), BF),
            jax.ShapeDtypeStruct((m, nheads * HD), BF),
            jax.ShapeDtypeStruct((m, 2 * nheads * HD), F32),
            jax.ShapeDtypeStruct((nprev * m, 2 * nheads * HD), BF),
        ],
        compiler_params=params(2, 21 if nprev == 1 else 60),
        cost_estimate=cost(12 * m * nheads * HD * (nprev + 1) * local_len, 20 * m * nheads * HD, m * nheads * (nprev + 1) * local_len),
    )(meta, q, kv, pv, dob, *tabs)


def join_kernel(nheads, dq_ref, dkv_ref, rv_ref, cosf, s1, s2, out_ref, sum_ref):
    i = pl.program_id(0)

    @pl.when(i == 0)
    def _():
        sum_ref[...] = jnp.zeros_like(sum_ref)

    for h in range(nheads):
        base = h * 3 * HD
        out_ref[:, base : base + HD] = dq_ref[:, h * HD : (h + 1) * HD]
        kc = slice(h * 2 * HD, h * 2 * HD + HD)
        vc = slice(h * 2 * HD + HD, (h + 1) * 2 * HD)
        dk = dkv_ref[:, kc] + rv_ref[:, kc].astype(F32)
        rot, rest = rotate_tile(dk, cosf[...], s1[...], s2[...], -1.0)
        out_ref[:, base + HD : base + HD + 128] = rot.astype(BF)
        out_ref[:, base + HD + 128 : base + 2 * HD] = rest.astype(BF)
        out_ref[:, base + 2 * HD : base + 3 * HD] = (dkv_ref[:, vc] + rv_ref[:, vc].astype(F32)).astype(BF)
    sum_ref[...] += jnp.sum(out_ref[...].astype(F32), axis=0, keepdims=True)


def join_call(dq, dkv, rv, tabs, nheads):
    m = dq.shape[0]
    local_len = tabs[0].shape[0]
    rows = 256
    per = local_len // rows

    def spec(c):
        return pl.BlockSpec((rows, c), lambda i: (i, 0))

    tab = pl.BlockSpec((rows, 128), lambda i: (i % per, 0))
    n = 3 * nheads * HD
    return pl.pallas_call(
        functools.partial(join_kernel, nheads),
        name="join",
        grid=(m // rows,),
        in_specs=[spec(nheads * HD), spec(2 * nheads * HD), spec(2 * nheads * HD), tab, tab, tab],
        out_specs=[spec(n), pl.BlockSpec((1, n), lambda i: (0, 0))],
        out_shape=[jax.ShapeDtypeStruct((m, n), BF), jax.ShapeDtypeStruct((1, n), F32)],
        compiler_params=params(1),
        cost_estimate=cost(10 * m * n, 8 * m * n),
    )(dq, dkv, rv, *tabs)


def hidden_kernel(h2, w0, w1, w2, w3, w4, w5, b_ref, gb_ref, dg_ref):
    u = nn_rows(h2, (w0, w1, w2, w3, w4, w5)) + b_ref[...]
    cdf = 0.5 * (1.0 + lax.erf(u * inv_sqrt_two))
    gb_ref[...] = (u * cdf).astype(BF)
    dg_ref[...] = (cdf + u * (jnp.exp(-0.5 * u * u) * inv_sqrt_tau)).astype(BF)


def hidden_call(h2, pieces, b_in):
    m, d = h2.shape
    f = pieces[0].shape[1]
    t = 256
    col = pl.BlockSpec((m, t), lambda j: (0, j))
    w_specs = [pl.BlockSpec((p.shape[0], t), lambda j: (0, j)) for p in pieces]
    return pl.pallas_call(
        hidden_kernel,
        name="hidden",
        grid=(f // t,),
        in_specs=[pl.BlockSpec((m, d), lambda j: (0, 0)), *w_specs, pl.BlockSpec((1, t), lambda j: (0, j))],
        out_specs=[col, col],
        out_shape=[jax.ShapeDtypeStruct((m, f), BF)] * 2,
        compiler_params=params(1),
        cost_estimate=cost(2 * m * d * f, 2 * (m * d + d * f + 2 * m * f), 2 * m * f),
    )(h2, *pieces, b_in)


def dhid_kernel(g, w0, w1, w2, w3, w4, w5, dg_ref, du_ref, sum_ref):
    a = nn_rows(g, (w0, w1, w2, w3, w4, w5))
    du = (a * dg_ref[...].astype(F32)).astype(BF)
    du_ref[...] = du
    sum_ref[...] = jnp.sum(du.astype(F32), axis=0, keepdims=True)


def dhid_call(g, pieces, dg):
    m, d = g.shape
    f = dg.shape[1]
    t = 256
    col = pl.BlockSpec((m, t), lambda j: (0, j))
    w_specs = [pl.BlockSpec((p.shape[0], t), lambda j: (0, j)) for p in pieces]
    return pl.pallas_call(
        dhid_kernel,
        name="dhid",
        grid=(f // t,),
        in_specs=[pl.BlockSpec((m, d), lambda j: (0, 0))] + w_specs + [col],
        out_specs=[col, pl.BlockSpec((1, t), lambda j: (0, j))],
        out_shape=[jax.ShapeDtypeStruct((m, f), BF), jax.ShapeDtypeStruct((1, f), F32)],
        compiler_params=params(1),
        cost_estimate=cost(2 * m * d * f, 2 * (m * d + d * f + 2 * m * f)),
    )(g, *pieces, dg)


def out_kernel(count, ob, gb, *refs):
    j = pl.program_id(0)
    ps, os, ya, yb = refs[:count], refs[count : 2 * count], refs[-2], refs[-1]
    each = 4 // count
    for k in range(4):

        @pl.when(j == k)
        def _():
            y = ya if k < 2 else yb
            y[...] = (nt(ob[...], ps[k // each][...]) + nt(gb[...], os[k // each][...])).astype(BF)


def piece_spec(count, i, cols, at=0, prefetch=False):
    each = 4 // count

    def place(j, *_):
        return (jnp.clip(j - i * each, 0, each - 1), at)

    if prefetch:
        return pl.BlockSpec((256, cols), lambda j, mt: place(j))
    return pl.BlockSpec((256, cols), lambda j: place(j))


def out_call(ob, gb, proj, out, scale=COST_SCALE):
    m, f = gb.shape
    nf = ob.shape[1]
    count = len(out)
    last = proj[0].shape[1] // nf - 1
    part = jax.ShapeDtypeStruct((m, 512), BF)
    return pl.pallas_call(
        functools.partial(out_kernel, count),
        name="outp",
        grid=(4,),
        in_specs=[pl.BlockSpec((m, nf), lambda j: (0, 0)), pl.BlockSpec((m, f), lambda j: (0, 0))]
        + [piece_spec(count, i, nf, last) for i in range(count)]
        + [piece_spec(count, i, f) for i in range(count)],
        out_specs=[
            pl.BlockSpec((m, 256), lambda j: (0, jnp.minimum(j, 1))),
            pl.BlockSpec((m, 256), lambda j: (0, jnp.maximum(j - 2, 0))),
        ],
        out_shape=[part, part],
        compiler_params=params(1),
        cost_estimate=cost(2048 * m * (f + nf), 2 * (m * f + m * nf + 1024 * (f + nf) + 1024 * m), k=scale),
    )(ob, gb, *proj, *out)


def back_kernel(meta, dqkv, du, w10, w11, w12, w20, w21, w22, x_ref, st_ref, ga, gf, prev, da_ref, db_ref, sums_ref):
    j = pl.program_id(0)
    for w1, w2, dn_ref, mine in ((w10, w20, da_ref, j < 2), (w11, w21, db_ref, j == 2), (w12, w22, db_ref, j == 3)):

        @pl.when(mine)
        def _():
            dh1 = nt(dqkv[...], w1[...])
            dh2 = nt(du[...], w2[...])
            xh = (x_ref[...].astype(F32) - st_ref[:, 0:1]) * st_ref[:, 1:2]
            dn_ref[...] = (dh1 * ga[...] + dh2 * gf[...]).astype(BF)
            sums_ref[0:1, :] = jnp.sum(dh1 * xh, axis=0, keepdims=True)
            sums_ref[1:2, :] = jnp.sum(dh1, axis=0, keepdims=True)
            sums_ref[2:3, :] = jnp.sum(dh2 * xh, axis=0, keepdims=True)
            sums_ref[3:4, :] = jnp.sum(dh2, axis=0, keepdims=True)


def back_call(meta, dqkv, du, g1, g2, x2, st, ga, gf, sums, half):
    m, d = x2.shape
    nq = dqkv.shape[1]
    f = du.shape[1]
    n = d // 4

    def absolute(rows):
        return pl.BlockSpec((rows, 256), lambda j, mt: (0, mt[1 + 4 * half + j]))

    part = jax.ShapeDtypeStruct((m, n), BF)
    at = slice(3 * half, 3 * half + 3)
    return pl.pallas_call(
        back_kernel,
        name="backn",
        grid_spec=pltpu.PrefetchScalarGridSpec(
            num_scalar_prefetch=1,
            grid=(4,),
            in_specs=[
                pl.BlockSpec((m, nq), lambda j, mt: (0, 0)),
                pl.BlockSpec((m, f), lambda j, mt: (0, 0)),
                pl.BlockSpec((256, nq), lambda j, mt: (jnp.minimum(j, 1), 0)),
                pl.BlockSpec((256, nq), lambda j, mt: (0, 0)),
                pl.BlockSpec((256, nq), lambda j, mt: (0, 0)),
                pl.BlockSpec((256, f), lambda j, mt: (jnp.minimum(j, 1), 0)),
                pl.BlockSpec((256, f), lambda j, mt: (0, 0)),
                pl.BlockSpec((256, f), lambda j, mt: (0, 0)),
                absolute(m),
                pl.BlockSpec((m, 128), lambda j, mt: (0, 0)),
                absolute(1),
                absolute(1),
                pl.BlockSpec(memory_space=pl.ANY),
            ],
            out_specs=[
                pl.BlockSpec((m, n // 2), lambda j, mt: (0, jnp.minimum(j, 1))),
                pl.BlockSpec((m, n // 2), lambda j, mt: (0, jnp.maximum(j - 2, 0))),
                absolute(4),
            ],
        ),
        out_shape=[part, part, jax.ShapeDtypeStruct((4, d), F32)],
        input_output_aliases={13: 2},
        compiler_params=params(1),
        cost_estimate=cost(4 * m * n * (f + nq), 2 * (m * f + m * nq + 2 * n * (f + nq) + 4 * m * n)),
    )(meta, dqkv, du, *g1[at], *g2[at], x2, st, ga, gf, sums)


def wgrad_kernel(pairs, adds, split, meta, *refs):
    j = pl.program_id(0)
    start = 0
    for p, count in enumerate(pairs):
        a, b = refs[2 * p], refs[2 * p + 1]

        @pl.when((j >= start) & (j < start + count))
        def _():
            y = tn(a[...], b[...])
            if adds:
                y = y + refs[2 * len(pairs)][...].astype(F32)
            if not split:
                refs[-1][...] = y.astype(BF)
                return
            keep, send = refs[-2:]
            n = y.shape[0] // 4
            swap = meta[2 + NBLK] > 0
            keep[:n] = y[:n].astype(BF)
            keep[n:] = jnp.where(swap, y[2 * n : 3 * n], y[n : 2 * n]).astype(BF)
            send[:n] = jnp.where(swap, y[n : 2 * n], y[2 * n : 3 * n]).astype(BF)
            send[n:] = y[3 * n :].astype(BF)

        start += count


def wgrad_call(meta, *flat, half, add=None, split=False):
    pairs = list(zip(flat[::2], flat[1::2]))
    m, d = pairs[0][0].shape
    t = 512
    counts = tuple(b.shape[1] // t for _, b in pairs)
    total = sum(counts)
    in_specs, ops, start = [], [], 0
    for (a, b), c in zip(pairs, counts):
        in_specs.append(pl.BlockSpec((m, d // 2), lambda j, mt: (0, half)))
        in_specs.append(
            pl.BlockSpec((m, t), lambda j, mt, s=start, c=c: (0, jnp.clip(j - s, 0, c - 1)))
        )
        ops += [a, b]
        start += c
    rows = d // 4 if split else d // 2
    if add is not None:
        in_specs.append(pl.BlockSpec((d // 2, t), lambda j, mt: (0, j)))
        ops.append(add)
    out_spec = pl.BlockSpec((rows, t), lambda j, mt: (0, j))
    out_shape = jax.ShapeDtypeStruct((rows, total * t), BF)
    return pl.pallas_call(
        functools.partial(wgrad_kernel, counts, add is not None, split),
        name="wgrad",
        grid_spec=pltpu.PrefetchScalarGridSpec(
            num_scalar_prefetch=1,
            grid=(total,),
            in_specs=in_specs,
            out_specs=[out_spec, out_spec] if split else out_spec,
        ),
        out_shape=[out_shape, out_shape] if split else out_shape,
        compiler_params=params(1),
        cost_estimate=cost(m * d * total * t, 2 * (m * d // 2 * len(pairs) + m * total * t + d * total * t)),
    )(meta, *ops)


def pack_kernel(*refs):
    out, at = refs[-1], 0
    for ref in refs[:-1]:
        n = ref.shape[0]
        out[at : at + n] = ref[...]
        at += n


def pack_call(*pieces):
    rows = sum(p.shape[0] for p in pieces)
    cols = pieces[0].shape[1]
    t = 512
    return pl.pallas_call(
        pack_kernel,
        name="pack",
        grid=(cols // t,),
        in_specs=[pl.BlockSpec((p.shape[0], t), lambda j: (0, j)) for p in pieces],
        out_specs=pl.BlockSpec((rows, t), lambda j: (0, j)),
        out_shape=jax.ShapeDtypeStruct((rows, cols), BF),
        compiler_params=params(1),
        cost_estimate=cost(0, 4 * rows * cols),
    )(*pieces)


def half_sum_kernel(keep, got, mid, send):
    n = mid.shape[0]
    mid[...] = keep[:n].astype(F32) + got[:n].astype(F32)
    send[...] = (keep[n:].astype(F32) + got[n:].astype(F32)).astype(BF)


def half_sum_call(keep, got):
    rows, cols = keep.shape
    t = 512
    n = rows // 2
    small = pl.BlockSpec((n, t), lambda j: (0, j))
    return pl.pallas_call(
        half_sum_kernel,
        name="hsum",
        grid=(cols // t,),
        in_specs=[pl.BlockSpec((rows, t), lambda j: (0, j))] * 2,
        out_specs=[small] * 2,
        out_shape=[jax.ShapeDtypeStruct((n, cols), F32), jax.ShapeDtypeStruct((n, cols), BF)],
        compiler_params=params(1),
        cost_estimate=cost(4 * n * cols, 14 * n * cols),
    )(keep, got)


def last_sum_kernel(plan, mid, got, *outs):
    j = pl.program_id(0)
    at = 0
    for (count, turned), out in zip(plan, outs):

        @pl.when((j >= at) & (j < at + count))
        def _():
            v = mid[...] + got[...].astype(F32)
            out[...] = v.T if turned else v

        at += count


def last_sum_call(mid, got, plan, scale):
    n, cols = mid.shape
    t = 512
    block = pl.BlockSpec((n, t), lambda j: (0, j))
    out_specs, out_shape, at = [], [], 0
    for count, turned in plan:
        def place(j, at=at, count=count):
            return jnp.clip(j - at, 0, count - 1)

        if turned:
            out_specs.append(pl.BlockSpec((t, n), lambda j, f=place: (f(j), 0)))
            out_shape.append(jax.ShapeDtypeStruct((count * t, n), F32))
        else:
            out_specs.append(pl.BlockSpec((n, t), lambda j, f=place: (0, f(j))))
            out_shape.append(jax.ShapeDtypeStruct((n, count * t), F32))
        at += count
    return pl.pallas_call(
        functools.partial(last_sum_kernel, plan),
        name="lsum",
        grid=(cols // t,),
        in_specs=[block, block],
        out_specs=out_specs,
        out_shape=out_shape,
        compiler_params=params(1),
        cost_estimate=cost(2 * n * cols, 10 * n * cols, k=scale),
    )(mid, got)


def by_role(meta, refs, body):
    @pl.when(meta[1 + NBLK] > 0)
    def _():
        body(refs[0::2])

    @pl.when(meta[1 + NBLK] == 0)
    def _():
        body(refs[1::2])


def block_out_kernel(local_len, first, meta, x_ref, b_ref, *refs):
    y_ref = refs[-1]
    rows = x_ref.shape[0]
    mask = row_valid(meta, (first + pl.program_id(0)) * rows, rows, local_len)

    def body(parts):
        for r in range(NBLK):
            col = block_cols(meta[1 + r] * 256)
            s = parts[r // 2][:, r % 2 * 256 : r % 2 * 256 + 256].astype(F32)
            y_ref[:, col] = (mask * (x_ref[:, col].astype(F32) + s + b_ref[:, col])).astype(BF)

    by_role(meta, refs[:8], body)


def input_grad_kernel(local_len, first, meta, x_ref, g_ref, st_ref, *refs):
    y_ref = refs[-1]
    rows = x_ref.shape[0]
    mask = row_valid(meta, (first + pl.program_id(0)) * rows, rows, local_len)
    mean = st_ref[:, 0:1]
    inv = st_ref[:, 1:2]
    d = x_ref.shape[1]

    def body(parts):
        def dn_of(r):
            return parts[r // 2][:, r % 2 * 256 : r % 2 * 256 + 256].astype(F32)

        one = jnp.zeros((rows, 256), F32)
        two = jnp.zeros((rows, 256), F32)
        for r in range(NBLK):
            dn = dn_of(r)
            one += dn
            two += dn * (x_ref[:, block_cols(meta[1 + r] * 256)].astype(F32) - mean)
        one = jnp.sum(one, axis=1, keepdims=True) / d
        two = jnp.sum(two, axis=1, keepdims=True) * inv / d
        slope = inv * inv * two
        shift = slope * mean - inv * one
        for r in range(NBLK):
            col = block_cols(meta[1 + r] * 256)
            y = g_ref[:, col].astype(F32) * mask + inv * dn_of(r)
            y_ref[:, col] = (y + (shift - slope * x_ref[:, col].astype(F32))).astype(BF)

    by_role(meta, refs[:8], body)


def rows_call(meta, *ops, body, name, specs, steps=None, into=None, scale=COST_SCALE):
    rows = 256
    m, d = ops[0].shape
    first, last = steps or (0, m // rows)
    made = {
        "row": pl.BlockSpec((rows, d), lambda i, mt: (first + i, 0)),
        "part": pl.BlockSpec((rows, d // 4), lambda i, mt: (first + i, 0)),
        "stat": pl.BlockSpec((rows, 128), lambda i, mt: (first + i, 0)),
        "vec": pl.BlockSpec((1, d), lambda i, mt: (0, 0)),
    }
    in_specs = [made[s] for s in specs]
    aliases = {}
    if into is not None:
        aliases = {1 + len(ops): 0}
        in_specs.append(pl.BlockSpec(memory_space=pl.ANY))
        ops += (into,)
    return pl.pallas_call(
        functools.partial(body, first),
        name=name,
        grid_spec=pltpu.PrefetchScalarGridSpec(
            num_scalar_prefetch=1,
            grid=(last - first,),
            in_specs=in_specs,
            out_specs=made["row"],
        ),
        out_shape=jax.ShapeDtypeStruct((m, d), BF),
        input_output_aliases=aliases,
        compiler_params=params(1),
        cost_estimate=cost(10 * (last - first) * rows * d, 8 * (last - first) * rows * d, k=scale),
    )(meta, *ops)


def after(v, *others):
    return lax.optimization_barrier((v,) + others)[0]


class Order:
    def __init__(self):
        self.last = ()

    def __call__(self, f, first, *rest, **named):
        out = f(after(first, *self.last), *rest, **named)
        self.last = (jax.tree.leaves(out)[0],)
        return out


def add_bf(a, b):
    return lax.optimization_barrier((a.astype(F32) + b.astype(F32)).astype(BF))


def pick_bf(a, b, middle, other):
    total = (a.astype(F32) + b.astype(F32)).astype(BF)
    return lax.optimization_barrier(jnp.where(middle > 0, total, other))


class Pipe:
    LAG = 3

    def __init__(self, run, middle, count):
        self.run, self.middle, self.count = run, middle, count
        self.parts, self.got, self.sums, self.crossed = [], [], [], []
        self.here, self.sent = [], []

    def send(self, part=None):
        step = len(self.got)
        back = step - self.LAG
        pairs = []
        v = part
        if part is not None:
            self.parts.append(part)
            pairs += [(0, 1), (3, 2)]
        if back >= 0:
            pairs += [(1, 0), (2, 3)]
            a, b = self.sums[back], self.crossed[back]
            if part is None:
                v = self.run(add_bf, a, b)
            else:
                v = self.run(pick_bf, a, b, self.middle, part)
        got = lax.ppermute(v, "tensor", pairs)
        self.got.append(got)
        if back >= 0:
            self.here.append(v)
            self.sent.append(got)

    def cross(self):
        k = len(self.sums)
        v = self.run(add_bf, self.parts[k], self.got[k])
        self.sums.append(v)
        self.crossed.append(lax.ppermute(v, "tensor", [(1, 2), (2, 1)]))


class PlainPipe:
    def __init__(self, run, middle, count):
        self.here, self.sent, self.sums = [], [], []

    def send(self, part=None):
        if part is not None:
            total = lax.psum(part, "tensor")
            self.here.append(total)
            self.sent.append(total)

    def cross(self):
        pass


class SmallMesh:
    def x(self, v):
        return lax.ppermute(v, "dp", [(0, 2), (2, 0), (1, 3), (3, 1)])

    def core(self, v):
        return lax.ppermute(v, "dp", [(0, 1), (1, 0), (2, 3), (3, 2)])

    def y(self, v):
        return lax.ppermute(v, "ctx", [(0, 1), (1, 0)])

    def perm(self):
        r = jnp.arange(NBLK, dtype=jnp.int32)
        dp = lax.axis_index("dp") ^ (((r >> 1) & 1) * 2 + (r >> 2))
        return dp * 2 + (lax.axis_index("ctx") ^ (r & 1))

    def middle(self):
        z = lax.axis_index("tensor")
        return ((z == 1) | (z == 2)).astype(jnp.int32)

    pipe = Pipe

    def first_hop(self, own, earlier=None):
        if earlier is None:
            return self.x(own), self.y(own)
        return self.x(after(own, earlier)), self.y(own)

    def second_hop(self, hop, earlier=()):
        return self.x(after(hop[1], hop[0], *earlier))

    def waited(self, hop):
        return hop

    def near_pieces(self, near):
        return near

    def near(self, run, own, hop):
        v = run(pack_call, own, hop[1])
        return v, self.core(v)

    def pieces(self, near, hop, diag, earlier=()):
        return near[0], hop[0], diag, near[1], self.core(after(hop[0], *earlier[:1])), self.core(after(diag, *earlier))

    def turn(self, v, first):
        pairs = []
        for dp in range(4):
            for c in range(2):
                to = (dp ^ 2) * 2 + c if dp % 2 != first else dp * 2 + (c ^ 1)
                pairs.append((dp * 2 + c, to))
        return lax.ppermute(v, ("dp", "ctx"), pairs)

    def scatter_cross(self, theirs):
        return self.core(theirs)

    def scatter_own(self, run, meta, pairs, got):
        keep, send = run(wgrad_call, meta, *pairs, half=0, add=got, split=True)
        return keep, self.turn(send, 1)

    def scatter_half(self, run, parts):
        mid, send = run(half_sum_call, *parts)
        return mid, self.turn(send, 0)

    def scatter_last(self, run, plan, parts, scale=COST_SCALE):
        return run(last_sum_call, *parts, plan=plan, scale=scale)

    def previous(self, kv, slots):
        return lax.ppermute(kv, "ctx", [(0, 1)])

    def give_back(self, dpv, dkv, slots):
        return dkv, lax.ppermute(dpv, "ctx", [(1, 0)])

    def small_sum(self, run, v, step):
        def add(a, b):
            return a + b

        if step == 0:
            got = self.core(v)
        elif step == 1:
            got = self.x(v)
        elif step == 2:
            got = self.y(v)
        elif step == 3:
            got = lax.ppermute(v, "tensor", [(0, 1), (1, 0), (2, 3), (3, 2)])
        else:
            got = lax.ppermute(v, "tensor", [(0, 2), (2, 0), (1, 3), (3, 1)])
        return lambda: run(add, v, got)


class AnyMesh:
    def perm(self):
        return jnp.arange(NBLK, dtype=jnp.int32)

    def middle(self):
        return jnp.ones((), jnp.int32)

    pipe = PlainPipe

    def first_hop(self, own, earlier=None):
        return lax.all_gather(own, ("dp", "ctx"), axis=0, tiled=True)

    def second_hop(self, hop, earlier=()):
        return ()

    def waited(self, hop):
        return (hop,)

    def near_pieces(self, near):
        return near

    def near(self, run, own, hop):
        return hop[:512], hop[1024:1536]

    def pieces(self, near, hop, diag, earlier=()):
        return near[0], hop[512:768], hop[768:1024], near[1], hop[1536:1792], hop[1792:]

    def scatter_cross(self, theirs):
        return theirs

    def scatter_own(self, run, meta, pairs, got):
        full = jnp.concatenate([run(wgrad_call, meta, *pairs, half=0), got], axis=0)
        return lax.psum_scatter(full, ("dp", "ctx"), scatter_dimension=0, tiled=True).astype(F32)

    def scatter_half(self, run, parts):
        return parts

    def scatter_last(self, run, plan, parts, scale=None):
        outs, at = [], 0
        for count, turned in plan:
            v = parts[:, at * 512 : (at + count) * 512]
            outs.append(v.T if turned else v)
            at += count
        return outs

    def previous(self, kv, slots):
        own = kv.reshape(slots, -1, kv.shape[1])
        full = lax.all_gather(own, "ctx", axis=1, tiled=True)
        return full.reshape(-1, kv.shape[1])

    def give_back(self, dpv, dkv, slots):
        cols = dkv.shape[1]
        full = dpv.reshape(slots, -1, cols)
        got = lax.psum_scatter(full, "ctx", scatter_dimension=1, tiled=True)
        return dkv, got.reshape(-1, cols)

    def small_sum(self, run, v, step):
        got = v
        if step == 0:
            got = lax.psum(v, ("dp", "ctx"))
        elif step == 3:
            got = lax.psum(v, "tensor")
        return lambda: got


def rotary_tables(positions):
    half_rot = ROT // 2
    lane = jnp.arange(128, dtype=jnp.int32)
    exponent = (lane % half_rot).astype(F32) * (2.0 / ROT)
    angles = positions[:, None] * jnp.exp(-math.log(10000.0) * exponent)[None, :]
    cos_all, sin_all = jnp.cos(angles), jnp.sin(angles)
    cosf = jnp.where(lane < ROT, cos_all, 1.0)
    s1 = jnp.where(lane < half_rot, -sin_all, 0.0)
    s2 = jnp.where((lane >= half_rot) & (lane < ROT), sin_all, 0.0)
    return cosf, s1, s2


def local(small, block_input, out_grad, lengths, attn_gain, attn_shift, ffn_gain, ffn_shift, w_qkv, b_qkv, w_proj, b_proj, w_in, b_in, w_out, b_out):
    comm = SmallMesh() if small else AnyMesh()
    slots, local_len, d = block_input.shape
    m = slots * local_len
    nheads = b_qkv.shape[0] // (3 * HD)
    nq = 3 * nheads * HD
    ctx = lax.axis_index("ctx")
    core = lax.axis_index("dp") % 2
    meta = jnp.concatenate(
        [ctx[None].astype(jnp.int32), comm.perm(), comm.middle()[None], core[None].astype(jnp.int32), lengths]
    )

    run = Order()
    x2 = block_input.reshape(m, d)
    og2 = out_grad.reshape(m, d)
    ga, sa, gf, sf = (v.reshape(1, d) for v in (attn_gain, attn_shift, ffn_gain, ffn_shift))
    bq = b_qkv.reshape(1, nq)
    positions = ctx * local_len + jnp.arange(local_len, dtype=jnp.int32)
    tabs = rotary_tables(positions.astype(F32))

    own1 = jnp.concatenate([w_qkv, w_proj.T], axis=1).astype(BF)
    hop1 = comm.first_hop(own1)
    own2 = w_in.astype(BF)
    own3 = w_out.T.astype(BF)
    run.last = (own1, own2, own3)
    hop2 = comm.first_hop(own2, hop1[0])
    h1, g, stats, g_sum = run(norm_call, meta, x2, og2, ga, sa, local_len)
    diag1 = comm.second_hop(hop1)
    near1 = comm.near(run, own1, hop1)
    g1 = comm.pieces(near1, hop1, diag1)
    near2 = comm.near(run, own2, hop2)
    kv = run(kv_call, h1, g1, bq, tabs, nheads)
    pv = comm.previous(kv, slots)
    diag2 = comm.second_hop(hop2, (kv,))
    hop3 = comm.first_hop(own3, diag2)
    q, dob = run(qd_call, h1, g, g1, bq, tabs, nheads)
    g2 = comm.pieces(near2, hop2, diag2, (kv, q))
    diag3 = comm.second_hop(hop3)
    h2 = run(second_norm_call, meta, x2, stats, gf, sf)
    gb, dg = run(hidden_call, h2, g2, b_in.reshape(1, -1))
    near3 = comm.near(run, own3, hop3)
    ob, dq, dkv, dpv = run(attn_call, meta, q, kv, pv, dob, tabs, nheads)
    dkv, rv = comm.give_back(dpv, dkv, slots)
    g3 = comm.near_pieces(near3)

    pipe = comm.pipe(run, meta[1 + NBLK], 8)
    ff = gb.shape[1] // 512
    out0, out2 = run(out_call, ob, gb, (g1[0], g1[3]), g3, 0.01)
    pipe.send(out0)
    pipe.send(out2)
    g3 = comm.pieces(near3, hop3, diag3, (ob, out0))
    cross3 = comm.scatter_cross(run(wgrad_call, meta, g, gb, half=1))
    far = (1, 2, 4, 5)
    out1, out3 = run(out_call, ob, gb, [g1[k] for k in far], [g3[k] for k in far])
    pipe.cross()
    pipe.send(after(out1, *pipe.sums))
    du, bin_sum = run(dhid_call, g, g3, dg)
    pipe.cross()
    state3 = comm.scatter_own(run, meta, (g, gb), cross3)
    dqkv, bqkv_sum = run(join_call, dq, dkv, rv, tabs, nheads)
    pipe.send(out3)
    gain_sums = jnp.zeros((4, d), F32)
    pipe.cross()
    dn0, dn1, gain_sums = run(back_call, meta, dqkv, du, g1, g2, x2, stats, ga, gf, gain_sums, 0)
    pipe.send(dn0)
    pipe.cross()
    pipe.send(dn1)
    state3 = comm.scatter_half(run, state3)
    dn2, dn3, gain_sums = run(back_call, meta, dqkv, du, g1, g2, x2, stats, ga, gf, gain_sums, 1)
    pipe.cross()
    pipe.send(dn2)
    small = jnp.concatenate([gain_sums.reshape(-1), g_sum.reshape(-1), bqkv_sum.reshape(-1), bin_sum.reshape(-1)])
    add = comm.small_sum(run, small, 0)
    cross2 = comm.scatter_cross(run(wgrad_call, after(meta, jax.tree.leaves(state3)[-1]), h2, du, half=1))
    small = add()
    add = comm.small_sum(run, small, 1)
    theirs1 = run(wgrad_call, meta, h1, dqkv, g, ob, half=1)
    small = add()
    pipe.cross()
    pipe.send(dn3)
    state2 = comm.scatter_own(run, meta, (h2, du), cross2)
    cross1 = comm.scatter_cross(after(theirs1, *jax.tree.leaves(state2)[:1]))
    (grad_out,) = comm.scatter_last(run, ((ff, True),), state3)
    pipe.cross()
    pipe.send()
    state1 = comm.scatter_own(run, meta, (h1, dqkv, g, ob), cross1)
    pipe.cross()
    pipe.send()
    state2 = comm.scatter_half(run, state2)

    def sums_of(order):
        return [v for c in order for v in (pipe.here[c], pipe.sent[c])]

    out_ops = (meta, x2, (b_proj + b_out).reshape(1, d), *sums_of((0, 2, 1, 3)))
    out_half = functools.partial(
        rows_call, body=functools.partial(block_out_kernel, local_len), name="bout", specs=("row", "vec") + ("part",) * 8
    )
    block_output = run(out_half, *out_ops, steps=(0, 2))
    block_output = run(out_half, *out_ops, steps=(2, 4), into=block_output, scale=0.01).reshape(slots, local_len, d)
    pipe.send()
    (grad_in,) = comm.scatter_last(run, ((ff, False),), state2, 0.01)
    add = comm.small_sum(run, after(small, pipe.sent[5], pipe.here[-1], *jax.tree.leaves(state1)[-1:]), 2)
    state1 = comm.scatter_half(run, state1)
    small = add()
    gains = small[: 4 * d]
    group = small[4 * d :]
    add = comm.small_sum(run, after(gains, *jax.tree.leaves(state1)[:1]), 3)
    input_grad = run(
        rows_call, meta, x2, og2, stats, *sums_of(range(4, 8)),
        body=functools.partial(input_grad_kernel, local_len), name="igrad", specs=("row", "row", "stat") + ("part",) * 8,
    ).reshape(slots, local_len, d)
    gains = add()
    add = comm.small_sum(run, gains, 4)
    grad_qkv, grad_proj = comm.scatter_last(run, ((nq // 512, False), (nheads * HD // 512, True)), state1)
    gains = add().reshape(4, d)
    bias_grad = group[:d]
    return (
        block_output,
        input_grad,
        gains[0],
        gains[1],
        gains[2],
        gains[3],
        grad_qkv,
        group[d : d + nq],
        grad_proj,
        bias_grad,
        grad_in,
        group[d + nq :],
        grad_out,
        bias_grad,
    )


def solution(mesh):
    small = mesh.shape["dp"] == 4 and mesh.shape["ctx"] == 2 and mesh.shape["tensor"] == 4
    placed = (
        P("dp", "ctx", None),
        P("dp", "ctx", None),
        P("dp"),
        P(),
        P(),
        P(),
        P(),
        P(("dp", "ctx"), "tensor"),
        P("tensor"),
        P("tensor", ("dp", "ctx")),
        P(),
        P(("dp", "ctx"), "tensor"),
        P("tensor"),
        P("tensor", ("dp", "ctx")),
        P(),
    )
    return jax.shard_map(
        functools.partial(local, small),
        mesh=mesh,
        in_specs=placed,
        out_specs=(
            P("dp", "ctx", None),
            P("dp", "ctx", None),
            P(),
            P(),
            P(),
            P(),
            P(("dp", "ctx"), "tensor"),
            P("tensor"),
            P("tensor", ("dp", "ctx")),
            P(),
            P(("dp", "ctx"), "tensor"),
            P("tensor"),
            P("tensor", ("dp", "ctx")),
            P(),
        ),
        check_vma=False,
    )
```

```python
import functools
import math

import jax
import jax.numpy as jnp
from jax import lax
from jax.experimental import pallas as pl
from jax.experimental.pallas import tpu as pltpu
from jax.sharding import PartitionSpec as P

HD = 256
ROT = 64
NBLK = 8
BF = jnp.bfloat16
F32 = jnp.float32

neg_big = -1e30
inv_sqrt_two = 0.7071067811865476
inv_sqrt_tau = 0.3989422804014327


COST_SCALE = 100


def cost(flops, nbytes, trans=0, k=COST_SCALE):
    flops = max(flops, 300 * nbytes)
    return pl.CostEstimate(flops=int(k * flops), bytes_accessed=int(k * nbytes), transcendentals=int(k * trans))


def params(n, mb=18):
    return pltpu.CompilerParams(
        dimension_semantics=("arbitrary",) * n, vmem_limit_bytes=int(mb * 1024 * 1024)
    )


def nn(a, b):
    return lax.dot_general(a, b, (((1,), (0,)), ((), ())), preferred_element_type=F32)


def nn_rows(a, pieces):
    total, at = None, 0
    for w in pieces:
        y = nn(a[:, at : at + w.shape[0]], w[...])
        total = y if total is None else total + y
        at += w.shape[0]
    return total


def nt(a, b):
    return lax.dot_general(a, b, (((1,), (1,)), ((), ())), preferred_element_type=F32)


def tn(a, b):
    return lax.dot_general(a, b, (((0,), (0,)), ((), ())), preferred_element_type=F32)


def block_cols(r):
    return pl.ds(pl.multiple_of(r, 128), 256)


def row_valid(meta, row0, rows, local_len):
    slot = row0 // local_len
    pos = meta[0] * local_len + row0 % local_len + lax.broadcasted_iota(jnp.int32, (rows, 1), 0)
    return (pos < meta[3 + NBLK + slot]).astype(F32)


def norm_kernel(local_len, meta, x_ref, g_ref, ga, sa, h1_ref, g_out, st_ref, gs_ref):
    rows = x_ref.shape[0]
    i = pl.program_id(0)
    x = x_ref[...].astype(F32)
    mean = jnp.mean(x, axis=-1, keepdims=True)
    cen = x - mean
    inv = lax.rsqrt(jnp.mean(cen * cen, axis=-1, keepdims=True) + 1e-05)
    mask = row_valid(meta, i * rows, rows, local_len)
    lane = lax.broadcasted_iota(jnp.int32, (rows, 128), 1)
    st_ref[...] = jnp.where(lane == 0, mean, inv)
    for r in range(NBLK):
        src = block_cols(meta[1 + r] * 256)
        dst = slice(r * 256, (r + 1) * 256)
        xh = (x_ref[:, src].astype(F32) - mean) * inv
        h1_ref[:, dst] = (xh * ga[:, src] + sa[:, src]).astype(BF)
        gm = g_ref[:, src].astype(F32) * mask
        g_out[:, dst] = gm.astype(BF)
        part = jnp.sum(gm, axis=0, keepdims=True)

        @pl.when(i == 0)
        def _():
            gs_ref[:, src] = part

        @pl.when(i > 0)
        def _():
            gs_ref[:, src] = gs_ref[:, src] + part


def second_norm_kernel(meta, x_ref, st_ref, gf, sf, h2_ref):
    for r in range(NBLK):
        src = block_cols(meta[1 + r] * 256)
        xh = (x_ref[:, src].astype(F32) - st_ref[:, 0:1]) * st_ref[:, 1:2]
        h2_ref[:, r * 256 : (r + 1) * 256] = (xh * gf[:, src] + sf[:, src]).astype(BF)


def second_norm_call(meta, x2, st, gf, sf):
    m, d = x2.shape
    rows = 256
    row_spec = pl.BlockSpec((rows, d), lambda i, mt: (i, 0))
    vec = pl.BlockSpec((1, d), lambda i, mt: (0, 0))
    return pl.pallas_call(
        second_norm_kernel,
        name="norm2",
        grid_spec=pltpu.PrefetchScalarGridSpec(
            num_scalar_prefetch=1,
            grid=(m // rows,),
            in_specs=[row_spec, pl.BlockSpec((rows, 128), lambda i, mt: (i, 0)), vec, vec],
            out_specs=row_spec,
        ),
        out_shape=jax.ShapeDtypeStruct((m, d), BF),
        compiler_params=params(1),
        cost_estimate=cost(5 * m * d, 4 * m * d),
    )(meta, x2, st, gf, sf)


def norm_call(meta, x2, g2, ga, sa, local_len):
    m, d = x2.shape
    rows = 256
    row_spec = pl.BlockSpec((rows, d), lambda i, mt: (i, 0))
    vec = pl.BlockSpec((1, d), lambda i, mt: (0, 0))
    return pl.pallas_call(
        functools.partial(norm_kernel, local_len),
        name="norm",
        grid_spec=pltpu.PrefetchScalarGridSpec(
            num_scalar_prefetch=1,
            grid=(m // rows,),
            in_specs=[row_spec, row_spec, vec, vec],
            out_specs=[row_spec, row_spec, pl.BlockSpec((rows, 128), lambda i, mt: (i, 0)), vec],
        ),
        out_shape=[jax.ShapeDtypeStruct((m, d), BF)] * 2
        + [jax.ShapeDtypeStruct((m, 128), F32), jax.ShapeDtypeStruct((1, d), F32)],
        compiler_params=params(1),
        cost_estimate=cost(20 * m * d, 10 * m * d),
    )(meta, x2, g2, ga, sa)


def rotate_tile(y, cosf, s1, s2, sign):
    head = y[:, :128]
    rot = (
        head * cosf
        + pltpu.roll(head, 96, 1) * (s1 * sign)
        + pltpu.roll(head, 32, 1) * (s2 * sign)
    )
    return rot, y[:, 128:]


def rotated(out, y, cosf, s1, s2):
    local_len = cosf.shape[0]
    for s in range(y.shape[0] // local_len):
        rows = slice(s * local_len, (s + 1) * local_len)
        rot, rest = rotate_tile(y[rows], cosf[...], s1[...], s2[...], 1.0)
        out[rows, :128] = rot.astype(BF)
        out[rows, 128:] = rest.astype(BF)


def kv_kernel(h1, w0, w1, w2, w3, w4, w5, b_ref, cosf, s1, s2, kv_ref):
    part = lax.rem(pl.program_id(0), 2)
    y = nn_rows(h1, (w0, w1, w2, w3, w4, w5)) + b_ref[...]

    @pl.when(part == 0)
    def _():
        rotated(kv_ref, y, cosf, s1, s2)

    @pl.when(part == 1)
    def _():
        kv_ref[...] = y.astype(BF)


def kv_call(h1, pieces, b_qkv, tabs, nheads):
    m, d = h1.shape
    local_len = tabs[0].shape[0]

    def src(j):
        return (0, (j // 2) * 3 + 1 + j % 2)

    tab = pl.BlockSpec((local_len, 128), lambda j: (0, 0))
    return pl.pallas_call(
        kv_kernel,
        name="kv",
        grid=(2 * nheads,),
        in_specs=[
            pl.BlockSpec((m, d), lambda j: (0, 0)),
            *[pl.BlockSpec((p.shape[0], HD), src) for p in pieces],
            pl.BlockSpec((1, HD), src),
            tab,
            tab,
            tab,
        ],
        out_specs=pl.BlockSpec((m, HD), lambda j: (0, j)),
        out_shape=jax.ShapeDtypeStruct((m, 2 * nheads * HD), BF),
        compiler_params=params(1),
        cost_estimate=cost(4 * m * d * nheads * HD, 2 * (m * d + 2 * d * nheads * HD + 2 * m * nheads * HD)),
    )(h1, *pieces, b_qkv, *tabs)


def qd_kernel(nheads, h1, g, w0, w1, w2, w3, w4, w5, b_ref, cosf, s1, s2, q_ref, dob_ref):
    j = pl.program_id(0)
    pieces = (w0, w1, w2, w3, w4, w5)

    @pl.when(j < nheads)
    def _():
        rotated(q_ref, nn_rows(h1, pieces) + b_ref[...], cosf, s1, s2)

    @pl.when(j >= nheads)
    def _():
        dob_ref[...] = nn_rows(g, pieces).astype(BF)


def qd_call(h1, g, pieces, b_qkv, tabs, nheads):
    m, d = h1.shape
    local_len = tabs[0].shape[0]
    full = pl.BlockSpec((m, d), lambda j: (0, 0))

    def src(j):
        return (0, jnp.where(j < nheads, 3 * j, 2 * nheads + j))

    tab = pl.BlockSpec((local_len, 128), lambda j: (0, 0))
    return pl.pallas_call(
        functools.partial(qd_kernel, nheads),
        name="qd",
        grid=(2 * nheads,),
        in_specs=[
            full,
            full,
            *[pl.BlockSpec((p.shape[0], HD), src) for p in pieces],
            pl.BlockSpec((1, HD), lambda j: (0, 3 * jnp.minimum(j, nheads - 1))),
            tab,
            tab,
            tab,
        ],
        out_specs=[
            pl.BlockSpec((m, HD), lambda j: (0, jnp.minimum(j, nheads - 1))),
            pl.BlockSpec((m, HD), lambda j: (0, jnp.maximum(j - nheads, 0))),
        ],
        out_shape=[jax.ShapeDtypeStruct((m, nheads * HD), BF)] * 2,
        compiler_params=params(1),
        cost_estimate=cost(4 * m * d * nheads * HD, 2 * (2 * m * d + 2 * d * nheads * HD + 2 * m * nheads * HD)),
    )(h1, g, *pieces, b_qkv, *tabs)


def attn_kernel(nprev, local_len, meta, q_ref, kv_ref, pv_ref, dob_ref, cosf, s1, s2, ob_ref, dq_ref, dkv_ref, dpv_ref, sc_ref, dq_acc):
    slot = pl.program_id(0)
    ctx = meta[0]
    length = meta[3 + NBLK + slot]
    scale = 1.0 / math.sqrt(HD)
    n_vis = jnp.minimum(ctx, (length + local_len - 1) // local_len)
    q = q_ref[...]
    dob = dob_ref[...]
    own_k = kv_ref[:, :HD]
    own_v = kv_ref[:, HD:]

    ri = lax.broadcasted_iota(jnp.int32, (local_len, local_len), 0)
    ci = lax.broadcasted_iota(jnp.int32, (local_len, local_len), 1)
    s_own = nt(q, own_k) * scale
    s_own = jnp.where((ci <= ri) & (ci < length - ctx * local_len), s_own, neg_big)
    sc_ref[nprev] = s_own

    def prev_rows(jb):
        return pl.ds(pl.multiple_of(jb * local_len, local_len), local_len)

    def score(jb, top):
        s = nt(q, pv_ref[prev_rows(jb), :HD]) * scale
        s = jnp.where(ci[:1] < length - jb * local_len, s, neg_big)
        sc_ref[jb] = s
        return jnp.maximum(top, jnp.max(s, axis=1, keepdims=True))

    top = lax.fori_loop(0, n_vis, score, jnp.max(s_own, axis=1, keepdims=True))

    e_own = jnp.exp(sc_ref[nprev] - top)
    sc_ref[nprev] = e_own

    def expo(jb, tot):
        e = jnp.exp(sc_ref[jb] - top)
        sc_ref[jb] = e
        return tot + jnp.sum(e, axis=1, keepdims=True)

    tot = lax.fori_loop(0, n_vis, expo, jnp.sum(e_own, axis=1, keepdims=True))
    inv = 1.0 / tot
    att = nn((sc_ref[nprev] * inv).astype(BF), own_v)

    def out_step(jb, acc):
        return acc + nn((sc_ref[jb] * inv).astype(BF), pv_ref[prev_rows(jb), HD:])

    att = lax.fori_loop(0, n_vis, out_step, att)
    ob_ref[...] = att.astype(BF)
    delta = jnp.sum(dob.astype(F32) * att, axis=1, keepdims=True)

    def back(p, k, v):
        pb = p.astype(BF)
        ds = (p * (nt(dob, v) - delta)).astype(BF)
        return nn(ds, k) * scale, tn(ds, q) * scale, tn(pb, dob)

    dq, dk, dv = back(sc_ref[nprev] * inv, own_k, own_v)
    dq_acc[...] = dq
    dkv_ref[:, :HD] = dk
    dkv_ref[:, HD:] = dv

    def back_step(jb, carry):
        rows = prev_rows(jb)
        dqp, dkp, dvp = back(sc_ref[jb] * inv, pv_ref[rows, :HD], pv_ref[rows, HD:])
        dq_acc[...] += dqp
        dpv_ref[rows, :HD] = dkp.astype(BF)
        dpv_ref[rows, HD:] = dvp.astype(BF)
        return carry

    lax.fori_loop(0, n_vis, back_step, 0)

    def clear(jb, carry):
        dpv_ref[prev_rows(jb), :] = jnp.zeros((local_len, 2 * HD), BF)
        return carry

    lax.fori_loop(n_vis, nprev, clear, 0)
    rot, rest = rotate_tile(dq_acc[...], cosf[...], s1[...], s2[...], -1.0)
    dq_ref[:, :128] = rot.astype(BF)
    dq_ref[:, 128:] = rest.astype(BF)


def attn_call(meta, q, kv, pv, dob, tabs, nheads):
    local_len = tabs[0].shape[0]
    slots = q.shape[0] // local_len
    nprev = pv.shape[0] // q.shape[0]
    one = pl.BlockSpec((local_len, HD), lambda s, h, mt: (s, h))
    two = pl.BlockSpec((local_len, 2 * HD), lambda s, h, mt: (s, h))
    prev = pl.BlockSpec((nprev * local_len, 2 * HD), lambda s, h, mt: (s, h))
    tab = pl.BlockSpec((local_len, 128), lambda s, h, mt: (0, 0))
    m = q.shape[0]
    return pl.pallas_call(
        functools.partial(attn_kernel, nprev, local_len),
        name="attn",
        grid_spec=pltpu.PrefetchScalarGridSpec(
            num_scalar_prefetch=1,
            grid=(slots, nheads),
            in_specs=[one, two, prev, one, tab, tab, tab],
            out_specs=[one, one, two, prev],
            scratch_shapes=[
                pltpu.VMEM((nprev + 1, local_len, local_len), F32),
                pltpu.VMEM((local_len, HD), F32),
            ],
        ),
        out_shape=[
            jax.ShapeDtypeStruct((m, nheads * HD), BF),
            jax.ShapeDtypeStruct((m, nheads * HD), BF),
            jax.ShapeDtypeStruct((m, 2 * nheads * HD), F32),
            jax.ShapeDtypeStruct((nprev * m, 2 * nheads * HD), BF),
        ],
        compiler_params=params(2, 18 if nprev == 1 else 60),
        cost_estimate=cost(12 * m * nheads * HD * (nprev + 1) * local_len, 20 * m * nheads * HD, m * nheads * (nprev + 1) * local_len),
    )(meta, q, kv, pv, dob, *tabs)


def join_kernel(nheads, dq_ref, dkv_ref, rv_ref, cosf, s1, s2, out_ref, sum_ref):
    i = pl.program_id(0)

    @pl.when(i == 0)
    def _():
        sum_ref[...] = jnp.zeros_like(sum_ref)

    for h in range(nheads):
        base = h * 3 * HD
        out_ref[:, base : base + HD] = dq_ref[:, h * HD : (h + 1) * HD]
        kc = slice(h * 2 * HD, h * 2 * HD + HD)
        vc = slice(h * 2 * HD + HD, (h + 1) * 2 * HD)
        dk = dkv_ref[:, kc] + rv_ref[:, kc].astype(F32)
        rot, rest = rotate_tile(dk, cosf[...], s1[...], s2[...], -1.0)
        out_ref[:, base + HD : base + HD + 128] = rot.astype(BF)
        out_ref[:, base + HD + 128 : base + 2 * HD] = rest.astype(BF)
        out_ref[:, base + 2 * HD : base + 3 * HD] = (dkv_ref[:, vc] + rv_ref[:, vc].astype(F32)).astype(BF)
    sum_ref[...] += jnp.sum(out_ref[...].astype(F32), axis=0, keepdims=True)


def join_call(dq, dkv, rv, tabs, nheads):
    m = dq.shape[0]
    local_len = tabs[0].shape[0]
    rows = 256
    per = local_len // rows

    def spec(c):
        return pl.BlockSpec((rows, c), lambda i: (i, 0))

    tab = pl.BlockSpec((rows, 128), lambda i: (i % per, 0))
    n = 3 * nheads * HD
    return pl.pallas_call(
        functools.partial(join_kernel, nheads),
        name="join",
        grid=(m // rows,),
        in_specs=[spec(nheads * HD), spec(2 * nheads * HD), spec(2 * nheads * HD), tab, tab, tab],
        out_specs=[spec(n), pl.BlockSpec((1, n), lambda i: (0, 0))],
        out_shape=[jax.ShapeDtypeStruct((m, n), BF), jax.ShapeDtypeStruct((1, n), F32)],
        compiler_params=params(1),
        cost_estimate=cost(10 * m * n, 8 * m * n),
    )(dq, dkv, rv, *tabs)


def hidden_kernel(h2, w0, w1, w2, w3, w4, w5, b_ref, gb_ref, dg_ref):
    u = nn_rows(h2, (w0, w1, w2, w3, w4, w5)) + b_ref[...]
    cdf = 0.5 * (1.0 + lax.erf(u * inv_sqrt_two))
    gb_ref[...] = (u * cdf).astype(BF)
    dg_ref[...] = (cdf + u * (jnp.exp(-0.5 * u * u) * inv_sqrt_tau)).astype(BF)


def hidden_call(h2, pieces, b_in):
    m, d = h2.shape
    f = pieces[0].shape[1]
    t = 256
    col = pl.BlockSpec((m, t), lambda j: (0, j))
    w_specs = [pl.BlockSpec((p.shape[0], t), lambda j: (0, j)) for p in pieces]
    return pl.pallas_call(
        hidden_kernel,
        name="hidden",
        grid=(f // t,),
        in_specs=[pl.BlockSpec((m, d), lambda j: (0, 0)), *w_specs, pl.BlockSpec((1, t), lambda j: (0, j))],
        out_specs=[col, col],
        out_shape=[jax.ShapeDtypeStruct((m, f), BF)] * 2,
        compiler_params=params(1),
        cost_estimate=cost(2 * m * d * f, 2 * (m * d + d * f + 2 * m * f), 2 * m * f),
    )(h2, *pieces, b_in)


def dhid_kernel(g, w0, w1, w2, w3, w4, w5, dg_ref, du_ref, sum_ref):
    a = nn_rows(g, (w0, w1, w2, w3, w4, w5))
    du = (a * dg_ref[...].astype(F32)).astype(BF)
    du_ref[...] = du
    sum_ref[...] = jnp.sum(du.astype(F32), axis=0, keepdims=True)


def dhid_call(g, pieces, dg):
    m, d = g.shape
    f = dg.shape[1]
    t = 256
    col = pl.BlockSpec((m, t), lambda j: (0, j))
    w_specs = [pl.BlockSpec((p.shape[0], t), lambda j: (0, j)) for p in pieces]
    return pl.pallas_call(
        dhid_kernel,
        name="dhid",
        grid=(f // t,),
        in_specs=[pl.BlockSpec((m, d), lambda j: (0, 0))] + w_specs + [col],
        out_specs=[col, pl.BlockSpec((1, t), lambda j: (0, j))],
        out_shape=[jax.ShapeDtypeStruct((m, f), BF), jax.ShapeDtypeStruct((1, f), F32)],
        compiler_params=params(1),
        cost_estimate=cost(2 * m * d * f, 2 * (m * d + d * f + 2 * m * f)),
    )(g, *pieces, dg)


def out_kernel(count, ob, gb, *refs):
    j = pl.program_id(0)
    ps, os, ya, yb = refs[:count], refs[count : 2 * count], refs[-2], refs[-1]
    each = 4 // count
    for k in range(4):

        @pl.when(j == k)
        def _():
            y = ya if k < 2 else yb
            y[...] = (nt(ob[...], ps[k // each][...]) + nt(gb[...], os[k // each][...])).astype(BF)


def piece_spec(count, i, cols, at=0, prefetch=False):
    each = 4 // count

    def place(j, *_):
        return (jnp.clip(j - i * each, 0, each - 1), at)

    if prefetch:
        return pl.BlockSpec((256, cols), lambda j, mt: place(j))
    return pl.BlockSpec((256, cols), lambda j: place(j))


def out_call(ob, gb, proj, out, scale=COST_SCALE):
    m, f = gb.shape
    nf = ob.shape[1]
    count = len(out)
    last = proj[0].shape[1] // nf - 1
    part = jax.ShapeDtypeStruct((m, 512), BF)
    return pl.pallas_call(
        functools.partial(out_kernel, count),
        name="outp",
        grid=(4,),
        in_specs=[pl.BlockSpec((m, nf), lambda j: (0, 0)), pl.BlockSpec((m, f), lambda j: (0, 0))]
        + [piece_spec(count, i, nf, last) for i in range(count)]
        + [piece_spec(count, i, f) for i in range(count)],
        out_specs=[
            pl.BlockSpec((m, 256), lambda j: (0, jnp.minimum(j, 1))),
            pl.BlockSpec((m, 256), lambda j: (0, jnp.maximum(j - 2, 0))),
        ],
        out_shape=[part, part],
        compiler_params=params(1),
        cost_estimate=cost(2048 * m * (f + nf), 2 * (m * f + m * nf + 1024 * (f + nf) + 1024 * m), k=scale),
    )(ob, gb, *proj, *out)


def back_kernel(meta, dqkv, du, w10, w11, w12, w20, w21, w22, x_ref, st_ref, ga, gf, prev, da_ref, db_ref, sums_ref):
    j = pl.program_id(0)
    for w1, w2, dn_ref, mine in ((w10, w20, da_ref, j < 2), (w11, w21, db_ref, j == 2), (w12, w22, db_ref, j == 3)):

        @pl.when(mine)
        def _():
            dh1 = nt(dqkv[...], w1[...])
            dh2 = nt(du[...], w2[...])
            xh = (x_ref[...].astype(F32) - st_ref[:, 0:1]) * st_ref[:, 1:2]
            dn_ref[...] = (dh1 * ga[...] + dh2 * gf[...]).astype(BF)
            sums_ref[0:1, :] = jnp.sum(dh1 * xh, axis=0, keepdims=True)
            sums_ref[1:2, :] = jnp.sum(dh1, axis=0, keepdims=True)
            sums_ref[2:3, :] = jnp.sum(dh2 * xh, axis=0, keepdims=True)
            sums_ref[3:4, :] = jnp.sum(dh2, axis=0, keepdims=True)


def back_call(meta, dqkv, du, g1, g2, x2, st, ga, gf, sums, half):
    m, d = x2.shape
    nq = dqkv.shape[1]
    f = du.shape[1]
    n = d // 4

    def absolute(rows):
        return pl.BlockSpec((rows, 256), lambda j, mt: (0, mt[1 + 4 * half + j]))

    part = jax.ShapeDtypeStruct((m, n), BF)
    at = slice(3 * half, 3 * half + 3)
    return pl.pallas_call(
        back_kernel,
        name="backn",
        grid_spec=pltpu.PrefetchScalarGridSpec(
            num_scalar_prefetch=1,
            grid=(4,),
            in_specs=[
                pl.BlockSpec((m, nq), lambda j, mt: (0, 0)),
                pl.BlockSpec((m, f), lambda j, mt: (0, 0)),
                pl.BlockSpec((256, nq), lambda j, mt: (jnp.minimum(j, 1), 0)),
                pl.BlockSpec((256, nq), lambda j, mt: (0, 0)),
                pl.BlockSpec((256, nq), lambda j, mt: (0, 0)),
                pl.BlockSpec((256, f), lambda j, mt: (jnp.minimum(j, 1), 0)),
                pl.BlockSpec((256, f), lambda j, mt: (0, 0)),
                pl.BlockSpec((256, f), lambda j, mt: (0, 0)),
                absolute(m),
                pl.BlockSpec((m, 128), lambda j, mt: (0, 0)),
                absolute(1),
                absolute(1),
                pl.BlockSpec(memory_space=pl.ANY),
            ],
            out_specs=[
                pl.BlockSpec((m, n // 2), lambda j, mt: (0, jnp.minimum(j, 1))),
                pl.BlockSpec((m, n // 2), lambda j, mt: (0, jnp.maximum(j - 2, 0))),
                absolute(4),
            ],
        ),
        out_shape=[part, part, jax.ShapeDtypeStruct((4, d), F32)],
        input_output_aliases={13: 2},
        compiler_params=params(1),
        cost_estimate=cost(4 * m * n * (f + nq), 2 * (m * f + m * nq + 2 * n * (f + nq) + 4 * m * n)),
    )(meta, dqkv, du, *g1[at], *g2[at], x2, st, ga, gf, sums)


def wgrad_kernel(pairs, adds, split, meta, *refs):
    j = pl.program_id(0)
    start = 0
    for p, count in enumerate(pairs):
        a, b = refs[2 * p], refs[2 * p + 1]

        @pl.when((j >= start) & (j < start + count))
        def _():
            y = tn(a[...], b[...])
            if adds:
                y = y + refs[2 * len(pairs)][...].astype(F32)
            if not split:
                refs[-1][...] = y.astype(BF)
                return
            keep, send = refs[-2:]
            n = y.shape[0] // 4
            swap = meta[2 + NBLK] > 0
            keep[:n] = y[:n].astype(BF)
            keep[n:] = jnp.where(swap, y[2 * n : 3 * n], y[n : 2 * n]).astype(BF)
            send[:n] = jnp.where(swap, y[n : 2 * n], y[2 * n : 3 * n]).astype(BF)
            send[n:] = y[3 * n :].astype(BF)

        start += count


def wgrad_call(meta, *flat, half, add=None, split=False):
    pairs = list(zip(flat[::2], flat[1::2]))
    m, d = pairs[0][0].shape
    t = 512
    counts = tuple(b.shape[1] // t for _, b in pairs)
    total = sum(counts)
    in_specs, ops, start = [], [], 0
    for (a, b), c in zip(pairs, counts):
        in_specs.append(pl.BlockSpec((m, d // 2), lambda j, mt: (0, half)))
        in_specs.append(
            pl.BlockSpec((m, t), lambda j, mt, s=start, c=c: (0, jnp.clip(j - s, 0, c - 1)))
        )
        ops += [a, b]
        start += c
    rows = d // 4 if split else d // 2
    if add is not None:
        in_specs.append(pl.BlockSpec((d // 2, t), lambda j, mt: (0, j)))
        ops.append(add)
    out_spec = pl.BlockSpec((rows, t), lambda j, mt: (0, j))
    out_shape = jax.ShapeDtypeStruct((rows, total * t), BF)
    return pl.pallas_call(
        functools.partial(wgrad_kernel, counts, add is not None, split),
        name="wgrad",
        grid_spec=pltpu.PrefetchScalarGridSpec(
            num_scalar_prefetch=1,
            grid=(total,),
            in_specs=in_specs,
            out_specs=[out_spec, out_spec] if split else out_spec,
        ),
        out_shape=[out_shape, out_shape] if split else out_shape,
        compiler_params=params(1),
        cost_estimate=cost(m * d * total * t, 2 * (m * d // 2 * len(pairs) + m * total * t + d * total * t)),
    )(meta, *ops)


def pack_kernel(*refs):
    out, at = refs[-1], 0
    for ref in refs[:-1]:
        n = ref.shape[0]
        out[at : at + n] = ref[...]
        at += n


def pack_call(*pieces):
    rows = sum(p.shape[0] for p in pieces)
    cols = pieces[0].shape[1]
    t = 512
    return pl.pallas_call(
        pack_kernel,
        name="pack",
        grid=(cols // t,),
        in_specs=[pl.BlockSpec((p.shape[0], t), lambda j: (0, j)) for p in pieces],
        out_specs=pl.BlockSpec((rows, t), lambda j: (0, j)),
        out_shape=jax.ShapeDtypeStruct((rows, cols), BF),
        compiler_params=params(1),
        cost_estimate=cost(0, 4 * rows * cols),
    )(*pieces)


def half_sum_kernel(keep, got, mid, send):
    n = mid.shape[0]
    mid[...] = keep[:n].astype(F32) + got[:n].astype(F32)
    send[...] = (keep[n:].astype(F32) + got[n:].astype(F32)).astype(BF)


def half_sum_call(keep, got):
    rows, cols = keep.shape
    t = 512
    n = rows // 2
    small = pl.BlockSpec((n, t), lambda j: (0, j))
    return pl.pallas_call(
        half_sum_kernel,
        name="hsum",
        grid=(cols // t,),
        in_specs=[pl.BlockSpec((rows, t), lambda j: (0, j))] * 2,
        out_specs=[small] * 2,
        out_shape=[jax.ShapeDtypeStruct((n, cols), F32), jax.ShapeDtypeStruct((n, cols), BF)],
        compiler_params=params(1),
        cost_estimate=cost(4 * n * cols, 14 * n * cols),
    )(keep, got)


def last_sum_kernel(plan, mid, got, *outs):
    j = pl.program_id(0)
    at = 0
    for (count, turned), out in zip(plan, outs):

        @pl.when((j >= at) & (j < at + count))
        def _():
            v = mid[...] + got[...].astype(F32)
            out[...] = v.T if turned else v

        at += count


def last_sum_call(mid, got, plan, scale):
    n, cols = mid.shape
    t = 512
    block = pl.BlockSpec((n, t), lambda j: (0, j))
    out_specs, out_shape, at = [], [], 0
    for count, turned in plan:
        def place(j, at=at, count=count):
            return jnp.clip(j - at, 0, count - 1)

        if turned:
            out_specs.append(pl.BlockSpec((t, n), lambda j, f=place: (f(j), 0)))
            out_shape.append(jax.ShapeDtypeStruct((count * t, n), F32))
        else:
            out_specs.append(pl.BlockSpec((n, t), lambda j, f=place: (0, f(j))))
            out_shape.append(jax.ShapeDtypeStruct((n, count * t), F32))
        at += count
    return pl.pallas_call(
        functools.partial(last_sum_kernel, plan),
        name="lsum",
        grid=(cols // t,),
        in_specs=[block, block],
        out_specs=out_specs,
        out_shape=out_shape,
        compiler_params=params(1),
        cost_estimate=cost(2 * n * cols, 10 * n * cols, k=scale),
    )(mid, got)


def by_role(meta, refs, body):
    @pl.when(meta[1 + NBLK] > 0)
    def _():
        body(refs[0::2])

    @pl.when(meta[1 + NBLK] == 0)
    def _():
        body(refs[1::2])


def block_out_kernel(local_len, first, meta, x_ref, b_ref, *refs):
    y_ref = refs[-1]
    rows = x_ref.shape[0]
    mask = row_valid(meta, (first + pl.program_id(0)) * rows, rows, local_len)

    def body(parts):
        for r in range(NBLK):
            col = block_cols(meta[1 + r] * 256)
            s = parts[r // 2][:, r % 2 * 256 : r % 2 * 256 + 256].astype(F32)
            y_ref[:, col] = (mask * (x_ref[:, col].astype(F32) + s + b_ref[:, col])).astype(BF)

    by_role(meta, refs[:8], body)


def input_grad_kernel(local_len, first, meta, x_ref, g_ref, st_ref, *refs):
    y_ref = refs[-1]
    rows = x_ref.shape[0]
    mask = row_valid(meta, (first + pl.program_id(0)) * rows, rows, local_len)
    mean = st_ref[:, 0:1]
    inv = st_ref[:, 1:2]
    d = x_ref.shape[1]

    def body(parts):
        def dn_of(r):
            return parts[r // 2][:, r % 2 * 256 : r % 2 * 256 + 256].astype(F32)

        one = jnp.zeros((rows, 256), F32)
        two = jnp.zeros((rows, 256), F32)
        for r in range(NBLK):
            dn = dn_of(r)
            one += dn
            two += dn * (x_ref[:, block_cols(meta[1 + r] * 256)].astype(F32) - mean)
        one = jnp.sum(one, axis=1, keepdims=True) / d
        two = jnp.sum(two, axis=1, keepdims=True) * inv / d
        slope = inv * inv * two
        shift = slope * mean - inv * one
        for r in range(NBLK):
            col = block_cols(meta[1 + r] * 256)
            y = g_ref[:, col].astype(F32) * mask + inv * dn_of(r)
            y_ref[:, col] = (y + (shift - slope * x_ref[:, col].astype(F32))).astype(BF)

    by_role(meta, refs[:8], body)


def rows_call(meta, *ops, body, name, specs, steps=None, into=None, scale=COST_SCALE):
    rows = 256
    m, d = ops[0].shape
    first, last = steps or (0, m // rows)
    made = {
        "row": pl.BlockSpec((rows, d), lambda i, mt: (first + i, 0)),
        "part": pl.BlockSpec((rows, d // 4), lambda i, mt: (first + i, 0)),
        "stat": pl.BlockSpec((rows, 128), lambda i, mt: (first + i, 0)),
        "vec": pl.BlockSpec((1, d), lambda i, mt: (0, 0)),
    }
    in_specs = [made[s] for s in specs]
    aliases = {}
    if into is not None:
        aliases = {1 + len(ops): 0}
        in_specs.append(pl.BlockSpec(memory_space=pl.ANY))
        ops += (into,)
    return pl.pallas_call(
        functools.partial(body, first),
        name=name,
        grid_spec=pltpu.PrefetchScalarGridSpec(
            num_scalar_prefetch=1,
            grid=(last - first,),
            in_specs=in_specs,
            out_specs=made["row"],
        ),
        out_shape=jax.ShapeDtypeStruct((m, d), BF),
        input_output_aliases=aliases,
        compiler_params=params(1),
        cost_estimate=cost(10 * (last - first) * rows * d, 8 * (last - first) * rows * d, k=scale),
    )(meta, *ops)


def after(v, *others):
    return lax.optimization_barrier((v,) + others)[0]


class Order:
    def __init__(self):
        self.last = ()

    def __call__(self, f, first, *rest, **named):
        out = f(after(first, *self.last), *rest, **named)
        self.last = (jax.tree.leaves(out)[0],)
        return out


def add_bf(a, b):
    return lax.optimization_barrier((a.astype(F32) + b.astype(F32)).astype(BF))


def pick_bf(a, b, middle, other):
    total = (a.astype(F32) + b.astype(F32)).astype(BF)
    return lax.optimization_barrier(jnp.where(middle > 0, total, other))


class Pipe:
    LAG = 3

    def __init__(self, run, middle, count):
        self.run, self.middle, self.count = run, middle, count
        self.parts, self.got, self.sums, self.crossed = [], [], [], []
        self.here, self.sent = [], []

    def send(self, part=None):
        step = len(self.got)
        back = step - self.LAG
        pairs = []
        v = part
        if part is not None:
            self.parts.append(part)
            pairs += [(0, 1), (3, 2)]
        if back >= 0:
            pairs += [(1, 0), (2, 3)]
            a, b = self.sums[back], self.crossed[back]
            if part is None:
                v = self.run(add_bf, a, b)
            else:
                v = self.run(pick_bf, a, b, self.middle, part)
        got = lax.ppermute(v, "tensor", pairs)
        self.got.append(got)
        if back >= 0:
            self.here.append(v)
            self.sent.append(got)

    def cross(self):
        k = len(self.sums)
        v = self.run(add_bf, self.parts[k], self.got[k])
        self.sums.append(v)
        self.crossed.append(lax.ppermute(v, "tensor", [(1, 2), (2, 1)]))


class PlainPipe:
    def __init__(self, run, middle, count):
        self.here, self.sent, self.sums = [], [], []

    def send(self, part=None):
        if part is not None:
            total = lax.psum(part, "tensor")
            self.here.append(total)
            self.sent.append(total)

    def cross(self):
        pass


class SmallMesh:
    def x(self, v):
        return lax.ppermute(v, "dp", [(0, 2), (2, 0), (1, 3), (3, 1)])

    def core(self, v):
        return lax.ppermute(v, "dp", [(0, 1), (1, 0), (2, 3), (3, 2)])

    def y(self, v):
        return lax.ppermute(v, "ctx", [(0, 1), (1, 0)])

    def perm(self):
        r = jnp.arange(NBLK, dtype=jnp.int32)
        dp = lax.axis_index("dp") ^ (((r >> 1) & 1) * 2 + (r >> 2))
        return dp * 2 + (lax.axis_index("ctx") ^ (r & 1))

    def middle(self):
        z = lax.axis_index("tensor")
        return ((z == 1) | (z == 2)).astype(jnp.int32)

    pipe = Pipe

    def first_hop(self, own, earlier=None):
        if earlier is None:
            return self.x(own), self.y(own)
        return self.x(after(own, earlier)), self.y(own)

    def second_hop(self, hop, earlier=()):
        return self.x(after(hop[1], hop[0], *earlier))

    def waited(self, hop):
        return hop

    def near_pieces(self, near):
        return near

    def near(self, run, own, hop):
        v = run(pack_call, own, hop[1])
        return v, self.core(v)

    def pieces(self, near, hop, diag, earlier=()):
        return near[0], hop[0], diag, near[1], self.core(after(hop[0], *earlier[:1])), self.core(after(diag, *earlier))

    def turn(self, v, first):
        pairs = []
        for dp in range(4):
            for c in range(2):
                to = (dp ^ 2) * 2 + c if dp % 2 != first else dp * 2 + (c ^ 1)
                pairs.append((dp * 2 + c, to))
        return lax.ppermute(v, ("dp", "ctx"), pairs)

    def scatter_cross(self, theirs):
        return self.core(theirs)

    def scatter_own(self, run, meta, pairs, got):
        keep, send = run(wgrad_call, meta, *pairs, half=0, add=got, split=True)
        return keep, self.turn(send, 1)

    def scatter_half(self, run, parts):
        mid, send = run(half_sum_call, *parts)
        return mid, self.turn(send, 0)

    def scatter_last(self, run, plan, parts, scale=COST_SCALE):
        return run(last_sum_call, *parts, plan=plan, scale=scale)

    def previous(self, kv, slots):
        return lax.ppermute(kv, "ctx", [(0, 1)])

    def give_back(self, dpv, dkv, slots):
        return dkv, lax.ppermute(dpv, "ctx", [(1, 0)])

    def small_sum(self, run, v, step):
        def add(a, b):
            return a + b

        if step == 0:
            got = self.core(v)
        elif step == 1:
            got = self.x(v)
        elif step == 2:
            got = self.y(v)
        elif step == 3:
            got = lax.ppermute(v, "tensor", [(0, 1), (1, 0), (2, 3), (3, 2)])
        else:
            got = lax.ppermute(v, "tensor", [(0, 2), (2, 0), (1, 3), (3, 1)])
        return lambda: run(add, v, got)


class AnyMesh:
    def perm(self):
        return jnp.arange(NBLK, dtype=jnp.int32)

    def middle(self):
        return jnp.ones((), jnp.int32)

    pipe = PlainPipe

    def first_hop(self, own, earlier=None):
        return lax.all_gather(own, ("dp", "ctx"), axis=0, tiled=True)

    def second_hop(self, hop, earlier=()):
        return ()

    def waited(self, hop):
        return (hop,)

    def near_pieces(self, near):
        return near

    def near(self, run, own, hop):
        return hop[:512], hop[1024:1536]

    def pieces(self, near, hop, diag, earlier=()):
        return near[0], hop[512:768], hop[768:1024], near[1], hop[1536:1792], hop[1792:]

    def scatter_cross(self, theirs):
        return theirs

    def scatter_own(self, run, meta, pairs, got):
        full = jnp.concatenate([run(wgrad_call, meta, *pairs, half=0), got], axis=0)
        return lax.psum_scatter(full, ("dp", "ctx"), scatter_dimension=0, tiled=True).astype(F32)

    def scatter_half(self, run, parts):
        return parts

    def scatter_last(self, run, plan, parts, scale=None):
        outs, at = [], 0
        for count, turned in plan:
            v = parts[:, at * 512 : (at + count) * 512]
            outs.append(v.T if turned else v)
            at += count
        return outs

    def previous(self, kv, slots):
        own = kv.reshape(slots, -1, kv.shape[1])
        full = lax.all_gather(own, "ctx", axis=1, tiled=True)
        return full.reshape(-1, kv.shape[1])

    def give_back(self, dpv, dkv, slots):
        cols = dkv.shape[1]
        full = dpv.reshape(slots, -1, cols)
        got = lax.psum_scatter(full, "ctx", scatter_dimension=1, tiled=True)
        return dkv, got.reshape(-1, cols)

    def small_sum(self, run, v, step):
        got = v
        if step == 0:
            got = lax.psum(v, ("dp", "ctx"))
        elif step == 3:
            got = lax.psum(v, "tensor")
        return lambda: got


def rotary_tables(positions):
    half_rot = ROT // 2
    lane = jnp.arange(128, dtype=jnp.int32)
    exponent = (lane % half_rot).astype(F32) * (2.0 / ROT)
    angles = positions[:, None] * jnp.exp(-math.log(10000.0) * exponent)[None, :]
    cos_all, sin_all = jnp.cos(angles), jnp.sin(angles)
    cosf = jnp.where(lane < ROT, cos_all, 1.0)
    s1 = jnp.where(lane < half_rot, -sin_all, 0.0)
    s2 = jnp.where((lane >= half_rot) & (lane < ROT), sin_all, 0.0)
    return cosf, s1, s2


def local(small, block_input, out_grad, lengths, attn_gain, attn_shift, ffn_gain, ffn_shift, w_qkv, b_qkv, w_proj, b_proj, w_in, b_in, w_out, b_out):
    comm = SmallMesh() if small else AnyMesh()
    slots, local_len, d = block_input.shape
    m = slots * local_len
    nheads = b_qkv.shape[0] // (3 * HD)
    nq = 3 * nheads * HD
    ctx = lax.axis_index("ctx")
    core = lax.axis_index("dp") % 2
    meta = jnp.concatenate(
        [ctx[None].astype(jnp.int32), comm.perm(), comm.middle()[None], core[None].astype(jnp.int32), lengths]
    )

    run = Order()
    x2 = block_input.reshape(m, d)
    og2 = out_grad.reshape(m, d)
    ga, sa, gf, sf = (v.reshape(1, d) for v in (attn_gain, attn_shift, ffn_gain, ffn_shift))
    bq = b_qkv.reshape(1, nq)
    positions = ctx * local_len + jnp.arange(local_len, dtype=jnp.int32)
    tabs = rotary_tables(positions.astype(F32))

    own1 = jnp.concatenate([w_qkv, w_proj.T], axis=1).astype(BF)
    hop1 = comm.first_hop(own1)
    own2 = w_in.astype(BF)
    own3 = w_out.T.astype(BF)
    run.last = (own1, own2, own3)
    hop2 = comm.first_hop(own2, hop1[0])
    h1, g, stats, g_sum = run(norm_call, meta, x2, og2, ga, sa, local_len)
    diag1 = comm.second_hop(hop1)
    near1 = comm.near(run, own1, hop1)
    g1 = comm.pieces(near1, hop1, diag1)
    near2 = comm.near(run, own2, hop2)
    kv = run(kv_call, h1, g1, bq, tabs, nheads)
    pv = comm.previous(kv, slots)
    diag2 = comm.second_hop(hop2, (kv,))
    hop3 = comm.first_hop(own3, diag2)
    q, dob = run(qd_call, h1, g, g1, bq, tabs, nheads)
    g2 = comm.pieces(near2, hop2, diag2, (kv, q))
    diag3 = comm.second_hop(hop3)
    h2 = run(second_norm_call, meta, x2, stats, gf, sf)
    gb, dg = run(hidden_call, h2, g2, b_in.reshape(1, -1))
    near3 = comm.near(run, own3, hop3)
    ob, dq, dkv, dpv = run(attn_call, meta, q, kv, pv, dob, tabs, nheads)
    dkv, rv = comm.give_back(dpv, dkv, slots)
    g3 = comm.near_pieces(near3)

    pipe = comm.pipe(run, meta[1 + NBLK], 8)
    ff = gb.shape[1] // 512
    out0, out2 = run(out_call, ob, gb, (g1[0], g1[3]), g3, 0.01)
    pipe.send(out0)
    pipe.send(out2)
    g3 = comm.pieces(near3, hop3, diag3, (ob, out0))
    cross3 = comm.scatter_cross(run(wgrad_call, meta, g, gb, half=1))
    far = (1, 2, 4, 5)
    out1, out3 = run(out_call, ob, gb, [g1[k] for k in far], [g3[k] for k in far])
    pipe.cross()
    pipe.send(after(out1, *pipe.sums))
    du, bin_sum = run(dhid_call, g, g3, dg)
    pipe.cross()
    state3 = comm.scatter_own(run, meta, (g, gb), cross3)
    dqkv, bqkv_sum = run(join_call, dq, dkv, rv, tabs, nheads)
    pipe.send(out3)
    gain_sums = jnp.zeros((4, d), F32)
    pipe.cross()
    dn0, dn1, gain_sums = run(back_call, meta, dqkv, du, g1, g2, x2, stats, ga, gf, gain_sums, 0)
    pipe.send(dn0)
    pipe.cross()
    pipe.send(dn1)
    state3 = comm.scatter_half(run, state3)
    dn2, dn3, gain_sums = run(back_call, meta, dqkv, du, g1, g2, x2, stats, ga, gf, gain_sums, 1)
    pipe.cross()
    pipe.send(dn2)
    small = jnp.concatenate([gain_sums.reshape(-1), g_sum.reshape(-1), bqkv_sum.reshape(-1), bin_sum.reshape(-1)])
    add = comm.small_sum(run, small, 0)
    cross2 = comm.scatter_cross(run(wgrad_call, after(meta, jax.tree.leaves(state3)[-1]), h2, du, half=1))
    small = add()
    add = comm.small_sum(run, small, 1)
    theirs1 = run(wgrad_call, meta, h1, dqkv, g, ob, half=1)
    small = add()
    pipe.cross()
    pipe.send(dn3)
    state2 = comm.scatter_own(run, meta, (h2, du), cross2)
    cross1 = comm.scatter_cross(after(theirs1, *jax.tree.leaves(state2)[:1]))
    (grad_out,) = comm.scatter_last(run, ((ff, True),), state3)
    pipe.cross()
    pipe.send()
    state1 = comm.scatter_own(run, meta, (h1, dqkv, g, ob), cross1)
    pipe.cross()
    pipe.send()
    state2 = comm.scatter_half(run, state2)

    def sums_of(order):
        return [v for c in order for v in (pipe.here[c], pipe.sent[c])]

    out_ops = (meta, x2, (b_proj + b_out).reshape(1, d), *sums_of((0, 2, 1, 3)))
    out_half = functools.partial(
        rows_call, body=functools.partial(block_out_kernel, local_len), name="bout", specs=("row", "vec") + ("part",) * 8
    )
    block_output = run(out_half, *out_ops, steps=(0, 2))
    block_output = run(out_half, *out_ops, steps=(2, 4), into=block_output, scale=0.01).reshape(slots, local_len, d)
    pipe.send()
    (grad_in,) = comm.scatter_last(run, ((ff, False),), state2, 0.01)
    add = comm.small_sum(run, after(small, pipe.sent[5], pipe.here[-1], *jax.tree.leaves(state1)[-1:]), 2)
    state1 = comm.scatter_half(run, state1)
    small = add()
    gains = small[: 4 * d]
    group = small[4 * d :]
    add = comm.small_sum(run, after(gains, *jax.tree.leaves(state1)[:1]), 3)
    input_grad = run(
        rows_call, meta, x2, og2, stats, *sums_of(range(4, 8)),
        body=functools.partial(input_grad_kernel, local_len), name="igrad", specs=("row", "row", "stat") + ("part",) * 8,
    ).reshape(slots, local_len, d)
    gains = add()
    add = comm.small_sum(run, gains, 4)
    grad_qkv, grad_proj = comm.scatter_last(run, ((nq // 512, False), (nheads * HD // 512, True)), state1)
    gains = add().reshape(4, d)
    bias_grad = group[:d]
    return (
        block_output,
        input_grad,
        gains[0],
        gains[1],
        gains[2],
        gains[3],
        grad_qkv,
        group[d : d + nq],
        grad_proj,
        bias_grad,
        grad_in,
        group[d + nq :],
        grad_out,
        bias_grad,
    )


def solution(mesh):
    small = mesh.shape["dp"] == 4 and mesh.shape["ctx"] == 2 and mesh.shape["tensor"] == 4
    placed = (
        P("dp", "ctx", None),
        P("dp", "ctx", None),
        P("dp"),
        P(),
        P(),
        P(),
        P(),
        P(("dp", "ctx"), "tensor"),
        P("tensor"),
        P("tensor", ("dp", "ctx")),
        P(),
        P(("dp", "ctx"), "tensor"),
        P("tensor"),
        P("tensor", ("dp", "ctx")),
        P(),
    )
    return jax.shard_map(
        functools.partial(local, small),
        mesh=mesh,
        in_specs=placed,
        out_specs=(
            P("dp", "ctx", None),
            P("dp", "ctx", None),
            P(),
            P(),
            P(),
            P(),
            P(("dp", "ctx"), "tensor"),
            P("tensor"),
            P("tensor", ("dp", "ctx")),
            P(),
            P(("dp", "ctx"), "tensor"),
            P("tensor"),
            P("tensor", ("dp", "ctx")),
            P(),
        ),
        check_vma=False,
    )
```
